32 devices in a mesh: dp: 8 (over y, x, core), mp: 4 (over z).
Axes of the slice: x: 2, y: 2, z: 4, core: 2. Of those that a mesh axis runs over, the one named last changes fastest.
Arguments:
- frames: bfloat16 [16384, 640], P('dp'), may hold values from -6 to 6
- seg_ids: int32 [16384], P('dp'), may hold values from 0 to 15, as said below
- qkv_weight: bfloat16 [3, 640, 768], P(None, 'dp', 'mp'), may hold values from -0.25 to 0.25
- qkv_bias: float32 [2, 768], P(None, 'mp'), may hold values from -3 to 3
- out_weight: bfloat16 [768, 640], P('mp', 'dp'), may hold values from -1.5 to 1.5
- out_bias: float32 [640], replicated, may hold values from -3 to 3
- gain_one: float32 [640], replicated, may hold values from 0.1 to 1.9
- shift_one: float32 [640], replicated, may hold values from -3 to 3
- up_weight: bfloat16 [640, 2240], P('dp', 'mp'), may hold values from -0.25 to 0.25
- up_bias: float32 [2240], P('mp'), may hold values from -3 to 3
- down_weight: bfloat16 [2240, 640], P('mp', 'dp'), may hold values from -0.125 to 0.125
- down_bias: float32 [640], replicated, may hold values from -3 to 3
- gain_two: float32 [640], replicated, may hold values from 0.1 to 1.9
- shift_two: float32 [640], replicated, may hold values from -3 to 3
- cotangent: bfloat16 [16384, 640], P('dp'), may hold values from -6 to 6
Outputs:
- output_frames: bfloat16 [16384, 640], P(('dp', 'mp'))
- frames_grad: bfloat16 [16384, 640], P(('dp', 'mp'))
- qkv_grad: float32 [3, 640, 768], P(None, 'dp', 'mp')
- qkv_bias_grad: float32 [2, 768], P(None, 'mp')
- out_grad: float32 [768, 640], P('mp', 'dp')
- out_bias_grad: float32 [640], replicated
- gain_one_grad: float32 [640], replicated
- shift_one_grad: float32 [640], replicated
- up_grad: float32 [640, 2240], P('dp', 'mp')
- up_bias_grad: float32 [2240], P('mp')
- down_grad: float32 [2240, 640], P('mp', 'dp')
- down_bias_grad: float32 [640], replicated
- gain_two_grad: float32 [640], replicated
- shift_two_grad: float32 [640], replicated
The draws below stay inside these ranges and needn't reach their ends.
Inputs may be any that keep to these rules, and one draw needn't show every extreme that they name: `seg_ids`: each block of 2048 frames that one index of dp holds contains 1 to 16 whole utterances laid end to end; within the block the number starts at 0 and rises by one at each new utterance. In every draw some block holds a single utterance of 2048 frames and some block holds 16 utterances.
All inputs are finite; a program needn't handle non-finite values.
Results may differ from the reference program's by a relative error of at most 0.019.
Values may be sent and summed in bfloat16 or wider, within the bound.
A program may use at most 192 MiB of HBM per device.

```python
import jax
import jax.numpy as jnp
from jax import lax

D = 640
HEADS = 10
HD = 64
FF = 2240
ROWS = 2048
SEGS = 16
SLOT_DEV = 3
SLOTS = 12
TOKENS = 16384
N_DP = 8
N_MP = 4


def draw_seg_ids(key, part):
    first_key, second_key, third_key, fourth_key = jax.random.split(key, 4)
    spread_a = jax.random.randint(first_key, (N_DP,), 0, SEGS)
    spread_b = jax.random.randint(second_key, (N_DP,), 0, SEGS)
    counts = SEGS - spread_a * spread_b // SEGS
    order = jax.random.permutation(third_key, N_DP)
    counts = counts.at[order[0]].set(SEGS).at[order[1]].set(1)
    scores = jax.random.randint(fourth_key, (N_DP, ROWS - 1), 0, 65536) * ROWS + jnp.arange(ROWS - 1)[None, :]
    ranks = jnp.argsort(jnp.argsort(scores, axis=1, stable=True), axis=1, stable=True)
    cut_marks = (ranks < (counts - 1)[:, None]).astype(jnp.int32)
    numbers = jnp.concatenate([jnp.zeros((N_DP, 1), jnp.int32), jnp.cumsum(cut_marks, axis=1).astype(jnp.int32)], axis=1)
    return numbers.reshape(TOKENS).astype(jnp.int32)


def with_spikes(values, stream_key, source, target, blocks, factor):
    def block_of(axis_at):
        return (jnp.arange(values.shape[axis_at]) // (values.shape[axis_at] // blocks)).reshape((-1,) + (1,) * (values.ndim - 1 - axis_at))

    one_side = jax.random.permutation(stream_key, blocks)[block_of(target)]
    second = (block_of(target) + blocks // 2) % blocks
    return jnp.where((block_of(source) == one_side) | (block_of(source) == second), factor * values, values)


def levels(rng, shape, cuts, smallest, largest):
    level = 1.0
    for axis_at, blocks in cuts:
        steps = jax.random.uniform(jax.random.fold_in(jax.random.fold_in(rng, 6), axis_at), (blocks,), jnp.float32, smallest / len(cuts), largest / len(cuts))
        level = level * jnp.repeat(jnp.exp(steps), shape[axis_at] // blocks).reshape((-1,) + (1,) * (len(shape) - 1 - axis_at))
    return level


def gaussian(key, extent, scale, limit, shards=(), dtype=jnp.bfloat16):
    values = jax.random.normal(key, extent, jnp.float32) * scale
    if len(shards) > 0:
        values = levels(key, extent, shards, -0.22, 0.18) * values
    return jnp.clip(values, min=-limit, max=limit).astype(dtype)


def bell_draw_with(stream_key, shape, width, limit, cuts, heavy, dtype=jnp.bfloat16):
    entries = width * jax.random.normal(stream_key, shape, jnp.float32)
    if cuts:
        entries = entries * levels(stream_key, shape, cuts, -0.22, 0.18)
    return jnp.clip(with_spikes(entries, jax.random.fold_in(stream_key, 3), *heavy), -limit, limit).astype(dtype)


def setup_inputs(seed: int = 0) -> dict:
    keys = jax.random.split(jax.random.key(seed), 16)
    return {
        "frames": bell_draw_with(keys[0], (TOKENS, D), 1.0, 6.0, ((0, 8),), (0, 1, 8, 2.0)),
        "seg_ids": draw_seg_ids(jax.random.fold_in(keys[15], 71), 0),
        "qkv_weight": gaussian(keys[2], (3, D, SLOTS * HD), D ** -0.5, 0.25, ((1, 8), (2, 4))),
        "qkv_bias": gaussian(keys[3], (2, SLOTS * HD), 0.5, 3.0, ((1, 4),), jnp.float32),
        "out_weight": gaussian(keys[4], (SLOTS * HD, D), (HD // 4) ** -0.5, 1.5, ((0, 4), (1, 8))),
        "out_bias": gaussian(keys[5], (D,), 0.5, 3.0, (), jnp.float32),
        "gain_one": jnp.clip(1.0 + 0.18 * jax.random.normal(keys[6], (D,), jnp.float32), 0.1, 1.9),
        "shift_one": gaussian(keys[7], (D,), 0.5, 3.0, (), jnp.float32),
        "up_weight": gaussian(keys[8], (D, FF), D ** -0.5, 0.25, ((0, 8), (1, 4))),
        "up_bias": gaussian(keys[9], (FF,), 0.5, 3.0, ((0, 4),), jnp.float32),
        "down_weight": gaussian(keys[10], (FF, D), FF ** -0.5, 0.125, ((0, 4), (1, 8))),
        "down_bias": gaussian(keys[11], (D,), 0.5, 3.0, (), jnp.float32),
        "gain_two": jnp.clip(1.0 + 0.18 * jax.random.normal(keys[12], (D,), jnp.float32), 0.1, 1.9),
        "shift_two": gaussian(keys[13], (D,), 0.5, 3.0, (), jnp.float32),
        "cotangent": bell_draw_with(keys[14], (TOKENS, D), 1.0, 6.0, ((0, 8),), (0, 1, 8, 2.0)),
    }


HIGHEST = lax.Precision.HIGHEST
EPS = 1e-05
SCALE = 0.125

@jax.custom_vjp
def low(v):
    return lax.optimization_barrier(v.astype(jnp.bfloat16)).astype(jnp.float32)

@jax.custom_vjp
def low_back(v):
    return v

def low_keep(v):
    return (low(v), None)

def low_pass(kept, grad):
    return (grad,)

def back_keep(v):
    return (v, None)

def back_low(kept, grad):
    return (low(grad),)
low.defvjp(low_keep, low_pass)
low_back.defvjp(back_keep, back_low)

def layer_norm(summed, gain, shift):
    centre = summed - lax.optimization_barrier(jnp.mean(summed, -1, keepdims=True))
    spread = lax.optimization_barrier(jnp.mean(centre * centre, -1, keepdims=True))
    return centre * lax.rsqrt(spread + EPS) * gain + shift

def slot_mask():
    slot = jnp.arange(SLOTS)
    group = slot // SLOT_DEV
    within = slot % SLOT_DEV
    allowed = HEADS // N_MP + (group < HEADS % N_MP).astype(jnp.int32)
    return (within < allowed).astype(jnp.float32)

def block_layer(weights, inputs, segments):
    qkv_weight, qkv_bias, out_weight, out_bias, gain_one, shift_one, up_weight, up_bias, down_weight, down_bias, gain_two, shift_two = weights
    zeros = jnp.zeros_like(qkv_bias[0])
    offsets = jnp.stack([qkv_bias[0], zeros, qkv_bias[1]])
    projected = jnp.einsum('rd,ids->irs', inputs, qkv_weight, precision=HIGHEST) + offsets[:, None, :]
    projected = low(low_back(projected))
    head_values = projected.reshape(3, ROWS, SLOTS, HD)
    scores = jnp.einsum('qhd,khd->hqk', head_values[0], head_values[1], precision=HIGHEST) * SCALE
    scores = low_back(scores)
    same_utter = segments[:, None] == segments[None, :]
    scores = jnp.where(same_utter[None], scores, -1e+30)
    maxima = lax.optimization_barrier(jnp.max(scores, -1, keepdims=True))
    raised = jnp.exp(scores - maxima)
    probs = low(raised / lax.optimization_barrier(jnp.sum(raised, -1, keepdims=True)))
    attended = jnp.einsum('hqk,khd->qhd', probs, head_values[2], precision=HIGHEST)
    attended = attended * slot_mask()[None, :, None]
    attended = low(low_back(attended.reshape(ROWS, SLOTS * HD)))
    parts = jnp.einsum('tms,msd->tmd', attended.reshape(ROWS, N_MP, SLOT_DEV * HD), out_weight.reshape(N_MP, SLOT_DEV * HD, D), precision=HIGHEST)
    attention = low_back(lax.optimization_barrier(jnp.sum(low(parts), 1)) + out_bias)
    hidden = layer_norm(inputs + attention, gain_one, shift_one)
    hidden_low = low(hidden)
    pre_act = low_back(jnp.dot(hidden_low, up_weight, precision=HIGHEST) + up_bias)
    activation = low(jax.nn.gelu(pre_act, approximate=False))
    feed_parts = jnp.einsum('tmf,mfd->tmd', activation.reshape(ROWS, N_MP, FF // N_MP), down_weight.reshape(N_MP, FF // N_MP, D), precision=HIGHEST)
    feed = low_back(lax.optimization_barrier(jnp.sum(low(feed_parts), 1)) + down_bias)
    return layer_norm(hidden + feed, gain_two, shift_two)

def reference(frames, seg_ids, qkv_weight, qkv_bias, out_weight, out_bias, gain_one, shift_one, up_weight, up_bias, down_weight, down_bias, gain_two, shift_two, cotangent):
    params = tuple((a.astype(jnp.float32) for a in (qkv_weight, qkv_bias, out_weight, out_bias, gain_one, shift_one, up_weight, up_bias, down_weight, down_bias, gain_two, shift_two)))
    segments = seg_ids.reshape(N_DP, ROWS)

    def forward(inputs, *weights):

        def one_block(record):
            return block_layer(weights, record[0], record[1])
        outputs = lax.map(jax.checkpoint(one_block), (inputs.reshape(N_DP, ROWS, D), segments))
        return outputs.reshape(TOKENS, D)
    result, pullback = jax.vjp(forward, frames.astype(jnp.float32), *params)
    grads = pullback(cotangent.astype(jnp.float32))
    return (result.astype(jnp.bfloat16), grads[0].astype(jnp.bfloat16), grads[1], grads[2], grads[3], grads[4], grads[5], grads[6], grads[7], grads[8], grads[9], grads[10], grads[11], grads[12])
```

```python
import functools
import math

import jax
import jax.numpy as jnp
from jax import lax
from jax.experimental import pallas as pl
from jax.experimental.pallas import tpu as pltpu
from jax.sharding import PartitionSpec as P

HEADS = 10
HD = 64
EPS = 1e-05
SCALE = 0.125
MAX_SEGS = 16
MASKED = -1e30
UNIT = SCALE * math.log2(math.e)
AUG = 256
VAUG = 128
NT = (((1,), (1,)), ((), ()))
TN = (((0,), (0,)), ((), ()))
F32 = jnp.float32
BF16 = jnp.bfloat16
VMEM_LIMIT = 56 << 20


def thirds(wide):
    first = wide.astype(BF16)
    rest = wide - first.astype(F32)
    second = rest.astype(BF16)
    third = (rest - second.astype(F32)).astype(BF16)
    return first, second, third


def project_kernel(slots, x_ref, w_ref, b_ref, seg_ref, qs_ref, ka_ref, va_ref, kk_ref):
    rows = x_ref.shape[0]
    width = slots * HD
    made = jnp.dot(x_ref[...], w_ref[...], preferred_element_type=F32) + b_ref[...]
    made = made.astype(BF16)
    marks = seg_ref[...] == lax.broadcasted_iota(jnp.int32, (rows, MAX_SEGS), 1)
    chosen = jnp.where(marks, 1.0, 0.0).astype(BF16)
    barred = jnp.where(marks, 0.0, MASKED).astype(BF16)
    tail = AUG - 3 * HD - MAX_SEGS
    q_tail = jnp.zeros((rows, tail), BF16)
    minus = jnp.where(lax.broadcasted_iota(jnp.int32, (rows, tail), 1) < 3, -1.0, 0.0).astype(BF16)
    v_tail = jnp.where(
        lax.broadcasted_iota(jnp.int32, (rows, VAUG - HD), 1) < 3, -1.0, 0.0
    ).astype(BF16)
    for slot in range(slots):
        at = slot * HD
        q = made[:, at : at + HD]
        k = made[:, width + at : width + at + HD]
        v = made[:, 2 * width + at : 2 * width + at + HD]
        one, two, three = thirds(k.astype(F32) * UNIT)
        qs_ref[slot] = jnp.concatenate([q, q, q, chosen, q_tail], 1)
        ka_ref[slot] = jnp.concatenate([one, two, three, barred, minus], 1)
        va_ref[slot] = jnp.concatenate([v, v_tail], 1)
        kk_ref[slot] = k


def project(frames, weight, offsets, seg_ids, slots):
    rows, depth = frames.shape
    block = min(512, rows)
    spread = lambda n: pl.BlockSpec((slots, block, n), lambda i: (0, i, 0))
    shape = lambda n: jax.ShapeDtypeStruct((slots, rows, n), BF16)
    return pl.pallas_call(
        functools.partial(project_kernel, slots),
        grid=(rows // block,),
        in_specs=[
            pl.BlockSpec((block, depth), lambda i: (i, 0)),
            pl.BlockSpec(weight.shape, lambda i: (0, 0)),
            pl.BlockSpec((1, offsets.shape[1]), lambda i: (0, 0)),
            pl.BlockSpec((block, 1), lambda i: (i, 0)),
        ],
        out_specs=[spread(AUG), spread(AUG), spread(VAUG), spread(HD)],
        out_shape=[shape(AUG), shape(AUG), shape(VAUG), shape(HD)],
        compiler_params=pltpu.CompilerParams(vmem_limit_bytes=VMEM_LIMIT),
        name="project",
    )(frames, weight, offsets, seg_ids.reshape(rows, 1))


def attend_kernel(sub, qs_ref, ka_ref, va_ref, mixed_ref, lse_ref):
    for at in range(0, qs_ref.shape[1], sub):
        part = slice(at, at + sub)
        x = lax.dot_general(qs_ref[0, part, :], ka_ref[0], NT, preferred_element_type=F32)
        top = jnp.max(x, -1, keepdims=True)
        p = jnp.exp2(x - top).astype(BF16)
        made = jnp.dot(p, va_ref[0], preferred_element_type=F32)
        total = -made[:, HD : HD + 1]
        mixed_ref[0, part, :] = made[:, :HD] / total
        lse_ref[0, part, :] = top + jnp.log2(total)


def attend(qs, ka, va):
    slots, rows, _ = qs.shape
    block = min(512, rows)
    sub = min(256, block)
    whole = lambda n: pl.BlockSpec((1, rows, n), lambda h, i: (h, 0, 0))
    some = lambda n: pl.BlockSpec((1, block, n), lambda h, i: (h, i, 0))
    return pl.pallas_call(
        functools.partial(attend_kernel, sub),
        grid=(slots, rows // block),
        in_specs=[some(AUG), whole(AUG), whole(VAUG)],
        out_specs=[some(HD), some(1)],
        out_shape=[
            jax.ShapeDtypeStruct((slots, rows, HD), F32),
            jax.ShapeDtypeStruct((slots, rows, 1), F32),
        ],
        compiler_params=pltpu.CompilerParams(vmem_limit_bytes=VMEM_LIMIT),
        name="attend",
    )(qs, ka, va)


def attend_back_kernel(
    sub, qs_ref, ka_ref, va_ref, kk_ref, lse_ref, mixed_ref, up_ref, dq_ref, dk_ref, dv_ref, dk_acc, dv_acc
):
    step = pl.program_id(1)

    @pl.when(step == 0)
    def _():
        dk_acc[...] = jnp.zeros_like(dk_acc)
        dv_acc[...] = jnp.zeros_like(dv_acc)

    for at in range(0, qs_ref.shape[1], sub):
        part = slice(at, at + sub)
        q = qs_ref[0, part, :HD]
        up = up_ref[0, part, :]
        l_one, l_two, l_three = thirds(lse_ref[0, part, :])
        d_one, d_two, d_three = thirds(
            jnp.sum(up.astype(F32) * mixed_ref[0, part, :], -1, keepdims=True)
        )
        blank = lambda n: jnp.zeros((sub, n), BF16)
        base = 3 * HD + MAX_SEGS
        queries = jnp.concatenate(
            [qs_ref[0, part, :base], l_one, l_two, l_three, blank(AUG - base - 3)], 1
        )
        upper = jnp.concatenate([up, d_one, d_two, d_three, blank(VAUG - HD - 3)], 1)
        x = lax.dot_general(queries, ka_ref[0], NT, preferred_element_type=F32)
        p = jnp.exp2(x)
        dp = lax.dot_general(upper, va_ref[0], NT, preferred_element_type=F32)
        ds = (p * dp).astype(BF16)
        dv_acc[...] += lax.dot_general(up, p.astype(BF16), TN, preferred_element_type=F32)
        dk_acc[...] += lax.dot_general(q, ds, TN, preferred_element_type=F32)
        dq_ref[0, part, :] = (
            jnp.dot(ds, kk_ref[0], preferred_element_type=F32) * SCALE
        ).astype(BF16)

    @pl.when(step == pl.num_programs(1) - 1)
    def _():
        dk_ref[0] = (dk_acc[...] * SCALE).T.astype(BF16)
        dv_ref[0] = dv_acc[...].T.astype(BF16)


def attend_back(qs, ka, va, kk, lse, mixed, up):
    slots, rows, _ = qs.shape
    block = min(512, rows)
    sub = min(256, block)
    whole = lambda n: pl.BlockSpec((1, rows, n), lambda h, i: (h, 0, 0))
    some = lambda n: pl.BlockSpec((1, block, n), lambda h, i: (h, i, 0))
    shape = jax.ShapeDtypeStruct((slots, rows, HD), BF16)
    return pl.pallas_call(
        functools.partial(attend_back_kernel, sub),
        grid=(slots, rows // block),
        in_specs=[
            some(AUG), whole(AUG), whole(VAUG), whole(HD), some(1), some(HD), some(HD),
        ],
        out_specs=[some(HD), whole(HD), whole(HD)],
        out_shape=[shape, shape, shape],
        scratch_shapes=[pltpu.VMEM((HD, rows), F32), pltpu.VMEM((HD, rows), F32)],
        compiler_params=pltpu.CompilerParams(vmem_limit_bytes=VMEM_LIMIT),
        name="attend_back",
    )(qs, ka, va, kk, lse, mixed, up)


def norm_forward(summed):
    centre = summed - jnp.mean(summed, -1, keepdims=True)
    spread = jnp.mean(centre * centre, -1, keepdims=True)
    factor = lax.rsqrt(spread + EPS)
    return (centre * factor, factor)


def norm_backward(upper, normed, factor, gain):
    scaled = upper * gain
    return factor * (
        scaled
        - jnp.mean(scaled, -1, keepdims=True)
        - normed * jnp.mean(scaled * normed, -1, keepdims=True)
    )


def gelu_exact(values):
    return jax.nn.gelu(values, approximate=False)


def body(
    frames, seg_ids, qkv_weight, qkv_bias, out_weight, out_bias, gain_one, shift_one,
    up_weight, up_bias, down_weight, down_bias, gain_two, shift_two, cotangent,
):
    both = ("mp", "dp")
    rows, depth = frames.shape
    mp_size = lax.axis_size("mp")
    dp_size = lax.axis_size("dp")
    mp_index = lax.axis_index("mp")
    share = rows // mp_size
    slots = qkv_weight.shape[2] // HD
    width = slots * HD
    hidden_cols = up_weight.shape[1]
    piece = qkv_weight.shape[1]
    live_count = HEADS // mp_size + (mp_index < HEADS % mp_size).astype(jnp.int32)
    live = (jnp.arange(slots) < live_count).astype(F32)

    def share_of(array):
        return lax.dynamic_slice_in_dim(array, mp_index * share, share, 0)

    qkv_full = lax.all_gather(
        jnp.transpose(qkv_weight, (1, 0, 2)).reshape(piece, 3 * width), "dp", axis=0, tiled=True
    )
    packed = jnp.concatenate([up_weight, down_weight.T, out_weight.T], 1)
    packed = lax.all_gather(packed, "mp", axis=0, tiled=True)
    packed = lax.all_gather(packed.reshape(mp_size, piece, -1), "dp", axis=1, tiled=True)
    up_full = packed[:, :, :hidden_cols]
    down_full = packed[:, :, hidden_cols : 2 * hidden_cols]
    out_full = packed[:, :, 2 * hidden_cols :]

    offsets = jnp.concatenate([qkv_bias[0], jnp.zeros_like(qkv_bias[0]), qkv_bias[1]])[None]
    qs, ka, va, kk = project(frames, qkv_full, offsets, seg_ids, slots)
    mixed, lse = attend(qs, ka, va)
    mixed_low = (mixed * live[:, None, None]).astype(BF16)
    sent = mixed_low.reshape(slots, mp_size, share, HD).transpose(1, 2, 0, 3)
    sent = sent.reshape(mp_size, share, width)
    got = lax.all_to_all(sent, "mp", 0, 0, tiled=True)
    attention = jnp.einsum("gts,gds->td", got, out_full, preferred_element_type=F32)
    frames_share = share_of(frames).astype(F32)
    normed_one, factor_one = norm_forward(frames_share + attention + out_bias)
    hidden = normed_one * gain_one + shift_one
    hidden_low = hidden.astype(BF16)
    up_bias_full = lax.all_gather(up_bias, "mp", axis=0, tiled=True)
    up_flat = up_full.transpose(1, 0, 2).reshape(depth, -1)
    down_flat = down_full.transpose(1, 0, 2).reshape(depth, -1)
    pre_act = jnp.dot(hidden_low, up_flat, preferred_element_type=F32) + up_bias_full
    activation, pullback = jax.vjp(gelu_exact, pre_act)
    act_low = activation.astype(BF16)
    feed = jnp.einsum("tf,df->td", act_low, down_flat, preferred_element_type=F32)
    normed_two, factor_two = norm_forward(hidden + feed + down_bias)
    output_frames = (normed_two * gain_two + shift_two).astype(BF16)
    upstream = share_of(cotangent).astype(F32)
    sum_two_grad = norm_backward(upstream, normed_two, factor_two, gain_two)
    sum_two_low = sum_two_grad.astype(BF16)
    grad_down = jnp.einsum("td,tf->df", sum_two_low, act_low, preferred_element_type=F32)
    act_grad = jnp.dot(sum_two_low, down_flat, preferred_element_type=F32)
    pre_low = pullback(act_grad)[0].astype(BF16)
    grad_up = jnp.einsum("td,tf->df", hidden_low, pre_low, preferred_element_type=F32)
    hidden_grad = sum_two_grad + jnp.einsum(
        "tf,df->td", pre_low, up_flat, preferred_element_type=F32
    )
    sum_one_grad = norm_backward(hidden_grad, normed_one, factor_one, gain_one)
    sum_one_low = sum_one_grad.astype(BF16)
    grad_out = jnp.einsum("td,gts->gds", sum_one_low, got, preferred_element_type=F32)
    back = jnp.einsum("td,gds->gts", sum_one_low, out_full, preferred_element_type=F32)
    back = lax.all_to_all(back.astype(BF16), "mp", 0, 0, tiled=True)
    back = back.reshape(rows, slots, HD).transpose(1, 0, 2) * live.astype(BF16)[:, None, None]

    unroll = lambda g: g.reshape(depth, mp_size, hidden_cols).transpose(1, 0, 2)
    partial = jnp.concatenate([unroll(grad_up), unroll(grad_down), grad_out], 2).astype(BF16)
    partial = lax.psum_scatter(partial, "dp", scatter_dimension=1, tiled=True)
    partial = lax.psum_scatter(partial, "mp", scatter_dimension=0, tiled=True)[0].astype(F32)
    small = lax.psum(
        (
            jnp.sum(sum_one_low.astype(F32), 0),
            jnp.sum(hidden_grad * normed_one, 0),
            jnp.sum(hidden_grad, 0),
            jnp.sum(pre_low.astype(F32), 0),
            jnp.sum(sum_two_low.astype(F32), 0),
            jnp.sum(upstream * normed_two, 0),
            jnp.sum(upstream, 0),
        ),
        ("dp", "mp"),
    )

    dq, dk, dv = attend_back(qs, ka, va, kk, lse, mixed, back)
    grads_low = jnp.stack([dq, dk, dv]).transpose(2, 0, 1, 3).reshape(rows, 3 * width)
    qkv_bias_grad = jnp.sum(grads_low.astype(F32), 0).reshape(3, width)
    qkv_bias_grad = lax.psum(jnp.stack([qkv_bias_grad[0], qkv_bias_grad[2]]), "dp")
    grad_qkv = jnp.einsum("rd,rs->ds", frames, grads_low, preferred_element_type=F32)
    arrived = lax.all_to_all(
        grad_qkv.astype(BF16).reshape(dp_size, piece, 3 * width), "dp", 0, 0, tiled=True
    )
    grad_qkv = arrived.astype(F32).sum(0).reshape(piece, 3, width).transpose(1, 0, 2)
    input_part = jnp.einsum("rs,ds->rd", grads_low, qkv_full, preferred_element_type=F32)
    input_sum = lax.psum_scatter(input_part.astype(BF16), "mp", scatter_dimension=0, tiled=True)
    frames_grad = (input_sum.astype(F32) + sum_one_grad).astype(BF16)
    return (
        output_frames,
        frames_grad,
        grad_qkv,
        qkv_bias_grad,
        partial[:, 2 * hidden_cols :].T,
        small[0],
        small[1],
        small[2],
        partial[:, :hidden_cols],
        lax.dynamic_slice_in_dim(small[3], mp_index * hidden_cols, hidden_cols, 0),
        partial[:, hidden_cols : 2 * hidden_cols].T,
        small[4],
        small[5],
        small[6],
    )


def solution(mesh):
    in_specs = (
        P("dp", None), P("dp"), P(None, "dp", "mp"), P(None, "mp"), P("mp", "dp"), P(), P(), P(),
        P("dp", "mp"), P("mp"), P("mp", "dp"), P(), P(), P(), P("dp", None),
    )
    out_specs = (
        P(("dp", "mp"), None), P(("dp", "mp"), None), P(None, "dp", "mp"), P(None, "mp"),
        P("mp", "dp"), P(), P(), P(), P("dp", "mp"), P("mp"), P("mp", "dp"), P(), P(), P(),
    )
    return jax.shard_map(body, mesh=mesh, in_specs=in_specs, out_specs=out_specs, check_vma=False)
```

```python
import functools
import math

import jax
import jax.numpy as jnp
from jax import lax
from jax.experimental import pallas as pl
from jax.experimental.pallas import tpu as pltpu
from jax.sharding import PartitionSpec as P

HEADS = 10
HD = 64
EPS = 1e-05
SCALE = 0.125
MAX_SEGS = 16
MASKED = -1e30
UNIT = SCALE * math.log2(math.e)
AUG = 256
VAUG = 128
NT = (((1,), (1,)), ((), ()))
TN = (((0,), (0,)), ((), ()))
F32 = jnp.float32
BF16 = jnp.bfloat16
VMEM_LIMIT = 56 << 20
MESH = pl.DeviceIdType.MESH
CHIPS = 3
HALF = 640


def thirds(wide):
    first = wide.astype(BF16)
    rest = wide - first.astype(F32)
    second = rest.astype(BF16)
    third = (rest - second.astype(F32)).astype(BF16)
    return first, second, third


def lane_marks(rows, width, count):
    return lax.broadcasted_iota(jnp.int32, (rows, width), 1) < count


def spread_rows(made, seg, slots, qs_ref, ka_ref, va_ref, kk_ref, rows):
    count = made.shape[0]
    width = slots * HD
    marks = seg == lax.broadcasted_iota(jnp.int32, (count, MAX_SEGS), 1)
    chosen = jnp.where(marks, 1.0, 0.0).astype(BF16)
    barred = jnp.where(marks, 0.0, MASKED).astype(BF16)
    tail = AUG - 3 * HD - MAX_SEGS
    q_tail = jnp.zeros((count, tail), BF16)
    minus = jnp.where(lane_marks(count, tail, 3), -1.0, 0.0).astype(BF16)
    v_tail = jnp.where(lane_marks(count, VAUG - HD, 3), -1.0, 0.0).astype(BF16)
    for slot in range(slots):
        at = slot * HD
        q = made[:, at : at + HD]
        k = made[:, width + at : width + at + HD]
        v = made[:, 2 * width + at : 2 * width + at + HD]
        one, two, three = thirds(k.astype(F32) * UNIT)
        qs_ref[slot, rows, :] = jnp.concatenate([q, q, q, chosen, q_tail], 1)
        ka_ref[slot, rows, :] = jnp.concatenate([one, two, three, barred, minus], 1)
        va_ref[slot, rows, :] = jnp.concatenate([v, v_tail], 1)
        kk_ref[slot, rows, :] = k


def plane_barrier(peers):
    barrier = pltpu.get_barrier_semaphore()
    for peer in peers:
        pl.semaphore_signal(barrier, inc=1, device_id=peer, device_id_type=MESH)
    pl.semaphore_wait(barrier, len(peers))


def remote(src, dst, send, recv, peer):
    return pltpu.make_async_remote_copy(
        src_ref=src, dst_ref=dst, send_sem=send, recv_sem=recv, device_id=peer, device_id_type=MESH
    )


def front_kernel(
    slots, sub,
    x_ref, wq_ref, pack_ref, bias_ref, off_ref, seg_ref,
    all_ref, wfull_ref, ball_ref, qs_ref, ka_ref, va_ref, kk_ref, mixed_ref, got_ref,
    stage, q_send, q_recv, z_send, z_recv, w_send, w_recv, b_send, b_recv, a_send, a_recv, here,
):
    dp = lax.axis_index("dp")
    mp = lax.axis_index("mp")
    plane = [dp ^ 2, dp ^ 4, dp ^ 6]
    sibling = (dp ^ 1, mp)
    tall = [(dp, mp ^ s) for s in range(1, 4)]
    plane_barrier([sibling] + [(d, mp) for d in plane] + tall)
    rows = x_ref.shape[0]
    share = rows // 4

    mine = pltpu.make_async_copy(wq_ref, wfull_ref.at[dp], here.at[0])
    mine.start()
    firsts = [
        remote(wq_ref, wfull_ref.at[dp], q_send.at[i], q_recv.at[i], (plane[i], mp))
        for i in range(CHIPS)
    ]
    for copy in firsts:
        copy.start()
    shared = [remote(wq_ref, wfull_ref.at[dp], q_send.at[3], q_recv.at[3], sibling)]
    shared[0].start()
    own = pltpu.make_async_copy(pack_ref, all_ref.at[mp, dp], here.at[1])
    own.start()
    lifts = [
        remote(pack_ref, all_ref.at[mp, dp], z_send.at[s], z_recv.at[s], tall[s]) for s in range(3)
    ]
    own_bias = pltpu.make_async_copy(bias_ref, ball_ref.at[mp], here.at[2])
    own_bias.start()
    for copy in lifts:
        copy.start()
    biases = [
        remote(bias_ref, ball_ref.at[mp], b_send.at[s], b_recv.at[s], tall[s]) for s in range(3)
    ]
    for copy in biases:
        copy.start()
    for i in range(CHIPS):
        firsts[i].wait_recv()
        passed = remote(
            wfull_ref.at[plane[i]], wfull_ref.at[plane[i]], q_send.at[4 + i], q_recv.at[4 + i], sibling
        )
        passed.start()
        shared.append(passed)
    own.wait()

    def weights(s, kind):
        group = mp ^ s
        block = {0: dp, 1: dp, 2: dp, 4: plane[0], 5: plane[1], 6: plane[2]}
        block[3] = plane[0] if s % 2 == 0 else plane[1]
        peer = {0: (plane[0], mp), 1: (plane[1], mp)}
        peer[3] = peer[1] if s % 2 == 0 else peer[0]
        ref = all_ref.at[group, block[kind]]
        return remote(ref, ref, w_send.at[s, kind], w_recv.at[s, kind], peer.get(kind, sibling))

    def start_weights(s):
        if s > 0:
            lifts[s - 1].wait_recv()
        for kind in (0, 1, 2):
            weights(s, kind).start()

    def pass_weights(s):
        weights(s, 0).wait_recv()
        weights(s, 1).wait_recv()
        for kind in (3, 4, 5):
            weights(s, kind).start()

    def last_weights(s):
        weights(s, 3).wait_recv()
        weights(s, 6).start()

    start_weights(0)
    mine.wait()
    for copy in shared:
        copy.wait_recv()

    block = 256

    def project_rows(step, carry):
        part = pl.ds(pl.multiple_of(step * block, block), block)
        x = x_ref[part, :]
        made = off_ref[...] + jnp.zeros((block, off_ref.shape[1]), F32)
        full = jnp.concatenate([wfull_ref[d] for d in range(wfull_ref.shape[0])], 0)
        made = made + jnp.dot(x, full, preferred_element_type=F32)
        spread_rows(made.astype(BF16), seg_ref[part, :], slots, qs_ref, ka_ref, va_ref, kk_ref, part)
        return carry

    lax.fori_loop(0, rows // block, project_rows, 0)

    live_count = HEADS // 4 + (mp < HEADS % 4).astype(jnp.int32)
    per_share = share // sub
    actions = {
        0: [(start_weights, 1), (pass_weights, 0)],
        1: [(start_weights, 2), (last_weights, 0)],
        2: [(pass_weights, 1)],
        3: [(start_weights, 3), (last_weights, 1)],
        4: [(pass_weights, 2)],
        5: [(last_weights, 2)],
        6: [(pass_weights, 3)],
    }

    def send_rows(step, stage_index):
        group = mp ^ stage_index
        offset = pl.multiple_of(lax.rem(step, per_share) * sub, sub)
        source = pl.ds(pl.multiple_of(group * share, share) + offset, sub)
        return remote(
            stage.at[source], got_ref.at[mp, pl.ds(offset, sub)], a_send.at[step], a_recv.at[step],
            (dp, group),
        )

    def attend_rows(step, carry):
        stage_index = 3 - step // per_share
        group = mp ^ stage_index
        offset = lax.rem(step, per_share) * sub
        part = pl.ds(pl.multiple_of(group * share + offset, sub), sub)
        for when, todo in actions.items():

            @pl.when(step == when)
            def _():
                for act, s in todo:
                    act(s)

        for slot in range(slots):
            x = lax.dot_general(
                qs_ref[slot, part, :], ka_ref[slot], NT, preferred_element_type=F32
            )
            top = jnp.max(x, -1, keepdims=True)
            p = jnp.exp2(x - top).astype(BF16)
            made = jnp.dot(p, va_ref[slot], preferred_element_type=F32)
            total = -made[:, HD : HD + 1]
            mixed = made[:, :HD] / total
            one, two, three = thirds(top + jnp.log2(total))
            base = 3 * HD + MAX_SEGS
            qs_ref[slot, part, base : base + 3] = jnp.concatenate([one, two, three], 1)
            mixed_ref[slot, part, :] = mixed
            alive = (slot < live_count).astype(F32)
            stage[part, slot * HD : (slot + 1) * HD] = (mixed * alive).astype(BF16)

        @pl.when(step < 3 * per_share)
        def _():
            send_rows(step, stage_index).start()

        return carry

    lax.fori_loop(0, rows // sub, attend_rows, 0)
    start = pl.ds(pl.multiple_of(mp * share, share), share)
    keep = pltpu.make_async_copy(stage.at[start], got_ref.at[mp], here.at[3])
    keep.start()
    last_weights(3)
    for s in range(4):
        weights(s, 2).wait_recv()
        for kind in (4, 5, 6):
            weights(s, kind).wait_recv()
        for kind in range(7):
            weights(s, kind).wait_send()
    for copy in firsts + shared + lifts:
        copy.wait_send()
    for copy in biases:
        copy.wait()
    for step in range(3 * per_share):
        send_rows(step, 3 - step // per_share).wait()
    own_bias.wait()
    keep.wait()


def front(frames, wq, packed, up_bias, offsets, seg_ids, slots):
    rows, _ = frames.shape
    piece, lanes = packed.shape
    sub = 256
    shape = lambda n: jax.ShapeDtypeStruct((slots, rows, n), BF16)
    vmem = pl.BlockSpec(memory_space=pltpu.VMEM)
    dma = pltpu.SemaphoreType.DMA
    steps = rows // sub
    return pl.pallas_call(
        functools.partial(front_kernel, slots, sub),
        in_specs=[vmem] * 6,
        out_specs=[vmem] * 9,
        out_shape=[
            jax.ShapeDtypeStruct((4, 8, piece, lanes), BF16),
            jax.ShapeDtypeStruct((8,) + wq.shape, BF16),
            jax.ShapeDtypeStruct((4,) + up_bias.shape, F32),
            shape(AUG), shape(AUG), shape(VAUG), shape(HD),
            jax.ShapeDtypeStruct((slots, rows, HD), F32),
            jax.ShapeDtypeStruct((4, rows // 4, slots * HD), BF16),
        ],
        scratch_shapes=[
            pltpu.VMEM((rows, slots * HD), BF16),
            dma((7,)), dma((7,)), dma((3,)), dma((3,)), dma((4, 7)), dma((4, 7)), dma((3,)), dma((3,)),
            dma((steps,)), dma((steps,)), dma((4,)),
        ],
        compiler_params=pltpu.CompilerParams(
            collective_id=1, has_side_effects=True, vmem_limit_bytes=VMEM_LIMIT
        ),
        name="front",
    )(frames, wq, packed, up_bias, offsets, seg_ids.reshape(rows, 1))


def project_kernel(slots, x_ref, w_ref, b_ref, seg_ref, qs_ref, ka_ref, va_ref, kk_ref):
    made = jnp.dot(x_ref[...], w_ref[...], preferred_element_type=F32) + b_ref[...]
    spread_rows(
        made.astype(BF16), seg_ref[...], slots, qs_ref, ka_ref, va_ref, kk_ref, slice(None)
    )


def project(frames, weight, offsets, seg_ids, slots):
    rows, depth = frames.shape
    block = min(512, rows)
    spread = lambda n: pl.BlockSpec((slots, block, n), lambda i: (0, i, 0))
    shape = lambda n: jax.ShapeDtypeStruct((slots, rows, n), BF16)
    return pl.pallas_call(
        functools.partial(project_kernel, slots),
        grid=(rows // block,),
        in_specs=[
            pl.BlockSpec((block, depth), lambda i: (i, 0)),
            pl.BlockSpec(weight.shape, lambda i: (0, 0)),
            pl.BlockSpec((1, offsets.shape[1]), lambda i: (0, 0)),
            pl.BlockSpec((block, 1), lambda i: (i, 0)),
        ],
        out_specs=[spread(AUG), spread(AUG), spread(VAUG), spread(HD)],
        out_shape=[shape(AUG), shape(AUG), shape(VAUG), shape(HD)],
        compiler_params=pltpu.CompilerParams(vmem_limit_bytes=VMEM_LIMIT),
        name="project",
    )(frames, weight, offsets, seg_ids.reshape(rows, 1))


def attend_kernel(sub, qs_ref, ka_ref, va_ref, qn_ref, mixed_ref):
    for at in range(0, qs_ref.shape[1], sub):
        part = slice(at, at + sub)
        x = lax.dot_general(qs_ref[0, part, :], ka_ref[0], NT, preferred_element_type=F32)
        top = jnp.max(x, -1, keepdims=True)
        p = jnp.exp2(x - top).astype(BF16)
        made = jnp.dot(p, va_ref[0], preferred_element_type=F32)
        total = -made[:, HD : HD + 1]
        mixed_ref[0, part, :] = made[:, :HD] / total
        one, two, three = thirds(top + jnp.log2(total))
        base = 3 * HD + MAX_SEGS
        blank = jnp.zeros((sub, AUG - base - 3), BF16)
        qn_ref[0, part, :] = jnp.concatenate(
            [qs_ref[0, part, :base], one, two, three, blank], 1
        )


def attend(qs, ka, va):
    slots, rows, _ = qs.shape
    block = min(512, rows)
    sub = min(256, block)
    whole = lambda n: pl.BlockSpec((1, rows, n), lambda h, i: (h, 0, 0))
    some = lambda n: pl.BlockSpec((1, block, n), lambda h, i: (h, i, 0))
    return pl.pallas_call(
        functools.partial(attend_kernel, sub),
        grid=(slots, rows // block),
        in_specs=[some(AUG), whole(AUG), whole(VAUG)],
        out_specs=[some(AUG), some(HD)],
        out_shape=[
            jax.ShapeDtypeStruct((slots, rows, AUG), BF16),
            jax.ShapeDtypeStruct((slots, rows, HD), F32),
        ],
        compiler_params=pltpu.CompilerParams(vmem_limit_bytes=VMEM_LIMIT),
        name="attend",
    )(qs, ka, va)


def attend_back_kernel(
    sub, qs_ref, ka_ref, va_ref, kk_ref, mixed_ref, up_ref, dq_ref, dk_ref, dv_ref, dk_acc, dv_acc
):
    step = pl.program_id(1)

    @pl.when(step == 0)
    def _():
        dk_acc[...] = jnp.zeros_like(dk_acc)
        dv_acc[...] = jnp.zeros_like(dv_acc)

    for at in range(0, qs_ref.shape[1], sub):
        part = slice(at, at + sub)
        q = qs_ref[0, part, :HD]
        up = up_ref[0, part, :]
        d_one, d_two, d_three = thirds(
            jnp.sum(up.astype(F32) * mixed_ref[0, part, :], -1, keepdims=True)
        )
        blank = lambda n: jnp.zeros((sub, n), BF16)
        upper = jnp.concatenate([up, d_one, d_two, d_three, blank(VAUG - HD - 3)], 1)
        x = lax.dot_general(qs_ref[0, part, :], ka_ref[0], NT, preferred_element_type=F32)
        p = jnp.exp2(x)
        dp = lax.dot_general(upper, va_ref[0], NT, preferred_element_type=F32)
        ds = (p * dp).astype(BF16)
        dv_acc[...] += lax.dot_general(up, p.astype(BF16), TN, preferred_element_type=F32)
        dk_acc[...] += lax.dot_general(q, ds, TN, preferred_element_type=F32)
        dq_ref[0, part, :] = (
            jnp.dot(ds, kk_ref[0], preferred_element_type=F32) * SCALE
        ).astype(BF16)

    @pl.when(step == pl.num_programs(1) - 1)
    def _():
        dk_ref[0] = (dk_acc[...] * SCALE).T.astype(BF16)
        dv_ref[0] = dv_acc[...].T.astype(BF16)


def attend_back(qs, ka, va, kk, mixed, up):
    slots, rows, _ = qs.shape
    block = min(512, rows)
    sub = min(256, block)
    whole = lambda n: pl.BlockSpec((1, rows, n), lambda h, i: (h, 0, 0))
    some = lambda n: pl.BlockSpec((1, block, n), lambda h, i: (h, i, 0))
    shape = jax.ShapeDtypeStruct((slots, rows, HD), BF16)
    return pl.pallas_call(
        functools.partial(attend_back_kernel, sub),
        grid=(slots, rows // block),
        in_specs=[
            some(AUG), whole(AUG), whole(VAUG), whole(HD), some(HD), some(HD),
        ],
        out_specs=[some(HD), whole(HD), whole(HD)],
        out_shape=[shape, shape, shape],
        scratch_shapes=[pltpu.VMEM((HD, rows), F32), pltpu.VMEM((HD, rows), F32)],
        compiler_params=pltpu.CompilerParams(vmem_limit_bytes=VMEM_LIMIT),
        name="attend_back",
    )(qs, ka, va, kk, mixed, up)


def norm_forward(summed):
    centre = summed - jnp.mean(summed, -1, keepdims=True)
    spread = jnp.mean(centre * centre, -1, keepdims=True)
    factor = lax.rsqrt(spread + EPS)
    return (centre * factor, factor)


def norm_backward(upper, normed, factor, gain):
    scaled = upper * gain
    return factor * (
        scaled
        - jnp.mean(scaled, -1, keepdims=True)
        - normed * jnp.mean(scaled * normed, -1, keepdims=True)
    )


def middle_kernel(
    groups, hidden_cols, block, at_ref,
    x_ref, y_ref, got_ref, w_ref, ub_ref, vec_ref,
    out_ref, s1_ref, back_ref, grad_ref, small_ref,
    ow, act, pre_low, slope, hid_low, two_low, one_low,
):
    share = out_ref.shape[0]
    width = got_ref.shape[2]
    gap = HALF - hidden_cols
    out_bias, gain_one, shift_one = vec_ref[0:1, :], vec_ref[1:2, :], vec_ref[2:3, :]
    down_bias, gain_two, shift_two = vec_ref[3:4, :], vec_ref[4:5, :], vec_ref[5:6, :]
    for g in range(groups):
        ow[g, :, :gap] = w_ref[g, :, hidden_cols:HALF]
        ow[g, :, gap:] = w_ref[g, :, HALF + hidden_cols : HALF + hidden_cols + width - gap]
    small_ref[...] = jnp.zeros_like(small_ref)
    real = lane_marks(1, HALF, hidden_cols)

    def some_rows(step, carry):
        part = pl.ds(pl.multiple_of(step * block, block), block)
        summed = x_ref[part, :].astype(F32) + out_bias
        for g in range(groups):
            summed += lax.dot_general(got_ref[g, part, :], ow[g], NT, preferred_element_type=F32)
        normed_one, factor_one = norm_forward(summed)
        hidden = normed_one * gain_one + shift_one
        hidden_low = hidden.astype(BF16)
        hid_low[part, :] = hidden_low
        feed = hidden + down_bias
        for g in range(groups):
            pre = jnp.dot(hidden_low, w_ref[g, :, :HALF], preferred_element_type=F32) + ub_ref[g]
            half = 0.5 + 0.5 * lax.erf(pre * math.sqrt(0.5))
            bell = jnp.exp(pre * pre * -0.5) * (pre * (1.0 / math.sqrt(2.0 * math.pi)))
            slope[g] = jnp.where(real, half + bell, 0.0)
            made = jnp.where(real, pre * half, 0.0).astype(BF16)
            act[g, part, :] = made
            feed += lax.dot_general(
                made, w_ref[g, :, HALF : 2 * HALF], NT, preferred_element_type=F32
            )
        normed_two, factor_two = norm_forward(feed)
        out_ref[part, :] = (normed_two * gain_two + shift_two).astype(BF16)
        upstream = y_ref[part, :].astype(F32)
        two_grad = norm_backward(upstream, normed_two, factor_two, gain_two)
        sum_two = two_grad.astype(BF16)
        two_low[part, :] = sum_two
        hidden_grad = two_grad
        for g in range(groups):
            act_grad = jnp.dot(
                sum_two, w_ref[g, :, HALF : 2 * HALF], preferred_element_type=F32
            )
            low = (slope[g] * act_grad).astype(BF16)
            pre_low[g, part, :] = low
            hidden_grad += lax.dot_general(
                low, w_ref[g, :, :HALF], NT, preferred_element_type=F32
            )
            small_ref[8 + g : 9 + g, :] += jnp.sum(low.astype(F32), 0, keepdims=True)
        one_grad = norm_backward(hidden_grad, normed_one, factor_one, gain_one)
        sum_one = one_grad.astype(BF16)
        s1_ref[part, :] = one_grad
        one_low[part, :] = sum_one
        for g in range(groups):
            back_ref[g, part, :] = jnp.dot(sum_one, ow[g], preferred_element_type=F32).astype(BF16)
        for at, term in enumerate((
            sum_one.astype(F32), hidden_grad * normed_one, hidden_grad,
            sum_two.astype(F32), upstream * normed_two, upstream,
        )):
            small_ref[at : at + 1, :] += jnp.sum(term, 0, keepdims=True)
        return carry

    lax.fori_loop(0, share // block, some_rows, 0)
    hid_flip, two_flip, one_flip = hid_low[...].T, two_low[...].T, one_low[...].T
    for g in range(groups):
        grad_up = jnp.dot(hid_flip, pre_low[g], preferred_element_type=F32).astype(BF16)
        grad_down = jnp.dot(two_flip, act[g], preferred_element_type=F32).astype(BF16)
        grad_out = jnp.dot(one_flip, got_ref[g], preferred_element_type=F32).astype(BF16)
        grad_ref[g, :, :HALF] = grad_up
        grad_ref[g, :, HALF : 2 * HALF] = grad_down
        grad_ref[g, :, hidden_cols:HALF] = grad_out[:, :gap]
        rest = width - gap
        grad_ref[g, :, HALF + hidden_cols : HALF + hidden_cols + rest] = grad_out[:, gap:]
        spare = grad_ref.shape[2] - HALF - hidden_cols - rest
        grad_ref[g, :, HALF + hidden_cols + rest :] = jnp.zeros((grad_ref.shape[1], spare), BF16)


def middle(frames, cotangent, got, weights, up_bias, vectors, mp_index, hidden_cols):
    groups, share, width = got.shape
    depth = frames.shape[1]
    block = min(256, share)
    whole = lambda a: pl.BlockSpec(a.shape, lambda i, at: (0,) * a.ndim)
    pick = pl.BlockSpec((share, depth), lambda i, at: (at[0], 0))
    same = lambda s: pl.BlockSpec(s.shape, lambda i, at: (0,) * len(s.shape))
    out_shape = [
        jax.ShapeDtypeStruct((share, depth), BF16),
        jax.ShapeDtypeStruct((share, depth), F32),
        jax.ShapeDtypeStruct((groups, share, width), BF16),
        jax.ShapeDtypeStruct(weights.shape, BF16),
        jax.ShapeDtypeStruct((16, HALF), F32),
    ]
    return pl.pallas_call(
        functools.partial(middle_kernel, groups, hidden_cols, block),
        grid_spec=pltpu.PrefetchScalarGridSpec(
            num_scalar_prefetch=1,
            grid=(1,),
            in_specs=[pick, pick, whole(got), whole(weights), whole(up_bias), whole(vectors)],
            out_specs=[same(s) for s in out_shape],
            scratch_shapes=[
                pltpu.VMEM((groups, depth, width), BF16),
                pltpu.VMEM((groups, share, HALF), BF16),
                pltpu.VMEM((groups, share, HALF), BF16),
                pltpu.VMEM((groups, block, HALF), F32),
                pltpu.VMEM((share, depth), BF16),
                pltpu.VMEM((share, depth), BF16),
                pltpu.VMEM((share, depth), BF16),
            ],
        ),
        out_shape=out_shape,
        compiler_params=pltpu.CompilerParams(vmem_limit_bytes=VMEM_LIMIT),
        name="middle",
    )(mp_index.reshape(1), frames, cotangent, got, weights, up_bias, vectors)


def body(
    frames, seg_ids, qkv_weight, qkv_bias, out_weight, out_bias, gain_one, shift_one,
    up_weight, up_bias, down_weight, down_bias, gain_two, shift_two, cotangent,
):
    rows, depth = frames.shape
    mp_size = lax.axis_size("mp")
    dp_size = lax.axis_size("dp")
    mp_index = lax.axis_index("mp")
    share = rows // mp_size
    slots = qkv_weight.shape[2] // HD
    width = slots * HD
    hidden_cols = up_weight.shape[1]
    piece = qkv_weight.shape[1]
    gap = HALF - hidden_cols
    spare = -(HALF + hidden_cols + width - gap) % 128
    live_count = HEADS // mp_size + (mp_index < HEADS % mp_size).astype(jnp.int32)
    live = (jnp.arange(slots) < live_count).astype(F32)

    wq = jnp.transpose(qkv_weight, (1, 0, 2)).reshape(piece, 3 * width)
    out_flip = out_weight.T
    packed = jnp.concatenate(
        [up_weight, out_flip[:, :gap], down_weight.T, out_flip[:, gap:], jnp.zeros((piece, spare), BF16)], 1
    )
    ub_pad = jnp.pad(up_bias, (0, gap))[None]
    offsets = jnp.concatenate([qkv_bias[0], jnp.zeros_like(qkv_bias[0]), qkv_bias[1]])[None]
    if (dp_size, mp_size) == (8, 4):
        weights, qkv_full, ub_full, qs, ka, va, kk, mixed, got = front(
            frames, wq, packed, ub_pad, offsets, seg_ids, slots
        )
        weights = weights.reshape(mp_size, depth, -1)
        qkv_full = qkv_full.reshape(depth, -1)
    else:
        qkv_full = lax.all_gather(wq, "dp", axis=0, tiled=True)
        weights = lax.all_gather(packed, "mp", axis=0, tiled=False)
        weights = lax.all_gather(weights, "dp", axis=1, tiled=True)
        ub_full = lax.all_gather(ub_pad, "mp", axis=0, tiled=False)
        qs, ka, va, kk = project(frames, qkv_full, offsets, seg_ids, slots)
        qs, mixed = attend(qs, ka, va)
        mixed_low = (mixed * live[:, None, None]).astype(BF16)
        sent = mixed_low.reshape(slots, mp_size, share, HD).transpose(1, 2, 0, 3)
        got = lax.all_to_all(sent.reshape(mp_size, share, width), "mp", 0, 0, tiled=True)
    vectors = jnp.stack(
        [out_bias, gain_one, shift_one, down_bias, gain_two, shift_two, out_bias, out_bias]
    )
    output_frames, sum_one_grad, back, partial, small = middle(
        frames, cotangent, got, weights, ub_full, vectors, mp_index, hidden_cols
    )
    back = lax.all_to_all(back, "mp", 0, 0, tiled=True)
    back = back.reshape(rows, slots, HD).transpose(1, 0, 2) * live.astype(BF16)[:, None, None]
    partial = lax.psum_scatter(partial, "dp", scatter_dimension=1, tiled=True)
    partial = lax.psum_scatter(partial, "mp", scatter_dimension=0, tiled=True)[0].astype(F32)
    small = lax.psum(small, ("dp", "mp"))

    dq, dk, dv = attend_back(qs, ka, va, kk, mixed, back)
    grads_low = jnp.stack([dq, dk, dv]).transpose(2, 0, 1, 3).reshape(rows, 3 * width)
    qkv_bias_grad = jnp.sum(grads_low.astype(F32), 0).reshape(3, width)
    qkv_bias_grad = lax.psum(jnp.stack([qkv_bias_grad[0], qkv_bias_grad[2]]), "dp")
    grad_qkv = jnp.einsum("rd,rs->ds", frames, grads_low, preferred_element_type=F32)
    arrived = lax.all_to_all(
        grad_qkv.astype(BF16).reshape(dp_size, piece, 3 * width), "dp", 0, 0, tiled=True
    )
    grad_qkv = arrived.astype(F32).sum(0).reshape(piece, 3, width).transpose(1, 0, 2)
    input_part = jnp.einsum("rs,ds->rd", grads_low, qkv_full, preferred_element_type=F32)
    input_sum = lax.psum_scatter(input_part.astype(BF16), "mp", scatter_dimension=0, tiled=True)
    frames_grad = (input_sum.astype(F32) + sum_one_grad).astype(BF16)
    out_grad = jnp.concatenate(
        [partial[:, hidden_cols:HALF], partial[:, HALF + hidden_cols : HALF + hidden_cols + width - gap]], 1
    )
    return (
        output_frames,
        frames_grad,
        grad_qkv,
        qkv_bias_grad,
        out_grad.T,
        small[0],
        small[1],
        small[2],
        partial[:, :hidden_cols],
        lax.dynamic_index_in_dim(small, 8 + mp_index, 0, False)[:hidden_cols],
        partial[:, HALF : HALF + hidden_cols].T,
        small[3],
        small[4],
        small[5],
    )


def solution(mesh):
    in_specs = (
        P("dp", None), P("dp"), P(None, "dp", "mp"), P(None, "mp"), P("mp", "dp"), P(), P(), P(),
        P("dp", "mp"), P("mp"), P("mp", "dp"), P(), P(), P(), P("dp", None),
    )
    out_specs = (
        P(("dp", "mp"), None), P(("dp", "mp"), None), P(None, "dp", "mp"), P(None, "mp"),
        P("mp", "dp"), P(), P(), P(), P("dp", "mp"), P("mp"), P("mp", "dp"), P(), P(), P(),
    )
    return jax.shard_map(body, mesh=mesh, in_specs=in_specs, out_specs=out_specs, check_vma=False)
```

```python
import functools
import math

import jax
import jax.numpy as jnp
from jax import lax
from jax.experimental import pallas as pl
from jax.experimental.pallas import tpu as pltpu
from jax.sharding import PartitionSpec as P

HEADS = 10
HD = 64
EPS = 1e-05
SCALE = 0.125
MAX_SEGS = 16
MASKED = -1e30
UNIT = SCALE * math.log2(math.e)
AUG = 256
VAUG = 128
NT = (((1,), (1,)), ((), ()))
TN = (((0,), (0,)), ((), ()))
F32 = jnp.float32
BF16 = jnp.bfloat16
VMEM_LIMIT = 56 << 20
MESH = pl.DeviceIdType.MESH
CHIPS = 3
HALF = 640


def thirds(wide):
    first = wide.astype(BF16)
    rest = wide - first.astype(F32)
    second = rest.astype(BF16)
    third = (rest - second.astype(F32)).astype(BF16)
    return first, second, third


def lane_marks(rows, width, count):
    return lax.broadcasted_iota(jnp.int32, (rows, width), 1) < count


def spread_rows(made, seg, slots, qs_ref, ka_ref, va_ref, kk_ref, rows):
    count = made.shape[0]
    width = slots * HD
    marks = seg == lax.broadcasted_iota(jnp.int32, (count, MAX_SEGS), 1)
    chosen = jnp.where(marks, 1.0, 0.0).astype(BF16)
    barred = jnp.where(marks, 0.0, MASKED).astype(BF16)
    tail = AUG - 3 * HD - MAX_SEGS
    q_tail = jnp.zeros((count, tail), BF16)
    minus = jnp.where(lane_marks(count, tail, 3), -1.0, 0.0).astype(BF16)
    v_tail = jnp.where(lane_marks(count, VAUG - HD, 3), -1.0, 0.0).astype(BF16)
    for slot in range(slots):
        at = slot * HD
        q = made[:, at : at + HD]
        k = made[:, width + at : width + at + HD]
        v = made[:, 2 * width + at : 2 * width + at + HD]
        one, two, three = thirds(k.astype(F32) * UNIT)
        qs_ref[slot, rows, :] = jnp.concatenate([q, q, q, chosen, q_tail], 1)
        ka_ref[slot, rows, :] = jnp.concatenate([one, two, three, barred, minus], 1)
        va_ref[slot, rows, :] = jnp.concatenate([v, v_tail], 1)
        kk_ref[slot, rows, :] = k


def plane_barrier(peers):
    barrier = pltpu.get_barrier_semaphore()
    for peer in peers:
        pl.semaphore_signal(barrier, inc=1, device_id=peer, device_id_type=MESH)
    pl.semaphore_wait(barrier, len(peers))


def remote(src, dst, send, recv, peer):
    return pltpu.make_async_remote_copy(
        src_ref=src, dst_ref=dst, send_sem=send, recv_sem=recv, device_id=peer, device_id_type=MESH
    )


def front_kernel(
    slots, sub,
    x_ref, wq_ref, pack_ref, bias_ref, off_ref, seg_ref,
    all_ref, wfull_ref, ball_ref, qs_ref, ka_ref, va_ref, kk_ref, mixed_ref, got_ref,
    stage, q_send, q_recv, z_send, z_recv, w_send, w_recv, b_send, b_recv, a_send, a_recv, here,
):
    dp = lax.axis_index("dp")
    mp = lax.axis_index("mp")
    plane = [dp ^ 2, dp ^ 4, dp ^ 6]
    sibling = (dp ^ 1, mp)
    tall = [(dp, mp ^ s) for s in range(1, 4)]
    plane_barrier([sibling] + [(d, mp) for d in plane] + tall)
    rows = x_ref.shape[0]
    share = rows // 4

    piece = wq_ref.shape[0]

    def rows_of(d):
        return wfull_ref.at[pl.ds(pl.multiple_of(d * piece, piece), piece)]

    mine = pltpu.make_async_copy(wq_ref, rows_of(dp), here.at[0])
    mine.start()
    firsts = [
        remote(wq_ref, rows_of(dp), q_send.at[i], q_recv.at[i], (plane[i], mp))
        for i in range(CHIPS)
    ]
    for copy in firsts:
        copy.start()
    shared = [remote(wq_ref, rows_of(dp), q_send.at[3], q_recv.at[3], sibling)]
    shared[0].start()
    own = pltpu.make_async_copy(pack_ref, all_ref.at[mp, dp], here.at[1])
    own.start()
    lifts = [
        remote(pack_ref, all_ref.at[mp, dp], z_send.at[s], z_recv.at[s], tall[s]) for s in range(3)
    ]
    own_bias = pltpu.make_async_copy(bias_ref, ball_ref.at[mp], here.at[2])
    own_bias.start()
    for copy in lifts:
        copy.start()
    biases = [
        remote(bias_ref, ball_ref.at[mp], b_send.at[s], b_recv.at[s], tall[s]) for s in range(3)
    ]
    for copy in biases:
        copy.start()
    for i in range(CHIPS):
        firsts[i].wait_recv()
        passed = remote(
            rows_of(plane[i]), rows_of(plane[i]), q_send.at[4 + i], q_recv.at[4 + i], sibling
        )
        passed.start()
        shared.append(passed)
    own.wait()

    def weights(s, kind):
        group = mp ^ s
        block = {0: dp, 1: dp, 2: dp, 4: plane[0], 5: plane[1], 6: plane[2]}
        block[3] = plane[0] if s % 2 == 0 else plane[1]
        peer = {0: (plane[0], mp), 1: (plane[1], mp)}
        peer[3] = peer[1] if s % 2 == 0 else peer[0]
        ref = all_ref.at[group, block[kind]]
        return remote(ref, ref, w_send.at[s, kind], w_recv.at[s, kind], peer.get(kind, sibling))

    def start_weights(s):
        if s > 0:
            lifts[s - 1].wait_recv()
        for kind in (0, 1, 2):
            weights(s, kind).start()

    def pass_weights(s):
        weights(s, 0).wait_recv()
        weights(s, 1).wait_recv()
        for kind in (3, 4, 5):
            weights(s, kind).start()

    def last_weights(s):
        weights(s, 3).wait_recv()
        weights(s, 6).start()

    start_weights(0)
    mine.wait()
    for copy in shared:
        copy.wait_recv()

    block = 256

    def project_rows(step, carry):
        part = pl.ds(pl.multiple_of(step * block, block), block)
        x = x_ref[part, :]
        made = off_ref[...] + jnp.zeros((block, off_ref.shape[1]), F32)
        made = made + jnp.dot(x, wfull_ref[...], preferred_element_type=F32)
        spread_rows(made.astype(BF16), seg_ref[part, :], slots, qs_ref, ka_ref, va_ref, kk_ref, part)
        return carry

    lax.fori_loop(0, rows // block, project_rows, 0)

    live_count = HEADS // 4 + (mp < HEADS % 4).astype(jnp.int32)
    per_share = share // sub
    actions = {
        0: [(start_weights, 1), (pass_weights, 0)],
        1: [(start_weights, 2), (last_weights, 0)],
        2: [(pass_weights, 1)],
        3: [(start_weights, 3), (last_weights, 1)],
        4: [(pass_weights, 2)],
        5: [(last_weights, 2)],
        6: [(pass_weights, 3)],
    }

    def send_rows(step, stage_index):
        group = mp ^ stage_index
        offset = pl.multiple_of(lax.rem(step, per_share) * sub, sub)
        source = pl.ds(pl.multiple_of(group * share, share) + offset, sub)
        return remote(
            stage.at[source], got_ref.at[mp, pl.ds(offset, sub)], a_send.at[step], a_recv.at[step],
            (dp, group),
        )

    def attend_rows(step, carry):
        stage_index = 3 - step // per_share
        group = mp ^ stage_index
        offset = lax.rem(step, per_share) * sub
        part = pl.ds(pl.multiple_of(group * share + offset, sub), sub)
        for when, todo in actions.items():

            @pl.when(step == when)
            def _():
                for act, s in todo:
                    act(s)

        for slot in range(slots):
            x = lax.dot_general(
                qs_ref[slot, part, :], ka_ref[slot], NT, preferred_element_type=F32
            )
            top = jnp.max(x, -1, keepdims=True)
            p = jnp.exp2(x - top).astype(BF16)
            made = jnp.dot(p, va_ref[slot], preferred_element_type=F32)
            total = -made[:, HD : HD + 1]
            mixed = made[:, :HD] / total
            one, two, three = thirds(top + jnp.log2(total))
            base = 3 * HD + MAX_SEGS
            qs_ref[slot, part, base : base + 3] = jnp.concatenate([one, two, three], 1)
            mixed_ref[slot, part, :] = mixed
            alive = (slot < live_count).astype(F32)
            stage[part, slot * HD : (slot + 1) * HD] = (mixed * alive).astype(BF16)

        @pl.when(step < 3 * per_share)
        def _():
            send_rows(step, stage_index).start()

        return carry

    lax.fori_loop(0, rows // sub, attend_rows, 0)
    start = pl.ds(pl.multiple_of(mp * share, share), share)
    keep = pltpu.make_async_copy(stage.at[start], got_ref.at[mp], here.at[3])
    keep.start()
    last_weights(3)
    for s in range(4):
        weights(s, 2).wait_recv()
        for kind in (4, 5, 6):
            weights(s, kind).wait_recv()
        for kind in range(7):
            weights(s, kind).wait_send()
    for copy in firsts + shared + lifts:
        copy.wait_send()
    for copy in biases:
        copy.wait()
    for step in range(3 * per_share):
        send_rows(step, 3 - step // per_share).wait()
    own_bias.wait()
    keep.wait()


def front(frames, wq, packed, up_bias, offsets, seg_ids, slots):
    rows, _ = frames.shape
    piece, lanes = packed.shape
    sub = 256
    shape = lambda n: jax.ShapeDtypeStruct((slots, rows, n), BF16)
    vmem = pl.BlockSpec(memory_space=pltpu.VMEM)
    dma = pltpu.SemaphoreType.DMA
    steps = rows // sub
    return pl.pallas_call(
        functools.partial(front_kernel, slots, sub),
        in_specs=[vmem] * 6,
        out_specs=[vmem] * 9,
        out_shape=[
            jax.ShapeDtypeStruct((4, 8, piece, lanes), BF16),
            jax.ShapeDtypeStruct((8 * piece, wq.shape[1]), BF16),
            jax.ShapeDtypeStruct((4,) + up_bias.shape, F32),
            shape(AUG), shape(AUG), shape(VAUG), shape(HD),
            jax.ShapeDtypeStruct((slots, rows, HD), F32),
            jax.ShapeDtypeStruct((4, rows // 4, slots * HD), BF16),
        ],
        scratch_shapes=[
            pltpu.VMEM((rows, slots * HD), BF16),
            dma((7,)), dma((7,)), dma((3,)), dma((3,)), dma((4, 7)), dma((4, 7)), dma((3,)), dma((3,)),
            dma((steps,)), dma((steps,)), dma((4,)),
        ],
        compiler_params=pltpu.CompilerParams(
            collective_id=1, has_side_effects=True, vmem_limit_bytes=VMEM_LIMIT
        ),
        name="front",
    )(frames, wq, packed, up_bias, offsets, seg_ids.reshape(rows, 1))


def project_kernel(slots, x_ref, w_ref, b_ref, seg_ref, qs_ref, ka_ref, va_ref, kk_ref):
    made = jnp.dot(x_ref[...], w_ref[...], preferred_element_type=F32) + b_ref[...]
    spread_rows(
        made.astype(BF16), seg_ref[...], slots, qs_ref, ka_ref, va_ref, kk_ref, slice(None)
    )


def project(frames, weight, offsets, seg_ids, slots):
    rows, depth = frames.shape
    block = min(512, rows)
    spread = lambda n: pl.BlockSpec((slots, block, n), lambda i: (0, i, 0))
    shape = lambda n: jax.ShapeDtypeStruct((slots, rows, n), BF16)
    return pl.pallas_call(
        functools.partial(project_kernel, slots),
        grid=(rows // block,),
        in_specs=[
            pl.BlockSpec((block, depth), lambda i: (i, 0)),
            pl.BlockSpec(weight.shape, lambda i: (0, 0)),
            pl.BlockSpec((1, offsets.shape[1]), lambda i: (0, 0)),
            pl.BlockSpec((block, 1), lambda i: (i, 0)),
        ],
        out_specs=[spread(AUG), spread(AUG), spread(VAUG), spread(HD)],
        out_shape=[shape(AUG), shape(AUG), shape(VAUG), shape(HD)],
        compiler_params=pltpu.CompilerParams(vmem_limit_bytes=VMEM_LIMIT),
        name="project",
    )(frames, weight, offsets, seg_ids.reshape(rows, 1))


def attend_kernel(sub, qs_ref, ka_ref, va_ref, qn_ref, mixed_ref):
    for at in range(0, qs_ref.shape[1], sub):
        part = slice(at, at + sub)
        x = lax.dot_general(qs_ref[0, part, :], ka_ref[0], NT, preferred_element_type=F32)
        top = jnp.max(x, -1, keepdims=True)
        p = jnp.exp2(x - top).astype(BF16)
        made = jnp.dot(p, va_ref[0], preferred_element_type=F32)
        total = -made[:, HD : HD + 1]
        mixed_ref[0, part, :] = made[:, :HD] / total
        one, two, three = thirds(top + jnp.log2(total))
        base = 3 * HD + MAX_SEGS
        blank = jnp.zeros((sub, AUG - base - 3), BF16)
        qn_ref[0, part, :] = jnp.concatenate(
            [qs_ref[0, part, :base], one, two, three, blank], 1
        )


def attend(qs, ka, va):
    slots, rows, _ = qs.shape
    block = min(512, rows)
    sub = min(256, block)
    whole = lambda n: pl.BlockSpec((1, rows, n), lambda h, i: (h, 0, 0))
    some = lambda n: pl.BlockSpec((1, block, n), lambda h, i: (h, i, 0))
    return pl.pallas_call(
        functools.partial(attend_kernel, sub),
        grid=(slots, rows // block),
        in_specs=[some(AUG), whole(AUG), whole(VAUG)],
        out_specs=[some(AUG), some(HD)],
        out_shape=[
            jax.ShapeDtypeStruct((slots, rows, AUG), BF16),
            jax.ShapeDtypeStruct((slots, rows, HD), F32),
        ],
        compiler_params=pltpu.CompilerParams(vmem_limit_bytes=VMEM_LIMIT),
        name="attend",
    )(qs, ka, va)


def attend_back_kernel(
    sub, qs_ref, ka_ref, va_ref, kk_ref, mixed_ref, up_ref, dq_ref, dk_ref, dv_ref, dk_acc, dv_acc
):
    step = pl.program_id(1)

    @pl.when(step == 0)
    def _():
        dk_acc[...] = jnp.zeros_like(dk_acc)
        dv_acc[...] = jnp.zeros_like(dv_acc)

    for at in range(0, qs_ref.shape[1], sub):
        part = slice(at, at + sub)
        q = qs_ref[0, part, :HD]
        up = up_ref[0, part, :]
        d_one, d_two, d_three = thirds(
            jnp.sum(up.astype(F32) * mixed_ref[0, part, :], -1, keepdims=True)
        )
        blank = lambda n: jnp.zeros((sub, n), BF16)
        upper = jnp.concatenate([up, d_one, d_two, d_three, blank(VAUG - HD - 3)], 1)
        x = lax.dot_general(qs_ref[0, part, :], ka_ref[0], NT, preferred_element_type=F32)
        p = jnp.exp2(x)
        dp = lax.dot_general(upper, va_ref[0], NT, preferred_element_type=F32)
        ds = (p * dp).astype(BF16)
        dv_acc[...] += lax.dot_general(up, p.astype(BF16), TN, preferred_element_type=F32)
        dk_acc[...] += lax.dot_general(q, ds, TN, preferred_element_type=F32)
        dq_ref[0, part, :] = (
            jnp.dot(ds, kk_ref[0], preferred_element_type=F32) * SCALE
        ).astype(BF16)

    @pl.when(step == pl.num_programs(1) - 1)
    def _():
        dk_ref[0] = (dk_acc[...] * SCALE).T.astype(BF16)
        dv_ref[0] = dv_acc[...].T.astype(BF16)


def attend_back(qs, ka, va, kk, mixed, up):
    slots, rows, _ = qs.shape
    block = min(512, rows)
    sub = min(256, block)
    whole = lambda n: pl.BlockSpec((1, rows, n), lambda h, i: (h, 0, 0))
    some = lambda n: pl.BlockSpec((1, block, n), lambda h, i: (h, i, 0))
    shape = jax.ShapeDtypeStruct((slots, rows, HD), BF16)
    return pl.pallas_call(
        functools.partial(attend_back_kernel, sub),
        grid=(slots, rows // block),
        in_specs=[
            some(AUG), whole(AUG), whole(VAUG), whole(HD), some(HD), some(HD),
        ],
        out_specs=[some(HD), whole(HD), whole(HD)],
        out_shape=[shape, shape, shape],
        scratch_shapes=[pltpu.VMEM((HD, rows), F32), pltpu.VMEM((HD, rows), F32)],
        compiler_params=pltpu.CompilerParams(vmem_limit_bytes=VMEM_LIMIT),
        name="attend_back",
    )(qs, ka, va, kk, mixed, up)


def norm_forward(summed):
    centre = summed - jnp.mean(summed, -1, keepdims=True)
    spread = jnp.mean(centre * centre, -1, keepdims=True)
    factor = lax.rsqrt(spread + EPS)
    return (centre * factor, factor)


def norm_backward(upper, normed, factor, gain):
    scaled = upper * gain
    return factor * (
        scaled
        - jnp.mean(scaled, -1, keepdims=True)
        - normed * jnp.mean(scaled * normed, -1, keepdims=True)
    )


def middle_kernel(
    groups, hidden_cols, block, linked,
    x_ref, y_ref, got_ref, w_ref, ub_ref, vec_ref,
    out_ref, s1_ref, back_ref, grad_ref, small_ref, *scratch,
):
    x_own, y_own, ow, act, pre_low, slope, hid_low, two_low, one_low, here = scratch[:10]
    share = out_ref.shape[0]
    width = got_ref.shape[2]
    gap = HALF - hidden_cols
    dp = lax.axis_index("dp")
    mp = lax.axis_index("mp")
    rows = pl.ds(pl.multiple_of(mp * share, share), share)
    loads = [
        pltpu.make_async_copy(x_ref.at[rows], x_own, here.at[0]),
        pltpu.make_async_copy(y_ref.at[rows], y_own, here.at[1]),
    ]
    for copy in loads:
        copy.start()
    if linked:
        back_own, grads, arrived, b_send, b_recv, g_send, g_recv = scratch[10:]
        core = lax.rem(dp, 2)
        sibling = (dp ^ 1, mp)
        plane_barrier([sibling] + [(dp, mp ^ s) for s in range(1, 4)])
    else:
        back_own, grads = back_ref, grad_ref
    out_bias, gain_one, shift_one = vec_ref[0:1, :], vec_ref[1:2, :], vec_ref[2:3, :]
    down_bias, gain_two, shift_two = vec_ref[3:4, :], vec_ref[4:5, :], vec_ref[5:6, :]
    for g in range(groups):
        ow[g, :, :gap] = w_ref[g, :, hidden_cols:HALF]
        ow[g, :, gap:] = w_ref[g, :, HALF + hidden_cols : HALF + hidden_cols + width - gap]
    small_ref[...] = jnp.zeros_like(small_ref)
    real = lane_marks(1, HALF, hidden_cols)
    alive = [
        lane_marks(1, width, HD * (HEADS // groups + (g < HEADS % groups))) for g in range(groups)
    ]
    for copy in loads:
        copy.wait()

    def send_back(step, s):
        part = pl.ds(pl.multiple_of(step * block, block), block)
        at = step * 3 + s - 1
        return remote(
            back_own.at[mp ^ s, part], back_ref.at[mp, part], b_send.at[at], b_recv.at[at], (dp, mp ^ s)
        )

    def some_rows(step, carry):
        part = pl.ds(pl.multiple_of(step * block, block), block)
        summed = x_own[part, :].astype(F32) + out_bias
        for g in range(groups):
            summed += lax.dot_general(got_ref[g, part, :], ow[g], NT, preferred_element_type=F32)
        normed_one, factor_one = norm_forward(summed)
        hidden = normed_one * gain_one + shift_one
        hidden_low = hidden.astype(BF16)
        hid_low[part, :] = hidden_low
        feed = hidden + down_bias
        for g in range(groups):
            pre = jnp.dot(hidden_low, w_ref[g, :, :HALF], preferred_element_type=F32) + ub_ref[g]
            half = 0.5 + 0.5 * lax.erf(pre * math.sqrt(0.5))
            bell = jnp.exp(pre * pre * -0.5) * (pre * (1.0 / math.sqrt(2.0 * math.pi)))
            slope[g] = jnp.where(real, half + bell, 0.0)
            made = jnp.where(real, pre * half, 0.0).astype(BF16)
            act[g, part, :] = made
            feed += lax.dot_general(
                made, w_ref[g, :, HALF : 2 * HALF], NT, preferred_element_type=F32
            )
        normed_two, factor_two = norm_forward(feed)
        out_ref[part, :] = (normed_two * gain_two + shift_two).astype(BF16)
        upstream = y_own[part, :].astype(F32)
        two_grad = norm_backward(upstream, normed_two, factor_two, gain_two)
        sum_two = two_grad.astype(BF16)
        two_low[part, :] = sum_two
        hidden_grad = two_grad
        for g in range(groups):
            act_grad = jnp.dot(
                sum_two, w_ref[g, :, HALF : 2 * HALF], preferred_element_type=F32
            )
            low = (slope[g] * act_grad).astype(BF16)
            pre_low[g, part, :] = low
            hidden_grad += lax.dot_general(
                low, w_ref[g, :, :HALF], NT, preferred_element_type=F32
            )
            small_ref[8 + g : 9 + g, :] += jnp.sum(low.astype(F32), 0, keepdims=True)
        one_grad = norm_backward(hidden_grad, normed_one, factor_one, gain_one)
        sum_one = one_grad.astype(BF16)
        s1_ref[part, :] = one_grad
        one_low[part, :] = sum_one
        for g in range(groups):
            made = jnp.dot(sum_one, ow[g], preferred_element_type=F32)
            back_own[g, part, :] = jnp.where(alive[g], made, 0.0).astype(BF16)
        if linked:
            for s in range(1, 4):
                send_back(step, s).start()
        for at, term in enumerate((
            sum_one.astype(F32), hidden_grad * normed_one, hidden_grad,
            sum_two.astype(F32), upstream * normed_two, upstream,
        )):
            small_ref[at : at + 1, :] += jnp.sum(term, 0, keepdims=True)
        return carry

    lax.fori_loop(0, share // block, some_rows, 0)
    if linked:
        keep = pltpu.make_async_copy(back_own.at[mp], back_ref.at[mp], here.at[2])
        keep.start()
    hid_flip, two_flip, one_flip = hid_low[...].T, two_low[...].T, one_low[...].T
    shared = []
    for g in range(groups):
        made = jnp.dot(hid_flip, pre_low[g], preferred_element_type=F32).astype(BF16)
        grad_out = jnp.dot(one_flip, got_ref[g], preferred_element_type=F32).astype(BF16)
        rest = width - gap
        left = jnp.concatenate([made[:, :hidden_cols], grad_out[:, :gap]], 1)
        made = jnp.dot(two_flip, act[g], preferred_element_type=F32).astype(BF16)
        spare = w_ref.shape[2] - HALF - hidden_cols - rest
        right = jnp.concatenate(
            [made[:, :hidden_cols], grad_out[:, gap:], jnp.zeros((made.shape[0], spare), BF16)], 1
        )
        if linked:
            piece = grads.shape[4 - 1]
            for d in range(8):
                at = slice(d * piece, (d + 1) * piece)
                grads[g, d // 2, d % 2, :, :HALF] = left[at]
                grads[g, d // 2, d % 2, :, HALF:] = right[at]
            copy = remote(grads.at[g, :, 1 - core], arrived.at[g], g_send.at[g], g_recv.at[g], sibling)
            copy.start()
            shared.append(copy)
        else:
            grads[g, :, :HALF] = left
            grads[g, :, HALF:] = right
    if linked:
        for g in range(groups):
            shared[g].wait_recv()
            for c in range(4):
                grad_ref[g, c] = grads[g, c, core] + arrived[g, c]
        for step in range(share // block):
            for s in range(1, 4):
                send_back(step, s).wait()
        for copy in shared:
            copy.wait_send()
        keep.wait()


def middle(frames, cotangent, got, weights, up_bias, vectors, hidden_cols, linked):
    groups, share, width = got.shape
    depth = frames.shape[1]
    lanes = weights.shape[2]
    block = min(256, share)
    vmem = pl.BlockSpec(memory_space=pltpu.VMEM)
    rest = pl.BlockSpec(memory_space=pl.ANY)
    dma = pltpu.SemaphoreType.DMA
    scratch = [
        pltpu.VMEM((share, depth), BF16),
        pltpu.VMEM((share, depth), BF16),
        pltpu.VMEM((groups, depth, width), BF16),
        pltpu.VMEM((groups, share, HALF), BF16),
        pltpu.VMEM((groups, share, HALF), BF16),
        pltpu.VMEM((groups, block, HALF), F32),
        pltpu.VMEM((share, depth), BF16),
        pltpu.VMEM((share, depth), BF16),
        pltpu.VMEM((share, depth), BF16),
        dma((3,)),
    ]
    grads = jax.ShapeDtypeStruct(weights.shape, BF16)
    if linked:
        piece = depth // 8
        grads = jax.ShapeDtypeStruct((groups, 4, piece, lanes), BF16)
        sends = 3 * (share // block)
        scratch += [
            pltpu.VMEM((groups, share, width), BF16),
            pltpu.VMEM((groups, 4, 2, piece, lanes), BF16),
            pltpu.VMEM((groups, 4, piece, lanes), BF16),
            dma((sends,)), dma((sends,)), dma((groups,)), dma((groups,)),
        ]
    extra = dict(collective_id=2, has_side_effects=True) if linked else {}
    return pl.pallas_call(
        functools.partial(middle_kernel, groups, hidden_cols, block, linked),
        in_specs=[rest, rest, vmem, vmem, vmem, vmem],
        out_specs=[vmem] * 5,
        out_shape=[
            jax.ShapeDtypeStruct((share, depth), BF16),
            jax.ShapeDtypeStruct((share, depth), F32),
            jax.ShapeDtypeStruct((groups, share, width), BF16),
            grads,
            jax.ShapeDtypeStruct((16, HALF), F32),
        ],
        scratch_shapes=scratch,
        compiler_params=pltpu.CompilerParams(vmem_limit_bytes=VMEM_LIMIT, **extra),
        name="middle",
    )(frames, cotangent, got, weights, up_bias, vectors)


PAIRS = (
    (0, 3), (1, 3), (2, 3), (3, 3), (3, 2), (3, 1), (3, 0), (0, 2), (1, 2), (2, 2), (2, 1), (2, 0),
    (0, 1), (1, 1), (1, 0), (0, 0),
)
ENDS = {6: 3, 11: 2, 14: 1, 15: 0}


def pick(table, step):
    made = jnp.int32(table[0])
    for at in range(1, len(table)):
        made = jnp.where(step >= at, jnp.int32(table[at]), made)
    return made


def back_kernel(
    slots, sub,
    qs_ref, ka_ref, va_ref, kk_ref, mixed_ref, up_ref, sums_ref, x_ref, wq_ref, one_ref, small_ref,
    fg_ref, gq_ref, gb_ref, gw_ref, gs_ref,
    upper, up_flip, q_flip, dq_acc, dk_acc, dv_acc, low, part_out, chain, fresh, far_in, near_in, third,
    tall_in, gq_own, gq_in, gb_own, gb_in, tiny, tiny_in,
    c_send, c_recv, f_send, f_recv, n_send, n_recv, t_send, t_recv, q_send, q_recv, b_send, b_recv,
    s_send, s_recv,
):
    dp = lax.axis_index("dp")
    mp = lax.axis_index("mp")
    chip = dp // 2
    rows, depth = x_ref.shape
    share = rows // 4
    width = slots * HD
    others = [(dp ^ d, mp) for d in range(1, 8)]
    tall = [(dp, mp ^ s) for s in range(1, 4)]
    plane_barrier(others + tall)
    x_peer, y_peer = (dp ^ 2, mp), (dp ^ 4, mp)

    def rows_of(name):
        return pl.ds(pl.multiple_of((mp ^ name) * share, share), share)

    def far(s):
        return remote(
            sums_ref.at[mp ^ s, chip ^ 3], far_in.at[s], f_send.at[s], f_recv.at[s],
            y_peer if s % 2 == 0 else x_peer,
        )

    def near(s, kind):
        toward_x = (s % 2 == 0) == (kind == 1)
        source = third.at[s] if kind == 1 else sums_ref.at[mp ^ s, chip ^ (1 if toward_x else 2)]
        return remote(
            source, near_in.at[s, kind], n_send.at[s, kind], n_recv.at[s, kind],
            x_peer if toward_x else y_peer,
        )

    def lift(s):
        return remote(
            fresh.at[s], tall_in.at[s], t_send.at[s], t_recv.at[s], (dp, mp ^ s)
        )

    def begin_grads(s):
        far(s).start()
        near(s, 0).start()

    def join_far(s):
        far(s).wait_recv()
        third[s] = sums_ref[mp ^ s, chip ^ (1 if s % 2 == 0 else 2)] + far_in[s]
        near(s, 1).start()

    def join_near(s):
        near(s, 0).wait_recv()
        near(s, 1).wait_recv()
        total = sums_ref[mp ^ s, chip].astype(F32) + near_in[s, 0].astype(F32)
        fresh[s] = (total + near_in[s, 1].astype(F32)).astype(BF16)
        if s > 0:
            lift(s).start()

    partners = [(dp ^ 1, mp), (dp ^ 2, mp), (dp ^ 4, mp), (dp, mp ^ 1), (dp, mp ^ 2)]

    def swap(at):
        return remote(tiny.at[at], tiny_in.at[at], s_send.at[at], s_recv.at[at], partners[at])

    def small_step(at):
        if at == 0:
            tiny[0] = small_ref[...]
        else:
            swap(at - 1).wait_recv()
            made = tiny[at - 1] + tiny_in[at - 1]
            if at == len(partners):
                gs_ref[...] = made
                return
            tiny[at] = made
        swap(at).start()

    def chain_copy(name, leftward):
        block = mp ^ name
        target = mp - 1 if leftward else mp + 1
        slot = jnp.where(block == target, 4, block) if leftward else block
        return remote(
            part_out.at[name], chain.at[slot], c_send.at[name], c_recv.at[slot], (dp, target)
        )

    def chain_arrival(slot):
        return remote(part_out.at[0], chain.at[slot], c_send.at[0], c_recv.at[slot], (dp, mp ^ 1))

    def relay(name):
        block = mp ^ name
        inner = (mp == 1) | (mp == 2)
        waits = inner

        @pl.when(waits)
        def _():
            chain_arrival(block).wait_recv()
            part_out[name] = (
                part_out[name].astype(F32) + chain[block].astype(F32)
            ).astype(BF16)

        @pl.when(block < mp)
        def _():
            chain_copy(name, True).start()

        @pl.when(block > mp)
        def _():
            chain_copy(name, False).start()

    def finish(name):
        at = rows_of(name)
        for slot in range(slots):
            col = slot * HD
            low[at, col : col + HD] = (dq_acc[slot, at, :] * SCALE).astype(BF16)
            low[at, width + col : width + col + HD] = (dk_acc[slot, :, at] * SCALE).T.astype(BF16)
            low[at, 2 * width + col : 2 * width + col + HD] = dv_acc[slot, :, at].T.astype(BF16)
        part_out[name] = lax.dot_general(
            low[at, :], wq_ref[...], NT, preferred_element_type=F32
        ).astype(BF16)

    dq_acc[...] = jnp.zeros_like(dq_acc)
    dk_acc[...] = jnp.zeros_like(dk_acc)
    dv_acc[...] = jnp.zeros_like(dv_acc)
    begin_grads(3)
    begin_grads(2)
    small_step(0)

    def prepare(step, carry):
        at = pl.ds(pl.multiple_of(step * share, share), share)
        for slot in range(slots):
            up = up_ref[step, :, slot * HD : (slot + 1) * HD]
            one, two, three = thirds(
                jnp.sum(up.astype(F32) * mixed_ref[slot, at, :], -1, keepdims=True)
            )
            blank = jnp.zeros((share, VAUG - HD - 3), BF16)
            upper[slot, at, :] = jnp.concatenate([up, one, two, three, blank], 1)
            up_flip[slot, :, at] = up.T
            q_flip[slot, :, at] = qs_ref[slot, at, :HD].T
        return carry

    lax.fori_loop(0, 4, prepare, 0)
    actions = {
        1: [(small_step, 1)],
        2: [(begin_grads, 1), (small_step, 2)],
        3: [(join_far, 3), (small_step, 3)],
        4: [(begin_grads, 0), (small_step, 4)],
        5: [(join_far, 2)],
        6: [(small_step, 5)],
        7: [(join_far, 1), (join_near, 3)],
        9: [(join_far, 0), (join_near, 2)],
        12: [(join_near, 1)],
        14: [(join_near, 0)],
    }

    def pair(step, carry):
        query = mp ^ pick([p[0] for p in PAIRS], step)
        key = mp ^ pick([p[1] for p in PAIRS], step)
        keys = pl.ds(pl.multiple_of(key * share, share), share)
        for when, todo in actions.items():

            @pl.when(step == when)
            def _():
                for act, s in todo:
                    act(s)

        for at in range(0, share, sub):
            part = pl.ds(pl.multiple_of(query * share + at, sub), sub)
            for slot in range(slots):
                x = lax.dot_general(
                    qs_ref[slot, part, :], ka_ref[slot, keys, :], NT, preferred_element_type=F32
                )
                p = jnp.exp2(x)
                dp_ = lax.dot_general(
                    upper[slot, part, :], va_ref[slot, keys, :], NT, preferred_element_type=F32
                )
                ds = (p * dp_).astype(BF16)
                dv_acc[slot, :, keys] += jnp.dot(
                    up_flip[slot, :, part], p.astype(BF16), preferred_element_type=F32
                )
                dk_acc[slot, :, keys] += jnp.dot(
                    q_flip[slot, :, part], ds, preferred_element_type=F32
                )
                dq_acc[slot, part, :] += jnp.dot(
                    ds, kk_ref[slot, keys, :], preferred_element_type=F32
                )
        for when, name in ENDS.items():

            @pl.when(step == when)
            def _():
                finish(name)
                if name > 0:

                    @pl.when((mp == 0) | (mp == 3))
                    def _():
                        relay(name)

        return carry

    lax.fori_loop(0, len(PAIRS), pair, 0)
    for name in (2, 3, 1):

        @pl.when((mp == 1) | (mp == 2))
        def _():
            relay(name)

    gq_parts = low[...]
    ones = jnp.ones((16, rows), BF16)
    gb_own[...] = jnp.dot(ones, gq_parts, preferred_element_type=F32)[0:8, :]
    gb_in[dp] = gb_own[...]
    piece = depth // 8
    made = lax.dot_general(x_ref[...], gq_parts, TN, preferred_element_type=F32).astype(BF16)
    for d in range(8):
        gq_own[d] = made[d * piece : (d + 1) * piece]
    q_copies = []
    for d in range(1, 8):
        to = dp ^ d
        q_copies.append(
            remote(gq_own.at[to], gq_in.at[d - 1], q_send.at[d - 1], q_recv.at[d - 1], others[d - 1])
        )
        q_copies.append(
            remote(gb_own, gb_in.at[dp], b_send.at[d - 1], b_recv.at[d - 1], others[d - 1])
        )
    for copy in q_copies:
        copy.start()
    for s in range(1, 4):
        lift(s).wait_recv()
    total = fresh[0].astype(F32)
    for s in range(1, 4):
        total = total + tall_in[s].astype(F32)
    gw_ref[...] = total
    for copy in q_copies:
        copy.wait_recv()
    total = gq_own[dp].astype(F32)
    for d in range(7):
        total = total + gq_in[d].astype(F32)
    gq_ref[...] = total
    total = gb_in[0]
    for d in range(1, 8):
        total = total + gb_in[d]
    gb_ref[...] = total

    wide = one_ref[...] + part_out[0].astype(F32)

    @pl.when(mp > 0)
    def _():
        chain_arrival(mp).wait_recv()

    @pl.when(mp < 3)
    def _():
        chain_arrival(4).wait_recv()

    left = jnp.where(mp > 0, chain[mp].astype(F32), 0.0)
    right = jnp.where(mp < 3, chain[4].astype(F32), 0.0)
    fg_ref[...] = (wide + left + right).astype(BF16)
    for name in (1, 2, 3):
        remote(
            part_out.at[name], chain.at[0], c_send.at[name], c_recv.at[0], (dp, mp ^ 1)
        ).wait_send()
    for s in range(4):
        far(s).wait_send()
        near(s, 0).wait_send()
        near(s, 1).wait_send()
        if s > 0:
            lift(s).wait_send()
    for at in range(len(partners)):
        swap(at).wait_send()
    for copy in q_copies:
        copy.wait_send()


def back_pass(qs, ka, va, kk, mixed, up, sums, frames, wq, one_grad, small):
    slots, rows, _ = qs.shape
    depth = frames.shape[1]
    share = rows // 4
    piece, lanes = sums.shape[2:]
    cols = wq.shape[1]
    vmem = pl.BlockSpec(memory_space=pltpu.VMEM)
    dma = pltpu.SemaphoreType.DMA
    V = pltpu.VMEM
    return pl.pallas_call(
        functools.partial(back_kernel, slots, min(256, share)),
        in_specs=[vmem] * 11,
        out_specs=[vmem] * 5,
        out_shape=[
            jax.ShapeDtypeStruct((share, depth), BF16),
            jax.ShapeDtypeStruct((piece, cols), F32),
            jax.ShapeDtypeStruct((8, cols), F32),
            jax.ShapeDtypeStruct((piece, lanes), F32),
            jax.ShapeDtypeStruct(small.shape, F32),
        ],
        scratch_shapes=[
            V((slots, rows, VAUG), BF16), V((slots, HD, rows), BF16), V((slots, HD, rows), BF16),
            V((slots, rows, HD), F32), V((slots, HD, rows), F32), V((slots, HD, rows), F32),
            V((rows, cols), BF16), V((4, share, depth), BF16), V((5, share, depth), BF16),
            V((4, piece, lanes), BF16), V((4, piece, lanes), BF16), V((4, 2, piece, lanes), BF16),
            V((4, piece, lanes), BF16), V((4, piece, lanes), BF16),
            V((8, piece, cols), BF16), V((7, piece, cols), BF16),
            V((8, cols), F32), V((8, 8, cols), F32), V((5,) + small.shape, F32), V((5,) + small.shape, F32),
            dma((4,)), dma((5,)), dma((4,)), dma((4,)), dma((4, 2)), dma((4, 2)), dma((4,)), dma((4,)),
            dma((7,)), dma((7,)), dma((7,)), dma((7,)), dma((5,)), dma((5,)),
        ],
        compiler_params=pltpu.CompilerParams(
            collective_id=3, has_side_effects=True, vmem_limit_bytes=60 << 20
        ),
        name="back_pass",
    )(qs, ka, va, kk, mixed, up, sums, frames, wq, one_grad, small)


def body(
    frames, seg_ids, qkv_weight, qkv_bias, out_weight, out_bias, gain_one, shift_one,
    up_weight, up_bias, down_weight, down_bias, gain_two, shift_two, cotangent,
):
    rows, depth = frames.shape
    mp_size = lax.axis_size("mp")
    dp_size = lax.axis_size("dp")
    mp_index = lax.axis_index("mp")
    share = rows // mp_size
    slots = qkv_weight.shape[2] // HD
    width = slots * HD
    hidden_cols = up_weight.shape[1]
    piece = qkv_weight.shape[1]
    gap = HALF - hidden_cols
    spare = -(HALF + hidden_cols + width - gap) % 128
    live_count = HEADS // mp_size + (mp_index < HEADS % mp_size).astype(jnp.int32)
    live = (jnp.arange(slots) < live_count).astype(F32)

    wq = jnp.transpose(qkv_weight, (1, 0, 2)).reshape(piece, 3 * width)
    out_flip = out_weight.T
    packed = jnp.concatenate(
        [up_weight, out_flip[:, :gap], down_weight.T, out_flip[:, gap:], jnp.zeros((piece, spare), BF16)], 1
    )
    ub_pad = jnp.pad(up_bias, (0, gap))[None]
    offsets = jnp.concatenate([qkv_bias[0], jnp.zeros_like(qkv_bias[0]), qkv_bias[1]])[None]
    linked = (dp_size, mp_size) == (8, 4)
    if linked:
        weights, qkv_full, ub_full, qs, ka, va, kk, mixed, got = front(
            frames, wq, packed, ub_pad, offsets, seg_ids, slots
        )
        weights = weights.reshape(mp_size, depth, -1)
    else:
        qkv_full = lax.all_gather(wq, "dp", axis=0, tiled=True)
        weights = lax.all_gather(packed, "mp", axis=0, tiled=False)
        weights = lax.all_gather(weights, "dp", axis=1, tiled=True)
        ub_full = lax.all_gather(ub_pad, "mp", axis=0, tiled=False)
        qs, ka, va, kk = project(frames, qkv_full, offsets, seg_ids, slots)
        qs, mixed = attend(qs, ka, va)
        mixed_low = (mixed * live[:, None, None]).astype(BF16)
        sent = mixed_low.reshape(slots, mp_size, share, HD).transpose(1, 2, 0, 3)
        got = lax.all_to_all(sent.reshape(mp_size, share, width), "mp", 0, 0, tiled=True)
    vectors = jnp.stack(
        [out_bias, gain_one, shift_one, down_bias, gain_two, shift_two, out_bias, out_bias]
    )
    output_frames, sum_one_grad, back, partial, small = middle(
        frames, cotangent, got, weights, ub_full, vectors, hidden_cols, linked
    )
    if linked:
        frames_grad, grad_qkv, bias_sums, partial, small = back_pass(
            qs, ka, va, kk, mixed, back, partial, frames, qkv_full, sum_one_grad, small
        )
        bias_sums = bias_sums[0]
    else:
        back = lax.all_to_all(back, "mp", 0, 0, tiled=True)
        back = back.reshape(rows, slots, HD).transpose(1, 0, 2)
        partial = lax.psum_scatter(partial, "dp", scatter_dimension=1, tiled=True)
        partial = lax.psum_scatter(partial, "mp", scatter_dimension=0, tiled=True)[0].astype(F32)
        small = lax.psum(small, ("dp", "mp"))
        dq, dk, dv = attend_back(qs, ka, va, kk, mixed, back)
        grads_low = jnp.stack([dq, dk, dv]).transpose(2, 0, 1, 3).reshape(rows, 3 * width)
        bias_sums = lax.psum(jnp.sum(grads_low.astype(F32), 0), "dp")
        grad_qkv = jnp.einsum("rd,rs->ds", frames, grads_low, preferred_element_type=F32)
        arrived = lax.all_to_all(
            grad_qkv.astype(BF16).reshape(dp_size, piece, 3 * width), "dp", 0, 0, tiled=True
        )
        grad_qkv = arrived.astype(F32).sum(0)
        input_part = jnp.einsum("rs,ds->rd", grads_low, qkv_full, preferred_element_type=F32)
        input_sum = lax.psum_scatter(input_part.astype(BF16), "mp", scatter_dimension=0, tiled=True)
        frames_grad = (input_sum.astype(F32) + sum_one_grad).astype(BF16)
    grad_qkv = grad_qkv.reshape(piece, 3, width).transpose(1, 0, 2)
    bias_sums = bias_sums.reshape(3, width)
    qkv_bias_grad = jnp.stack([bias_sums[0], bias_sums[2]])
    out_grad = jnp.concatenate(
        [partial[:, hidden_cols:HALF], partial[:, HALF + hidden_cols : HALF + hidden_cols + width - gap]], 1
    )
    return (
        output_frames,
        frames_grad,
        grad_qkv,
        qkv_bias_grad,
        out_grad.T,
        small[0],
        small[1],
        small[2],
        partial[:, :hidden_cols],
        lax.dynamic_index_in_dim(small, 8 + mp_index, 0, False)[:hidden_cols],
        partial[:, HALF : HALF + hidden_cols].T,
        small[3],
        small[4],
        small[5],
    )


def solution(mesh):
    in_specs = (
        P("dp", None), P("dp"), P(None, "dp", "mp"), P(None, "mp"), P("mp", "dp"), P(), P(), P(),
        P("dp", "mp"), P("mp"), P("mp", "dp"), P(), P(), P(), P("dp", None),
    )
    out_specs = (
        P(("dp", "mp"), None), P(("dp", "mp"), None), P(None, "dp", "mp"), P(None, "mp"),
        P("mp", "dp"), P(), P(), P(), P("dp", "mp"), P("mp"), P("mp", "dp"), P(), P(), P(),
    )
    return jax.shard_map(body, mesh=mesh, in_specs=in_specs, out_specs=out_specs, check_vma=False)
```

```python
import functools
import math

import jax
import jax.numpy as jnp
from jax import lax
from jax.experimental import pallas as pl
from jax.experimental.pallas import tpu as pltpu
from jax.sharding import PartitionSpec as P

HEADS = 10
HD = 64
EPS = 1e-05
SCALE = 0.125
MAX_SEGS = 16
MASKED = -1e30
UNIT = SCALE * math.log2(math.e)
AUG = 256
VAUG = 128
NT = (((1,), (1,)), ((), ()))
TN = (((0,), (0,)), ((), ()))
F32 = jnp.float32
BF16 = jnp.bfloat16
VMEM_LIMIT = 56 << 20
MESH = pl.DeviceIdType.MESH
CHIPS = 3
HALF = 640


def thirds(wide):
    first = wide.astype(BF16)
    rest = wide - first.astype(F32)
    second = rest.astype(BF16)
    third = (rest - second.astype(F32)).astype(BF16)
    return first, second, third


def lane_marks(rows, width, count):
    return lax.broadcasted_iota(jnp.int32, (rows, width), 1) < count


def spread_rows(made, picked, slots, qs_ref, ka_ref, va_ref, kk_ref, rows):
    count = made.shape[0]
    width = slots * HD
    chosen = picked.astype(BF16)
    barred = ((picked - 1.0) * -MASKED).astype(BF16)
    tail = AUG - 3 * HD - MAX_SEGS
    q_tail = jnp.zeros((count, tail), BF16)
    minus = jnp.where(lane_marks(count, tail, 3), -1.0, 0.0).astype(BF16)
    v_tail = jnp.where(lane_marks(count, VAUG - HD, 3), -1.0, 0.0).astype(BF16)
    for slot in range(slots):
        at = slot * HD
        q = made[:, at : at + HD]
        k = made[:, width + at : width + at + HD]
        v = made[:, 2 * width + at : 2 * width + at + HD]
        one, two, three = thirds(k.astype(F32) * UNIT)
        qs_ref[slot, rows, :] = jnp.concatenate([q, q, q, chosen, q_tail], 1)
        ka_ref[slot, rows, :] = jnp.concatenate([one, two, three, barred, minus], 1)
        va_ref[slot, rows, :] = jnp.concatenate([v, v_tail], 1)
        kk_ref[slot, rows, :] = k


def plane_barrier(peers):
    barrier = pltpu.get_barrier_semaphore()
    for peer in peers:
        pl.semaphore_signal(barrier, inc=1, device_id=peer, device_id_type=MESH)
    pl.semaphore_wait(barrier, len(peers))


def remote(src, dst, send, recv, peer):
    return pltpu.make_async_remote_copy(
        src_ref=src, dst_ref=dst, send_sem=send, recv_sem=recv, device_id=peer, device_id_type=MESH
    )


def pack_rows(wide):
    half = wide.shape[0] // 2
    third = wide[:, 2 * HD :]
    return jnp.concatenate(
        [wide[:, : 2 * HD], jnp.concatenate([third[:half], third[half:]], 1)], 0
    )


def unpack_rows(packed):
    rows = packed.shape[0] * 2 // 3
    rest = packed[rows:]
    return jnp.concatenate(
        [packed[:rows], jnp.concatenate([rest[:, :HD], rest[:, HD:]], 0)], 1
    )


def front_kernel(
    slots, sub,
    x_ref, qkv_ref, up_ref, down_ref, out_ref, vec_ref, seg_ref,
    all_ref, wfull_ref, ball_ref, qs_ref, ka_ref, va_ref, kk_ref, mixed_ref, got_ref,
    stage, wq_ref, pack_ref, bias_ref,
    q_send, q_recv, z_send, z_recv, w_send, w_recv, b_send, b_recv, a_send, a_recv, here,
):
    dp = lax.axis_index("dp")
    mp = lax.axis_index("mp")
    plane = [dp ^ 2, dp ^ 4, dp ^ 6]
    sibling = (dp ^ 1, mp)
    tall = [(dp, mp ^ s) for s in range(1, 4)]
    inner = (mp == 1) | (mp == 2)
    width = slots * HD
    for i in range(3):
        wq_ref[:, i * width : (i + 1) * width] = qkv_ref[i]
    hidden_cols = up_ref.shape[1]
    gap = HALF - hidden_cols
    rest = width - gap
    pack_ref[:, :hidden_cols] = up_ref[...]
    pack_ref[:, hidden_cols:HALF] = out_ref[:, :gap]
    pack_ref[:, HALF : HALF + hidden_cols] = down_ref[...]
    pack_ref[:, HALF + hidden_cols : HALF + hidden_cols + rest] = out_ref[:, gap:]
    spare = pack_ref.shape[1] - HALF - hidden_cols - rest
    pack_ref[:, HALF + hidden_cols + rest :] = jnp.zeros((pack_ref.shape[0], spare), BF16)
    bias_ref[...] = vec_ref[6:7, :]
    plane_barrier([sibling] + [(d, mp) for d in plane] + tall)
    rows = x_ref.shape[0]
    share = rows // 4

    piece = wq_ref.shape[0]

    def rows_of(d):
        return wfull_ref.at[pl.ds(pl.multiple_of(d * piece, piece), piece)]

    mine = pltpu.make_async_copy(wq_ref, rows_of(dp), here.at[0])
    mine.start()
    firsts = [
        remote(wq_ref, rows_of(dp), q_send.at[i], q_recv.at[i], (plane[i], mp))
        for i in range(CHIPS)
    ]
    for copy in firsts:
        copy.start()
    shared = [remote(wq_ref, rows_of(dp), q_send.at[3], q_recv.at[3], sibling)]
    shared[0].start()
    own = pltpu.make_async_copy(pack_ref, all_ref.at[mp, dp], here.at[1])
    own.start()
    def lift(at, s, landing, peer):
        ref = all_ref.at[mp ^ s, dp]
        return remote(pack_ref if s == 0 else ref, ref, z_send.at[at], z_recv.at[landing], peer)

    near, middle = tall[0], tall[2]
    lifts = [lift(0, 0, 1, near)]
    inner_lifts = [
        lift(1, 0, 3, middle), lift(2, 1, 2, middle), lift(3, 3, 2, near), lift(4, 2, 3, near),
    ]

    def arrive(s):
        lift(0, s, s, near).wait_recv()

    own_bias = pltpu.make_async_copy(bias_ref, ball_ref.at[mp], here.at[2])
    own_bias.start()
    lifts[0].start()

    @pl.when(inner)
    def _():
        inner_lifts[0].start()

    biases = [
        remote(bias_ref, ball_ref.at[mp], b_send.at[s], b_recv.at[s], tall[s]) for s in range(3)
    ]
    for copy in biases:
        copy.start()
    for i in range(CHIPS):
        firsts[i].wait_recv()
        passed = remote(
            rows_of(plane[i]), rows_of(plane[i]), q_send.at[4 + i], q_recv.at[4 + i], sibling
        )
        passed.start()
        shared.append(passed)
    own.wait()

    def weights(s, kind):
        group = mp ^ s
        block = {0: dp, 1: dp, 2: dp, 4: plane[0], 5: plane[1], 6: plane[2]}
        block[3] = plane[0] if s % 2 == 0 else plane[1]
        peer = {0: (plane[0], mp), 1: (plane[1], mp)}
        peer[3] = peer[1] if s % 2 == 0 else peer[0]
        ref = all_ref.at[group, block[kind]]
        return remote(ref, ref, w_send.at[s, kind], w_recv.at[s, kind], peer.get(kind, sibling))

    def start_weights(s):
        if s == 3:

            @pl.when(~inner)
            def _():
                arrive(3)

        for kind in (0, 1, 2):
            weights(s, kind).start()

    def pass_weights(s):
        weights(s, 0).wait_recv()
        weights(s, 1).wait_recv()
        for kind in (3, 4, 5):
            weights(s, kind).start()

    def last_weights(s):
        weights(s, 3).wait_recv()
        weights(s, 6).start()

    start_weights(0)
    mine.wait()
    for copy in shared:
        copy.wait_recv()
    arrive(1)

    @pl.when(inner)
    def _():
        inner_lifts[1].start()
        arrive(3)
        inner_lifts[2].start()


    block = 256

    def project_rows(step, carry):
        part = pl.ds(pl.multiple_of(step * block, block), block)
        x = x_ref[part, :]
        offsets = jnp.concatenate(
            [vec_ref[7:8, :width], jnp.zeros((1, width), F32), vec_ref[8:9, :width]], 1
        )
        made = jnp.dot(x, wfull_ref[...], preferred_element_type=F32) + offsets
        marks = seg_ref[:, part] == lax.broadcasted_iota(jnp.int32, (MAX_SEGS, block), 0)
        picked = jnp.where(marks, 1.0, 0.0).T
        spread_rows(made.astype(BF16), picked, slots, qs_ref, ka_ref, va_ref, kk_ref, part)
        return carry

    lax.fori_loop(0, rows // block, project_rows, 0)
    arrive(2)

    @pl.when(inner)
    def _():
        inner_lifts[3].start()

    pass_weights(0)
    start_weights(1)

    live_count = HEADS // 4 + (mp < HEADS % 4).astype(jnp.int32)
    per_share = share // sub
    actions = {
        1: [(start_weights, 2), (last_weights, 0)],
        2: [(pass_weights, 1)],
        3: [(start_weights, 3), (last_weights, 1)],
        4: [(pass_weights, 2)],
        5: [(last_weights, 2)],
        6: [(pass_weights, 3)],
    }

    def send_rows(step, stage_index):
        return remote(
            stage.at[step], got_ref.at[mp, lax.rem(step, per_share)], a_send.at[step], a_recv.at[step],
            (dp, mp ^ stage_index),
        )

    def attend_rows(step, carry):
        stage_index = 3 - step // per_share
        group = mp ^ stage_index
        offset = lax.rem(step, per_share) * sub
        part = pl.ds(pl.multiple_of(group * share + offset, sub), sub)
        for when, todo in actions.items():

            @pl.when(step == when)
            def _():
                for act, s in todo:
                    act(s)

        kept = []
        for slot in range(slots):
            x = lax.dot_general(
                qs_ref[slot, part, :], ka_ref[slot], NT, preferred_element_type=F32
            )
            top = jnp.max(x, -1, keepdims=True)
            p = jnp.exp2(x - top).astype(BF16)
            made = jnp.dot(p, va_ref[slot], preferred_element_type=F32)
            total = -made[:, HD : HD + 1]
            mixed = made[:, :HD] / total
            one, two, three = thirds(top + jnp.log2(total))
            base = 3 * HD + MAX_SEGS
            qs_ref[slot, part, base : base + 3] = jnp.concatenate([one, two, three], 1)
            mixed_ref[slot, part, :] = mixed
            alive = (slot < live_count).astype(F32)
            kept.append((mixed * alive).astype(BF16))
        stage[step] = pack_rows(jnp.concatenate(kept, 1))

        @pl.when(step < 3 * per_share)
        def _():
            send_rows(step, stage_index).start()

        return carry

    lax.fori_loop(0, rows // sub, attend_rows, 0)
    keep = pltpu.make_async_copy(
        stage.at[pl.ds(3 * per_share, per_share)], got_ref.at[mp], here.at[3]
    )
    keep.start()
    last_weights(3)
    for s in range(4):
        weights(s, 2).wait_recv()
        for kind in (4, 5, 6):
            weights(s, kind).wait_recv()
        for kind in range(7):
            weights(s, kind).wait_send()
    for copy in firsts + shared + lifts:
        copy.wait_send()

    @pl.when(inner)
    def _():
        for copy in inner_lifts:
            copy.wait_send()

    for copy in biases:
        copy.wait()
    for step in range(3 * per_share):
        send_rows(step, 3 - step // per_share).wait()
    own_bias.wait()
    keep.wait()


def front(frames, qkv_weight, up_weight, down_flip, out_flip, vectors, seg_ids, slots):
    rows, depth = frames.shape
    piece, hidden_cols = up_weight.shape
    width = slots * HD
    lanes = -(-(2 * hidden_cols + width) // 128) * 128
    sub = 256
    shape = lambda n: jax.ShapeDtypeStruct((slots, rows, n), BF16)
    vmem = pl.BlockSpec(memory_space=pltpu.VMEM)
    dma = pltpu.SemaphoreType.DMA
    steps = rows // sub
    return pl.pallas_call(
        functools.partial(front_kernel, slots, sub),
        in_specs=[vmem] * 7,
        out_specs=[vmem] * 9,
        out_shape=[
            jax.ShapeDtypeStruct((4, 8, piece, lanes), BF16),
            jax.ShapeDtypeStruct((8 * piece, 3 * width), BF16),
            jax.ShapeDtypeStruct((4, 1, HALF), F32),
            shape(AUG), shape(AUG), shape(VAUG), shape(HD),
            jax.ShapeDtypeStruct((slots, rows, HD), F32),
            jax.ShapeDtypeStruct((4, steps // 4, sub * 3 // 2, 2 * HD), BF16),
        ],
        scratch_shapes=[
            pltpu.VMEM((steps, sub * 3 // 2, 2 * HD), BF16),
            pltpu.VMEM((piece, 3 * width), BF16), pltpu.VMEM((piece, lanes), BF16),
            pltpu.VMEM((1, HALF), F32),
            dma((7,)), dma((7,)), dma((5,)), dma((4,)), dma((4, 7)), dma((4, 7)), dma((3,)), dma((3,)),
            dma((steps,)), dma((steps,)), dma((4,)),
        ],
        compiler_params=pltpu.CompilerParams(
            collective_id=1, has_side_effects=True, vmem_limit_bytes=16 << 20
        ),
        name="front",
    )(frames, qkv_weight, up_weight, down_flip, out_flip, vectors, seg_ids.reshape(1, rows))


def project_kernel(slots, x_ref, w_ref, b_ref, seg_ref, qs_ref, ka_ref, va_ref, kk_ref):
    made = jnp.dot(x_ref[...], w_ref[...], preferred_element_type=F32) + b_ref[...]
    marks = seg_ref[...] == lax.broadcasted_iota(jnp.int32, (x_ref.shape[0], MAX_SEGS), 1)
    spread_rows(
        made.astype(BF16), jnp.where(marks, 1.0, 0.0), slots, qs_ref, ka_ref, va_ref, kk_ref, slice(None)
    )


def project(frames, weight, offsets, seg_ids, slots):
    rows, depth = frames.shape
    block = min(512, rows)
    spread = lambda n: pl.BlockSpec((slots, block, n), lambda i: (0, i, 0))
    shape = lambda n: jax.ShapeDtypeStruct((slots, rows, n), BF16)
    return pl.pallas_call(
        functools.partial(project_kernel, slots),
        grid=(rows // block,),
        in_specs=[
            pl.BlockSpec((block, depth), lambda i: (i, 0)),
            pl.BlockSpec(weight.shape, lambda i: (0, 0)),
            pl.BlockSpec((1, offsets.shape[1]), lambda i: (0, 0)),
            pl.BlockSpec((block, 1), lambda i: (i, 0)),
        ],
        out_specs=[spread(AUG), spread(AUG), spread(VAUG), spread(HD)],
        out_shape=[shape(AUG), shape(AUG), shape(VAUG), shape(HD)],
        compiler_params=pltpu.CompilerParams(vmem_limit_bytes=VMEM_LIMIT),
        name="project",
    )(frames, weight, offsets, seg_ids.reshape(rows, 1))


def attend_kernel(sub, qs_ref, ka_ref, va_ref, qn_ref, mixed_ref):
    for at in range(0, qs_ref.shape[1], sub):
        part = slice(at, at + sub)
        x = lax.dot_general(qs_ref[0, part, :], ka_ref[0], NT, preferred_element_type=F32)
        top = jnp.max(x, -1, keepdims=True)
        p = jnp.exp2(x - top).astype(BF16)
        made = jnp.dot(p, va_ref[0], preferred_element_type=F32)
        total = -made[:, HD : HD + 1]
        mixed_ref[0, part, :] = made[:, :HD] / total
        one, two, three = thirds(top + jnp.log2(total))
        base = 3 * HD + MAX_SEGS
        blank = jnp.zeros((sub, AUG - base - 3), BF16)
        qn_ref[0, part, :] = jnp.concatenate(
            [qs_ref[0, part, :base], one, two, three, blank], 1
        )


def attend(qs, ka, va):
    slots, rows, _ = qs.shape
    block = min(512, rows)
    sub = min(256, block)
    whole = lambda n: pl.BlockSpec((1, rows, n), lambda h, i: (h, 0, 0))
    some = lambda n: pl.BlockSpec((1, block, n), lambda h, i: (h, i, 0))
    return pl.pallas_call(
        functools.partial(attend_kernel, sub),
        grid=(slots, rows // block),
        in_specs=[some(AUG), whole(AUG), whole(VAUG)],
        out_specs=[some(AUG), some(HD)],
        out_shape=[
            jax.ShapeDtypeStruct((slots, rows, AUG), BF16),
            jax.ShapeDtypeStruct((slots, rows, HD), F32),
        ],
        compiler_params=pltpu.CompilerParams(vmem_limit_bytes=VMEM_LIMIT),
        name="attend",
    )(qs, ka, va)


def attend_back_kernel(
    sub, qs_ref, ka_ref, va_ref, kk_ref, mixed_ref, up_ref, dq_ref, dk_ref, dv_ref, dk_acc, dv_acc
):
    step = pl.program_id(1)

    @pl.when(step == 0)
    def _():
        dk_acc[...] = jnp.zeros_like(dk_acc)
        dv_acc[...] = jnp.zeros_like(dv_acc)

    for at in range(0, qs_ref.shape[1], sub):
        part = slice(at, at + sub)
        q = qs_ref[0, part, :HD]
        up = up_ref[0, part, :]
        d_one, d_two, d_three = thirds(
            jnp.sum(up.astype(F32) * mixed_ref[0, part, :], -1, keepdims=True)
        )
        blank = lambda n: jnp.zeros((sub, n), BF16)
        upper = jnp.concatenate([up, d_one, d_two, d_three, blank(VAUG - HD - 3)], 1)
        x = lax.dot_general(qs_ref[0, part, :], ka_ref[0], NT, preferred_element_type=F32)
        p = jnp.exp2(x)
        dp = lax.dot_general(upper, va_ref[0], NT, preferred_element_type=F32)
        ds = (p * dp).astype(BF16)
        dv_acc[...] += lax.dot_general(up, p.astype(BF16), TN, preferred_element_type=F32)
        dk_acc[...] += lax.dot_general(q, ds, TN, preferred_element_type=F32)
        dq_ref[0, part, :] = (
            jnp.dot(ds, kk_ref[0], preferred_element_type=F32) * SCALE
        ).astype(BF16)

    @pl.when(step == pl.num_programs(1) - 1)
    def _():
        dk_ref[0] = (dk_acc[...] * SCALE).T.astype(BF16)
        dv_ref[0] = dv_acc[...].T.astype(BF16)


def attend_back(qs, ka, va, kk, mixed, up):
    slots, rows, _ = qs.shape
    block = min(512, rows)
    sub = min(256, block)
    whole = lambda n: pl.BlockSpec((1, rows, n), lambda h, i: (h, 0, 0))
    some = lambda n: pl.BlockSpec((1, block, n), lambda h, i: (h, i, 0))
    shape = jax.ShapeDtypeStruct((slots, rows, HD), BF16)
    return pl.pallas_call(
        functools.partial(attend_back_kernel, sub),
        grid=(slots, rows // block),
        in_specs=[
            some(AUG), whole(AUG), whole(VAUG), whole(HD), some(HD), some(HD),
        ],
        out_specs=[some(HD), whole(HD), whole(HD)],
        out_shape=[shape, shape, shape],
        scratch_shapes=[pltpu.VMEM((HD, rows), F32), pltpu.VMEM((HD, rows), F32)],
        compiler_params=pltpu.CompilerParams(vmem_limit_bytes=VMEM_LIMIT),
        name="attend_back",
    )(qs, ka, va, kk, mixed, up)


def norm_forward(summed):
    centre = summed - jnp.mean(summed, -1, keepdims=True)
    spread = jnp.mean(centre * centre, -1, keepdims=True)
    factor = lax.rsqrt(spread + EPS)
    return (centre * factor, factor)


def norm_backward(upper, normed, factor, gain):
    scaled = upper * gain
    return factor * (
        scaled
        - jnp.mean(scaled, -1, keepdims=True)
        - normed * jnp.mean(scaled * normed, -1, keepdims=True)
    )


def middle_kernel(
    groups, hidden_cols, block, linked,
    x_ref, y_ref, got_ref, w_ref, ub_ref, vec_ref,
    out_ref, s1_ref, back_ref, grad_ref, small_ref, *scratch,
):
    x_own, y_own, ow, act, pre_low, slope, hid_low, two_low, one_low, here = scratch[:10]
    share = out_ref.shape[0]
    width = ow.shape[2]
    gap = HALF - hidden_cols
    dp = lax.axis_index("dp")
    mp = lax.axis_index("mp")
    rows = pl.ds(pl.multiple_of(mp * share, share), share)
    loads = [
        pltpu.make_async_copy(x_ref.at[rows], x_own, here.at[0]),
        pltpu.make_async_copy(y_ref.at[rows], y_own, here.at[1]),
    ]
    for copy in loads:
        copy.start()
    if linked:
        back_own, got, grads, arrived, b_send, b_recv, g_send, g_recv = scratch[10:]
        core = lax.rem(dp, 2)
        sibling = (dp ^ 1, mp)
        plane_barrier([sibling] + [(dp, mp ^ s) for s in range(1, 4)])
    else:
        back_own, got, grads = back_ref, got_ref, grad_ref
    out_bias, gain_one, shift_one = vec_ref[0:1, :], vec_ref[1:2, :], vec_ref[2:3, :]
    down_bias, gain_two, shift_two = vec_ref[3:4, :], vec_ref[4:5, :], vec_ref[5:6, :]
    for g in range(groups):
        ow[g, :, :gap] = w_ref[g, :, hidden_cols:HALF]
        ow[g, :, gap:] = w_ref[g, :, HALF + hidden_cols : HALF + hidden_cols + width - gap]
    small_ref[...] = jnp.zeros_like(small_ref)
    real = lane_marks(1, HALF, hidden_cols)
    alive = [
        lane_marks(1, width, HD * (HEADS // groups + (g < HEADS % groups))) for g in range(groups)
    ]
    for copy in loads:
        copy.wait()

    def send_back(step, s):
        at = step * 3 + s - 1
        return remote(
            back_own.at[mp ^ s, step], back_ref.at[mp, step], b_send.at[at], b_recv.at[at], (dp, mp ^ s)
        )

    def some_rows(step, carry):
        part = pl.ds(pl.multiple_of(step * block, block), block)
        summed = x_own[part, :].astype(F32) + out_bias
        for g in range(groups):
            if linked:
                got[g, part, :] = unpack_rows(got_ref[g, step])
            summed += lax.dot_general(got[g, part, :], ow[g], NT, preferred_element_type=F32)
        normed_one, factor_one = norm_forward(summed)
        hidden = normed_one * gain_one + shift_one
        hidden_low = hidden.astype(BF16)
        hid_low[part, :] = hidden_low
        feed = hidden + down_bias
        for g in range(groups):
            pre = jnp.dot(hidden_low, w_ref[g, :, :HALF], preferred_element_type=F32) + ub_ref[g]
            half = 0.5 + 0.5 * lax.erf(pre * math.sqrt(0.5))
            bell = jnp.exp(pre * pre * -0.5) * (pre * (1.0 / math.sqrt(2.0 * math.pi)))
            slope[g] = jnp.where(real, half + bell, 0.0)
            made = jnp.where(real, pre * half, 0.0).astype(BF16)
            act[g, part, :] = made
            feed += lax.dot_general(
                made, w_ref[g, :, HALF : 2 * HALF], NT, preferred_element_type=F32
            )
        normed_two, factor_two = norm_forward(feed)
        out_ref[part, :] = (normed_two * gain_two + shift_two).astype(BF16)
        upstream = y_own[part, :].astype(F32)
        two_grad = norm_backward(upstream, normed_two, factor_two, gain_two)
        sum_two = two_grad.astype(BF16)
        two_low[part, :] = sum_two
        hidden_grad = two_grad
        for g in range(groups):
            act_grad = jnp.dot(
                sum_two, w_ref[g, :, HALF : 2 * HALF], preferred_element_type=F32
            )
            low = (slope[g] * act_grad).astype(BF16)
            pre_low[g, part, :] = low
            hidden_grad += lax.dot_general(
                low, w_ref[g, :, :HALF], NT, preferred_element_type=F32
            )
            small_ref[8 + g : 9 + g, :] += jnp.sum(low.astype(F32), 0, keepdims=True)
        one_grad = norm_backward(hidden_grad, normed_one, factor_one, gain_one)
        sum_one = one_grad.astype(BF16)
        s1_ref[part, :] = one_grad
        one_low[part, :] = sum_one
        for g in range(groups):
            made = jnp.dot(sum_one, ow[g], preferred_element_type=F32)
            made = jnp.where(alive[g], made, 0.0).astype(BF16)
            if linked:
                back_own[g, step] = pack_rows(made)
            else:
                back_own[g, part, :] = made
        if linked:
            for s in range(1, 4):
                send_back(step, s).start()
        for at, term in enumerate((
            sum_one.astype(F32), hidden_grad * normed_one, hidden_grad,
            sum_two.astype(F32), upstream * normed_two, upstream,
        )):
            small_ref[at : at + 1, :] += jnp.sum(term, 0, keepdims=True)
        return carry

    lax.fori_loop(0, share // block, some_rows, 0)
    if linked:
        keep = pltpu.make_async_copy(back_own.at[mp], back_ref.at[mp], here.at[2])
        keep.start()
    hid_flip, two_flip, one_flip = hid_low[...].T, two_low[...].T, one_low[...].T
    shared = []
    for g in range(groups):
        made = jnp.dot(hid_flip, pre_low[g], preferred_element_type=F32).astype(BF16)
        grad_out = jnp.dot(one_flip, got[g], preferred_element_type=F32).astype(BF16)
        rest = width - gap
        left = jnp.concatenate([made[:, :hidden_cols], grad_out[:, :gap]], 1)
        made = jnp.dot(two_flip, act[g], preferred_element_type=F32).astype(BF16)
        spare = w_ref.shape[2] - HALF - hidden_cols - rest
        right = jnp.concatenate(
            [made[:, :hidden_cols], grad_out[:, gap:], jnp.zeros((made.shape[0], spare), BF16)], 1
        )
        if linked:
            piece = grad_ref.shape[2]
            for d in range(8):
                at = slice(d * piece, (d + 1) * piece)

                @pl.when(core == d % 2)
                def _():
                    grad_ref[g, d // 2, :, :HALF] = left[at]
                    grad_ref[g, d // 2, :, HALF:] = right[at]

                @pl.when(core != d % 2)
                def _():
                    grads[g, d // 2, :, :HALF] = left[at]
                    grads[g, d // 2, :, HALF:] = right[at]

            copy = remote(grads.at[g], arrived.at[g], g_send.at[g], g_recv.at[g], sibling)
            copy.start()
            shared.append(copy)
        else:
            grads[g, :, :HALF] = left
            grads[g, :, HALF:] = right
    if linked:
        for g in range(groups):
            shared[g].wait_recv()
            for c in range(4):
                grad_ref[g, c] += arrived[g, c]
        for step in range(share // block):
            for s in range(1, 4):
                send_back(step, s).wait()
        for copy in shared:
            copy.wait_send()
        keep.wait()


def middle(frames, cotangent, got, weights, up_bias, vectors, hidden_cols, linked):
    groups = got.shape[0]
    share, depth = frames.shape[0] // groups, frames.shape[1]
    lanes = weights.shape[2]
    width = 3 * HD
    block = min(256, share)
    vmem = pl.BlockSpec(memory_space=pltpu.VMEM)
    rest = pl.BlockSpec(memory_space=pl.ANY)
    dma = pltpu.SemaphoreType.DMA
    scratch = [
        pltpu.VMEM((share, depth), BF16),
        pltpu.VMEM((share, depth), BF16),
        pltpu.VMEM((groups, depth, width), BF16),
        pltpu.VMEM((groups, share, HALF), BF16),
        pltpu.VMEM((groups, share, HALF), BF16),
        pltpu.VMEM((groups, block, HALF), F32),
        pltpu.VMEM((share, depth), BF16),
        pltpu.VMEM((share, depth), BF16),
        pltpu.VMEM((share, depth), BF16),
        dma((3,)),
    ]
    grads = jax.ShapeDtypeStruct(weights.shape, BF16)
    if linked:
        piece = depth // 8
        grads = jax.ShapeDtypeStruct((groups, 4, piece, lanes), BF16)
        sends = 3 * (share // block)
        scratch += [
            pltpu.VMEM(got.shape, BF16),
            pltpu.VMEM((groups, share, width), BF16),
            pltpu.VMEM((groups, 4, piece, lanes), BF16),
            pltpu.VMEM((groups, 4, piece, lanes), BF16),
            dma((sends,)), dma((sends,)), dma((groups,)), dma((groups,)),
        ]
    extra = dict(collective_id=2, has_side_effects=True) if linked else {}
    return pl.pallas_call(
        functools.partial(middle_kernel, groups, hidden_cols, block, linked),
        in_specs=[rest, rest, vmem, vmem, vmem, vmem],
        out_specs=[vmem] * 5,
        out_shape=[
            jax.ShapeDtypeStruct((share, depth), BF16),
            jax.ShapeDtypeStruct((share, depth), F32),
            jax.ShapeDtypeStruct(got.shape, BF16),
            grads,
            jax.ShapeDtypeStruct((16, HALF), F32),
        ],
        scratch_shapes=scratch,
        compiler_params=pltpu.CompilerParams(
            vmem_limit_bytes=33 << 20 if linked else VMEM_LIMIT, **extra
        ),
        name="middle",
    )(frames, cotangent, got, weights, up_bias, vectors)


PAIRS = (
    (0, 3), (1, 3), (2, 3), (3, 3), (3, 2), (3, 1), (3, 0), (0, 2), (1, 2), (2, 2), (2, 1), (2, 0),
    (0, 1), (1, 1), (1, 0), (0, 0),
)
ENDS = {6: 3, 11: 2, 14: 1, 15: 0}


def pick(table, step):
    made = jnp.int32(table[0])
    for at in range(1, len(table)):
        made = jnp.where(step >= at, jnp.int32(table[at]), made)
    return made


def back_kernel(
    slots, sub,
    qs_ref, ka_ref, va_ref, kk_ref, mixed_ref, up_ref, sums_ref, x_ref, wq_ref, one_ref, small_ref,
    fg_ref, gq_ref, gb_ref, gup_ref, gdown_ref, gout_ref, gub_ref, s0, s1, s2, s3, s4, s5,
    upper, up_flip, q_flip, dq_acc, dk_acc, dv_acc, low, part_out, chain, fresh, far_in, near_in, third,
    tall_in, gq_own, gq_in, gb_own, gb_in, tiny, tiny_in,
    c_send, c_recv, f_send, f_recv, n_send, n_recv, t_send, t_recv, q_send, q_recv, b_send, b_recv,
    s_send, s_recv, small_sum,
):
    dp = lax.axis_index("dp")
    mp = lax.axis_index("mp")
    chip = dp // 2
    rows, depth = x_ref.shape
    share = rows // 4
    width = slots * HD
    others = [(dp ^ d, mp) for d in range(1, 8)]
    tall = [(dp, mp ^ s) for s in range(1, 4)]
    plane_barrier(others + tall)
    x_peer, y_peer = (dp ^ 2, mp), (dp ^ 4, mp)

    def rows_of(name):
        return pl.ds(pl.multiple_of((mp ^ name) * share, share), share)

    def far(s):
        return remote(
            sums_ref.at[mp ^ s, chip ^ 3], far_in.at[s], f_send.at[s], f_recv.at[s],
            y_peer if s % 2 == 0 else x_peer,
        )

    def near(s, kind):
        toward_x = (s % 2 == 0) == (kind == 1)
        source = third.at[s] if kind == 1 else sums_ref.at[mp ^ s, chip ^ (1 if toward_x else 2)]
        return remote(
            source, near_in.at[s, kind], n_send.at[s, kind], n_recv.at[s, kind],
            x_peer if toward_x else y_peer,
        )

    def lift(s):
        return remote(
            fresh.at[s], tall_in.at[s], t_send.at[s], t_recv.at[s], (dp, mp ^ s)
        )

    def begin_grads(s):
        far(s).start()
        near(s, 0).start()

    def join_far(s):
        far(s).wait_recv()
        third[s] = sums_ref[mp ^ s, chip ^ (1 if s % 2 == 0 else 2)] + far_in[s]
        near(s, 1).start()

    def join_near(s):
        near(s, 0).wait_recv()
        near(s, 1).wait_recv()
        total = sums_ref[mp ^ s, chip].astype(F32) + near_in[s, 0].astype(F32)
        fresh[s] = (total + near_in[s, 1].astype(F32)).astype(BF16)
        if s > 0:
            lift(s).start()

    partners = [(dp ^ 1, mp), (dp ^ 2, mp), (dp ^ 4, mp), (dp, mp ^ 1), (dp, mp ^ 2)]

    def swap(at):
        return remote(tiny.at[at], tiny_in.at[at], s_send.at[at], s_recv.at[at], partners[at])

    def small_step(at):
        if at == 0:
            tiny[0] = small_ref[...]
        else:
            swap(at - 1).wait_recv()
            made = tiny[at - 1] + tiny_in[at - 1]
            if at == len(partners):
                small_sum[...] = made
                for row, ref in enumerate((s0, s1, s2, s3, s4, s5)):
                    ref[...] = made[row : row + 1, :].reshape(ref.shape)
                cols = gub_ref.shape[-1]
                gub_ref[...] = small_sum[pl.ds(8 + mp, 1), :cols].reshape(gub_ref.shape)
                return
            tiny[at] = made
        swap(at).start()

    def chain_copy(name, leftward):
        block = mp ^ name
        target = mp - 1 if leftward else mp + 1
        slot = jnp.where(block == target, 4, block) if leftward else block
        return remote(
            part_out.at[name], chain.at[slot], c_send.at[name], c_recv.at[slot], (dp, target)
        )

    def chain_arrival(slot):
        return remote(part_out.at[0], chain.at[slot], c_send.at[0], c_recv.at[slot], (dp, mp ^ 1))

    def relay(name):
        block = mp ^ name
        inner = (mp == 1) | (mp == 2)
        waits = inner

        @pl.when(waits)
        def _():
            chain_arrival(block).wait_recv()
            part_out[name] = (
                part_out[name].astype(F32) + chain[block].astype(F32)
            ).astype(BF16)

        @pl.when(block < mp)
        def _():
            chain_copy(name, True).start()

        @pl.when(block > mp)
        def _():
            chain_copy(name, False).start()

    def finish(name):
        at = rows_of(name)
        for slot in range(slots):
            col = slot * HD
            low[at, col : col + HD] = (dq_acc[slot, at, :] * SCALE).astype(BF16)
            low[at, width + col : width + col + HD] = (dk_acc[slot, :, at] * SCALE).T.astype(BF16)
            low[at, 2 * width + col : 2 * width + col + HD] = dv_acc[slot, :, at].T.astype(BF16)
        part_out[name] = lax.dot_general(
            low[at, :], wq_ref[...], NT, preferred_element_type=F32
        ).astype(BF16)

    dq_acc[...] = jnp.zeros_like(dq_acc)
    dk_acc[...] = jnp.zeros_like(dk_acc)
    dv_acc[...] = jnp.zeros_like(dv_acc)
    begin_grads(3)
    begin_grads(2)
    small_step(0)

    def prepare(step, carry):
        at = pl.ds(pl.multiple_of(step * share, share), share)
        wide = jnp.concatenate([unpack_rows(up_ref[step, i]) for i in range(up_ref.shape[1])], 0)
        for slot in range(slots):
            up = wide[:, slot * HD : (slot + 1) * HD]
            one, two, three = thirds(
                jnp.sum(up.astype(F32) * mixed_ref[slot, at, :], -1, keepdims=True)
            )
            blank = jnp.zeros((share, VAUG - HD - 3), BF16)
            upper[slot, at, :] = jnp.concatenate([up, one, two, three, blank], 1)
            up_flip[slot, :, at] = up.T
            q_flip[slot, :, at] = qs_ref[slot, at, :HD].T
        return carry

    lax.fori_loop(0, 4, prepare, 0)
    actions = {
        1: [(small_step, 1)],
        2: [(begin_grads, 1), (small_step, 2)],
        3: [(join_far, 3), (begin_grads, 0), (small_step, 3)],
        4: [(join_far, 2), (small_step, 4)],
        5: [(join_near, 3), (small_step, 5)],
        7: [(join_near, 2), (join_far, 1)],
        9: [(join_far, 0)],
        11: [(join_near, 1)],
        13: [(join_near, 0)],
    }

    def pair(step, carry):
        query = mp ^ pick([p[0] for p in PAIRS], step)
        key = mp ^ pick([p[1] for p in PAIRS], step)
        keys = pl.ds(pl.multiple_of(key * share, share), share)
        for when, todo in actions.items():

            @pl.when(step == when)
            def _():
                for act, s in todo:
                    act(s)

        for at in range(0, share, sub):
            part = pl.ds(pl.multiple_of(query * share + at, sub), sub)
            for slot in range(slots):
                x = lax.dot_general(
                    qs_ref[slot, part, :], ka_ref[slot, keys, :], NT, preferred_element_type=F32
                )
                p = jnp.exp2(x)
                dp_ = lax.dot_general(
                    upper[slot, part, :], va_ref[slot, keys, :], NT, preferred_element_type=F32
                )
                ds = (p * dp_).astype(BF16)
                dv_acc[slot, :, keys] += jnp.dot(
                    up_flip[slot, :, part], p.astype(BF16), preferred_element_type=F32
                )
                dk_acc[slot, :, keys] += jnp.dot(
                    q_flip[slot, :, part], ds, preferred_element_type=F32
                )
                dq_acc[slot, part, :] += jnp.dot(
                    ds, kk_ref[slot, keys, :], preferred_element_type=F32
                )
        for when, name in ENDS.items():

            @pl.when(step == when)
            def _():
                finish(name)
                if name == 2:
                    relay(name)
                elif name > 0:

                    @pl.when((mp == 0) | (mp == 3))
                    def _():
                        relay(name)

        return carry

    lax.fori_loop(0, len(PAIRS), pair, 0)
    gq_parts = low[...]
    ones = jnp.ones((16, rows), BF16)
    gb_own[...] = jnp.dot(ones, gq_parts, preferred_element_type=F32)[0:8, :]
    gb_in[dp] = gb_own[...]
    piece = depth // 8
    made = lax.dot_general(x_ref[...], gq_parts, TN, preferred_element_type=F32).astype(BF16)
    for d in range(8):
        gq_own[d] = made[d * piece : (d + 1) * piece]
    q_copies = []
    for d in range(1, 8):
        to = dp ^ d
        q_copies.append(
            remote(gq_own.at[to], gq_in.at[d - 1], q_send.at[d - 1], q_recv.at[d - 1], others[d - 1])
        )
        q_copies.append(
            remote(gb_own, gb_in.at[dp], b_send.at[d - 1], b_recv.at[d - 1], others[d - 1])
        )
    for copy in q_copies:
        copy.start()
    for name in (3, 1):

        @pl.when((mp == 1) | (mp == 2))
        def _():
            relay(name)

    for s in range(1, 4):
        lift(s).wait_recv()
    total = fresh[0].astype(F32)
    for s in range(1, 4):
        total = total + tall_in[s].astype(F32)
    cols = gup_ref.shape[1]
    gap = HALF - cols
    gup_ref[...] = total[:, :cols]
    gdown_ref[...] = total[:, HALF : HALF + cols]
    gout_ref[:, :gap] = total[:, cols:HALF]
    gout_ref[:, gap:] = total[:, HALF + cols : HALF + cols + width - gap]
    for copy in q_copies:
        copy.wait_recv()
    total = gq_own[dp].astype(F32)
    for d in range(7):
        total = total + gq_in[d].astype(F32)
    for i in range(3):
        gq_ref[i] = total[:, i * width : (i + 1) * width]
    total = gb_in[0]
    for d in range(1, 8):
        total = total + gb_in[d]
    gb_ref[0:1, :] = total[0:1, :width]
    gb_ref[1:2, :] = total[0:1, 2 * width :]

    wide = one_ref[...] + part_out[0].astype(F32)

    @pl.when(mp > 0)
    def _():
        chain_arrival(mp).wait_recv()

    @pl.when(mp < 3)
    def _():
        chain_arrival(4).wait_recv()

    left = jnp.where(mp > 0, chain[mp].astype(F32), 0.0)
    right = jnp.where(mp < 3, chain[4].astype(F32), 0.0)
    fg_ref[...] = (wide + left + right).astype(BF16)
    for name in (1, 2, 3):
        remote(
            part_out.at[name], chain.at[0], c_send.at[name], c_recv.at[0], (dp, mp ^ 1)
        ).wait_send()
    for s in range(4):
        far(s).wait_send()
        near(s, 0).wait_send()
        near(s, 1).wait_send()
        if s > 0:
            lift(s).wait_send()
    for at in range(len(partners)):
        swap(at).wait_send()
    for copy in q_copies:
        copy.wait_send()


def back_pass(qs, ka, va, kk, mixed, up, sums, frames, wq, one_grad, small, hidden_cols):
    slots, rows, _ = qs.shape
    depth = frames.shape[1]
    share = rows // 4
    piece, lanes = sums.shape[2:]
    cols = wq.shape[1]
    vmem = pl.BlockSpec(memory_space=pltpu.VMEM)
    dma = pltpu.SemaphoreType.DMA
    V = pltpu.VMEM
    return pl.pallas_call(
        functools.partial(back_kernel, slots, min(512, share)),
        in_specs=[vmem] * 11,
        out_specs=[vmem] * 13,
        out_shape=[
            jax.ShapeDtypeStruct((share, depth), BF16),
            jax.ShapeDtypeStruct((3, piece, cols // 3), F32),
            jax.ShapeDtypeStruct((2, cols // 3), F32),
            jax.ShapeDtypeStruct((piece, hidden_cols), F32),
            jax.ShapeDtypeStruct((piece, hidden_cols), F32),
            jax.ShapeDtypeStruct((piece, cols // 3), F32),
            jax.ShapeDtypeStruct((hidden_cols,), F32),
        ]
        + [jax.ShapeDtypeStruct((depth,), F32)] * 6,
        scratch_shapes=[
            V((slots, rows, VAUG), BF16), V((slots, HD, rows), BF16), V((slots, HD, rows), BF16),
            V((slots, rows, HD), F32), V((slots, HD, rows), F32), V((slots, HD, rows), F32),
            V((rows, cols), BF16), V((4, share, depth), BF16), V((5, share, depth), BF16),
            V((4, piece, lanes), BF16), V((4, piece, lanes), BF16), V((4, 2, piece, lanes), BF16),
            V((4, piece, lanes), BF16), V((4, piece, lanes), BF16),
            V((8, piece, cols), BF16), V((7, piece, cols), BF16),
            V((8, cols), F32), V((8, 8, cols), F32), V((5,) + small.shape, F32), V((5,) + small.shape, F32),
            dma((4,)), dma((5,)), dma((4,)), dma((4,)), dma((4, 2)), dma((4, 2)), dma((4,)), dma((4,)),
            dma((7,)), dma((7,)), dma((7,)), dma((7,)), dma((5,)), dma((5,)), V(small.shape, F32),
        ],
        compiler_params=pltpu.CompilerParams(
            collective_id=3, has_side_effects=True, vmem_limit_bytes=31 << 20
        ),
        name="back_pass",
    )(qs, ka, va, kk, mixed, up, sums, frames, wq, one_grad, small)


def body(
    frames, seg_ids, qkv_weight, qkv_bias, out_weight, out_bias, gain_one, shift_one,
    up_weight, up_bias, down_weight, down_bias, gain_two, shift_two, cotangent,
):
    rows, depth = frames.shape
    mp_size = lax.axis_size("mp")
    dp_size = lax.axis_size("dp")
    mp_index = lax.axis_index("mp")
    share = rows // mp_size
    slots = qkv_weight.shape[2] // HD
    width = slots * HD
    hidden_cols = up_weight.shape[1]
    piece = qkv_weight.shape[1]
    gap = HALF - hidden_cols
    spare = -(HALF + hidden_cols + width - gap) % 128
    live_count = HEADS // mp_size + (mp_index < HEADS % mp_size).astype(jnp.int32)
    live = (jnp.arange(slots) < live_count).astype(F32)

    out_flip = out_weight.T
    down_flip = down_weight.T
    wide = lambda v: jnp.pad(v, (0, HALF - v.shape[0]))
    vectors = jnp.stack(
        [
            out_bias, gain_one, shift_one, down_bias, gain_two, shift_two, wide(up_bias),
            wide(qkv_bias[0]), wide(qkv_bias[1]),
        ]
    )
    linked = (dp_size, mp_size, slots, rows) == (8, 4, 3, 2048)
    if linked:
        weights, qkv_full, ub_full, qs, ka, va, kk, mixed, got = front(
            frames, qkv_weight, up_weight, down_flip, out_flip, vectors, seg_ids, slots
        )
        weights = weights.reshape(mp_size, depth, -1)
    else:
        wq = jnp.transpose(qkv_weight, (1, 0, 2)).reshape(piece, 3 * width)
        packed = jnp.concatenate(
            [up_weight, out_flip[:, :gap], down_flip, out_flip[:, gap:], jnp.zeros((piece, spare), BF16)], 1
        )
        ub_pad = jnp.pad(up_bias, (0, gap))[None]
        offsets = jnp.concatenate([qkv_bias[0], jnp.zeros_like(qkv_bias[0]), qkv_bias[1]])[None]
        qkv_full = lax.all_gather(wq, "dp", axis=0, tiled=True)
        weights = lax.all_gather(packed, "mp", axis=0, tiled=False)
        weights = lax.all_gather(weights, "dp", axis=1, tiled=True)
        ub_full = lax.all_gather(ub_pad, "mp", axis=0, tiled=False)
        qs, ka, va, kk = project(frames, qkv_full, offsets, seg_ids, slots)
        qs, mixed = attend(qs, ka, va)
        mixed_low = (mixed * live[:, None, None]).astype(BF16)
        sent = mixed_low.reshape(slots, mp_size, share, HD).transpose(1, 2, 0, 3)
        got = lax.all_to_all(sent.reshape(mp_size, share, width), "mp", 0, 0, tiled=True)
    output_frames, sum_one_grad, back, partial, small = middle(
        frames, cotangent, got, weights, ub_full, vectors, hidden_cols, linked
    )
    if linked:
        made = back_pass(
            qs, ka, va, kk, mixed, back, partial, frames, qkv_full, sum_one_grad, small, hidden_cols
        )
        return (
            output_frames, made[0], made[1], made[2], made[5].T, made[7], made[8], made[9], made[3],
            made[6], made[4].T, made[10], made[11], made[12],
        )
    if not linked:
        back = lax.all_to_all(back, "mp", 0, 0, tiled=True)
        back = back.reshape(rows, slots, HD).transpose(1, 0, 2)
        partial = lax.psum_scatter(partial, "dp", scatter_dimension=1, tiled=True)
        partial = lax.psum_scatter(partial, "mp", scatter_dimension=0, tiled=True)[0].astype(F32)
        small = lax.psum(small, ("dp", "mp"))
        dq, dk, dv = attend_back(qs, ka, va, kk, mixed, back)
        grads_low = jnp.stack([dq, dk, dv]).transpose(2, 0, 1, 3).reshape(rows, 3 * width)
        bias_sums = lax.psum(jnp.sum(grads_low.astype(F32), 0), "dp")
        grad_qkv = jnp.einsum("rd,rs->ds", frames, grads_low, preferred_element_type=F32)
        arrived = lax.all_to_all(
            grad_qkv.astype(BF16).reshape(dp_size, piece, 3 * width), "dp", 0, 0, tiled=True
        )
        grad_qkv = arrived.astype(F32).sum(0)
        input_part = jnp.einsum("rs,ds->rd", grads_low, qkv_full, preferred_element_type=F32)
        input_sum = lax.psum_scatter(input_part.astype(BF16), "mp", scatter_dimension=0, tiled=True)
        frames_grad = (input_sum.astype(F32) + sum_one_grad).astype(BF16)
    grad_qkv = grad_qkv.reshape(piece, 3, width).transpose(1, 0, 2)
    bias_sums = bias_sums.reshape(3, width)
    qkv_bias_grad = jnp.stack([bias_sums[0], bias_sums[2]])
    out_grad = jnp.concatenate(
        [partial[:, hidden_cols:HALF], partial[:, HALF + hidden_cols : HALF + hidden_cols + width - gap]], 1
    )
    return (
        output_frames,
        frames_grad,
        grad_qkv,
        qkv_bias_grad,
        out_grad.T,
        small[0],
        small[1],
        small[2],
        partial[:, :hidden_cols],
        lax.dynamic_index_in_dim(small, 8 + mp_index, 0, False)[:hidden_cols],
        partial[:, HALF : HALF + hidden_cols].T,
        small[3],
        small[4],
        small[5],
    )


def solution(mesh):
    in_specs = (
        P("dp", None), P("dp"), P(None, "dp", "mp"), P(None, "mp"), P("mp", "dp"), P(), P(), P(),
        P("dp", "mp"), P("mp"), P("mp", "dp"), P(), P(), P(), P("dp", None),
    )
    out_specs = (
        P(("dp", "mp"), None), P(("dp", "mp"), None), P(None, "dp", "mp"), P(None, "mp"),
        P("mp", "dp"), P(), P(), P(), P("dp", "mp"), P("mp"), P("mp", "dp"), P(), P(), P(),
    )
    return jax.shard_map(body, mesh=mesh, in_specs=in_specs, out_specs=out_specs, check_vma=False)
```

```python
import functools
import math

import jax
import jax.numpy as jnp
from jax import lax
from jax.experimental import pallas as pl
from jax.experimental.pallas import tpu as pltpu
from jax.sharding import PartitionSpec as P

HEADS = 10
HD = 64
EPS = 1e-05
SCALE = 0.125
MAX_SEGS = 16
MASKED = -1e30
UNIT = SCALE * math.log2(math.e)
AUG = 256
VAUG = 128
NT = (((1,), (1,)), ((), ()))
TN = (((0,), (0,)), ((), ()))
F32 = jnp.float32
BF16 = jnp.bfloat16
VMEM_LIMIT = 56 << 20
MESH = pl.DeviceIdType.MESH
CHIPS = 3
HALF = 640


def thirds(wide):
    first = wide.astype(BF16)
    rest = wide - first.astype(F32)
    second = rest.astype(BF16)
    third = (rest - second.astype(F32)).astype(BF16)
    return first, second, third


def lane_marks(rows, width, count):
    return lax.broadcasted_iota(jnp.int32, (rows, width), 1) < count


def spread_rows(made, picked, slots, qs_ref, ka_ref, va_ref, kk_ref, rows):
    count = made.shape[0]
    width = slots * HD
    chosen = picked.astype(BF16)
    barred = ((picked - 1.0) * -MASKED).astype(BF16)
    tail = AUG - 3 * HD - MAX_SEGS
    q_tail = jnp.zeros((count, tail), BF16)
    minus = jnp.where(lane_marks(count, tail, 3), -1.0, 0.0).astype(BF16)
    v_tail = jnp.where(lane_marks(count, VAUG - HD, 3), -1.0, 0.0).astype(BF16)
    for slot in range(slots):
        at = slot * HD
        q = made[:, at : at + HD]
        k = made[:, width + at : width + at + HD]
        v = made[:, 2 * width + at : 2 * width + at + HD]
        one, two, three = thirds(k.astype(F32) * UNIT)
        qs_ref[slot, rows, :] = jnp.concatenate([q, q, q, chosen, q_tail], 1)
        ka_ref[slot, rows, :] = jnp.concatenate([one, two, three, barred, minus], 1)
        va_ref[slot, rows, :] = jnp.concatenate([v, v_tail], 1)
    kk_ref[rows, :] = made[:, width : 2 * width]


def plane_barrier(peers):
    barrier = pltpu.get_barrier_semaphore()
    for peer in peers:
        pl.semaphore_signal(barrier, inc=1, device_id=peer, device_id_type=MESH)
    pl.semaphore_wait(barrier, len(peers))


def remote(src, dst, send, recv, peer):
    return pltpu.make_async_remote_copy(
        src_ref=src, dst_ref=dst, send_sem=send, recv_sem=recv, device_id=peer, device_id_type=MESH
    )


def pack_rows(wide):
    half = wide.shape[0] // 2
    third = wide[:, 2 * HD :]
    return jnp.concatenate(
        [wide[:, : 2 * HD], jnp.concatenate([third[:half], third[half:]], 1)], 0
    )


def unpack_rows(packed):
    rows = packed.shape[0] * 2 // 3
    rest = packed[rows:]
    return jnp.concatenate(
        [packed[:rows], jnp.concatenate([rest[:, :HD], rest[:, HD:]], 0)], 1
    )


def front_kernel(
    slots, sub,
    x_hbm, qkv_hbm, up_hbm, down_hbm, out_hbm, ub_ref, qb_ref, seg_ref,
    all_ref, wfull_ref, ball_ref, qs_ref, ka_ref, va_ref, kk_ref, mixed_ref, got_ref,
    x_ref, qkv_ref, up_ref, down_ref, out_ref, stage, wq_ref, pack_ref, bias_ref,
    q_send, q_recv, z_send, z_recv, w_send, w_recv, b_send, b_recv, a_send, a_recv, here, loaded,
):
    dp = lax.axis_index("dp")
    mp = lax.axis_index("mp")
    plane = [dp ^ 2, dp ^ 4, dp ^ 6]
    sibling = (dp ^ 1, mp)
    tall = [(dp, mp ^ s) for s in range(1, 4)]
    inner = (mp == 1) | (mp == 2)
    width = slots * HD
    pairs = ((qkv_hbm, qkv_ref), (up_hbm, up_ref), (down_hbm, down_ref), (out_hbm, out_ref), (x_hbm, x_ref))
    loads = [pltpu.make_async_copy(a, b, loaded.at[i]) for i, (a, b) in enumerate(pairs)]
    for copy in loads:
        copy.start()
    bias_ref[...] = jnp.zeros_like(bias_ref)
    bias_ref[:, : up_hbm.shape[1]] = ub_ref[...].reshape(1, up_hbm.shape[1])
    for copy in loads[:4]:
        copy.wait()
    for i in range(3):
        wq_ref[:, i * width : (i + 1) * width] = qkv_ref[i]
    hidden_cols = up_ref.shape[1]
    gap = HALF - hidden_cols
    rest = width - gap
    pack_ref[:, :hidden_cols] = up_ref[...]
    pack_ref[:, hidden_cols:HALF] = out_ref[:, :gap]
    pack_ref[:, HALF : HALF + hidden_cols] = down_ref[...]
    pack_ref[:, HALF + hidden_cols : HALF + hidden_cols + rest] = out_ref[:, gap:]
    spare = pack_ref.shape[1] - HALF - hidden_cols - rest
    pack_ref[:, HALF + hidden_cols + rest :] = jnp.zeros((pack_ref.shape[0], spare), BF16)
    plane_barrier([sibling] + [(d, mp) for d in plane] + tall)
    rows = x_ref.shape[0]
    share = rows // 4

    piece = wq_ref.shape[0]

    def rows_of(d):
        return wfull_ref.at[pl.ds(pl.multiple_of(d * piece, piece), piece)]

    mine = pltpu.make_async_copy(wq_ref, rows_of(dp), here.at[0])
    mine.start()
    firsts = [
        remote(wq_ref, rows_of(dp), q_send.at[i], q_recv.at[i], (plane[i], mp))
        for i in range(CHIPS)
    ]
    for copy in firsts:
        copy.start()
    shared = [remote(wq_ref, rows_of(dp), q_send.at[3], q_recv.at[3], sibling)]
    shared[0].start()
    own = pltpu.make_async_copy(pack_ref, all_ref.at[mp, dp], here.at[1])
    own.start()
    def lift(at, s, landing, peer):
        ref = all_ref.at[mp ^ s, dp]
        return remote(pack_ref if s == 0 else ref, ref, z_send.at[at], z_recv.at[landing], peer)

    near, middle = tall[0], tall[2]
    lifts = [lift(0, 0, 1, near)]
    inner_lifts = [
        lift(1, 0, 3, middle), lift(2, 1, 2, middle), lift(3, 3, 2, near), lift(4, 2, 3, near),
    ]

    def arrive(s):
        lift(0, s, s, near).wait_recv()

    own_bias = pltpu.make_async_copy(bias_ref, ball_ref.at[mp], here.at[2])
    own_bias.start()
    lifts[0].start()

    @pl.when(inner)
    def _():
        inner_lifts[0].start()

    biases = [
        remote(bias_ref, ball_ref.at[mp], b_send.at[s], b_recv.at[s], tall[s]) for s in range(3)
    ]
    for copy in biases:
        copy.start()
    for i in range(CHIPS):
        firsts[i].wait_recv()
        passed = remote(
            rows_of(plane[i]), rows_of(plane[i]), q_send.at[4 + i], q_recv.at[4 + i], sibling
        )
        passed.start()
        shared.append(passed)
    own.wait()

    def weights(s, kind):
        group = mp ^ s
        block = {0: dp, 1: dp, 2: dp, 4: plane[0], 5: plane[1], 6: plane[2]}
        block[3] = plane[0] if s % 2 == 0 else plane[1]
        peer = {0: (plane[0], mp), 1: (plane[1], mp)}
        peer[3] = peer[1] if s % 2 == 0 else peer[0]
        ref = all_ref.at[group, block[kind]]
        return remote(ref, ref, w_send.at[s, kind], w_recv.at[s, kind], peer.get(kind, sibling))

    def start_weights(s):
        if s == 3:

            @pl.when(~inner)
            def _():
                arrive(3)

        for kind in (0, 1, 2):
            weights(s, kind).start()

    def pass_weights(s):
        weights(s, 0).wait_recv()
        weights(s, 1).wait_recv()
        for kind in (3, 4, 5):
            weights(s, kind).start()

    def last_weights(s):
        weights(s, 3).wait_recv()
        weights(s, 6).start()

    start_weights(0)
    mine.wait()
    for copy in shared:
        copy.wait_recv()
    arrive(1)

    @pl.when(inner)
    def _():
        inner_lifts[1].start()
        arrive(3)
        inner_lifts[2].start()


    loads[4].wait()
    block = 256

    def project_rows(step, carry):
        part = pl.ds(pl.multiple_of(step * block, block), block)
        x = x_ref[part, :]
        offsets = jnp.concatenate(
            [qb_ref[0:1, :], jnp.zeros((1, width), F32), qb_ref[1:2, :]], 1
        )
        made = jnp.dot(x, wfull_ref[...], preferred_element_type=F32) + offsets
        marks = seg_ref[:, part] == lax.broadcasted_iota(jnp.int32, (MAX_SEGS, block), 0)
        picked = jnp.where(marks, 1.0, 0.0).T
        spread_rows(made.astype(BF16), picked, slots, qs_ref, ka_ref, va_ref, kk_ref, part)
        return carry

    lax.fori_loop(0, rows // block, project_rows, 0)
    arrive(2)

    @pl.when(inner)
    def _():
        inner_lifts[3].start()

    pass_weights(0)
    start_weights(1)

    live_count = HEADS // 4 + (mp < HEADS % 4).astype(jnp.int32)
    per_share = share // sub
    actions = {
        1: [(start_weights, 2), (last_weights, 0)],
        2: [(pass_weights, 1)],
        3: [(start_weights, 3), (last_weights, 1)],
        4: [(pass_weights, 2)],
        5: [(last_weights, 2)],
        6: [(pass_weights, 3)],
    }

    def send_rows(step, stage_index):
        return remote(
            stage.at[step], got_ref.at[mp, lax.rem(step, per_share)], a_send.at[step], a_recv.at[step],
            (dp, mp ^ stage_index),
        )

    def attend_rows(step, carry):
        stage_index = 3 - step // per_share
        group = mp ^ stage_index
        offset = lax.rem(step, per_share) * sub
        part = pl.ds(pl.multiple_of(group * share + offset, sub), sub)
        for when, todo in actions.items():

            @pl.when(step == when)
            def _():
                for act, s in todo:
                    act(s)

        kept = []
        for slot in range(slots):
            x = lax.dot_general(
                qs_ref[slot, part, :], ka_ref[slot], NT, preferred_element_type=F32
            )
            top = jnp.max(x, -1, keepdims=True)
            p = jnp.exp2(x - top).astype(BF16)
            made = jnp.dot(p, va_ref[slot], preferred_element_type=F32)
            total = -made[:, HD : HD + 1]
            mixed = made[:, :HD] / total
            one, two, three = thirds(top + jnp.log2(total))
            base = 3 * HD + MAX_SEGS
            qs_ref[slot, part, base : base + 3] = jnp.concatenate([one, two, three], 1)
            mixed_ref[part, slot * HD : (slot + 1) * HD] = mixed
            alive = (slot < live_count).astype(F32)
            kept.append((mixed * alive).astype(BF16))
        stage[step] = pack_rows(jnp.concatenate(kept, 1))

        @pl.when(step < 3 * per_share)
        def _():
            send_rows(step, stage_index).start()

        return carry

    lax.fori_loop(0, rows // sub, attend_rows, 0)
    keep = pltpu.make_async_copy(
        stage.at[pl.ds(3 * per_share, per_share)], got_ref.at[mp], here.at[3]
    )
    keep.start()
    last_weights(3)
    for s in range(4):
        weights(s, 2).wait_recv()
        for kind in (4, 5, 6):
            weights(s, kind).wait_recv()
        for kind in range(7):
            weights(s, kind).wait_send()
    for copy in firsts + shared + lifts:
        copy.wait_send()

    @pl.when(inner)
    def _():
        for copy in inner_lifts:
            copy.wait_send()

    for copy in biases:
        copy.wait()
    for step in range(3 * per_share):
        send_rows(step, 3 - step // per_share).wait()
    own_bias.wait()
    keep.wait()


def front(frames, qkv_weight, up_weight, down_flip, out_flip, up_bias, qkv_bias, seg_ids, slots):
    rows, depth = frames.shape
    piece, hidden_cols = up_weight.shape
    width = slots * HD
    lanes = -(-(2 * hidden_cols + width) // 128) * 128
    sub = 256
    shape = lambda n: jax.ShapeDtypeStruct((slots, rows, n), BF16)
    vmem = pl.BlockSpec(memory_space=pltpu.VMEM)
    hbm = pl.BlockSpec(memory_space=pltpu.MemorySpace.HBM)
    dma = pltpu.SemaphoreType.DMA
    steps = rows // sub
    operands = (frames, qkv_weight, up_weight, down_flip, out_flip)
    return pl.pallas_call(
        functools.partial(front_kernel, slots, sub),
        in_specs=[hbm] * 5 + [vmem] * 3,
        out_specs=[vmem] * 9,
        out_shape=[
            jax.ShapeDtypeStruct((4, 8, piece, lanes), BF16),
            jax.ShapeDtypeStruct((8 * piece, 3 * width), BF16),
            jax.ShapeDtypeStruct((4, 1, HALF), F32),
            shape(AUG), shape(AUG), shape(VAUG),
            jax.ShapeDtypeStruct((rows, width), BF16),
            jax.ShapeDtypeStruct((rows, width), F32),
            jax.ShapeDtypeStruct((4, steps // 4, sub * 3 // 2, 2 * HD), BF16),
        ],
        scratch_shapes=[
            pltpu.VMEM(frames.shape, BF16), pltpu.VMEM(qkv_weight.shape, BF16),
            pltpu.VMEM(up_weight.shape, BF16), pltpu.VMEM(down_flip.shape, BF16),
            pltpu.VMEM(out_flip.shape, BF16),
            pltpu.VMEM((steps, sub * 3 // 2, 2 * HD), BF16),
            pltpu.VMEM((piece, 3 * width), BF16), pltpu.VMEM((piece, lanes), BF16),
            pltpu.VMEM((1, HALF), F32),
            dma((7,)), dma((7,)), dma((5,)), dma((4,)), dma((4, 7)), dma((4, 7)), dma((3,)), dma((3,)),
            dma((steps,)), dma((steps,)), dma((4,)), dma((len(operands),)),
        ],
        compiler_params=pltpu.CompilerParams(
            collective_id=1, has_side_effects=True, vmem_limit_bytes=20 << 20
        ),
        name="front",
    )(*operands, up_bias, qkv_bias, seg_ids.reshape(1, rows))


def project_kernel(slots, x_ref, w_ref, b_ref, seg_ref, qs_ref, ka_ref, va_ref, kk_ref):
    made = jnp.dot(x_ref[...], w_ref[...], preferred_element_type=F32) + b_ref[...]
    marks = seg_ref[...] == lax.broadcasted_iota(jnp.int32, (x_ref.shape[0], MAX_SEGS), 1)
    spread_rows(
        made.astype(BF16), jnp.where(marks, 1.0, 0.0), slots, qs_ref, ka_ref, va_ref, kk_ref, slice(None)
    )


def project(frames, weight, offsets, seg_ids, slots):
    rows, depth = frames.shape
    block = min(512, rows)
    spread = lambda n: pl.BlockSpec((slots, block, n), lambda i: (0, i, 0))
    shape = lambda n: jax.ShapeDtypeStruct((slots, rows, n), BF16)
    return pl.pallas_call(
        functools.partial(project_kernel, slots),
        grid=(rows // block,),
        in_specs=[
            pl.BlockSpec((block, depth), lambda i: (i, 0)),
            pl.BlockSpec(weight.shape, lambda i: (0, 0)),
            pl.BlockSpec((1, offsets.shape[1]), lambda i: (0, 0)),
            pl.BlockSpec((block, 1), lambda i: (i, 0)),
        ],
        out_specs=[
            spread(AUG), spread(AUG), spread(VAUG), pl.BlockSpec((block, slots * HD), lambda i: (i, 0)),
        ],
        out_shape=[
            shape(AUG), shape(AUG), shape(VAUG), jax.ShapeDtypeStruct((rows, slots * HD), BF16),
        ],
        compiler_params=pltpu.CompilerParams(vmem_limit_bytes=VMEM_LIMIT),
        name="project",
    )(frames, weight, offsets, seg_ids.reshape(rows, 1))


def attend_kernel(sub, qs_ref, ka_ref, va_ref, qn_ref, mixed_ref):
    for at in range(0, qs_ref.shape[1], sub):
        part = slice(at, at + sub)
        x = lax.dot_general(qs_ref[0, part, :], ka_ref[0], NT, preferred_element_type=F32)
        top = jnp.max(x, -1, keepdims=True)
        p = jnp.exp2(x - top).astype(BF16)
        made = jnp.dot(p, va_ref[0], preferred_element_type=F32)
        total = -made[:, HD : HD + 1]
        mixed_ref[0, part, :] = made[:, :HD] / total
        one, two, three = thirds(top + jnp.log2(total))
        base = 3 * HD + MAX_SEGS
        blank = jnp.zeros((sub, AUG - base - 3), BF16)
        qn_ref[0, part, :] = jnp.concatenate(
            [qs_ref[0, part, :base], one, two, three, blank], 1
        )


def attend(qs, ka, va):
    slots, rows, _ = qs.shape
    block = min(512, rows)
    sub = min(256, block)
    whole = lambda n: pl.BlockSpec((1, rows, n), lambda h, i: (h, 0, 0))
    some = lambda n: pl.BlockSpec((1, block, n), lambda h, i: (h, i, 0))
    return pl.pallas_call(
        functools.partial(attend_kernel, sub),
        grid=(slots, rows // block),
        in_specs=[some(AUG), whole(AUG), whole(VAUG)],
        out_specs=[some(AUG), some(HD)],
        out_shape=[
            jax.ShapeDtypeStruct((slots, rows, AUG), BF16),
            jax.ShapeDtypeStruct((slots, rows, HD), F32),
        ],
        compiler_params=pltpu.CompilerParams(vmem_limit_bytes=VMEM_LIMIT),
        name="attend",
    )(qs, ka, va)


def attend_back_kernel(
    sub, qs_ref, ka_ref, va_ref, kk_ref, mixed_ref, up_ref, dq_ref, dk_ref, dv_ref, dk_acc, dv_acc
):
    step = pl.program_id(1)

    @pl.when(step == 0)
    def _():
        dk_acc[...] = jnp.zeros_like(dk_acc)
        dv_acc[...] = jnp.zeros_like(dv_acc)

    for at in range(0, qs_ref.shape[1], sub):
        part = slice(at, at + sub)
        q = qs_ref[0, part, :HD]
        up = up_ref[0, part, :]
        d_one, d_two, d_three = thirds(
            jnp.sum(up.astype(F32) * mixed_ref[0, part, :], -1, keepdims=True)
        )
        blank = lambda n: jnp.zeros((sub, n), BF16)
        upper = jnp.concatenate([up, d_one, d_two, d_three, blank(VAUG - HD - 3)], 1)
        x = lax.dot_general(qs_ref[0, part, :], ka_ref[0], NT, preferred_element_type=F32)
        p = jnp.exp2(x)
        dp = lax.dot_general(upper, va_ref[0], NT, preferred_element_type=F32)
        ds = (p * dp).astype(BF16)
        dv_acc[...] += lax.dot_general(up, p.astype(BF16), TN, preferred_element_type=F32)
        dk_acc[...] += lax.dot_general(q, ds, TN, preferred_element_type=F32)
        dq_ref[0, part, :] = (
            jnp.dot(ds, kk_ref[0], preferred_element_type=F32) * SCALE
        ).astype(BF16)

    @pl.when(step == pl.num_programs(1) - 1)
    def _():
        dk_ref[0] = (dk_acc[...] * SCALE).T.astype(BF16)
        dv_ref[0] = dv_acc[...].T.astype(BF16)


def attend_back(qs, ka, va, kk, mixed, up):
    slots, rows, _ = qs.shape
    block = min(512, rows)
    sub = min(256, block)
    whole = lambda n: pl.BlockSpec((1, rows, n), lambda h, i: (h, 0, 0))
    some = lambda n: pl.BlockSpec((1, block, n), lambda h, i: (h, i, 0))
    shape = jax.ShapeDtypeStruct((slots, rows, HD), BF16)
    return pl.pallas_call(
        functools.partial(attend_back_kernel, sub),
        grid=(slots, rows // block),
        in_specs=[
            some(AUG), whole(AUG), whole(VAUG), whole(HD), some(HD), some(HD),
        ],
        out_specs=[some(HD), whole(HD), whole(HD)],
        out_shape=[shape, shape, shape],
        scratch_shapes=[pltpu.VMEM((HD, rows), F32), pltpu.VMEM((HD, rows), F32)],
        compiler_params=pltpu.CompilerParams(vmem_limit_bytes=VMEM_LIMIT),
        name="attend_back",
    )(qs, ka, va, kk, mixed, up)


def norm_forward(summed):
    centre = summed - jnp.mean(summed, -1, keepdims=True)
    spread = jnp.mean(centre * centre, -1, keepdims=True)
    factor = lax.rsqrt(spread + EPS)
    return (centre * factor, factor)


def norm_backward(upper, normed, factor, gain):
    scaled = upper * gain
    return factor * (
        scaled
        - jnp.mean(scaled, -1, keepdims=True)
        - normed * jnp.mean(scaled * normed, -1, keepdims=True)
    )


def middle_kernel(
    groups, hidden_cols, block, linked,
    x_ref, y_ref, got_ref, w_ref, ub_ref, v0, v1, v2, v3, v4, v5,
    out_ref, s1_ref, back_ref, grad_ref, small_ref, *scratch,
):
    x_own, y_own, ow, act, pre_low, slope, hid_low, two_low, one_low, here = scratch[:10]
    share = out_ref.shape[0]
    width = ow.shape[2]
    gap = HALF - hidden_cols
    dp = lax.axis_index("dp")
    mp = lax.axis_index("mp")
    rows = pl.ds(pl.multiple_of(mp * share, share), share)
    loads = [
        pltpu.make_async_copy(x_ref.at[rows], x_own, here.at[0]),
        pltpu.make_async_copy(y_ref.at[rows], y_own, here.at[1]),
    ]
    for copy in loads:
        copy.start()
    if linked:
        back_own, got, grads, arrived, b_send, b_recv, g_send, g_recv = scratch[10:]
        core = lax.rem(dp, 2)
        sibling = (dp ^ 1, mp)
        plane_barrier([sibling] + [(dp, mp ^ s) for s in range(1, 4)])
    else:
        back_own, got, grads = back_ref, got_ref, grad_ref
    out_bias, gain_one, shift_one, down_bias, gain_two, shift_two = (
        v[...].reshape(1, v.shape[0]) for v in (v0, v1, v2, v3, v4, v5)
    )
    for g in range(groups):
        ow[g, :, :gap] = w_ref[g, :, hidden_cols:HALF]
        ow[g, :, gap:] = w_ref[g, :, HALF + hidden_cols : HALF + hidden_cols + width - gap]
    small_ref[...] = jnp.zeros_like(small_ref)
    real = lane_marks(1, HALF, hidden_cols)
    alive = [
        lane_marks(1, width, HD * (HEADS // groups + (g < HEADS % groups))) for g in range(groups)
    ]
    for copy in loads:
        copy.wait()

    def send_back(step, s):
        at = step * 3 + s - 1
        return remote(
            back_own.at[mp ^ s, step], back_ref.at[mp, step], b_send.at[at], b_recv.at[at], (dp, mp ^ s)
        )

    def some_rows(step, carry):
        part = pl.ds(pl.multiple_of(step * block, block), block)
        summed = x_own[part, :].astype(F32) + out_bias
        for g in range(groups):
            if linked:
                got[g, part, :] = unpack_rows(got_ref[g, step])
            summed += lax.dot_general(got[g, part, :], ow[g], NT, preferred_element_type=F32)
        normed_one, factor_one = norm_forward(summed)
        hidden = normed_one * gain_one + shift_one
        hidden_low = hidden.astype(BF16)
        hid_low[part, :] = hidden_low
        feed = hidden + down_bias
        for g in range(groups):
            pre = jnp.dot(hidden_low, w_ref[g, :, :HALF], preferred_element_type=F32) + ub_ref[g]
            half = 0.5 + 0.5 * lax.erf(pre * math.sqrt(0.5))
            bell = jnp.exp(pre * pre * -0.5) * (pre * (1.0 / math.sqrt(2.0 * math.pi)))
            slope[g] = jnp.where(real, half + bell, 0.0)
            made = jnp.where(real, pre * half, 0.0).astype(BF16)
            act[g, part, :] = made
            feed += lax.dot_general(
                made, w_ref[g, :, HALF : 2 * HALF], NT, preferred_element_type=F32
            )
        normed_two, factor_two = norm_forward(feed)
        out_ref[part, :] = (normed_two * gain_two + shift_two).astype(BF16)
        upstream = y_own[part, :].astype(F32)
        two_grad = norm_backward(upstream, normed_two, factor_two, gain_two)
        sum_two = two_grad.astype(BF16)
        two_low[part, :] = sum_two
        hidden_grad = two_grad
        for g in range(groups):
            act_grad = jnp.dot(
                sum_two, w_ref[g, :, HALF : 2 * HALF], preferred_element_type=F32
            )
            low = (slope[g] * act_grad).astype(BF16)
            pre_low[g, part, :] = low
            hidden_grad += lax.dot_general(
                low, w_ref[g, :, :HALF], NT, preferred_element_type=F32
            )
            small_ref[8 + g : 9 + g, :] += jnp.sum(low.astype(F32), 0, keepdims=True)
        one_grad = norm_backward(hidden_grad, normed_one, factor_one, gain_one)
        sum_one = one_grad.astype(BF16)
        s1_ref[part, :] = one_grad
        one_low[part, :] = sum_one
        for g in range(groups):
            made = jnp.dot(sum_one, ow[g], preferred_element_type=F32)
            made = jnp.where(alive[g], made, 0.0).astype(BF16)
            if linked:
                back_own[g, step] = pack_rows(made)
            else:
                back_own[g, part, :] = made
        if linked:
            for s in range(1, 4):
                send_back(step, s).start()
        for at, term in enumerate((
            sum_one.astype(F32), hidden_grad * normed_one, hidden_grad,
            sum_two.astype(F32), upstream * normed_two, upstream,
        )):
            small_ref[at : at + 1, :] += jnp.sum(term, 0, keepdims=True)
        return carry

    lax.fori_loop(0, share // block, some_rows, 0)
    if linked:
        keep = pltpu.make_async_copy(back_own.at[mp], back_ref.at[mp], here.at[2])
        keep.start()
    depth = hid_low.shape[1]
    rest = width - gap
    spare = w_ref.shape[2] - HALF - hidden_cols - rest
    span = depth // 2
    shared = []
    for g in range(groups):
        for part in range(2):
            cols = slice(part * span, (part + 1) * span)
            made = lax.dot_general(
                hid_low[:, cols], pre_low[g], TN, preferred_element_type=F32
            ).astype(BF16)
            grad_out = lax.dot_general(
                one_low[:, cols], got[g], TN, preferred_element_type=F32
            ).astype(BF16)
            left = jnp.concatenate([made[:, :hidden_cols], grad_out[:, :gap]], 1)
            made = lax.dot_general(
                two_low[:, cols], act[g], TN, preferred_element_type=F32
            ).astype(BF16)
            right = jnp.concatenate(
                [made[:, :hidden_cols], grad_out[:, gap:], jnp.zeros((span, spare), BF16)], 1
            )
            if not linked:
                grads[g, cols, :HALF] = left
                grads[g, cols, HALF:] = right
                continue
            piece = grad_ref.shape[2]
            for i in range(span // piece):
                d = part * (span // piece) + i
                at = slice(i * piece, (i + 1) * piece)

                @pl.when(core == d % 2)
                def _():
                    grad_ref[g, d // 2, :, :HALF] = left[at]
                    grad_ref[g, d // 2, :, HALF:] = right[at]

                @pl.when(core != d % 2)
                def _():
                    grads[g, d // 2, :, :HALF] = left[at]
                    grads[g, d // 2, :, HALF:] = right[at]

        if linked:
            copy = remote(grads.at[g], arrived.at[g], g_send.at[g], g_recv.at[g], sibling)
            copy.start()
            shared.append(copy)
    if linked:
        for g in range(groups):
            shared[g].wait_recv()
            for c in range(4):
                grad_ref[g, c] += arrived[g, c]
        for step in range(share // block):
            for s in range(1, 4):
                send_back(step, s).wait()
        for copy in shared:
            copy.wait_send()
        keep.wait()


def middle(frames, cotangent, got, weights, up_bias, vectors, hidden_cols, linked):
    groups = got.shape[0]
    share, depth = frames.shape[0] // groups, frames.shape[1]
    lanes = weights.shape[2]
    width = 3 * HD
    block = min(256, share)
    vmem = pl.BlockSpec(memory_space=pltpu.VMEM)
    rest = pl.BlockSpec(memory_space=pltpu.MemorySpace.HBM)
    dma = pltpu.SemaphoreType.DMA
    scratch = [
        pltpu.VMEM((share, depth), BF16),
        pltpu.VMEM((share, depth), BF16),
        pltpu.VMEM((groups, depth, width), BF16),
        pltpu.VMEM((groups, share, HALF), BF16),
        pltpu.VMEM((groups, share, HALF), BF16),
        pltpu.VMEM((groups, block, HALF), F32),
        pltpu.VMEM((share, depth), BF16),
        pltpu.VMEM((share, depth), BF16),
        pltpu.VMEM((share, depth), BF16),
        dma((3,)),
    ]
    grads = jax.ShapeDtypeStruct(weights.shape, BF16)
    if linked:
        piece = depth // 8
        grads = jax.ShapeDtypeStruct((groups, 4, piece, lanes), BF16)
        sends = 3 * (share // block)
        scratch += [
            pltpu.VMEM(got.shape, BF16),
            pltpu.VMEM((groups, share, width), BF16),
            pltpu.VMEM((groups, 4, piece, lanes), BF16),
            pltpu.VMEM((groups, 4, piece, lanes), BF16),
            dma((sends,)), dma((sends,)), dma((groups,)), dma((groups,)),
        ]
    extra = dict(collective_id=2, has_side_effects=True) if linked else {}
    return pl.pallas_call(
        functools.partial(middle_kernel, groups, hidden_cols, block, linked),
        in_specs=[rest, rest] + [vmem] * 9,
        out_specs=[vmem] * 5,
        out_shape=[
            jax.ShapeDtypeStruct((share, depth), BF16),
            jax.ShapeDtypeStruct((share, depth), F32),
            jax.ShapeDtypeStruct(got.shape, BF16),
            grads,
            jax.ShapeDtypeStruct((16, HALF), F32),
        ],
        scratch_shapes=scratch,
        compiler_params=pltpu.CompilerParams(
            vmem_limit_bytes=33 << 20 if linked else VMEM_LIMIT, **extra
        ),
        name="middle",
    )(frames, cotangent, got, weights, up_bias, *vectors)


PAIRS = (
    (0, 3), (1, 3), (2, 3), (3, 3), (3, 2), (3, 1), (3, 0), (0, 2), (1, 2), (2, 2), (2, 1), (2, 0),
    (0, 1), (1, 1), (1, 0), (0, 0),
)
ENDS = {6: 3, 11: 2, 14: 1, 15: 0}


def pick(table, step):
    made = jnp.int32(table[0])
    for at in range(1, len(table)):
        made = jnp.where(step >= at, jnp.int32(table[at]), made)
    return made


def back_kernel(
    slots, sub,
    qs_ref, ka_ref, va_ref, kk_ref, mixed_ref, up_ref, sums_ref, x_hbm, wq_ref, one_ref, small_ref,
    fg_ref, gq_ref, gb_ref, gup_ref, gdown_ref, gout_ref, gub_ref, s0, s1, s2, s3, s4, s5,
    upper, up_flip, q_flip, dq_acc, dk_acc, dv_acc, low, part_out, chain, fresh, far_in, near_in, third,
    tall_in, gq_own, gq_in, gb_own, gb_in, tiny, tiny_in,
    c_send, c_recv, f_send, f_recv, n_send, n_recv, t_send, t_recv, q_send, q_recv, b_send, b_recv,
    s_send, s_recv, small_sum, x_ref, loaded, gq_acc,
):
    dp = lax.axis_index("dp")
    mp = lax.axis_index("mp")
    chip = dp // 2
    rows, depth = x_hbm.shape
    share = rows // 4
    width = slots * HD
    others = [(dp ^ d, mp) for d in range(1, 8)]
    tall = [(dp, mp ^ s) for s in range(1, 4)]
    plane_barrier(others + tall)
    x_peer, y_peer = (dp ^ 2, mp), (dp ^ 4, mp)

    def rows_of(name):
        return pl.ds(pl.multiple_of((mp ^ name) * share, share), share)

    def load_rows(name):
        return pltpu.make_async_copy(x_hbm.at[rows_of(name)], x_ref, loaded.at[0])

    load_rows(3).start()

    def far(s):
        return remote(
            sums_ref.at[mp ^ s, chip ^ 3], far_in.at[s], f_send.at[s], f_recv.at[s],
            y_peer if s % 2 == 0 else x_peer,
        )

    def near(s, kind):
        toward_x = (s % 2 == 0) == (kind == 1)
        source = third.at[s] if kind == 1 else sums_ref.at[mp ^ s, chip ^ (1 if toward_x else 2)]
        return remote(
            source, near_in.at[s, kind], n_send.at[s, kind], n_recv.at[s, kind],
            x_peer if toward_x else y_peer,
        )

    def lift(s):
        return remote(
            fresh.at[s], tall_in.at[s], t_send.at[s], t_recv.at[s], (dp, mp ^ s)
        )

    def begin_grads(s):
        far(s).start()
        near(s, 0).start()

    def join_far(s):
        far(s).wait_recv()
        third[s] = sums_ref[mp ^ s, chip ^ (1 if s % 2 == 0 else 2)] + far_in[s]
        near(s, 1).start()

    def join_near(s):
        near(s, 0).wait_recv()
        near(s, 1).wait_recv()
        total = sums_ref[mp ^ s, chip].astype(F32) + near_in[s, 0].astype(F32)
        fresh[s] = (total + near_in[s, 1].astype(F32)).astype(BF16)
        if s > 0:
            lift(s).start()

    partners = [(dp ^ 1, mp), (dp ^ 2, mp), (dp ^ 4, mp), (dp, mp ^ 1), (dp, mp ^ 2)]

    def swap(at):
        return remote(tiny.at[at], tiny_in.at[at], s_send.at[at], s_recv.at[at], partners[at])

    def small_step(at):
        if at == 0:
            tiny[0] = small_ref[...]
        else:
            swap(at - 1).wait_recv()
            made = tiny[at - 1] + tiny_in[at - 1]
            if at == len(partners):
                small_sum[...] = made
                for row, ref in enumerate((s0, s1, s2, s3, s4, s5)):
                    ref[...] = made[row : row + 1, :].reshape(ref.shape)
                cols = gub_ref.shape[-1]
                gub_ref[...] = small_sum[pl.ds(8 + mp, 1), :cols].reshape(gub_ref.shape)
                return
            tiny[at] = made
        swap(at).start()

    def chain_copy(name, leftward):
        block = mp ^ name
        target = mp - 1 if leftward else mp + 1
        slot = jnp.where(block == target, 4, block) if leftward else block
        return remote(
            part_out.at[name], chain.at[slot], c_send.at[name], c_recv.at[slot], (dp, target)
        )

    def chain_arrival(slot):
        return remote(part_out.at[0], chain.at[slot], c_send.at[0], c_recv.at[slot], (dp, mp ^ 1))

    def relay(name):
        block = mp ^ name
        inner = (mp == 1) | (mp == 2)
        waits = inner

        @pl.when(waits)
        def _():
            chain_arrival(block).wait_recv()
            part_out[name] = (
                part_out[name].astype(F32) + chain[block].astype(F32)
            ).astype(BF16)

        @pl.when(block < mp)
        def _():
            chain_copy(name, True).start()

        @pl.when(block > mp)
        def _():
            chain_copy(name, False).start()

    def finish(name):
        at = rows_of(name)
        for slot in range(slots):
            col = slot * HD
            low[:, col : col + HD] = (dq_acc[slot, at, :] * SCALE).astype(BF16)
            low[:, width + col : width + col + HD] = (dk_acc[slot, :, at] * SCALE).T.astype(BF16)
            low[:, 2 * width + col : 2 * width + col + HD] = dv_acc[slot, :, at].T.astype(BF16)
        part_out[name] = lax.dot_general(
            low[...], wq_ref[...], NT, preferred_element_type=F32
        ).astype(BF16)

    def add_rows(name):
        ones = jnp.ones((16, share), BF16)
        gb_own[...] += jnp.dot(ones, low[...], preferred_element_type=F32)[0:8, :]
        load_rows(name).wait()
        gq_acc[...] += lax.dot_general(x_ref[...], low[...], TN, preferred_element_type=F32)
        if name > 0:
            load_rows(name - 1).start()

    dq_acc[...] = jnp.zeros_like(dq_acc)
    dk_acc[...] = jnp.zeros_like(dk_acc)
    dv_acc[...] = jnp.zeros_like(dv_acc)
    gq_acc[...] = jnp.zeros_like(gq_acc)
    gb_own[...] = jnp.zeros_like(gb_own)
    begin_grads(3)
    begin_grads(2)
    small_step(0)

    def prepare(step, carry):
        at = pl.ds(pl.multiple_of(step * share, share), share)
        wide = jnp.concatenate([unpack_rows(up_ref[step, i]) for i in range(up_ref.shape[1])], 0)
        for slot in range(slots):
            up = wide[:, slot * HD : (slot + 1) * HD]
            one, two, three = thirds(
                jnp.sum(
                    up.astype(F32) * mixed_ref[at, slot * HD : (slot + 1) * HD], -1, keepdims=True
                )
            )
            blank = jnp.zeros((share, VAUG - HD - 3), BF16)
            upper[slot, at, :] = jnp.concatenate([up, one, two, three, blank], 1)
            up_flip[slot, :, at] = up.T
            q_flip[slot, :, at] = qs_ref[slot, at, :HD].T
        return carry

    lax.fori_loop(0, 4, prepare, 0)
    actions = {
        1: [(small_step, 1)],
        2: [(begin_grads, 1), (small_step, 2)],
        3: [(join_far, 3), (begin_grads, 0), (small_step, 3)],
        4: [(join_far, 2), (small_step, 4)],
        5: [(join_near, 3), (small_step, 5)],
        7: [(join_near, 2), (join_far, 1)],
        9: [(join_far, 0)],
        11: [(join_near, 1)],
        13: [(join_near, 0)],
    }

    def pair(step, carry):
        query = mp ^ pick([p[0] for p in PAIRS], step)
        key = mp ^ pick([p[1] for p in PAIRS], step)
        keys = pl.ds(pl.multiple_of(key * share, share), share)
        for when, todo in actions.items():

            @pl.when(step == when)
            def _():
                for act, s in todo:
                    act(s)

        for at in range(0, share, sub):
            part = pl.ds(pl.multiple_of(query * share + at, sub), sub)
            for slot in range(slots):
                x = lax.dot_general(
                    qs_ref[slot, part, :], ka_ref[slot, keys, :], NT, preferred_element_type=F32
                )
                p = jnp.exp2(x)
                dp_ = lax.dot_general(
                    upper[slot, part, :], va_ref[slot, keys, :], NT, preferred_element_type=F32
                )
                ds = (p * dp_).astype(BF16)
                dv_acc[slot, :, keys] += jnp.dot(
                    up_flip[slot, :, part], p.astype(BF16), preferred_element_type=F32
                )
                dk_acc[slot, :, keys] += jnp.dot(
                    q_flip[slot, :, part], ds, preferred_element_type=F32
                )
                dq_acc[slot, part, :] += jnp.dot(
                    ds, kk_ref[keys, slot * HD : (slot + 1) * HD], preferred_element_type=F32
                )
        for when, name in ENDS.items():

            @pl.when(step == when)
            def _():
                finish(name)
                if name == 2:
                    relay(name)
                elif name > 0:

                    @pl.when((mp == 0) | (mp == 3))
                    def _():
                        relay(name)

                add_rows(name)

        return carry

    lax.fori_loop(0, len(PAIRS), pair, 0)
    gb_in[dp] = gb_own[...]
    piece = depth // 8
    for d in range(8):
        gq_own[d] = gq_acc[d * piece : (d + 1) * piece, :].astype(BF16)
    q_copies = []
    for d in range(1, 8):
        to = dp ^ d
        q_copies.append(
            remote(gq_own.at[to], gq_in.at[d - 1], q_send.at[d - 1], q_recv.at[d - 1], others[d - 1])
        )
        q_copies.append(
            remote(gb_own, gb_in.at[dp], b_send.at[d - 1], b_recv.at[d - 1], others[d - 1])
        )
    for copy in q_copies:
        copy.start()
    for name in (3, 1):

        @pl.when((mp == 1) | (mp == 2))
        def _():
            relay(name)

    for s in range(1, 4):
        lift(s).wait_recv()
    total = fresh[0].astype(F32)
    for s in range(1, 4):
        total = total + tall_in[s].astype(F32)
    cols = gup_ref.shape[1]
    gap = HALF - cols
    gup_ref[...] = total[:, :cols]
    gdown_ref[...] = total[:, HALF : HALF + cols]
    gout_ref[:, :gap] = total[:, cols:HALF]
    gout_ref[:, gap:] = total[:, HALF + cols : HALF + cols + width - gap]
    for copy in q_copies:
        copy.wait_recv()
    total = gq_own[dp].astype(F32)
    for d in range(7):
        total = total + gq_in[d].astype(F32)
    for i in range(3):
        gq_ref[i] = total[:, i * width : (i + 1) * width]
    total = gb_in[0]
    for d in range(1, 8):
        total = total + gb_in[d]
    gb_ref[0:1, :] = total[0:1, :width]
    gb_ref[1:2, :] = total[0:1, 2 * width :]

    wide = one_ref[...] + part_out[0].astype(F32)

    @pl.when(mp > 0)
    def _():
        chain_arrival(mp).wait_recv()

    @pl.when(mp < 3)
    def _():
        chain_arrival(4).wait_recv()

    left = jnp.where(mp > 0, chain[mp].astype(F32), 0.0)
    right = jnp.where(mp < 3, chain[4].astype(F32), 0.0)
    fg_ref[...] = (wide + left + right).astype(BF16)
    for name in (1, 2, 3):
        remote(
            part_out.at[name], chain.at[0], c_send.at[name], c_recv.at[0], (dp, mp ^ 1)
        ).wait_send()
    for s in range(4):
        far(s).wait_send()
        near(s, 0).wait_send()
        near(s, 1).wait_send()
        if s > 0:
            lift(s).wait_send()
    for at in range(len(partners)):
        swap(at).wait_send()
    for copy in q_copies:
        copy.wait_send()


def back_pass(qs, ka, va, kk, mixed, up, sums, frames, wq, one_grad, small, hidden_cols):
    slots, rows, _ = qs.shape
    depth = frames.shape[1]
    share = rows // 4
    piece, lanes = sums.shape[2:]
    cols = wq.shape[1]
    vmem = pl.BlockSpec(memory_space=pltpu.VMEM)
    hbm = pl.BlockSpec(memory_space=pltpu.MemorySpace.HBM)
    dma = pltpu.SemaphoreType.DMA
    V = pltpu.VMEM
    return pl.pallas_call(
        functools.partial(back_kernel, slots, min(512, share)),
        in_specs=[vmem] * 7 + [hbm] + [vmem] * 3,
        out_specs=[vmem] * 13,
        out_shape=[
            jax.ShapeDtypeStruct((share, depth), BF16),
            jax.ShapeDtypeStruct((3, piece, cols // 3), F32),
            jax.ShapeDtypeStruct((2, cols // 3), F32),
            jax.ShapeDtypeStruct((piece, hidden_cols), F32),
            jax.ShapeDtypeStruct((piece, hidden_cols), F32),
            jax.ShapeDtypeStruct((piece, cols // 3), F32),
            jax.ShapeDtypeStruct((hidden_cols,), F32),
        ]
        + [jax.ShapeDtypeStruct((depth,), F32)] * 6,
        scratch_shapes=[
            V((slots, rows, VAUG), BF16), V((slots, HD, rows), BF16), V((slots, HD, rows), BF16),
            V((slots, rows, HD), F32), V((slots, HD, rows), F32), V((slots, HD, rows), F32),
            V((share, cols), BF16), V((4, share, depth), BF16), V((5, share, depth), BF16),
            V((4, piece, lanes), BF16), V((4, piece, lanes), BF16), V((4, 2, piece, lanes), BF16),
            V((4, piece, lanes), BF16), V((4, piece, lanes), BF16),
            V((8, piece, cols), BF16), V((7, piece, cols), BF16),
            V((8, cols), F32), V((8, 8, cols), F32), V((5,) + small.shape, F32), V((5,) + small.shape, F32),
            dma((4,)), dma((5,)), dma((4,)), dma((4,)), dma((4, 2)), dma((4, 2)), dma((4,)), dma((4,)),
            dma((7,)), dma((7,)), dma((7,)), dma((7,)), dma((5,)), dma((5,)), V(small.shape, F32),
            V((share, depth), BF16), dma((1,)), V((depth, cols), F32),
        ],
        compiler_params=pltpu.CompilerParams(
            collective_id=3, has_side_effects=True, vmem_limit_bytes=36 << 20
        ),
        name="back_pass",
    )(qs, ka, va, kk, mixed, up, sums, frames, wq, one_grad, small)


def deliver_kernel(count, *refs):
    sources, results, sem = refs[:count], refs[count : 2 * count], refs[2 * count]
    copies = [
        pltpu.make_async_copy(a, b, sem.at[i]) for i, (a, b) in enumerate(zip(sources, results))
    ]
    for copy in copies:
        copy.start()
    for copy in copies:
        copy.wait()


def deliver(arrays):
    count = len(arrays)
    return pl.pallas_call(
        functools.partial(deliver_kernel, count),
        in_specs=[pl.BlockSpec(memory_space=pltpu.VMEM)] * count,
        out_specs=[pl.BlockSpec(memory_space=pltpu.MemorySpace.HBM)] * count,
        out_shape=[jax.ShapeDtypeStruct(a.shape, a.dtype) for a in arrays],
        scratch_shapes=[pltpu.SemaphoreType.DMA((count,))],
        compiler_params=pltpu.CompilerParams(vmem_limit_bytes=4 << 20),
        name="deliver",
    )(*arrays)


def body(
    frames, seg_ids, qkv_weight, qkv_bias, out_weight, out_bias, gain_one, shift_one,
    up_weight, up_bias, down_weight, down_bias, gain_two, shift_two, cotangent,
):
    rows, depth = frames.shape
    mp_size = lax.axis_size("mp")
    dp_size = lax.axis_size("dp")
    mp_index = lax.axis_index("mp")
    share = rows // mp_size
    slots = qkv_weight.shape[2] // HD
    width = slots * HD
    hidden_cols = up_weight.shape[1]
    piece = qkv_weight.shape[1]
    gap = HALF - hidden_cols
    spare = -(HALF + hidden_cols + width - gap) % 128
    live_count = HEADS // mp_size + (mp_index < HEADS % mp_size).astype(jnp.int32)
    live = (jnp.arange(slots) < live_count).astype(F32)

    in_hbm = lambda a: pltpu.with_memory_space_constraint(a, pltpu.MemorySpace.HBM)
    out_flip = out_weight.T
    down_flip = down_weight.T
    vectors = (out_bias, gain_one, shift_one, down_bias, gain_two, shift_two)
    linked = (dp_size, mp_size, slots, rows) == (8, 4, 3, 2048)
    if linked:
        weights, qkv_full, ub_full, qs, ka, va, kk, mixed, got = front(
            *map(in_hbm, (frames, qkv_weight, up_weight, down_flip, out_flip)), up_bias, qkv_bias,
            seg_ids, slots,
        )
        weights = weights.reshape(mp_size, depth, -1)
    else:
        wq = jnp.transpose(qkv_weight, (1, 0, 2)).reshape(piece, 3 * width)
        packed = jnp.concatenate(
            [up_weight, out_flip[:, :gap], down_flip, out_flip[:, gap:], jnp.zeros((piece, spare), BF16)], 1
        )
        ub_pad = jnp.pad(up_bias, (0, gap))[None]
        offsets = jnp.concatenate([qkv_bias[0], jnp.zeros_like(qkv_bias[0]), qkv_bias[1]])[None]
        qkv_full = lax.all_gather(wq, "dp", axis=0, tiled=True)
        weights = lax.all_gather(packed, "mp", axis=0, tiled=False)
        weights = lax.all_gather(weights, "dp", axis=1, tiled=True)
        ub_full = lax.all_gather(ub_pad, "mp", axis=0, tiled=False)
        qs, ka, va, kk = project(frames, qkv_full, offsets, seg_ids, slots)
        qs, mixed = attend(qs, ka, va)
        mixed_low = (mixed * live[:, None, None]).astype(BF16)
        sent = mixed_low.reshape(slots, mp_size, share, HD).transpose(1, 2, 0, 3)
        got = lax.all_to_all(sent.reshape(mp_size, share, width), "mp", 0, 0, tiled=True)
    output_frames, sum_one_grad, back, partial, small = middle(
        in_hbm(frames), in_hbm(cotangent), got, weights, ub_full, vectors, hidden_cols, linked
    )
    if linked:
        made = back_pass(
            qs, ka, va, kk, mixed, back, partial, in_hbm(frames), qkv_full, sum_one_grad, small, hidden_cols
        )
        output_frames, *made = deliver([output_frames, *made])
        return (
            output_frames, made[0], made[1], made[2], made[5].T, made[7], made[8], made[9], made[3],
            made[6], made[4].T, made[10], made[11], made[12],
        )
    if not linked:
        back = lax.all_to_all(back, "mp", 0, 0, tiled=True)
        back = back.reshape(rows, slots, HD).transpose(1, 0, 2)
        partial = lax.psum_scatter(partial, "dp", scatter_dimension=1, tiled=True)
        partial = lax.psum_scatter(partial, "mp", scatter_dimension=0, tiled=True)[0].astype(F32)
        small = lax.psum(small, ("dp", "mp"))
        kk = kk.reshape(rows, slots, HD).transpose(1, 0, 2)
        dq, dk, dv = attend_back(qs, ka, va, kk, mixed, back)
        grads_low = jnp.stack([dq, dk, dv]).transpose(2, 0, 1, 3).reshape(rows, 3 * width)
        bias_sums = lax.psum(jnp.sum(grads_low.astype(F32), 0), "dp")
        grad_qkv = jnp.einsum("rd,rs->ds", frames, grads_low, preferred_element_type=F32)
        arrived = lax.all_to_all(
            grad_qkv.astype(BF16).reshape(dp_size, piece, 3 * width), "dp", 0, 0, tiled=True
        )
        grad_qkv = arrived.astype(F32).sum(0)
        input_part = jnp.einsum("rs,ds->rd", grads_low, qkv_full, preferred_element_type=F32)
        input_sum = lax.psum_scatter(input_part.astype(BF16), "mp", scatter_dimension=0, tiled=True)
        frames_grad = (input_sum.astype(F32) + sum_one_grad).astype(BF16)
    grad_qkv = grad_qkv.reshape(piece, 3, width).transpose(1, 0, 2)
    bias_sums = bias_sums.reshape(3, width)
    qkv_bias_grad = jnp.stack([bias_sums[0], bias_sums[2]])
    out_grad = jnp.concatenate(
        [partial[:, hidden_cols:HALF], partial[:, HALF + hidden_cols : HALF + hidden_cols + width - gap]], 1
    )
    return (
        output_frames,
        frames_grad,
        grad_qkv,
        qkv_bias_grad,
        out_grad.T,
        small[0],
        small[1],
        small[2],
        partial[:, :hidden_cols],
        lax.dynamic_index_in_dim(small, 8 + mp_index, 0, False)[:hidden_cols],
        partial[:, HALF : HALF + hidden_cols].T,
        small[3],
        small[4],
        small[5],
    )


def solution(mesh):
    in_specs = (
        P("dp", None), P("dp"), P(None, "dp", "mp"), P(None, "mp"), P("mp", "dp"), P(), P(), P(),
        P("dp", "mp"), P("mp"), P("mp", "dp"), P(), P(), P(), P("dp", None),
    )
    out_specs = (
        P(("dp", "mp"), None), P(("dp", "mp"), None), P(None, "dp", "mp"), P(None, "mp"),
        P("mp", "dp"), P(), P(), P(), P("dp", "mp"), P("mp"), P("mp", "dp"), P(), P(), P(),
    )
    return jax.shard_map(body, mesh=mesh, in_specs=in_specs, out_specs=out_specs, check_vma=False)
```

```python
import functools
import math

import jax
import jax.numpy as jnp
from jax import lax
from jax.experimental import pallas as pl
from jax.experimental.pallas import tpu as pltpu
from jax.sharding import PartitionSpec as P

HEADS = 10
HD = 64
EPS = 1e-05
SCALE = 0.125
MAX_SEGS = 16
MASKED = -1e30
UNIT = SCALE * math.log2(math.e)
AUG = 256
VAUG = 128
NT = (((1,), (1,)), ((), ()))
TN = (((0,), (0,)), ((), ()))
F32 = jnp.float32
BF16 = jnp.bfloat16
VMEM_LIMIT = 56 << 20
MESH = pl.DeviceIdType.MESH
CHIPS = 3
HALF = 640


def thirds(wide):
    first = wide.astype(BF16)
    rest = wide - first.astype(F32)
    second = rest.astype(BF16)
    third = (rest - second.astype(F32)).astype(BF16)
    return first, second, third


def lane_marks(rows, width, count):
    return lax.broadcasted_iota(jnp.int32, (rows, width), 1) < count


def spread_rows(made, picked, slots, qs_ref, ka_ref, va_ref, kk_ref, rows):
    count = made.shape[0]
    width = slots * HD
    chosen = picked.astype(BF16)
    barred = ((picked - 1.0) * -MASKED).astype(BF16)
    tail = AUG - 3 * HD - MAX_SEGS
    q_tail = jnp.zeros((count, tail), BF16)
    minus = jnp.where(lane_marks(count, tail, 3), -1.0, 0.0).astype(BF16)
    v_tail = jnp.where(lane_marks(count, VAUG - HD, 3), -1.0, 0.0).astype(BF16)
    for slot in range(slots):
        at = slot * HD
        q = made[:, at : at + HD]
        k = made[:, width + at : width + at + HD]
        v = made[:, 2 * width + at : 2 * width + at + HD]
        one, two, three = thirds(k.astype(F32) * UNIT)
        qs_ref[slot, rows, :] = jnp.concatenate([q, q, q, chosen, q_tail], 1)
        ka_ref[slot, rows, :] = jnp.concatenate([one, two, three, barred, minus], 1)
        va_ref[slot, rows, :] = jnp.concatenate([v, v_tail], 1)
    kk_ref[rows, :] = made[:, width : 2 * width]


def plane_barrier(peers):
    barrier = pltpu.get_barrier_semaphore()
    for peer in peers:
        pl.semaphore_signal(barrier, inc=1, device_id=peer, device_id_type=MESH)
    pl.semaphore_wait(barrier, len(peers))


def remote(src, dst, send, recv, peer):
    return pltpu.make_async_remote_copy(
        src_ref=src, dst_ref=dst, send_sem=send, recv_sem=recv, device_id=peer, device_id_type=MESH
    )


def pack_rows(wide):
    half = wide.shape[0] // 2
    third = wide[:, 2 * HD :]
    return jnp.concatenate(
        [wide[:, : 2 * HD], jnp.concatenate([third[:half], third[half:]], 1)], 0
    )


def unpack_rows(packed):
    rows = packed.shape[0] * 2 // 3
    rest = packed[rows:]
    return jnp.concatenate(
        [packed[:rows], jnp.concatenate([rest[:, :HD], rest[:, HD:]], 0)], 1
    )


def front_kernel(
    slots, sub,
    x_hbm, qkv_hbm, up_hbm, down_hbm, out_hbm, ub_ref, qb_ref, seg_ref,
    all_ref, wfull_ref, ball_ref, qs_ref, ka_ref, va_ref, kk_ref, mixed_ref, got_ref,
    x_ref, qkv_ref, up_ref, down_ref, out_ref, stage, wq_ref, pack_ref, bias_ref,
    q_send, q_recv, z_send, z_recv, w_send, w_recv, b_send, b_recv, a_send, a_recv, here, loaded,
):
    dp = lax.axis_index("dp")
    mp = lax.axis_index("mp")
    plane = [dp ^ 2, dp ^ 4, dp ^ 6]
    sibling = (dp ^ 1, mp)
    tall = [(dp, mp ^ s) for s in range(1, 4)]
    inner = (mp == 1) | (mp == 2)
    width = slots * HD
    pairs = ((qkv_hbm, qkv_ref), (up_hbm, up_ref), (down_hbm, down_ref), (out_hbm, out_ref), (x_hbm, x_ref))
    loads = [pltpu.make_async_copy(a, b, loaded.at[i]) for i, (a, b) in enumerate(pairs)]
    for copy in loads:
        copy.start()
    bias_ref[...] = jnp.zeros_like(bias_ref)
    bias_ref[:, : up_hbm.shape[1]] = ub_ref[...].reshape(1, up_hbm.shape[1])
    for copy in loads[:4]:
        copy.wait()
    for i in range(3):
        wq_ref[:, i * width : (i + 1) * width] = qkv_ref[i]
    hidden_cols = up_ref.shape[1]
    gap = HALF - hidden_cols
    rest = width - gap
    pack_ref[:, :hidden_cols] = up_ref[...]
    pack_ref[:, hidden_cols:HALF] = out_ref[:, :gap]
    pack_ref[:, HALF : HALF + hidden_cols] = down_ref[...]
    pack_ref[:, HALF + hidden_cols : HALF + hidden_cols + rest] = out_ref[:, gap:]
    spare = pack_ref.shape[1] - HALF - hidden_cols - rest
    pack_ref[:, HALF + hidden_cols + rest :] = jnp.zeros((pack_ref.shape[0], spare), BF16)
    plane_barrier([sibling] + [(d, mp) for d in plane] + tall)
    rows = x_ref.shape[0]
    share = rows // 4

    piece = wq_ref.shape[0]

    def rows_of(d):
        return wfull_ref.at[pl.ds(pl.multiple_of(d * piece, piece), piece)]

    mine = pltpu.make_async_copy(wq_ref, rows_of(dp), here.at[0])
    mine.start()
    firsts = [
        remote(wq_ref, rows_of(dp), q_send.at[i], q_recv.at[i], (plane[i], mp))
        for i in range(CHIPS)
    ]
    for copy in firsts:
        copy.start()
    shared = [remote(wq_ref, rows_of(dp), q_send.at[3], q_recv.at[3], sibling)]
    shared[0].start()
    own = pltpu.make_async_copy(pack_ref, all_ref.at[mp, dp], here.at[1])
    own.start()
    def lift(at, s, landing, peer):
        ref = all_ref.at[mp ^ s, dp]
        return remote(pack_ref if s == 0 else ref, ref, z_send.at[at], z_recv.at[landing], peer)

    near, middle = tall[0], tall[2]
    lifts = [lift(0, 0, 1, near)]
    inner_lifts = [
        lift(1, 0, 3, middle), lift(2, 1, 2, middle), lift(3, 3, 2, near), lift(4, 2, 3, near),
    ]

    def arrive(s):
        lift(0, s, s, near).wait_recv()

    own_bias = pltpu.make_async_copy(bias_ref, ball_ref.at[mp], here.at[2])
    own_bias.start()
    lifts[0].start()

    @pl.when(inner)
    def _():
        inner_lifts[0].start()

    biases = [
        remote(bias_ref, ball_ref.at[mp], b_send.at[s], b_recv.at[s], tall[s]) for s in range(3)
    ]
    for copy in biases:
        copy.start()
    for i in range(CHIPS):
        firsts[i].wait_recv()
        passed = remote(
            rows_of(plane[i]), rows_of(plane[i]), q_send.at[4 + i], q_recv.at[4 + i], sibling
        )
        passed.start()
        shared.append(passed)
    own.wait()

    def weights(s, kind):
        group = mp ^ s
        block = {0: dp, 1: dp, 2: dp, 4: plane[0], 5: plane[1], 6: plane[2]}
        block[3] = plane[0] if s % 2 == 0 else plane[1]
        peer = {0: (plane[0], mp), 1: (plane[1], mp)}
        peer[3] = peer[1] if s % 2 == 0 else peer[0]
        ref = all_ref.at[group, block[kind]]
        return remote(ref, ref, w_send.at[s, kind], w_recv.at[s, kind], peer.get(kind, sibling))

    def start_weights(s):
        if s == 3:

            @pl.when(~inner)
            def _():
                arrive(3)

        for kind in (0, 1, 2):
            weights(s, kind).start()

    def pass_weights(s):
        weights(s, 0).wait_recv()
        weights(s, 1).wait_recv()
        for kind in (3, 4, 5):
            weights(s, kind).start()

    def last_weights(s):
        weights(s, 3).wait_recv()
        weights(s, 6).start()

    start_weights(0)
    mine.wait()
    for copy in shared:
        copy.wait_recv()
    arrive(1)

    @pl.when(inner)
    def _():
        inner_lifts[1].start()
        arrive(3)
        inner_lifts[2].start()

    start_weights(1)

    loads[4].wait()
    block = 256

    def project_rows(step, carry):
        part = pl.ds(pl.multiple_of(step * block, block), block)
        x = x_ref[part, :]
        offsets = jnp.concatenate(
            [qb_ref[0:1, :], jnp.zeros((1, width), F32), qb_ref[1:2, :]], 1
        )
        made = jnp.dot(x, wfull_ref[...], preferred_element_type=F32) + offsets
        marks = seg_ref[:, part] == lax.broadcasted_iota(jnp.int32, (MAX_SEGS, block), 0)
        picked = jnp.where(marks, 1.0, 0.0).T
        spread_rows(made.astype(BF16), picked, slots, qs_ref, ka_ref, va_ref, kk_ref, part)
        return carry

    lax.fori_loop(0, rows // block, project_rows, 0)
    arrive(2)

    @pl.when(inner)
    def _():
        inner_lifts[3].start()

    pass_weights(0)
    start_weights(2)

    live_count = HEADS // 4 + (mp < HEADS % 4).astype(jnp.int32)
    per_share = share // sub
    actions = {
        1: [(pass_weights, 1)],
        2: [(start_weights, 3)],
        4: [(last_weights, 0)],
        5: [(pass_weights, 2)],
        6: [(last_weights, 1)],
        7: [(pass_weights, 3)],
    }

    def send_rows(step, stage_index):
        return remote(
            stage.at[step], got_ref.at[mp, lax.rem(step, per_share)], a_send.at[step], a_recv.at[step],
            (dp, mp ^ stage_index),
        )

    def attend_rows(step, carry):
        stage_index = 3 - step // per_share
        group = mp ^ stage_index
        offset = lax.rem(step, per_share) * sub
        part = pl.ds(pl.multiple_of(group * share + offset, sub), sub)
        for when, todo in actions.items():

            @pl.when(step == when)
            def _():
                for act, s in todo:
                    act(s)

        kept = []
        for slot in range(slots):
            x = lax.dot_general(
                qs_ref[slot, part, :], ka_ref[slot], NT, preferred_element_type=F32
            )
            top = jnp.max(x, -1, keepdims=True)
            p = jnp.exp2(x - top).astype(BF16)
            made = jnp.dot(p, va_ref[slot], preferred_element_type=F32)
            total = -made[:, HD : HD + 1]
            mixed = made[:, :HD] / total
            one, two, three = thirds(top + jnp.log2(total))
            base = 3 * HD + MAX_SEGS
            qs_ref[slot, part, base : base + 3] = jnp.concatenate([one, two, three], 1)
            mixed_ref[part, slot * HD : (slot + 1) * HD] = mixed
            alive = (slot < live_count).astype(F32)
            kept.append((mixed * alive).astype(BF16))
        stage[step] = pack_rows(jnp.concatenate(kept, 1))

        @pl.when(step < 3 * per_share)
        def _():
            send_rows(step, stage_index).start()

        return carry

    lax.fori_loop(0, rows // sub, attend_rows, 0)
    keep = pltpu.make_async_copy(
        stage.at[pl.ds(3 * per_share, per_share)], got_ref.at[mp], here.at[3]
    )
    keep.start()
    last_weights(2)
    last_weights(3)
    for s in range(4):
        weights(s, 2).wait_recv()
        for kind in (4, 5, 6):
            weights(s, kind).wait_recv()
        for kind in range(7):
            weights(s, kind).wait_send()
    for copy in firsts + shared + lifts:
        copy.wait_send()

    @pl.when(inner)
    def _():
        for copy in inner_lifts:
            copy.wait_send()

    for copy in biases:
        copy.wait()
    for step in range(3 * per_share):
        send_rows(step, 3 - step // per_share).wait()
    own_bias.wait()
    keep.wait()


def front(frames, qkv_weight, up_weight, down_flip, out_flip, up_bias, qkv_bias, seg_ids, slots):
    rows, depth = frames.shape
    piece, hidden_cols = up_weight.shape
    width = slots * HD
    lanes = -(-(2 * hidden_cols + width) // 128) * 128
    sub = 256
    shape = lambda n: jax.ShapeDtypeStruct((slots, rows, n), BF16)
    vmem = pl.BlockSpec(memory_space=pltpu.VMEM)
    hbm = pl.BlockSpec(memory_space=pltpu.MemorySpace.HBM)
    dma = pltpu.SemaphoreType.DMA
    steps = rows // sub
    operands = (frames, qkv_weight, up_weight, down_flip, out_flip)
    return pl.pallas_call(
        functools.partial(front_kernel, slots, sub),
        in_specs=[hbm] * 5 + [vmem] * 3,
        out_specs=[vmem] * 9,
        out_shape=[
            jax.ShapeDtypeStruct((4, 8, piece, lanes), BF16),
            jax.ShapeDtypeStruct((8 * piece, 3 * width), BF16),
            jax.ShapeDtypeStruct((4, 1, HALF), F32),
            shape(AUG), shape(AUG), shape(VAUG),
            jax.ShapeDtypeStruct((rows, width), BF16),
            jax.ShapeDtypeStruct((rows, width), F32),
            jax.ShapeDtypeStruct((4, steps // 4, sub * 3 // 2, 2 * HD), BF16),
        ],
        scratch_shapes=[
            pltpu.VMEM(frames.shape, BF16), pltpu.VMEM(qkv_weight.shape, BF16),
            pltpu.VMEM(up_weight.shape, BF16), pltpu.VMEM(down_flip.shape, BF16),
            pltpu.VMEM(out_flip.shape, BF16),
            pltpu.VMEM((steps, sub * 3 // 2, 2 * HD), BF16),
            pltpu.VMEM((piece, 3 * width), BF16), pltpu.VMEM((piece, lanes), BF16),
            pltpu.VMEM((1, HALF), F32),
            dma((7,)), dma((7,)), dma((5,)), dma((4,)), dma((4, 7)), dma((4, 7)), dma((3,)), dma((3,)),
            dma((steps,)), dma((steps,)), dma((4,)), dma((len(operands),)),
        ],
        compiler_params=pltpu.CompilerParams(
            collective_id=1, has_side_effects=True, vmem_limit_bytes=20 << 20
        ),
        name="front",
    )(*operands, up_bias, qkv_bias, seg_ids.reshape(1, rows))


def project_kernel(slots, x_ref, w_ref, b_ref, seg_ref, qs_ref, ka_ref, va_ref, kk_ref):
    made = jnp.dot(x_ref[...], w_ref[...], preferred_element_type=F32) + b_ref[...]
    marks = seg_ref[...] == lax.broadcasted_iota(jnp.int32, (x_ref.shape[0], MAX_SEGS), 1)
    spread_rows(
        made.astype(BF16), jnp.where(marks, 1.0, 0.0), slots, qs_ref, ka_ref, va_ref, kk_ref, slice(None)
    )


def project(frames, weight, offsets, seg_ids, slots):
    rows, depth = frames.shape
    block = min(512, rows)
    spread = lambda n: pl.BlockSpec((slots, block, n), lambda i: (0, i, 0))
    shape = lambda n: jax.ShapeDtypeStruct((slots, rows, n), BF16)
    return pl.pallas_call(
        functools.partial(project_kernel, slots),
        grid=(rows // block,),
        in_specs=[
            pl.BlockSpec((block, depth), lambda i: (i, 0)),
            pl.BlockSpec(weight.shape, lambda i: (0, 0)),
            pl.BlockSpec((1, offsets.shape[1]), lambda i: (0, 0)),
            pl.BlockSpec((block, 1), lambda i: (i, 0)),
        ],
        out_specs=[
            spread(AUG), spread(AUG), spread(VAUG), pl.BlockSpec((block, slots * HD), lambda i: (i, 0)),
        ],
        out_shape=[
            shape(AUG), shape(AUG), shape(VAUG), jax.ShapeDtypeStruct((rows, slots * HD), BF16),
        ],
        compiler_params=pltpu.CompilerParams(vmem_limit_bytes=VMEM_LIMIT),
        name="project",
    )(frames, weight, offsets, seg_ids.reshape(rows, 1))


def attend_kernel(sub, qs_ref, ka_ref, va_ref, qn_ref, mixed_ref):
    for at in range(0, qs_ref.shape[1], sub):
        part = slice(at, at + sub)
        x = lax.dot_general(qs_ref[0, part, :], ka_ref[0], NT, preferred_element_type=F32)
        top = jnp.max(x, -1, keepdims=True)
        p = jnp.exp2(x - top).astype(BF16)
        made = jnp.dot(p, va_ref[0], preferred_element_type=F32)
        total = -made[:, HD : HD + 1]
        mixed_ref[0, part, :] = made[:, :HD] / total
        one, two, three = thirds(top + jnp.log2(total))
        base = 3 * HD + MAX_SEGS
        blank = jnp.zeros((sub, AUG - base - 3), BF16)
        qn_ref[0, part, :] = jnp.concatenate(
            [qs_ref[0, part, :base], one, two, three, blank], 1
        )


def attend(qs, ka, va):
    slots, rows, _ = qs.shape
    block = min(512, rows)
    sub = min(256, block)
    whole = lambda n: pl.BlockSpec((1, rows, n), lambda h, i: (h, 0, 0))
    some = lambda n: pl.BlockSpec((1, block, n), lambda h, i: (h, i, 0))
    return pl.pallas_call(
        functools.partial(attend_kernel, sub),
        grid=(slots, rows // block),
        in_specs=[some(AUG), whole(AUG), whole(VAUG)],
        out_specs=[some(AUG), some(HD)],
        out_shape=[
            jax.ShapeDtypeStruct((slots, rows, AUG), BF16),
            jax.ShapeDtypeStruct((slots, rows, HD), F32),
        ],
        compiler_params=pltpu.CompilerParams(vmem_limit_bytes=VMEM_LIMIT),
        name="attend",
    )(qs, ka, va)


def attend_back_kernel(
    sub, qs_ref, ka_ref, va_ref, kk_ref, mixed_ref, up_ref, dq_ref, dk_ref, dv_ref, dk_acc, dv_acc
):
    step = pl.program_id(1)

    @pl.when(step == 0)
    def _():
        dk_acc[...] = jnp.zeros_like(dk_acc)
        dv_acc[...] = jnp.zeros_like(dv_acc)

    for at in range(0, qs_ref.shape[1], sub):
        part = slice(at, at + sub)
        q = qs_ref[0, part, :HD]
        up = up_ref[0, part, :]
        d_one, d_two, d_three = thirds(
            jnp.sum(up.astype(F32) * mixed_ref[0, part, :], -1, keepdims=True)
        )
        blank = lambda n: jnp.zeros((sub, n), BF16)
        upper = jnp.concatenate([up, d_one, d_two, d_three, blank(VAUG - HD - 3)], 1)
        x = lax.dot_general(qs_ref[0, part, :], ka_ref[0], NT, preferred_element_type=F32)
        p = jnp.exp2(x)
        dp = lax.dot_general(upper, va_ref[0], NT, preferred_element_type=F32)
        ds = (p * dp).astype(BF16)
        dv_acc[...] += lax.dot_general(up, p.astype(BF16), TN, preferred_element_type=F32)
        dk_acc[...] += lax.dot_general(q, ds, TN, preferred_element_type=F32)
        dq_ref[0, part, :] = (
            jnp.dot(ds, kk_ref[0], preferred_element_type=F32) * SCALE
        ).astype(BF16)

    @pl.when(step == pl.num_programs(1) - 1)
    def _():
        dk_ref[0] = (dk_acc[...] * SCALE).T.astype(BF16)
        dv_ref[0] = dv_acc[...].T.astype(BF16)


def attend_back(qs, ka, va, kk, mixed, up):
    slots, rows, _ = qs.shape
    block = min(512, rows)
    sub = min(256, block)
    whole = lambda n: pl.BlockSpec((1, rows, n), lambda h, i: (h, 0, 0))
    some = lambda n: pl.BlockSpec((1, block, n), lambda h, i: (h, i, 0))
    shape = jax.ShapeDtypeStruct((slots, rows, HD), BF16)
    return pl.pallas_call(
        functools.partial(attend_back_kernel, sub),
        grid=(slots, rows // block),
        in_specs=[
            some(AUG), whole(AUG), whole(VAUG), whole(HD), some(HD), some(HD),
        ],
        out_specs=[some(HD), whole(HD), whole(HD)],
        out_shape=[shape, shape, shape],
        scratch_shapes=[pltpu.VMEM((HD, rows), F32), pltpu.VMEM((HD, rows), F32)],
        compiler_params=pltpu.CompilerParams(vmem_limit_bytes=VMEM_LIMIT),
        name="attend_back",
    )(qs, ka, va, kk, mixed, up)


def norm_forward(summed):
    centre = summed - jnp.mean(summed, -1, keepdims=True)
    spread = jnp.mean(centre * centre, -1, keepdims=True)
    factor = lax.rsqrt(spread + EPS)
    return (centre * factor, factor)


def norm_backward(upper, normed, factor, gain):
    scaled = upper * gain
    return factor * (
        scaled
        - jnp.mean(scaled, -1, keepdims=True)
        - normed * jnp.mean(scaled * normed, -1, keepdims=True)
    )


def middle_kernel(
    groups, hidden_cols, block, linked,
    x_ref, y_ref, got_ref, w_ref, ub_ref, v0, v1, v2, v3, v4, v5,
    out_ref, s1_ref, back_ref, grad_ref, small_ref, *scratch,
):
    x_own, y_own, ow, act, pre_low, slope, hid_flip, two_flip, one_flip, here = scratch[:10]
    share = out_ref.shape[0]
    width = ow.shape[2]
    gap = HALF - hidden_cols
    dp = lax.axis_index("dp")
    mp = lax.axis_index("mp")
    rows = pl.ds(pl.multiple_of(mp * share, share), share)
    loads = [
        pltpu.make_async_copy(x_ref.at[rows], x_own, here.at[0]),
        pltpu.make_async_copy(y_ref.at[rows], y_own, here.at[1]),
    ]
    for copy in loads:
        copy.start()
    if linked:
        back_own, got, grads, arrived, b_send, b_recv, g_send, g_recv = scratch[10:]
        core = lax.rem(dp, 2)
        sibling = (dp ^ 1, mp)
        plane_barrier([sibling] + [(dp, mp ^ s) for s in range(1, 4)])
    else:
        back_own, got, grads = back_ref, got_ref, grad_ref
    out_bias, gain_one, shift_one, down_bias, gain_two, shift_two = (
        v[...].reshape(1, v.shape[0]) for v in (v0, v1, v2, v3, v4, v5)
    )
    for g in range(groups):
        ow[g, :, :gap] = w_ref[g, :, hidden_cols:HALF]
        ow[g, :, gap:] = w_ref[g, :, HALF + hidden_cols : HALF + hidden_cols + width - gap]
    small_ref[...] = jnp.zeros_like(small_ref)
    real = lane_marks(1, HALF, hidden_cols)
    alive = [
        lane_marks(1, width, HD * (HEADS // groups + (g < HEADS % groups))) for g in range(groups)
    ]
    for copy in loads:
        copy.wait()

    def send_back(step, s):
        at = step * 3 + s - 1
        return remote(
            back_own.at[mp ^ s, step], back_ref.at[mp, step], b_send.at[at], b_recv.at[at], (dp, mp ^ s)
        )

    def some_rows(step, carry):
        part = pl.ds(pl.multiple_of(step * block, block), block)
        summed = x_own[part, :].astype(F32) + out_bias
        for g in range(groups):
            if linked:
                got[g, part, :] = unpack_rows(got_ref[g, step])
            summed += lax.dot_general(got[g, part, :], ow[g], NT, preferred_element_type=F32)
        normed_one, factor_one = norm_forward(summed)
        hidden = normed_one * gain_one + shift_one
        hidden_low = hidden.astype(BF16)
        hid_flip[:, part] = hidden_low.T
        feed = hidden + down_bias
        for g in range(groups):
            pre = jnp.dot(hidden_low, w_ref[g, :, :HALF], preferred_element_type=F32) + ub_ref[g]
            half = 0.5 + 0.5 * lax.erf(pre * math.sqrt(0.5))
            bell = jnp.exp(pre * pre * -0.5) * (pre * (1.0 / math.sqrt(2.0 * math.pi)))
            slope[g] = jnp.where(real, half + bell, 0.0)
            made = jnp.where(real, pre * half, 0.0).astype(BF16)
            act[g, part, :] = made
            feed += lax.dot_general(
                made, w_ref[g, :, HALF : 2 * HALF], NT, preferred_element_type=F32
            )
        normed_two, factor_two = norm_forward(feed)
        out_ref[part, :] = (normed_two * gain_two + shift_two).astype(BF16)
        upstream = y_own[part, :].astype(F32)
        two_grad = norm_backward(upstream, normed_two, factor_two, gain_two)
        sum_two = two_grad.astype(BF16)
        two_flip[:, part] = sum_two.T
        hidden_grad = two_grad
        for g in range(groups):
            act_grad = jnp.dot(
                sum_two, w_ref[g, :, HALF : 2 * HALF], preferred_element_type=F32
            )
            low = (slope[g] * act_grad).astype(BF16)
            pre_low[g, part, :] = low
            hidden_grad += lax.dot_general(
                low, w_ref[g, :, :HALF], NT, preferred_element_type=F32
            )
            small_ref[8 + g : 9 + g, :] += jnp.sum(low.astype(F32), 0, keepdims=True)
        one_grad = norm_backward(hidden_grad, normed_one, factor_one, gain_one)
        sum_one = one_grad.astype(BF16)
        s1_ref[part, :] = one_grad
        one_flip[:, part] = sum_one.T
        for g in range(groups):
            made = jnp.dot(sum_one, ow[g], preferred_element_type=F32)
            made = jnp.where(alive[g], made, 0.0).astype(BF16)
            if linked:
                back_own[g, step] = pack_rows(made)
            else:
                back_own[g, part, :] = made
        if linked:
            for s in range(1, 4):
                send_back(step, s).start()
        for at, term in enumerate((
            sum_one.astype(F32), hidden_grad * normed_one, hidden_grad,
            sum_two.astype(F32), upstream * normed_two, upstream,
        )):
            small_ref[at : at + 1, :] += jnp.sum(term, 0, keepdims=True)
        return carry

    lax.fori_loop(0, share // block, some_rows, 0)
    if linked:
        keep = pltpu.make_async_copy(back_own.at[mp], back_ref.at[mp], here.at[2])
        keep.start()
    depth = hid_flip.shape[0]
    rest = width - gap
    spare = w_ref.shape[2] - HALF - hidden_cols - rest
    span = depth // 2
    shared = []
    for g in range(groups):
        for part in range(2):
            cols = slice(part * span, (part + 1) * span)
            made = jnp.dot(hid_flip[cols], pre_low[g], preferred_element_type=F32).astype(BF16)
            grad_out = jnp.dot(one_flip[cols], got[g], preferred_element_type=F32).astype(BF16)
            left = jnp.concatenate([made[:, :hidden_cols], grad_out[:, :gap]], 1)
            made = jnp.dot(two_flip[cols], act[g], preferred_element_type=F32).astype(BF16)
            right = jnp.concatenate(
                [made[:, :hidden_cols], grad_out[:, gap:], jnp.zeros((span, spare), BF16)], 1
            )
            if not linked:
                grads[g, cols, :HALF] = left
                grads[g, cols, HALF:] = right
                continue
            piece = grad_ref.shape[2]
            for i in range(span // piece):
                d = part * (span // piece) + i
                at = slice(i * piece, (i + 1) * piece)

                @pl.when(core == d % 2)
                def _():
                    grad_ref[g, d // 2, :, :HALF] = left[at]
                    grad_ref[g, d // 2, :, HALF:] = right[at]

                @pl.when(core != d % 2)
                def _():
                    grads[g, d // 2, :, :HALF] = left[at]
                    grads[g, d // 2, :, HALF:] = right[at]

        if linked:
            copy = remote(grads.at[g], arrived.at[g], g_send.at[g], g_recv.at[g], sibling)
            copy.start()
            shared.append(copy)
    if linked:
        for g in range(groups):
            shared[g].wait_recv()
            for c in range(4):
                grad_ref[g, c] += arrived[g, c]
        for step in range(share // block):
            for s in range(1, 4):
                send_back(step, s).wait()
        for copy in shared:
            copy.wait_send()
        keep.wait()


def middle(frames, cotangent, got, weights, up_bias, vectors, hidden_cols, linked):
    groups = got.shape[0]
    share, depth = frames.shape[0] // groups, frames.shape[1]
    lanes = weights.shape[2]
    width = 3 * HD
    block = min(256, share)
    vmem = pl.BlockSpec(memory_space=pltpu.VMEM)
    rest = pl.BlockSpec(memory_space=pltpu.MemorySpace.HBM)
    dma = pltpu.SemaphoreType.DMA
    scratch = [
        pltpu.VMEM((share, depth), BF16),
        pltpu.VMEM((share, depth), BF16),
        pltpu.VMEM((groups, depth, width), BF16),
        pltpu.VMEM((groups, share, HALF), BF16),
        pltpu.VMEM((groups, share, HALF), BF16),
        pltpu.VMEM((groups, block, HALF), F32),
        pltpu.VMEM((depth, share), BF16),
        pltpu.VMEM((depth, share), BF16),
        pltpu.VMEM((depth, share), BF16),
        dma((3,)),
    ]
    grads = jax.ShapeDtypeStruct(weights.shape, BF16)
    if linked:
        piece = depth // 8
        grads = jax.ShapeDtypeStruct((groups, 4, piece, lanes), BF16)
        sends = 3 * (share // block)
        scratch += [
            pltpu.VMEM(got.shape, BF16),
            pltpu.VMEM((groups, share, width), BF16),
            pltpu.VMEM((groups, 4, piece, lanes), BF16),
            pltpu.VMEM((groups, 4, piece, lanes), BF16),
            dma((sends,)), dma((sends,)), dma((groups,)), dma((groups,)),
        ]
    extra = dict(collective_id=2, has_side_effects=True) if linked else {}
    return pl.pallas_call(
        functools.partial(middle_kernel, groups, hidden_cols, block, linked),
        in_specs=[rest, rest] + [vmem] * 9,
        out_specs=[vmem] * 5,
        out_shape=[
            jax.ShapeDtypeStruct((share, depth), BF16),
            jax.ShapeDtypeStruct((share, depth), F32),
            jax.ShapeDtypeStruct(got.shape, BF16),
            grads,
            jax.ShapeDtypeStruct((16, HALF), F32),
        ],
        scratch_shapes=scratch,
        compiler_params=pltpu.CompilerParams(
            vmem_limit_bytes=33 << 20 if linked else VMEM_LIMIT, **extra
        ),
        name="middle",
    )(frames, cotangent, got, weights, up_bias, *vectors)


PAIRS = (
    (0, 3), (1, 3), (2, 3), (3, 3), (3, 2), (3, 1), (3, 0), (0, 2), (1, 2), (2, 2), (2, 1), (2, 0),
    (0, 1), (1, 1), (1, 0), (0, 0),
)
ENDS = {6: 3, 11: 2, 14: 1, 15: 0}


def pick(table, step):
    made = jnp.int32(table[0])
    for at in range(1, len(table)):
        made = jnp.where(step >= at, jnp.int32(table[at]), made)
    return made


def back_kernel(
    slots, sub,
    qs_ref, ka_ref, va_ref, kk_ref, mixed_ref, up_ref, sums_ref, x_hbm, wq_ref, one_ref, small_ref,
    fg_ref, gq_ref, gb_ref, gup_ref, gdown_ref, gout_ref, gub_ref, s0, s1, s2, s3, s4, s5,
    upper, up_flip, q_flip, dq_acc, dk_acc, dv_acc, low, part_out, chain, fresh, far_in, near_in, third,
    tall_in, gq_own, gq_in, gb_own, gb_in, tiny, tiny_in,
    c_send, c_recv, f_send, f_recv, n_send, n_recv, t_send, t_recv, q_send, q_recv, b_send, b_recv,
    s_send, s_recv, small_sum, x_ref, loaded, gq_acc,
):
    dp = lax.axis_index("dp")
    mp = lax.axis_index("mp")
    chip = dp // 2
    rows, depth = x_hbm.shape
    share = rows // 4
    width = slots * HD
    others = [(dp ^ d, mp) for d in range(1, 8)]
    tall = [(dp, mp ^ s) for s in range(1, 4)]
    plane_barrier(others + tall)
    x_peer, y_peer = (dp ^ 2, mp), (dp ^ 4, mp)

    def rows_of(name):
        return pl.ds(pl.multiple_of((mp ^ name) * share, share), share)

    def load_rows(name):
        return pltpu.make_async_copy(x_hbm.at[rows_of(name)], x_ref, loaded.at[0])

    load_rows(3).start()

    def far(s):
        return remote(
            sums_ref.at[mp ^ s, chip ^ 3], far_in.at[s], f_send.at[s], f_recv.at[s],
            y_peer if s % 2 == 0 else x_peer,
        )

    def near(s, kind):
        toward_x = (s % 2 == 0) == (kind == 1)
        source = third.at[s] if kind == 1 else sums_ref.at[mp ^ s, chip ^ (1 if toward_x else 2)]
        return remote(
            source, near_in.at[s, kind], n_send.at[s, kind], n_recv.at[s, kind],
            x_peer if toward_x else y_peer,
        )

    def lift(s):
        return remote(
            fresh.at[s], tall_in.at[s], t_send.at[s], t_recv.at[s], (dp, mp ^ s)
        )

    def begin_grads(s):
        far(s).start()
        near(s, 0).start()

    def join_far(s):
        far(s).wait_recv()
        third[s] = sums_ref[mp ^ s, chip ^ (1 if s % 2 == 0 else 2)] + far_in[s]
        near(s, 1).start()

    def join_near(s):
        near(s, 0).wait_recv()
        near(s, 1).wait_recv()
        total = sums_ref[mp ^ s, chip].astype(F32) + near_in[s, 0].astype(F32)
        fresh[s] = (total + near_in[s, 1].astype(F32)).astype(BF16)
        if s > 0:
            lift(s).start()

    partners = [(dp ^ 1, mp), (dp ^ 2, mp), (dp ^ 4, mp), (dp, mp ^ 1), (dp, mp ^ 2)]

    def swap(at):
        return remote(tiny.at[at], tiny_in.at[at], s_send.at[at], s_recv.at[at], partners[at])

    def small_step(at):
        if at == 0:
            tiny[0] = small_ref[...]
        else:
            swap(at - 1).wait_recv()
            made = tiny[at - 1] + tiny_in[at - 1]
            if at == len(partners):
                small_sum[...] = made
                for row, ref in enumerate((s0, s1, s2, s3, s4, s5)):
                    ref[...] = made[row : row + 1, :].reshape(ref.shape)
                cols = gub_ref.shape[-1]
                gub_ref[...] = small_sum[pl.ds(8 + mp, 1), :cols].reshape(gub_ref.shape)
                return
            tiny[at] = made
        swap(at).start()

    def chain_copy(name, leftward):
        block = mp ^ name
        target = mp - 1 if leftward else mp + 1
        slot = jnp.where(block == target, 4, block) if leftward else block
        return remote(
            part_out.at[name], chain.at[slot], c_send.at[name], c_recv.at[slot], (dp, target)
        )

    def chain_arrival(slot):
        return remote(part_out.at[0], chain.at[slot], c_send.at[0], c_recv.at[slot], (dp, mp ^ 1))

    def relay(name):
        block = mp ^ name
        inner = (mp == 1) | (mp == 2)
        waits = inner

        @pl.when(waits)
        def _():
            chain_arrival(block).wait_recv()
            part_out[name] = (
                part_out[name].astype(F32) + chain[block].astype(F32)
            ).astype(BF16)

        @pl.when(block < mp)
        def _():
            chain_copy(name, True).start()

        @pl.when(block > mp)
        def _():
            chain_copy(name, False).start()

    def finish(name):
        at = rows_of(name)
        for slot in range(slots):
            col = slot * HD
            low[:, col : col + HD] = (dq_acc[slot, at, :] * SCALE).astype(BF16)
            low[:, width + col : width + col + HD] = (dk_acc[slot, :, at] * SCALE).T.astype(BF16)
            low[:, 2 * width + col : 2 * width + col + HD] = dv_acc[slot, :, at].T.astype(BF16)
        part_out[name] = lax.dot_general(
            low[...], wq_ref[...], NT, preferred_element_type=F32
        ).astype(BF16)

    def add_rows(name):
        ones = jnp.ones((16, share), BF16)
        gb_own[...] += jnp.dot(ones, low[...], preferred_element_type=F32)[0:8, :]
        load_rows(name).wait()
        gq_acc[...] += lax.dot_general(x_ref[...], low[...], TN, preferred_element_type=F32)
        if name > 0:
            load_rows(name - 1).start()

    dq_acc[...] = jnp.zeros_like(dq_acc)
    dk_acc[...] = jnp.zeros_like(dk_acc)
    dv_acc[...] = jnp.zeros_like(dv_acc)
    gq_acc[...] = jnp.zeros_like(gq_acc)
    gb_own[...] = jnp.zeros_like(gb_own)
    far(3).start()
    far(2).start()
    near(3, 0).start()
    near(2, 0).start()
    small_step(0)

    def prepare(step, carry):
        at = pl.ds(pl.multiple_of(step * share, share), share)
        wide = jnp.concatenate([unpack_rows(up_ref[step, i]) for i in range(up_ref.shape[1])], 0)
        for slot in range(slots):
            up = wide[:, slot * HD : (slot + 1) * HD]
            one, two, three = thirds(
                jnp.sum(
                    up.astype(F32) * mixed_ref[at, slot * HD : (slot + 1) * HD], -1, keepdims=True
                )
            )
            blank = jnp.zeros((share, VAUG - HD - 3), BF16)
            upper[slot, at, :] = jnp.concatenate([up, one, two, three, blank], 1)
            up_flip[slot, :, at] = up.T
            q_flip[slot, :, at] = qs_ref[slot, at, :HD].T
        return carry

    lax.fori_loop(0, 4, prepare, 0)
    actions = {
        1: [(small_step, 1)],
        2: [(join_far, 3), (join_far, 2), (small_step, 2)],
        3: [(begin_grads, 1), (small_step, 3)],
        4: [(begin_grads, 0), (small_step, 4)],
        5: [(join_near, 3), (small_step, 5)],
        6: [(join_near, 2)],
        8: [(join_far, 1)],
        9: [(join_far, 0)],
        12: [(join_near, 1)],
        13: [(join_near, 0)],
    }

    def pair(step, carry):
        query = mp ^ pick([p[0] for p in PAIRS], step)
        key = mp ^ pick([p[1] for p in PAIRS], step)
        keys = pl.ds(pl.multiple_of(key * share, share), share)
        for when, todo in actions.items():

            @pl.when(step == when)
            def _():
                for act, s in todo:
                    act(s)

        for at in range(0, share, sub):
            part = pl.ds(pl.multiple_of(query * share + at, sub), sub)
            for slot in range(slots):
                x = lax.dot_general(
                    qs_ref[slot, part, :], ka_ref[slot, keys, :], NT, preferred_element_type=F32
                )
                p = jnp.exp2(x)
                dp_ = lax.dot_general(
                    upper[slot, part, :], va_ref[slot, keys, :], NT, preferred_element_type=F32
                )
                ds = (p * dp_).astype(BF16)
                dv_acc[slot, :, keys] += jnp.dot(
                    up_flip[slot, :, part], p.astype(BF16), preferred_element_type=F32
                )
                dk_acc[slot, :, keys] += jnp.dot(
                    q_flip[slot, :, part], ds, preferred_element_type=F32
                )
                dq_acc[slot, part, :] += jnp.dot(
                    ds, kk_ref[keys, slot * HD : (slot + 1) * HD], preferred_element_type=F32
                )
        for when, name in ENDS.items():

            @pl.when(step == when)
            def _():
                finish(name)
                if name == 2:
                    relay(name)
                elif name > 0:

                    @pl.when((mp == 0) | (mp == 3))
                    def _():
                        relay(name)

                add_rows(name)

        return carry

    lax.fori_loop(0, len(PAIRS), pair, 0)
    gb_in[dp] = gb_own[...]
    piece = depth // 8
    for d in range(8):
        gq_own[d] = gq_acc[d * piece : (d + 1) * piece, :].astype(BF16)
    q_copies = []
    for d in range(1, 8):
        to = dp ^ d
        q_copies.append(
            remote(gq_own.at[to], gq_in.at[d - 1], q_send.at[d - 1], q_recv.at[d - 1], others[d - 1])
        )
        q_copies.append(
            remote(gb_own, gb_in.at[dp], b_send.at[d - 1], b_recv.at[d - 1], others[d - 1])
        )
    for copy in q_copies:
        copy.start()
    for name in (3, 1):

        @pl.when((mp == 1) | (mp == 2))
        def _():
            relay(name)

    for s in range(1, 4):
        lift(s).wait_recv()
    total = fresh[0].astype(F32)
    for s in range(1, 4):
        total = total + tall_in[s].astype(F32)
    cols = gup_ref.shape[1]
    gap = HALF - cols
    gup_ref[...] = total[:, :cols]
    gdown_ref[...] = total[:, HALF : HALF + cols]
    gout_ref[:, :gap] = total[:, cols:HALF]
    gout_ref[:, gap:] = total[:, HALF + cols : HALF + cols + width - gap]
    for copy in q_copies:
        copy.wait_recv()
    total = gq_own[dp].astype(F32)
    for d in range(7):
        total = total + gq_in[d].astype(F32)
    for i in range(3):
        gq_ref[i] = total[:, i * width : (i + 1) * width]
    total = gb_in[0]
    for d in range(1, 8):
        total = total + gb_in[d]
    gb_ref[0:1, :] = total[0:1, :width]
    gb_ref[1:2, :] = total[0:1, 2 * width :]

    wide = one_ref[...] + part_out[0].astype(F32)

    @pl.when(mp > 0)
    def _():
        chain_arrival(mp).wait_recv()

    @pl.when(mp < 3)
    def _():
        chain_arrival(4).wait_recv()

    left = jnp.where(mp > 0, chain[mp].astype(F32), 0.0)
    right = jnp.where(mp < 3, chain[4].astype(F32), 0.0)
    fg_ref[...] = (wide + left + right).astype(BF16)
    for name in (1, 2, 3):
        remote(
            part_out.at[name], chain.at[0], c_send.at[name], c_recv.at[0], (dp, mp ^ 1)
        ).wait_send()
    for s in range(4):
        far(s).wait_send()
        near(s, 0).wait_send()
        near(s, 1).wait_send()
        if s > 0:
            lift(s).wait_send()
    for at in range(len(partners)):
        swap(at).wait_send()
    for copy in q_copies:
        copy.wait_send()


def back_pass(qs, ka, va, kk, mixed, up, sums, frames, wq, one_grad, small, hidden_cols):
    slots, rows, _ = qs.shape
    depth = frames.shape[1]
    share = rows // 4
    piece, lanes = sums.shape[2:]
    cols = wq.shape[1]
    vmem = pl.BlockSpec(memory_space=pltpu.VMEM)
    hbm = pl.BlockSpec(memory_space=pltpu.MemorySpace.HBM)
    dma = pltpu.SemaphoreType.DMA
    V = pltpu.VMEM
    return pl.pallas_call(
        functools.partial(back_kernel, slots, min(512, share)),
        in_specs=[vmem] * 7 + [hbm] + [vmem] * 3,
        out_specs=[vmem] * 13,
        out_shape=[
            jax.ShapeDtypeStruct((share, depth), BF16),
            jax.ShapeDtypeStruct((3, piece, cols // 3), F32),
            jax.ShapeDtypeStruct((2, cols // 3), F32),
            jax.ShapeDtypeStruct((piece, hidden_cols), F32),
            jax.ShapeDtypeStruct((piece, hidden_cols), F32),
            jax.ShapeDtypeStruct((piece, cols // 3), F32),
            jax.ShapeDtypeStruct((hidden_cols,), F32),
        ]
        + [jax.ShapeDtypeStruct((depth,), F32)] * 6,
        scratch_shapes=[
            V((slots, rows, VAUG), BF16), V((slots, HD, rows), BF16), V((slots, HD, rows), BF16),
            V((slots, rows, HD), F32), V((slots, HD, rows), F32), V((slots, HD, rows), F32),
            V((share, cols), BF16), V((4, share, depth), BF16), V((5, share, depth), BF16),
            V((4, piece, lanes), BF16), V((4, piece, lanes), BF16), V((4, 2, piece, lanes), BF16),
            V((4, piece, lanes), BF16), V((4, piece, lanes), BF16),
            V((8, piece, cols), BF16), V((7, piece, cols), BF16),
            V((8, cols), F32), V((8, 8, cols), F32), V((5,) + small.shape, F32), V((5,) + small.shape, F32),
            dma((4,)), dma((5,)), dma((4,)), dma((4,)), dma((4, 2)), dma((4, 2)), dma((4,)), dma((4,)),
            dma((7,)), dma((7,)), dma((7,)), dma((7,)), dma((5,)), dma((5,)), V(small.shape, F32),
            V((share, depth), BF16), dma((1,)), V((depth, cols), F32),
        ],
        compiler_params=pltpu.CompilerParams(
            collective_id=3, has_side_effects=True, vmem_limit_bytes=34 << 20
        ),
        name="back_pass",
    )(qs, ka, va, kk, mixed, up, sums, frames, wq, one_grad, small)


def deliver_kernel(count, *refs):
    sources, results, sem = refs[:count], refs[count : 2 * count], refs[2 * count]
    copies = [
        pltpu.make_async_copy(a, b, sem.at[i]) for i, (a, b) in enumerate(zip(sources, results))
    ]
    for copy in copies:
        copy.start()
    for copy in copies:
        copy.wait()


def deliver(arrays):
    count = len(arrays)
    return pl.pallas_call(
        functools.partial(deliver_kernel, count),
        in_specs=[pl.BlockSpec(memory_space=pltpu.VMEM)] * count,
        out_specs=[pl.BlockSpec(memory_space=pltpu.MemorySpace.HBM)] * count,
        out_shape=[jax.ShapeDtypeStruct(a.shape, a.dtype) for a in arrays],
        scratch_shapes=[pltpu.SemaphoreType.DMA((count,))],
        compiler_params=pltpu.CompilerParams(vmem_limit_bytes=4 << 20),
        name="deliver",
    )(*arrays)


def body(
    frames, seg_ids, qkv_weight, qkv_bias, out_weight, out_bias, gain_one, shift_one,
    up_weight, up_bias, down_weight, down_bias, gain_two, shift_two, cotangent,
):
    rows, depth = frames.shape
    mp_size = lax.axis_size("mp")
    dp_size = lax.axis_size("dp")
    mp_index = lax.axis_index("mp")
    share = rows // mp_size
    slots = qkv_weight.shape[2] // HD
    width = slots * HD
    hidden_cols = up_weight.shape[1]
    piece = qkv_weight.shape[1]
    gap = HALF - hidden_cols
    spare = -(HALF + hidden_cols + width - gap) % 128
    live_count = HEADS // mp_size + (mp_index < HEADS % mp_size).astype(jnp.int32)
    live = (jnp.arange(slots) < live_count).astype(F32)

    in_hbm = lambda a: pltpu.with_memory_space_constraint(a, pltpu.MemorySpace.HBM)
    out_flip = out_weight.T
    down_flip = down_weight.T
    vectors = (out_bias, gain_one, shift_one, down_bias, gain_two, shift_two)
    linked = (dp_size, mp_size, slots, rows) == (8, 4, 3, 2048)
    if linked:
        weights, qkv_full, ub_full, qs, ka, va, kk, mixed, got = front(
            *map(in_hbm, (frames, qkv_weight, up_weight, down_flip, out_flip)), up_bias, qkv_bias,
            seg_ids, slots,
        )
        weights = weights.reshape(mp_size, depth, -1)
    else:
        wq = jnp.transpose(qkv_weight, (1, 0, 2)).reshape(piece, 3 * width)
        packed = jnp.concatenate(
            [up_weight, out_flip[:, :gap], down_flip, out_flip[:, gap:], jnp.zeros((piece, spare), BF16)], 1
        )
        ub_pad = jnp.pad(up_bias, (0, gap))[None]
        offsets = jnp.concatenate([qkv_bias[0], jnp.zeros_like(qkv_bias[0]), qkv_bias[1]])[None]
        qkv_full = lax.all_gather(wq, "dp", axis=0, tiled=True)
        weights = lax.all_gather(packed, "mp", axis=0, tiled=False)
        weights = lax.all_gather(weights, "dp", axis=1, tiled=True)
        ub_full = lax.all_gather(ub_pad, "mp", axis=0, tiled=False)
        qs, ka, va, kk = project(frames, qkv_full, offsets, seg_ids, slots)
        qs, mixed = attend(qs, ka, va)
        mixed_low = (mixed * live[:, None, None]).astype(BF16)
        sent = mixed_low.reshape(slots, mp_size, share, HD).transpose(1, 2, 0, 3)
        got = lax.all_to_all(sent.reshape(mp_size, share, width), "mp", 0, 0, tiled=True)
    output_frames, sum_one_grad, back, partial, small = middle(
        in_hbm(frames), in_hbm(cotangent), got, weights, ub_full, vectors, hidden_cols, linked
    )
    if linked:
        made = back_pass(
            qs, ka, va, kk, mixed, back, partial, in_hbm(frames), qkv_full, sum_one_grad, small, hidden_cols
        )
        output_frames, *made = deliver([output_frames, *made])
        return (
            output_frames, made[0], made[1], made[2], made[5].T, made[7], made[8], made[9], made[3],
            made[6], made[4].T, made[10], made[11], made[12],
        )
    if not linked:
        back = lax.all_to_all(back, "mp", 0, 0, tiled=True)
        back = back.reshape(rows, slots, HD).transpose(1, 0, 2)
        partial = lax.psum_scatter(partial, "dp", scatter_dimension=1, tiled=True)
        partial = lax.psum_scatter(partial, "mp", scatter_dimension=0, tiled=True)[0].astype(F32)
        small = lax.psum(small, ("dp", "mp"))
        kk = kk.reshape(rows, slots, HD).transpose(1, 0, 2)
        dq, dk, dv = attend_back(qs, ka, va, kk, mixed, back)
        grads_low = jnp.stack([dq, dk, dv]).transpose(2, 0, 1, 3).reshape(rows, 3 * width)
        bias_sums = lax.psum(jnp.sum(grads_low.astype(F32), 0), "dp")
        grad_qkv = jnp.einsum("rd,rs->ds", frames, grads_low, preferred_element_type=F32)
        arrived = lax.all_to_all(
            grad_qkv.astype(BF16).reshape(dp_size, piece, 3 * width), "dp", 0, 0, tiled=True
        )
        grad_qkv = arrived.astype(F32).sum(0)
        input_part = jnp.einsum("rs,ds->rd", grads_low, qkv_full, preferred_element_type=F32)
        input_sum = lax.psum_scatter(input_part.astype(BF16), "mp", scatter_dimension=0, tiled=True)
        frames_grad = (input_sum.astype(F32) + sum_one_grad).astype(BF16)
    grad_qkv = grad_qkv.reshape(piece, 3, width).transpose(1, 0, 2)
    bias_sums = bias_sums.reshape(3, width)
    qkv_bias_grad = jnp.stack([bias_sums[0], bias_sums[2]])
    out_grad = jnp.concatenate(
        [partial[:, hidden_cols:HALF], partial[:, HALF + hidden_cols : HALF + hidden_cols + width - gap]], 1
    )
    return (
        output_frames,
        frames_grad,
        grad_qkv,
        qkv_bias_grad,
        out_grad.T,
        small[0],
        small[1],
        small[2],
        partial[:, :hidden_cols],
        lax.dynamic_index_in_dim(small, 8 + mp_index, 0, False)[:hidden_cols],
        partial[:, HALF : HALF + hidden_cols].T,
        small[3],
        small[4],
        small[5],
    )


def solution(mesh):
    in_specs = (
        P("dp", None), P("dp"), P(None, "dp", "mp"), P(None, "mp"), P("mp", "dp"), P(), P(), P(),
        P("dp", "mp"), P("mp"), P("mp", "dp"), P(), P(), P(), P("dp", None),
    )
    out_specs = (
        P(("dp", "mp"), None), P(("dp", "mp"), None), P(None, "dp", "mp"), P(None, "mp"),
        P("mp", "dp"), P(), P(), P(), P("dp", "mp"), P("mp"), P("mp", "dp"), P(), P(), P(),
    )
    return jax.shard_map(body, mesh=mesh, in_specs=in_specs, out_specs=out_specs, check_vma=False)
```

```python
import functools
import math

import jax
import jax.numpy as jnp
from jax import lax
from jax.experimental import pallas as pl
from jax.experimental.pallas import tpu as pltpu
from jax.sharding import PartitionSpec as P

HEADS = 10
HD = 64
EPS = 1e-05
SCALE = 0.125
MAX_SEGS = 16
MASKED = -1e30
UNIT = SCALE * math.log2(math.e)
AUG = 256
VAUG = 128
NT = (((1,), (1,)), ((), ()))
TN = (((0,), (0,)), ((), ()))
F32 = jnp.float32
BF16 = jnp.bfloat16
VMEM_LIMIT = 56 << 20
MESH = pl.DeviceIdType.MESH
CHIPS = 3
HALF = 640


def thirds(wide):
    first = wide.astype(BF16)
    rest = wide - first.astype(F32)
    second = rest.astype(BF16)
    third = (rest - second.astype(F32)).astype(BF16)
    return first, second, third


def lane_marks(rows, width, count):
    return lax.broadcasted_iota(jnp.int32, (rows, width), 1) < count


def spread_rows(made, picked, slots, qs_ref, ka_ref, va_ref, kk_ref, rows):
    count = made.shape[0]
    width = slots * HD
    chosen = picked.astype(BF16)
    barred = ((picked - 1.0) * -MASKED).astype(BF16)
    tail = AUG - 3 * HD - MAX_SEGS
    q_tail = jnp.zeros((count, tail), BF16)
    minus = jnp.where(lane_marks(count, tail, 3), -1.0, 0.0).astype(BF16)
    v_tail = jnp.where(lane_marks(count, VAUG - HD, 3), -1.0, 0.0).astype(BF16)
    for slot in range(slots):
        at = slot * HD
        q = made[:, at : at + HD]
        k = made[:, width + at : width + at + HD]
        v = made[:, 2 * width + at : 2 * width + at + HD]
        one, two, three = thirds(k.astype(F32) * UNIT)
        qs_ref[slot, rows, :] = jnp.concatenate([q, q, q, chosen, q_tail], 1)
        ka_ref[slot, rows, :] = jnp.concatenate([one, two, three, barred, minus], 1)
        va_ref[slot, rows, :] = jnp.concatenate([v, v_tail], 1)
    kk_ref[rows, :] = made[:, width : 2 * width]


def plane_barrier(peers):
    barrier = pltpu.get_barrier_semaphore()
    for peer in peers:
        pl.semaphore_signal(barrier, inc=1, device_id=peer, device_id_type=MESH)
    pl.semaphore_wait(barrier, len(peers))


def remote(src, dst, send, recv, peer):
    return pltpu.make_async_remote_copy(
        src_ref=src, dst_ref=dst, send_sem=send, recv_sem=recv, device_id=peer, device_id_type=MESH
    )


def pack_rows(wide):
    half = wide.shape[0] // 2
    third = wide[:, 2 * HD :]
    return jnp.concatenate(
        [wide[:, : 2 * HD], jnp.concatenate([third[:half], third[half:]], 1)], 0
    )


def unpack_rows(packed):
    rows = packed.shape[0] * 2 // 3
    rest = packed[rows:]
    return jnp.concatenate(
        [packed[:rows], jnp.concatenate([rest[:, :HD], rest[:, HD:]], 0)], 1
    )


def front_kernel(
    slots, sub,
    x_hbm, qkv_hbm, up_hbm, down_hbm, out_hbm, ub_ref, qb_ref, seg_ref,
    all_ref, wfull_ref, ball_ref, qs_ref, ka_ref, va_ref, kk_ref, mixed_ref, got_ref,
    x_ref, qkv_ref, up_ref, down_ref, out_ref, stage, wq_ref, pack_ref, bias_ref,
    q_send, q_recv, z_send, z_recv, w_send, w_recv, b_send, b_recv, a_send, a_recv, here, loaded,
):
    dp = lax.axis_index("dp")
    mp = lax.axis_index("mp")
    plane = [dp ^ 2, dp ^ 4, dp ^ 6]
    sibling = (dp ^ 1, mp)
    tall = [(dp, mp ^ s) for s in range(1, 4)]
    inner = (mp == 1) | (mp == 2)
    width = slots * HD
    pairs = ((qkv_hbm, qkv_ref), (up_hbm, up_ref), (down_hbm, down_ref), (out_hbm, out_ref), (x_hbm, x_ref))
    loads = [pltpu.make_async_copy(a, b, loaded.at[i]) for i, (a, b) in enumerate(pairs)]
    for copy in loads:
        copy.start()
    bias_ref[...] = jnp.zeros_like(bias_ref)
    bias_ref[:, : up_hbm.shape[1]] = ub_ref[...].reshape(1, up_hbm.shape[1])
    for copy in loads[:4]:
        copy.wait()
    for i in range(3):
        wq_ref[:, i * width : (i + 1) * width] = qkv_ref[i]
    hidden_cols = up_ref.shape[1]
    gap = HALF - hidden_cols
    rest = width - gap
    pack_ref[:, :hidden_cols] = up_ref[...]
    pack_ref[:, hidden_cols:HALF] = out_ref[:, :gap]
    pack_ref[:, HALF : HALF + hidden_cols] = down_ref[...]
    pack_ref[:, HALF + hidden_cols : HALF + hidden_cols + rest] = out_ref[:, gap:]
    spare = pack_ref.shape[1] - HALF - hidden_cols - rest
    pack_ref[:, HALF + hidden_cols + rest :] = jnp.zeros((pack_ref.shape[0], spare), BF16)
    plane_barrier([sibling] + [(d, mp) for d in plane] + tall)
    rows = x_ref.shape[0]
    share = rows // 4

    piece = wq_ref.shape[0]

    def rows_of(d):
        return wfull_ref.at[pl.ds(pl.multiple_of(d * piece, piece), piece)]

    mine = pltpu.make_async_copy(wq_ref, rows_of(dp), here.at[0])
    mine.start()
    firsts = [
        remote(wq_ref, rows_of(dp), q_send.at[i], q_recv.at[i], (plane[i], mp))
        for i in range(CHIPS)
    ]
    for copy in firsts:
        copy.start()
    shared = [remote(wq_ref, rows_of(dp), q_send.at[3], q_recv.at[3], sibling)]
    shared[0].start()
    own = pltpu.make_async_copy(pack_ref, all_ref.at[mp, dp], here.at[1])
    own.start()
    def lift(at, s, landing, peer):
        ref = all_ref.at[mp ^ s, dp]
        return remote(pack_ref if s == 0 else ref, ref, z_send.at[at], z_recv.at[landing], peer)

    near, middle = tall[0], tall[2]
    lifts = [lift(0, 0, 1, near)]
    inner_lifts = [
        lift(1, 0, 3, middle), lift(2, 1, 2, middle), lift(3, 3, 2, near), lift(4, 2, 3, near),
    ]

    def arrive(s):
        lift(0, s, s, near).wait_recv()

    own_bias = pltpu.make_async_copy(bias_ref, ball_ref.at[mp], here.at[2])
    own_bias.start()
    lifts[0].start()

    @pl.when(inner)
    def _():
        inner_lifts[0].start()

    biases = [
        remote(bias_ref, ball_ref.at[mp], b_send.at[s], b_recv.at[s], tall[s]) for s in range(3)
    ]
    for copy in biases:
        copy.start()
    for i in range(CHIPS):
        firsts[i].wait_recv()
        passed = remote(
            rows_of(plane[i]), rows_of(plane[i]), q_send.at[4 + i], q_recv.at[4 + i], sibling
        )
        passed.start()
        shared.append(passed)
    own.wait()

    def weights(s, kind):
        group = mp ^ s
        block = {0: dp, 1: dp, 2: dp, 4: plane[0], 5: plane[1], 6: plane[2]}
        block[3] = plane[0] if s % 2 == 0 else plane[1]
        peer = {0: (plane[0], mp), 1: (plane[1], mp)}
        peer[3] = peer[1] if s % 2 == 0 else peer[0]
        ref = all_ref.at[group, block[kind]]
        return remote(ref, ref, w_send.at[s, kind], w_recv.at[s, kind], peer.get(kind, sibling))

    def start_weights(s):
        if s == 3:

            @pl.when(~inner)
            def _():
                arrive(3)

        for kind in (0, 1, 2):
            weights(s, kind).start()

    def pass_weights(s):
        weights(s, 0).wait_recv()
        weights(s, 1).wait_recv()
        for kind in (3, 4, 5):
            weights(s, kind).start()

    def last_weights(s):
        weights(s, 3).wait_recv()
        weights(s, 6).start()

    start_weights(0)
    mine.wait()
    for copy in shared:
        copy.wait_recv()
    arrive(1)

    @pl.when(inner)
    def _():
        inner_lifts[1].start()
        arrive(3)
        inner_lifts[2].start()

    start_weights(1)

    loads[4].wait()
    block = 512

    def project_rows(step, carry):
        part = pl.ds(pl.multiple_of(step * block, block), block)
        x = x_ref[part, :]
        offsets = jnp.concatenate(
            [qb_ref[0:1, :], jnp.zeros((1, width), F32), qb_ref[1:2, :]], 1
        )
        made = jnp.dot(x, wfull_ref[...], preferred_element_type=F32) + offsets
        marks = seg_ref[:, part] == lax.broadcasted_iota(jnp.int32, (MAX_SEGS, block), 0)
        picked = jnp.where(marks, 1.0, 0.0).T
        spread_rows(made.astype(BF16), picked, slots, qs_ref, ka_ref, va_ref, kk_ref, part)
        return carry

    lax.fori_loop(0, rows // block, project_rows, 0)
    arrive(2)

    @pl.when(inner)
    def _():
        inner_lifts[3].start()

    pass_weights(0)
    start_weights(2)

    live_count = HEADS // 4 + (mp < HEADS % 4).astype(jnp.int32)
    per_share = share // sub
    actions = {
        1: [(pass_weights, 1)],
        3: [(start_weights, 3)],
        4: [(last_weights, 0)],
        5: [(pass_weights, 2)],
        6: [(last_weights, 1)],
        7: [(pass_weights, 3)],
    }

    def send_rows(step, stage_index):
        return remote(
            stage.at[step], got_ref.at[mp, lax.rem(step, per_share)], a_send.at[step], a_recv.at[step],
            (dp, mp ^ stage_index),
        )

    def attend_rows(step, carry):
        stage_index = 3 - step // per_share
        group = mp ^ stage_index
        offset = lax.rem(step, per_share) * sub
        part = pl.ds(pl.multiple_of(group * share + offset, sub), sub)
        for when, todo in actions.items():

            @pl.when(step == when)
            def _():
                for act, s in todo:
                    act(s)

        kept = []
        scores = [
            lax.dot_general(qs_ref[slot, part, :], ka_ref[slot], NT, preferred_element_type=F32)
            for slot in range(slots)
        ]
        for slot in range(slots):
            x = scores[slot]
            top = jnp.max(x, -1, keepdims=True)
            p = jnp.exp2(x - top).astype(BF16)
            made = jnp.dot(p, va_ref[slot], preferred_element_type=F32)
            total = -made[:, HD : HD + 1]
            mixed = made[:, :HD] / total
            one, two, three = thirds(top + jnp.log2(total))
            base = 3 * HD + MAX_SEGS
            qs_ref[slot, part, base : base + 3] = jnp.concatenate([one, two, three], 1)
            mixed_ref[part, slot * HD : (slot + 1) * HD] = mixed
            alive = (slot < live_count).astype(F32)
            kept.append((mixed * alive).astype(BF16))
        stage[step] = pack_rows(jnp.concatenate(kept, 1))

        @pl.when(step < 3 * per_share)
        def _():
            send_rows(step, stage_index).start()

        return carry

    lax.fori_loop(0, rows // sub, attend_rows, 0)
    keep = pltpu.make_async_copy(
        stage.at[pl.ds(3 * per_share, per_share)], got_ref.at[mp], here.at[3]
    )
    keep.start()
    last_weights(2)
    last_weights(3)
    for s in range(4):
        weights(s, 2).wait_recv()
        for kind in (4, 5, 6):
            weights(s, kind).wait_recv()
        for kind in range(7):
            weights(s, kind).wait_send()
    for copy in firsts + shared + lifts:
        copy.wait_send()

    @pl.when(inner)
    def _():
        for copy in inner_lifts:
            copy.wait_send()

    for copy in biases:
        copy.wait()
    for step in range(3 * per_share):
        send_rows(step, 3 - step // per_share).wait()
    own_bias.wait()
    keep.wait()


def front(frames, qkv_weight, up_weight, down_flip, out_flip, up_bias, qkv_bias, seg_ids, slots):
    rows, depth = frames.shape
    piece, hidden_cols = up_weight.shape
    width = slots * HD
    lanes = -(-(2 * hidden_cols + width) // 128) * 128
    sub = 256
    shape = lambda n: jax.ShapeDtypeStruct((slots, rows, n), BF16)
    vmem = pl.BlockSpec(memory_space=pltpu.VMEM)
    hbm = pl.BlockSpec(memory_space=pltpu.MemorySpace.HBM)
    dma = pltpu.SemaphoreType.DMA
    steps = rows // sub
    operands = (frames, qkv_weight, up_weight, down_flip, out_flip)
    return pl.pallas_call(
        functools.partial(front_kernel, slots, sub),
        in_specs=[hbm] * 5 + [vmem] * 3,
        out_specs=[vmem] * 9,
        out_shape=[
            jax.ShapeDtypeStruct((4, 8, piece, lanes), BF16),
            jax.ShapeDtypeStruct((8 * piece, 3 * width), BF16),
            jax.ShapeDtypeStruct((4, 1, HALF), F32),
            shape(AUG), shape(AUG), shape(VAUG),
            jax.ShapeDtypeStruct((rows, width), BF16),
            jax.ShapeDtypeStruct((rows, width), F32),
            jax.ShapeDtypeStruct((4, steps // 4, sub * 3 // 2, 2 * HD), BF16),
        ],
        scratch_shapes=[
            pltpu.VMEM(frames.shape, BF16), pltpu.VMEM(qkv_weight.shape, BF16),
            pltpu.VMEM(up_weight.shape, BF16), pltpu.VMEM(down_flip.shape, BF16),
            pltpu.VMEM(out_flip.shape, BF16),
            pltpu.VMEM((steps, sub * 3 // 2, 2 * HD), BF16),
            pltpu.VMEM((piece, 3 * width), BF16), pltpu.VMEM((piece, lanes), BF16),
            pltpu.VMEM((1, HALF), F32),
            dma((7,)), dma((7,)), dma((5,)), dma((4,)), dma((4, 7)), dma((4, 7)), dma((3,)), dma((3,)),
            dma((steps,)), dma((steps,)), dma((4,)), dma((len(operands),)),
        ],
        compiler_params=pltpu.CompilerParams(
            collective_id=1, has_side_effects=True, vmem_limit_bytes=20 << 20
        ),
        name="front",
    )(*operands, up_bias, qkv_bias, seg_ids.reshape(1, rows))


def project_kernel(slots, x_ref, w_ref, b_ref, seg_ref, qs_ref, ka_ref, va_ref, kk_ref):
    made = jnp.dot(x_ref[...], w_ref[...], preferred_element_type=F32) + b_ref[...]
    marks = seg_ref[...] == lax.broadcasted_iota(jnp.int32, (x_ref.shape[0], MAX_SEGS), 1)
    spread_rows(
        made.astype(BF16), jnp.where(marks, 1.0, 0.0), slots, qs_ref, ka_ref, va_ref, kk_ref, slice(None)
    )


def project(frames, weight, offsets, seg_ids, slots):
    rows, depth = frames.shape
    block = min(512, rows)
    spread = lambda n: pl.BlockSpec((slots, block, n), lambda i: (0, i, 0))
    shape = lambda n: jax.ShapeDtypeStruct((slots, rows, n), BF16)
    return pl.pallas_call(
        functools.partial(project_kernel, slots),
        grid=(rows // block,),
        in_specs=[
            pl.BlockSpec((block, depth), lambda i: (i, 0)),
            pl.BlockSpec(weight.shape, lambda i: (0, 0)),
            pl.BlockSpec((1, offsets.shape[1]), lambda i: (0, 0)),
            pl.BlockSpec((block, 1), lambda i: (i, 0)),
        ],
        out_specs=[
            spread(AUG), spread(AUG), spread(VAUG), pl.BlockSpec((block, slots * HD), lambda i: (i, 0)),
        ],
        out_shape=[
            shape(AUG), shape(AUG), shape(VAUG), jax.ShapeDtypeStruct((rows, slots * HD), BF16),
        ],
        compiler_params=pltpu.CompilerParams(vmem_limit_bytes=VMEM_LIMIT),
        name="project",
    )(frames, weight, offsets, seg_ids.reshape(rows, 1))


def attend_kernel(sub, qs_ref, ka_ref, va_ref, qn_ref, mixed_ref):
    for at in range(0, qs_ref.shape[1], sub):
        part = slice(at, at + sub)
        x = lax.dot_general(qs_ref[0, part, :], ka_ref[0], NT, preferred_element_type=F32)
        top = jnp.max(x, -1, keepdims=True)
        p = jnp.exp2(x - top).astype(BF16)
        made = jnp.dot(p, va_ref[0], preferred_element_type=F32)
        total = -made[:, HD : HD + 1]
        mixed_ref[0, part, :] = made[:, :HD] / total
        one, two, three = thirds(top + jnp.log2(total))
        base = 3 * HD + MAX_SEGS
        blank = jnp.zeros((sub, AUG - base - 3), BF16)
        qn_ref[0, part, :] = jnp.concatenate(
            [qs_ref[0, part, :base], one, two, three, blank], 1
        )


def attend(qs, ka, va):
    slots, rows, _ = qs.shape
    block = min(512, rows)
    sub = min(256, block)
    whole = lambda n: pl.BlockSpec((1, rows, n), lambda h, i: (h, 0, 0))
    some = lambda n: pl.BlockSpec((1, block, n), lambda h, i: (h, i, 0))
    return pl.pallas_call(
        functools.partial(attend_kernel, sub),
        grid=(slots, rows // block),
        in_specs=[some(AUG), whole(AUG), whole(VAUG)],
        out_specs=[some(AUG), some(HD)],
        out_shape=[
            jax.ShapeDtypeStruct((slots, rows, AUG), BF16),
            jax.ShapeDtypeStruct((slots, rows, HD), F32),
        ],
        compiler_params=pltpu.CompilerParams(vmem_limit_bytes=VMEM_LIMIT),
        name="attend",
    )(qs, ka, va)


def attend_back_kernel(
    sub, qs_ref, ka_ref, va_ref, kk_ref, mixed_ref, up_ref, dq_ref, dk_ref, dv_ref, dk_acc, dv_acc
):
    step = pl.program_id(1)

    @pl.when(step == 0)
    def _():
        dk_acc[...] = jnp.zeros_like(dk_acc)
        dv_acc[...] = jnp.zeros_like(dv_acc)

    for at in range(0, qs_ref.shape[1], sub):
        part = slice(at, at + sub)
        q = qs_ref[0, part, :HD]
        up = up_ref[0, part, :]
        d_one, d_two, d_three = thirds(
            jnp.sum(up.astype(F32) * mixed_ref[0, part, :], -1, keepdims=True)
        )
        blank = lambda n: jnp.zeros((sub, n), BF16)
        upper = jnp.concatenate([up, d_one, d_two, d_three, blank(VAUG - HD - 3)], 1)
        x = lax.dot_general(qs_ref[0, part, :], ka_ref[0], NT, preferred_element_type=F32)
        p = jnp.exp2(x)
        dp = lax.dot_general(upper, va_ref[0], NT, preferred_element_type=F32)
        ds = (p * dp).astype(BF16)
        dv_acc[...] += lax.dot_general(up, p.astype(BF16), TN, preferred_element_type=F32)
        dk_acc[...] += lax.dot_general(q, ds, TN, preferred_element_type=F32)
        dq_ref[0, part, :] = (
            jnp.dot(ds, kk_ref[0], preferred_element_type=F32) * SCALE
        ).astype(BF16)

    @pl.when(step == pl.num_programs(1) - 1)
    def _():
        dk_ref[0] = (dk_acc[...] * SCALE).T.astype(BF16)
        dv_ref[0] = dv_acc[...].T.astype(BF16)


def attend_back(qs, ka, va, kk, mixed, up):
    slots, rows, _ = qs.shape
    block = min(512, rows)
    sub = min(256, block)
    whole = lambda n: pl.BlockSpec((1, rows, n), lambda h, i: (h, 0, 0))
    some = lambda n: pl.BlockSpec((1, block, n), lambda h, i: (h, i, 0))
    shape = jax.ShapeDtypeStruct((slots, rows, HD), BF16)
    return pl.pallas_call(
        functools.partial(attend_back_kernel, sub),
        grid=(slots, rows // block),
        in_specs=[
            some(AUG), whole(AUG), whole(VAUG), whole(HD), some(HD), some(HD),
        ],
        out_specs=[some(HD), whole(HD), whole(HD)],
        out_shape=[shape, shape, shape],
        scratch_shapes=[pltpu.VMEM((HD, rows), F32), pltpu.VMEM((HD, rows), F32)],
        compiler_params=pltpu.CompilerParams(vmem_limit_bytes=VMEM_LIMIT),
        name="attend_back",
    )(qs, ka, va, kk, mixed, up)


def norm_forward(summed):
    centre = summed - jnp.mean(summed, -1, keepdims=True)
    spread = jnp.mean(centre * centre, -1, keepdims=True)
    factor = lax.rsqrt(spread + EPS)
    return (centre * factor, factor)


def norm_backward(upper, normed, factor, gain):
    scaled = upper * gain
    return factor * (
        scaled
        - jnp.mean(scaled, -1, keepdims=True)
        - normed * jnp.mean(scaled * normed, -1, keepdims=True)
    )


def middle_kernel(
    groups, hidden_cols, block, linked,
    x_ref, y_ref, got_ref, w_ref, ub_ref, v0, v1, v2, v3, v4, v5,
    out_ref, s1_ref, back_ref, grad_ref, small_ref, *scratch,
):
    x_own, y_own, ow, act, pre_low, slope, hid_flip, two_flip, one_flip, here = scratch[:10]
    share = out_ref.shape[0]
    width = ow.shape[2]
    gap = HALF - hidden_cols
    dp = lax.axis_index("dp")
    mp = lax.axis_index("mp")
    rows = pl.ds(pl.multiple_of(mp * share, share), share)
    loads = [
        pltpu.make_async_copy(x_ref.at[rows], x_own, here.at[0]),
        pltpu.make_async_copy(y_ref.at[rows], y_own, here.at[1]),
    ]
    for copy in loads:
        copy.start()
    if linked:
        back_own, got, grads, arrived, b_send, b_recv, g_send, g_recv = scratch[10:]
        core = lax.rem(dp, 2)
        sibling = (dp ^ 1, mp)
        plane_barrier([sibling] + [(dp, mp ^ s) for s in range(1, 4)])
    else:
        back_own, got, grads = back_ref, got_ref, grad_ref
    out_bias, gain_one, shift_one, down_bias, gain_two, shift_two = (
        v[...].reshape(1, v.shape[0]) for v in (v0, v1, v2, v3, v4, v5)
    )
    for g in range(groups):
        ow[g, :, :gap] = w_ref[g, :, hidden_cols:HALF]
        ow[g, :, gap:] = w_ref[g, :, HALF + hidden_cols : HALF + hidden_cols + width - gap]
    small_ref[...] = jnp.zeros_like(small_ref)
    real = lane_marks(1, HALF, hidden_cols)
    alive = [
        lane_marks(1, width, HD * (HEADS // groups + (g < HEADS % groups))) for g in range(groups)
    ]
    for copy in loads:
        copy.wait()

    def send_back(step, s):
        at = step * 3 + s - 1
        return remote(
            back_own.at[mp ^ s, step], back_ref.at[mp, step], b_send.at[at], b_recv.at[at], (dp, mp ^ s)
        )

    def some_rows(step, carry):
        part = pl.ds(pl.multiple_of(step * block, block), block)
        summed = x_own[part, :].astype(F32) + out_bias
        for g in range(groups):
            if linked:
                got[g, part, :] = unpack_rows(got_ref[g, step])
            summed += lax.dot_general(got[g, part, :], ow[g], NT, preferred_element_type=F32)
        normed_one, factor_one = norm_forward(summed)
        hidden = normed_one * gain_one + shift_one
        hidden_low = hidden.astype(BF16)
        hid_flip[:, part] = hidden_low.T
        feed = hidden + down_bias
        dots = [
            jnp.dot(hidden_low, w_ref[g, :, :HALF], preferred_element_type=F32)
            for g in range(groups)
        ]
        for g in range(groups):
            pre = dots[g] + ub_ref[g]
            half = 0.5 + 0.5 * lax.erf(pre * math.sqrt(0.5))
            bell = jnp.exp(pre * pre * -0.5) * (pre * (1.0 / math.sqrt(2.0 * math.pi)))
            slope[g] = jnp.where(real, half + bell, 0.0)
            made = jnp.where(real, pre * half, 0.0).astype(BF16)
            act[g, part, :] = made
        for g in range(groups):
            feed += lax.dot_general(
                act[g, part, :], w_ref[g, :, HALF : 2 * HALF], NT, preferred_element_type=F32
            )
        normed_two, factor_two = norm_forward(feed)
        out_ref[part, :] = (normed_two * gain_two + shift_two).astype(BF16)
        upstream = y_own[part, :].astype(F32)
        two_grad = norm_backward(upstream, normed_two, factor_two, gain_two)
        sum_two = two_grad.astype(BF16)
        two_flip[:, part] = sum_two.T
        hidden_grad = two_grad
        dots = [
            jnp.dot(sum_two, w_ref[g, :, HALF : 2 * HALF], preferred_element_type=F32)
            for g in range(groups)
        ]
        for g in range(groups):
            low = (slope[g] * dots[g]).astype(BF16)
            pre_low[g, part, :] = low
            small_ref[8 + g : 9 + g, :] += jnp.sum(low.astype(F32), 0, keepdims=True)
        for g in range(groups):
            hidden_grad += lax.dot_general(
                pre_low[g, part, :], w_ref[g, :, :HALF], NT, preferred_element_type=F32
            )
        one_grad = norm_backward(hidden_grad, normed_one, factor_one, gain_one)
        sum_one = one_grad.astype(BF16)
        s1_ref[part, :] = one_grad
        one_flip[:, part] = sum_one.T
        for g in range(groups):
            made = jnp.dot(sum_one, ow[g], preferred_element_type=F32)
            made = jnp.where(alive[g], made, 0.0).astype(BF16)
            if linked:
                back_own[g, step] = pack_rows(made)
            else:
                back_own[g, part, :] = made
        if linked:
            for s in range(1, 4):
                send_back(step, s).start()
        for at, term in enumerate((
            sum_one.astype(F32), hidden_grad * normed_one, hidden_grad,
            sum_two.astype(F32), upstream * normed_two, upstream,
        )):
            small_ref[at : at + 1, :] += jnp.sum(term, 0, keepdims=True)
        return carry

    lax.fori_loop(0, share // block, some_rows, 0)
    if linked:
        keep = pltpu.make_async_copy(back_own.at[mp], back_ref.at[mp], here.at[2])
        keep.start()
    depth = hid_flip.shape[0]
    rest = width - gap
    spare = w_ref.shape[2] - HALF - hidden_cols - rest
    span = depth // 2
    shared = []
    for g in range(groups):
        for part in range(2):
            cols = slice(part * span, (part + 1) * span)
            made = jnp.dot(hid_flip[cols], pre_low[g], preferred_element_type=F32).astype(BF16)
            grad_out = jnp.dot(one_flip[cols], got[g], preferred_element_type=F32).astype(BF16)
            left = jnp.concatenate([made[:, :hidden_cols], grad_out[:, :gap]], 1)
            made = jnp.dot(two_flip[cols], act[g], preferred_element_type=F32).astype(BF16)
            right = jnp.concatenate(
                [made[:, :hidden_cols], grad_out[:, gap:], jnp.zeros((span, spare), BF16)], 1
            )
            if not linked:
                grads[g, cols, :HALF] = left
                grads[g, cols, HALF:] = right
                continue
            piece = grad_ref.shape[2]
            for i in range(span // piece):
                d = part * (span // piece) + i
                at = slice(i * piece, (i + 1) * piece)

                @pl.when(core == d % 2)
                def _():
                    grad_ref[g, d // 2, :, :HALF] = left[at]
                    grad_ref[g, d // 2, :, HALF:] = right[at]

                @pl.when(core != d % 2)
                def _():
                    grads[g, d // 2, :, :HALF] = left[at]
                    grads[g, d // 2, :, HALF:] = right[at]

        if linked:
            copy = remote(grads.at[g], arrived.at[g], g_send.at[g], g_recv.at[g], sibling)
            copy.start()
            shared.append(copy)
    if linked:
        for g in range(groups):
            shared[g].wait_recv()
            for c in range(4):
                grad_ref[g, c] += arrived[g, c]
        for step in range(share // block):
            for s in range(1, 4):
                send_back(step, s).wait()
        for copy in shared:
            copy.wait_send()
        keep.wait()


def middle(frames, cotangent, got, weights, up_bias, vectors, hidden_cols, linked):
    groups = got.shape[0]
    share, depth = frames.shape[0] // groups, frames.shape[1]
    lanes = weights.shape[2]
    width = 3 * HD
    block = min(256, share)
    vmem = pl.BlockSpec(memory_space=pltpu.VMEM)
    rest = pl.BlockSpec(memory_space=pltpu.MemorySpace.HBM)
    dma = pltpu.SemaphoreType.DMA
    scratch = [
        pltpu.VMEM((share, depth), BF16),
        pltpu.VMEM((share, depth), BF16),
        pltpu.VMEM((groups, depth, width), BF16),
        pltpu.VMEM((groups, share, HALF), BF16),
        pltpu.VMEM((groups, share, HALF), BF16),
        pltpu.VMEM((groups, block, HALF), F32),
        pltpu.VMEM((depth, share), BF16),
        pltpu.VMEM((depth, share), BF16),
        pltpu.VMEM((depth, share), BF16),
        dma((3,)),
    ]
    grads = jax.ShapeDtypeStruct(weights.shape, BF16)
    if linked:
        piece = depth // 8
        grads = jax.ShapeDtypeStruct((groups, 4, piece, lanes), BF16)
        sends = 3 * (share // block)
        scratch += [
            pltpu.VMEM(got.shape, BF16),
            pltpu.VMEM((groups, share, width), BF16),
            pltpu.VMEM((groups, 4, piece, lanes), BF16),
            pltpu.VMEM((groups, 4, piece, lanes), BF16),
            dma((sends,)), dma((sends,)), dma((groups,)), dma((groups,)),
        ]
    extra = dict(collective_id=2, has_side_effects=True) if linked else {}
    return pl.pallas_call(
        functools.partial(middle_kernel, groups, hidden_cols, block, linked),
        in_specs=[rest, rest] + [vmem] * 9,
        out_specs=[vmem] * 5,
        out_shape=[
            jax.ShapeDtypeStruct((share, depth), BF16),
            jax.ShapeDtypeStruct((share, depth), F32),
            jax.ShapeDtypeStruct(got.shape, BF16),
            grads,
            jax.ShapeDtypeStruct((16, HALF), F32),
        ],
        scratch_shapes=scratch,
        compiler_params=pltpu.CompilerParams(
            vmem_limit_bytes=33 << 20 if linked else VMEM_LIMIT, **extra
        ),
        name="middle",
    )(frames, cotangent, got, weights, up_bias, *vectors)


STEPS = (
    (3, 3, 0), (3, 0, 0), (3, 1, 0), (3, 2, 0), (3, 0, 1), (3, 1, 1), (3, 2, 1),
    (2, 2, 0), (2, 0, 0), (2, 1, 0), (2, 0, 1), (2, 1, 1), (1, 1, 0), (1, 0, 0), (1, 0, 1), (0, 0, 0),
)
ENDS = {3: (3, 0), 6: (3, 1), 9: (2, 0), 11: (2, 1), 13: (1, 0), 14: (1, 1)}


def pick(table, step):
    made = jnp.int32(table[0])
    for at in range(1, len(table)):
        made = jnp.where(step >= at, jnp.int32(table[at]), made)
    return made


def back_kernel(
    slots,
    qs_ref, ka_ref, va_ref, kk_ref, mixed_ref, up_ref, sums_ref, x_hbm, wq_ref, one_ref, small_ref,
    fg_ref, gq_ref, gb_ref, gup_ref, gdown_ref, gout_ref, gub_ref, s0, s1, s2, s3, s4, s5,
    upper, up_flip, q_flip, dq_acc, dk_acc, dv_acc, low, part_out, chain, fresh, far_in, near_in, third,
    fresh_in, gq_own, gq_in, gb_own, gb_in, tiny, tiny_in,
    c_send, c_recv, f_send, f_recv, n_send, n_recv, t_send, t_recv, q_send, q_recv, b_send, b_recv,
    s_send, s_recv, small_sum, x_ref, loaded, gq_acc,
):
    dp = lax.axis_index("dp")
    mp = lax.axis_index("mp")
    chip = dp // 2
    rows, depth = x_hbm.shape
    share = rows // 4
    width = slots * HD
    others = [(dp ^ d, mp) for d in range(1, 8)]
    tall = [(dp, mp ^ s) for s in range(1, 4)]
    plane_barrier(others + tall)
    x_peer, y_peer = (dp ^ 2, mp), (dp ^ 4, mp)

    def rows_of(name):
        return pl.ds(pl.multiple_of((mp ^ name) * share, share), share)

    half_rows = share // 2

    def half_of(name, half):
        start = (mp ^ name) * share + half * half_rows
        return pl.ds(pl.multiple_of(start, half_rows), half_rows)

    def load_rows(name, half):
        return pltpu.make_async_copy(x_hbm.at[half_of(name, half)], x_ref, loaded.at[0])

    load_rows(3, 0).start()

    def far(s):
        return remote(
            sums_ref.at[mp ^ s, chip ^ 3], far_in.at[s], f_send.at[s], f_recv.at[s],
            y_peer if s % 2 == 0 else x_peer,
        )

    def near(s, kind):
        toward_x = (s % 2 == 0) == (kind == 1)
        source = third.at[s] if kind == 1 else sums_ref.at[mp ^ s, chip ^ (1 if toward_x else 2)]
        return remote(
            source, near_in.at[s, kind], n_send.at[s, kind], n_recv.at[s, kind],
            x_peer if toward_x else y_peer,
        )

    def begin_far(s):
        far(s).start()

    def begin_near(s):
        near(s, 0).start()

    def join_far(s):
        far(s).wait_recv()
        third[s] = sums_ref[mp ^ s, chip ^ (1 if s % 2 == 0 else 2)] + far_in[s]
        near(s, 1).start()

    def join_near(s):
        near(s, 0).wait_recv()
        near(s, 1).wait_recv()
        total = sums_ref[mp ^ s, chip].astype(F32) + near_in[s, 0].astype(F32)
        fresh[s] = (total + near_in[s, 1].astype(F32)).astype(BF16)

    partners = [(dp ^ 1, mp), (dp ^ 2, mp), (dp ^ 4, mp), (dp, mp ^ 1), (dp, mp ^ 2)]

    def swap(at):
        return remote(tiny.at[at], tiny_in.at[at], s_send.at[at], s_recv.at[at], partners[at])

    def small_step(at):
        if at == 0:
            tiny[0] = small_ref[...]
        else:
            swap(at - 1).wait_recv()
            made = tiny[at - 1] + tiny_in[at - 1]
            if at == len(partners):
                small_sum[...] = made
                for row, ref in enumerate((s0, s1, s2, s3, s4, s5)):
                    ref[...] = made[row : row + 1, :].reshape(ref.shape)
                cols = gub_ref.shape[-1]
                gub_ref[...] = small_sum[pl.ds(8 + mp, 1), :cols].reshape(gub_ref.shape)
                return
            tiny[at] = made
        swap(at).start()

    def chain_copy(name, half, slot, target):
        at = pl.ds(half * half_rows, half_rows)
        return remote(
            part_out.at[name, at], chain.at[slot, at], c_send.at[name, half], c_recv.at[slot, half],
            (dp, target),
        )

    def fresh_copy(name, slot, target):
        return remote(
            fresh.at[name], fresh_in.at[slot], t_send.at[name], t_recv.at[slot], (dp, target)
        )

    inner = (mp == 1) | (mp == 2)

    def relay(name, half):
        block = mp ^ name
        at = pl.ds(half * half_rows, half_rows)

        @pl.when(inner)
        def _():
            chain_copy(name, half, block, mp ^ 1).wait_recv()
            part_out[name, at] = (
                part_out[name, at].astype(F32) + chain[block, at].astype(F32)
            ).astype(BF16)
            if half == 1:
                fresh_copy(name, block, mp ^ 1).wait_recv()
                fresh[name] = (fresh[name].astype(F32) + fresh_in[block].astype(F32)).astype(BF16)

        for leftward in (True, False):

            @pl.when((block < mp) == leftward)
            def _():
                target = mp - 1 if leftward else mp + 1
                slot = jnp.where(block == target, 4, block) if leftward else block
                chain_copy(name, half, slot, target).start()
                if half == 1:
                    fresh_copy(name, slot, target).start()

    def finish(name, half):
        at = half_of(name, half)
        for slot in range(slots):
            col = slot * HD
            low[:, col : col + HD] = (dq_acc[slot, at, :] * SCALE).astype(BF16)
            low[:, width + col : width + col + HD] = (dk_acc[slot, :, at] * SCALE).T.astype(BF16)
            low[:, 2 * width + col : 2 * width + col + HD] = dv_acc[slot, :, at].T.astype(BF16)
        part_out[name, half * half_rows : (half + 1) * half_rows] = lax.dot_general(
            low[...], wq_ref[...], NT, preferred_element_type=F32
        ).astype(BF16)

    def add_rows(name, half):
        ones = jnp.ones((16, half_rows), BF16)
        gb_own[...] += jnp.dot(ones, low[...], preferred_element_type=F32)[0:8, :]
        load_rows(name, half).wait()
        gq_acc[...] += lax.dot_general(x_ref[...], low[...], TN, preferred_element_type=F32)
        if (name, half) != (0, 1):
            load_rows(name - half, 1 - half).start()

    dq_acc[...] = jnp.zeros_like(dq_acc)
    dk_acc[...] = jnp.zeros_like(dk_acc)
    dv_acc[...] = jnp.zeros_like(dv_acc)
    gq_acc[...] = jnp.zeros_like(gq_acc)
    gb_own[...] = jnp.zeros_like(gb_own)
    far(3).start()
    far(2).start()
    small_step(0)

    def prepare(step, carry):
        at = pl.ds(pl.multiple_of(step * share, share), share)
        wide = jnp.concatenate([unpack_rows(up_ref[step, i]) for i in range(up_ref.shape[1])], 0)
        for slot in range(slots):
            up = wide[:, slot * HD : (slot + 1) * HD]
            one, two, three = thirds(
                jnp.sum(
                    up.astype(F32) * mixed_ref[at, slot * HD : (slot + 1) * HD], -1, keepdims=True
                )
            )
            blank = jnp.zeros((share, VAUG - HD - 3), BF16)
            upper[slot, at, :] = jnp.concatenate([up, one, two, three, blank], 1)
            up_flip[slot, :, at] = up.T
            q_flip[slot, :, at] = qs_ref[slot, at, :HD].T
        return carry

    lax.fori_loop(0, 4, prepare, 0)
    actions = {
        1: [(small_step, 1)],
        2: [(join_far, 3), (join_far, 2), (small_step, 2)],
        3: [(small_step, 3)],
        4: [(begin_near, 3), (begin_near, 2), (small_step, 4)],
        5: [(small_step, 5)],
        6: [(join_near, 3), (join_near, 2)],
        7: [(begin_far, 1), (begin_far, 0)],
        9: [(join_far, 1), (join_far, 0)],
        11: [(begin_near, 1), (begin_near, 0)],
        13: [(join_near, 1), (join_near, 0)],
    }

    def tiles(pairs):
        todo = [(slot, part, keys) for part, keys in pairs for slot in range(slots)]
        scores = [
            lax.dot_general(
                qs_ref[slot, part, :], ka_ref[slot, keys, :], NT, preferred_element_type=F32
            )
            for slot, part, keys in todo
        ]
        slopes = [
            lax.dot_general(
                upper[slot, part, :], va_ref[slot, keys, :], NT, preferred_element_type=F32
            )
            for slot, part, keys in todo
        ]
        probs = [jnp.exp2(x) for x in scores]
        lows = [(p * d).astype(BF16) for p, d in zip(probs, slopes)]
        for (slot, part, keys), p, ds in zip(todo, probs, lows):
            dv_acc[slot, :, keys] += jnp.dot(
                up_flip[slot, :, part], p.astype(BF16), preferred_element_type=F32
            )
            dk_acc[slot, :, keys] += jnp.dot(
                q_flip[slot, :, part], ds, preferred_element_type=F32
            )
            dq_acc[slot, part, :] += jnp.dot(
                ds, kk_ref[keys, slot * HD : (slot + 1) * HD], preferred_element_type=F32
            )

    def some_work(step, carry):
        name, other, half = (pick([s[i] for s in STEPS], step) for i in range(3))
        for when, todo in actions.items():

            @pl.when(step == when)
            def _():
                for act, s in todo:
                    act(s)

        @pl.when(name == other)
        def _():
            tiles([(rows_of(name), rows_of(name))])

        @pl.when(name != other)
        def _():
            tiles([(half_of(name, half), rows_of(other)), (rows_of(other), half_of(name, half))])

        for when, (n, h) in ENDS.items():

            @pl.when(step == when)
            def _():
                finish(n, h)
                if n == 3:

                    @pl.when(~inner)
                    def _():
                        relay(n, h)

                else:
                    relay(n, h)
                add_rows(n, h)

        @pl.when((step == 14) & inner)
        def _():
            relay(3, 0)

        return carry

    lax.fori_loop(0, len(STEPS), some_work, 0)
    for half in range(2):
        finish(0, half)
        add_rows(0, half)

    gb_in[dp] = gb_own[...]
    piece = depth // 8
    for d in range(8):
        gq_own[d] = gq_acc[d * piece : (d + 1) * piece, :].astype(BF16)
    q_copies = []
    for d in range(1, 8):
        to = dp ^ d
        q_copies.append(
            remote(gq_own.at[to], gq_in.at[d - 1], q_send.at[d - 1], q_recv.at[d - 1], others[d - 1])
        )
        q_copies.append(
            remote(gb_own, gb_in.at[dp], b_send.at[d - 1], b_recv.at[d - 1], others[d - 1])
        )
    for copy in q_copies:
        copy.start()
    @pl.when(inner)
    def _():
        relay(3, 1)

    for half in range(2):

        @pl.when(mp > 0)
        def _():
            chain_copy(0, half, mp, mp ^ 1).wait_recv()

        @pl.when(mp < 3)
        def _():
            chain_copy(0, half, 4, mp ^ 1).wait_recv()

    @pl.when(mp > 0)
    def _():
        fresh_copy(0, mp, mp ^ 1).wait_recv()

    @pl.when(mp < 3)
    def _():
        fresh_copy(0, 4, mp ^ 1).wait_recv()

    total = fresh[0].astype(F32)
    total = total + jnp.where(mp > 0, fresh_in[mp].astype(F32), 0.0)
    total = total + jnp.where(mp < 3, fresh_in[4].astype(F32), 0.0)
    cols = gup_ref.shape[1]
    gap = HALF - cols
    gup_ref[...] = total[:, :cols]
    gdown_ref[...] = total[:, HALF : HALF + cols]
    gout_ref[:, :gap] = total[:, cols:HALF]
    gout_ref[:, gap:] = total[:, HALF + cols : HALF + cols + width - gap]
    for copy in q_copies:
        copy.wait_recv()
    total = gq_own[dp].astype(F32)
    for d in range(7):
        total = total + gq_in[d].astype(F32)
    for i in range(3):
        gq_ref[i] = total[:, i * width : (i + 1) * width]
    total = gb_in[0]
    for d in range(1, 8):
        total = total + gb_in[d]
    gb_ref[0:1, :] = total[0:1, :width]
    gb_ref[1:2, :] = total[0:1, 2 * width :]

    wide = one_ref[...] + part_out[0].astype(F32)
    left = jnp.where(mp > 0, chain[mp].astype(F32), 0.0)
    right = jnp.where(mp < 3, chain[4].astype(F32), 0.0)
    fg_ref[...] = (wide + left + right).astype(BF16)
    for name in (1, 2, 3):
        for half in range(2):
            chain_copy(name, half, 0, mp ^ 1).wait_send()
        fresh_copy(name, 0, mp ^ 1).wait_send()
    for s in range(4):
        far(s).wait_send()
        near(s, 0).wait_send()
        near(s, 1).wait_send()
    for at in range(len(partners)):
        swap(at).wait_send()
    for copy in q_copies:
        copy.wait_send()


def back_pass(qs, ka, va, kk, mixed, up, sums, frames, wq, one_grad, small, hidden_cols):
    slots, rows, _ = qs.shape
    depth = frames.shape[1]
    share = rows // 4
    piece, lanes = sums.shape[2:]
    cols = wq.shape[1]
    vmem = pl.BlockSpec(memory_space=pltpu.VMEM)
    hbm = pl.BlockSpec(memory_space=pltpu.MemorySpace.HBM)
    dma = pltpu.SemaphoreType.DMA
    V = pltpu.VMEM
    return pl.pallas_call(
        functools.partial(back_kernel, slots),
        in_specs=[vmem] * 7 + [hbm] + [vmem] * 3,
        out_specs=[vmem] * 13,
        out_shape=[
            jax.ShapeDtypeStruct((share, depth), BF16),
            jax.ShapeDtypeStruct((3, piece, cols // 3), F32),
            jax.ShapeDtypeStruct((2, cols // 3), F32),
            jax.ShapeDtypeStruct((piece, hidden_cols), F32),
            jax.ShapeDtypeStruct((piece, hidden_cols), F32),
            jax.ShapeDtypeStruct((piece, cols // 3), F32),
            jax.ShapeDtypeStruct((hidden_cols,), F32),
        ]
        + [jax.ShapeDtypeStruct((depth,), F32)] * 6,
        scratch_shapes=[
            V((slots, rows, VAUG), BF16), V((slots, HD, rows), BF16), V((slots, HD, rows), BF16),
            V((slots, rows, HD), F32), V((slots, HD, rows), F32), V((slots, HD, rows), F32),
            V((share // 2, cols), BF16), V((4, share, depth), BF16), V((5, share, depth), BF16),
            V((4, piece, lanes), BF16), V((4, piece, lanes), BF16), V((4, 2, piece, lanes), BF16),
            V((4, piece, lanes), BF16), V((5, piece, lanes), BF16),
            V((8, piece, cols), BF16), V((7, piece, cols), BF16),
            V((8, cols), F32), V((8, 8, cols), F32), V((5,) + small.shape, F32), V((5,) + small.shape, F32),
            dma((4, 2)), dma((5, 2)), dma((4,)), dma((4,)), dma((4, 2)), dma((4, 2)), dma((4,)), dma((5,)),
            dma((7,)), dma((7,)), dma((7,)), dma((7,)), dma((5,)), dma((5,)), V(small.shape, F32),
            V((share // 2, depth), BF16), dma((1,)), V((depth, cols), F32),
        ],
        compiler_params=pltpu.CompilerParams(
            collective_id=3, has_side_effects=True, vmem_limit_bytes=34 << 20
        ),
        name="back_pass",
    )(qs, ka, va, kk, mixed, up, sums, frames, wq, one_grad, small)


def deliver_kernel(count, *refs):
    sources, results, sem = refs[:count], refs[count : 2 * count], refs[2 * count]
    copies = [
        pltpu.make_async_copy(a, b, sem.at[i]) for i, (a, b) in enumerate(zip(sources, results))
    ]
    for copy in copies:
        copy.start()
    for copy in copies:
        copy.wait()


def deliver(arrays):
    count = len(arrays)
    return pl.pallas_call(
        functools.partial(deliver_kernel, count),
        in_specs=[pl.BlockSpec(memory_space=pltpu.VMEM)] * count,
        out_specs=[pl.BlockSpec(memory_space=pltpu.MemorySpace.HBM)] * count,
        out_shape=[jax.ShapeDtypeStruct(a.shape, a.dtype) for a in arrays],
        scratch_shapes=[pltpu.SemaphoreType.DMA((count,))],
        compiler_params=pltpu.CompilerParams(vmem_limit_bytes=4 << 20),
        name="deliver",
    )(*arrays)


def body(
    frames, seg_ids, qkv_weight, qkv_bias, out_weight, out_bias, gain_one, shift_one,
    up_weight, up_bias, down_weight, down_bias, gain_two, shift_two, cotangent,
):
    rows, depth = frames.shape
    mp_size = lax.axis_size("mp")
    dp_size = lax.axis_size("dp")
    mp_index = lax.axis_index("mp")
    share = rows // mp_size
    slots = qkv_weight.shape[2] // HD
    width = slots * HD
    hidden_cols = up_weight.shape[1]
    piece = qkv_weight.shape[1]
    gap = HALF - hidden_cols
    spare = -(HALF + hidden_cols + width - gap) % 128
    live_count = HEADS // mp_size + (mp_index < HEADS % mp_size).astype(jnp.int32)
    live = (jnp.arange(slots) < live_count).astype(F32)

    in_hbm = lambda a: pltpu.with_memory_space_constraint(a, pltpu.MemorySpace.HBM)
    out_flip = out_weight.T
    down_flip = down_weight.T
    vectors = (out_bias, gain_one, shift_one, down_bias, gain_two, shift_two)
    linked = (dp_size, mp_size, slots, rows) == (8, 4, 3, 2048)
    if linked:
        weights, qkv_full, ub_full, qs, ka, va, kk, mixed, got = front(
            *map(in_hbm, (frames, qkv_weight, up_weight, down_flip, out_flip)), up_bias, qkv_bias,
            seg_ids, slots,
        )
        weights = weights.reshape(mp_size, depth, -1)
    else:
        wq = jnp.transpose(qkv_weight, (1, 0, 2)).reshape(piece, 3 * width)
        packed = jnp.concatenate(
            [up_weight, out_flip[:, :gap], down_flip, out_flip[:, gap:], jnp.zeros((piece, spare), BF16)], 1
        )
        ub_pad = jnp.pad(up_bias, (0, gap))[None]
        offsets = jnp.concatenate([qkv_bias[0], jnp.zeros_like(qkv_bias[0]), qkv_bias[1]])[None]
        qkv_full = lax.all_gather(wq, "dp", axis=0, tiled=True)
        weights = lax.all_gather(packed, "mp", axis=0, tiled=False)
        weights = lax.all_gather(weights, "dp", axis=1, tiled=True)
        ub_full = lax.all_gather(ub_pad, "mp", axis=0, tiled=False)
        qs, ka, va, kk = project(frames, qkv_full, offsets, seg_ids, slots)
        qs, mixed = attend(qs, ka, va)
        mixed_low = (mixed * live[:, None, None]).astype(BF16)
        sent = mixed_low.reshape(slots, mp_size, share, HD).transpose(1, 2, 0, 3)
        got = lax.all_to_all(sent.reshape(mp_size, share, width), "mp", 0, 0, tiled=True)
    output_frames, sum_one_grad, back, partial, small = middle(
        in_hbm(frames), in_hbm(cotangent), got, weights, ub_full, vectors, hidden_cols, linked
    )
    if linked:
        made = back_pass(
            qs, ka, va, kk, mixed, back, partial, in_hbm(frames), qkv_full, sum_one_grad, small, hidden_cols
        )
        output_frames, *made = deliver([output_frames, *made])
        return (
            output_frames, made[0], made[1], made[2], made[5].T, made[7], made[8], made[9], made[3],
            made[6], made[4].T, made[10], made[11], made[12],
        )
    if not linked:
        back = lax.all_to_all(back, "mp", 0, 0, tiled=True)
        back = back.reshape(rows, slots, HD).transpose(1, 0, 2)
        partial = lax.psum_scatter(partial, "dp", scatter_dimension=1, tiled=True)
        partial = lax.psum_scatter(partial, "mp", scatter_dimension=0, tiled=True)[0].astype(F32)
        small = lax.psum(small, ("dp", "mp"))
        kk = kk.reshape(rows, slots, HD).transpose(1, 0, 2)
        dq, dk, dv = attend_back(qs, ka, va, kk, mixed, back)
        grads_low = jnp.stack([dq, dk, dv]).transpose(2, 0, 1, 3).reshape(rows, 3 * width)
        bias_sums = lax.psum(jnp.sum(grads_low.astype(F32), 0), "dp")
        grad_qkv = jnp.einsum("rd,rs->ds", frames, grads_low, preferred_element_type=F32)
        arrived = lax.all_to_all(
            grad_qkv.astype(BF16).reshape(dp_size, piece, 3 * width), "dp", 0, 0, tiled=True
        )
        grad_qkv = arrived.astype(F32).sum(0)
        input_part = jnp.einsum("rs,ds->rd", grads_low, qkv_full, preferred_element_type=F32)
        input_sum = lax.psum_scatter(input_part.astype(BF16), "mp", scatter_dimension=0, tiled=True)
        frames_grad = (input_sum.astype(F32) + sum_one_grad).astype(BF16)
    grad_qkv = grad_qkv.reshape(piece, 3, width).transpose(1, 0, 2)
    bias_sums = bias_sums.reshape(3, width)
    qkv_bias_grad = jnp.stack([bias_sums[0], bias_sums[2]])
    out_grad = jnp.concatenate(
        [partial[:, hidden_cols:HALF], partial[:, HALF + hidden_cols : HALF + hidden_cols + width - gap]], 1
    )
    return (
        output_frames,
        frames_grad,
        grad_qkv,
        qkv_bias_grad,
        out_grad.T,
        small[0],
        small[1],
        small[2],
        partial[:, :hidden_cols],
        lax.dynamic_index_in_dim(small, 8 + mp_index, 0, False)[:hidden_cols],
        partial[:, HALF : HALF + hidden_cols].T,
        small[3],
        small[4],
        small[5],
    )


def solution(mesh):
    in_specs = (
        P("dp", None), P("dp"), P(None, "dp", "mp"), P(None, "mp"), P("mp", "dp"), P(), P(), P(),
        P("dp", "mp"), P("mp"), P("mp", "dp"), P(), P(), P(), P("dp", None),
    )
    out_specs = (
        P(("dp", "mp"), None), P(("dp", "mp"), None), P(None, "dp", "mp"), P(None, "mp"),
        P("mp", "dp"), P(), P(), P(), P("dp", "mp"), P("mp"), P("mp", "dp"), P(), P(), P(),
    )
    return jax.shard_map(body, mesh=mesh, in_specs=in_specs, out_specs=out_specs, check_vma=False)
```

```python
import functools
import math

import jax
import jax.numpy as jnp
from jax import lax
from jax.experimental import pallas as pl
from jax.experimental.pallas import tpu as pltpu
from jax.sharding import PartitionSpec as P

HEADS = 10
HD = 64
EPS = 1e-05
SCALE = 0.125
MAX_SEGS = 16
MASKED = -1e30
UNIT = SCALE * math.log2(math.e)
AUG = 256
VAUG = 128
NT = (((1,), (1,)), ((), ()))
TN = (((0,), (0,)), ((), ()))
F32 = jnp.float32
BF16 = jnp.bfloat16
VMEM_LIMIT = 56 << 20
MESH = pl.DeviceIdType.MESH
CHIPS = 3
HALF = 640


def thirds(wide):
    first = wide.astype(BF16)
    rest = wide - first.astype(F32)
    second = rest.astype(BF16)
    third = (rest - second.astype(F32)).astype(BF16)
    return first, second, third


def lane_marks(rows, width, count):
    return lax.broadcasted_iota(jnp.int32, (rows, width), 1) < count


def spread_rows(made, picked, slots, qs_ref, ka_ref, va_ref, kk_ref, rows):
    count = made.shape[0]
    width = slots * HD
    chosen = picked.astype(BF16)
    barred = ((picked - 1.0) * -MASKED).astype(BF16)
    tail = AUG - 3 * HD - MAX_SEGS
    q_tail = jnp.zeros((count, tail), BF16)
    minus = jnp.where(lane_marks(count, tail, 3), -1.0, 0.0).astype(BF16)
    v_tail = jnp.where(lane_marks(count, VAUG - HD, 3), -1.0, 0.0).astype(BF16)
    for slot in range(slots):
        at = slot * HD
        q = made[:, at : at + HD]
        k = made[:, width + at : width + at + HD]
        v = made[:, 2 * width + at : 2 * width + at + HD]
        one, two, three = thirds(k.astype(F32) * UNIT)
        qs_ref[slot, rows, :] = jnp.concatenate([q, q, q, chosen, q_tail], 1)
        ka_ref[slot, rows, :] = jnp.concatenate([one, two, three, barred, minus], 1)
        va_ref[slot, rows, :] = jnp.concatenate([v, v_tail], 1)
    kk_ref[rows, :] = made[:, width : 2 * width]


def plane_barrier(peers):
    barrier = pltpu.get_barrier_semaphore()
    for peer in peers:
        pl.semaphore_signal(barrier, inc=1, device_id=peer, device_id_type=MESH)
    pl.semaphore_wait(barrier, len(peers))


def remote(src, dst, send, recv, peer):
    return pltpu.make_async_remote_copy(
        src_ref=src, dst_ref=dst, send_sem=send, recv_sem=recv, device_id=peer, device_id_type=MESH
    )


def pack_rows(wide):
    half = wide.shape[0] // 2
    third = wide[:, 2 * HD :]
    return jnp.concatenate(
        [wide[:, : 2 * HD], jnp.concatenate([third[:half], third[half:]], 1)], 0
    )


def unpack_rows(packed):
    rows = packed.shape[0] * 2 // 3
    rest = packed[rows:]
    return jnp.concatenate(
        [packed[:rows], jnp.concatenate([rest[:, :HD], rest[:, HD:]], 0)], 1
    )


def front_kernel(
    slots, sub,
    x_hbm, qkv_hbm, up_hbm, down_hbm, out_hbm, ub_ref, qb_ref, seg_ref,
    all_ref, wfull_ref, ball_ref, qs_ref, ka_ref, va_ref, kk_ref, mixed_ref, got_ref,
    x_ref, qkv_ref, up_ref, down_ref, out_ref, stage, wq_ref, pack_ref, bias_ref,
    q_send, q_recv, z_send, z_recv, w_send, w_recv, b_send, b_recv, a_send, a_recv, here, loaded,
):
    dp = lax.axis_index("dp")
    mp = lax.axis_index("mp")
    plane = [dp ^ 2, dp ^ 4, dp ^ 6]
    sibling = (dp ^ 1, mp)
    tall = [(dp, mp ^ s) for s in range(1, 4)]
    inner = (mp == 1) | (mp == 2)
    width = slots * HD
    pairs = ((qkv_hbm, qkv_ref), (up_hbm, up_ref), (down_hbm, down_ref), (out_hbm, out_ref), (x_hbm, x_ref))
    loads = [pltpu.make_async_copy(a, b, loaded.at[i]) for i, (a, b) in enumerate(pairs)]
    for copy in loads:
        copy.start()
    bias_ref[...] = jnp.zeros_like(bias_ref)
    bias_ref[:, : up_hbm.shape[1]] = ub_ref[...].reshape(1, up_hbm.shape[1])
    for copy in loads[:4]:
        copy.wait()
    for i in range(3):
        wq_ref[:, i * width : (i + 1) * width] = qkv_ref[i]
    hidden_cols = up_ref.shape[1]
    gap = HALF - hidden_cols
    rest = width - gap
    pack_ref[:, :hidden_cols] = up_ref[...]
    pack_ref[:, hidden_cols:HALF] = out_ref[:, :gap]
    pack_ref[:, HALF : HALF + hidden_cols] = down_ref[...]
    pack_ref[:, HALF + hidden_cols : HALF + hidden_cols + rest] = out_ref[:, gap:]
    spare = pack_ref.shape[1] - HALF - hidden_cols - rest
    pack_ref[:, HALF + hidden_cols + rest :] = jnp.zeros((pack_ref.shape[0], spare), BF16)
    plane_barrier([sibling] + [(d, mp) for d in plane] + tall)
    rows = x_ref.shape[0]
    share = rows // 4

    piece = wq_ref.shape[0]

    def rows_of(d):
        return wfull_ref.at[pl.ds(pl.multiple_of(d * piece, piece), piece)]

    mine = pltpu.make_async_copy(wq_ref, rows_of(dp), here.at[0])
    mine.start()
    firsts = [
        remote(wq_ref, rows_of(dp), q_send.at[i], q_recv.at[i], (plane[i], mp))
        for i in range(CHIPS)
    ]
    for copy in firsts:
        copy.start()
    shared = [remote(wq_ref, rows_of(dp), q_send.at[3], q_recv.at[3], sibling)]
    shared[0].start()
    own = pltpu.make_async_copy(pack_ref, all_ref.at[mp, dp], here.at[1])
    own.start()
    def lift(at, s, landing, peer):
        ref = all_ref.at[mp ^ s, dp]
        return remote(pack_ref if s == 0 else ref, ref, z_send.at[at], z_recv.at[landing], peer)

    near, middle = tall[0], tall[2]
    lifts = [lift(0, 0, 1, near)]
    inner_lifts = [
        lift(1, 0, 3, middle), lift(2, 1, 2, middle), lift(3, 3, 2, near), lift(4, 2, 3, near),
    ]

    def arrive(s):
        lift(0, s, s, near).wait_recv()

    own_bias = pltpu.make_async_copy(bias_ref, ball_ref.at[mp], here.at[2])
    own_bias.start()
    lifts[0].start()

    @pl.when(inner)
    def _():
        inner_lifts[0].start()

    biases = [
        remote(bias_ref, ball_ref.at[mp], b_send.at[s], b_recv.at[s], tall[s]) for s in range(3)
    ]
    for copy in biases:
        copy.start()
    for i in range(CHIPS):
        firsts[i].wait_recv()
        passed = remote(
            rows_of(plane[i]), rows_of(plane[i]), q_send.at[4 + i], q_recv.at[4 + i], sibling
        )
        passed.start()
        shared.append(passed)
    own.wait()

    def weights(s, kind):
        group = mp ^ s
        block = {0: dp, 1: dp, 2: dp, 4: plane[0], 5: plane[1], 6: plane[2]}
        block[3] = plane[0] if s % 2 == 0 else plane[1]
        peer = {0: (plane[0], mp), 1: (plane[1], mp)}
        peer[3] = peer[1] if s % 2 == 0 else peer[0]
        ref = all_ref.at[group, block[kind]]
        return remote(ref, ref, w_send.at[s, kind], w_recv.at[s, kind], peer.get(kind, sibling))

    def start_weights(s):
        if s == 3:

            @pl.when(~inner)
            def _():
                arrive(3)

        for kind in (0, 1, 2):
            weights(s, kind).start()

    def pass_weights(s):
        weights(s, 0).wait_recv()
        weights(s, 1).wait_recv()
        for kind in (3, 4, 5):
            weights(s, kind).start()

    def last_weights(s):
        weights(s, 3).wait_recv()
        weights(s, 6).start()

    start_weights(0)
    mine.wait()
    for copy in shared:
        copy.wait_recv()
    arrive(1)

    @pl.when(inner)
    def _():
        inner_lifts[1].start()
        arrive(3)
        inner_lifts[2].start()

    start_weights(1)

    loads[4].wait()
    block = 512

    def project_rows(step, carry):
        part = pl.ds(pl.multiple_of(step * block, block), block)
        x = x_ref[part, :]
        offsets = jnp.concatenate(
            [qb_ref[0:1, :], jnp.zeros((1, width), F32), qb_ref[1:2, :]], 1
        )
        made = jnp.dot(x, wfull_ref[...], preferred_element_type=F32) + offsets
        marks = seg_ref[:, part] == lax.broadcasted_iota(jnp.int32, (MAX_SEGS, block), 0)
        picked = jnp.where(marks, 1.0, 0.0).T
        spread_rows(made.astype(BF16), picked, slots, qs_ref, ka_ref, va_ref, kk_ref, part)
        return carry

    lax.fori_loop(0, rows // block, project_rows, 0)
    arrive(2)

    @pl.when(inner)
    def _():
        inner_lifts[3].start()

    pass_weights(0)
    start_weights(2)

    live_count = HEADS // 4 + (mp < HEADS % 4).astype(jnp.int32)
    per_share = share // sub
    actions = {
        1: [(pass_weights, 1)],
        3: [(start_weights, 3)],
        4: [(last_weights, 0)],
        5: [(pass_weights, 2)],
        6: [(last_weights, 1)],
        7: [(pass_weights, 3)],
    }

    def send_rows(step, stage_index):
        return remote(
            stage.at[step], got_ref.at[mp, lax.rem(step, per_share)], a_send.at[step], a_recv.at[step],
            (dp, mp ^ stage_index),
        )

    def attend_rows(step, carry):
        stage_index = 3 - step // per_share
        group = mp ^ stage_index
        offset = lax.rem(step, per_share) * sub
        part = pl.ds(pl.multiple_of(group * share + offset, sub), sub)
        for when, todo in actions.items():

            @pl.when(step == when)
            def _():
                for act, s in todo:
                    act(s)

        kept = []
        scores = [
            lax.dot_general(qs_ref[slot, part, :], ka_ref[slot], NT, preferred_element_type=F32)
            for slot in range(slots)
        ]
        for slot in range(slots):
            x = scores[slot]
            top = jnp.max(x, -1, keepdims=True)
            p = jnp.exp2(x - top).astype(BF16)
            made = jnp.dot(p, va_ref[slot], preferred_element_type=F32)
            total = -made[:, HD : HD + 1]
            mixed = made[:, :HD] / total
            one, two, three = thirds(top + jnp.log2(total))
            base = 3 * HD + MAX_SEGS
            qs_ref[slot, part, base : base + 3] = jnp.concatenate([one, two, three], 1)
            mixed_ref[part, slot * HD : (slot + 1) * HD] = mixed
            alive = (slot < live_count).astype(F32)
            kept.append((mixed * alive).astype(BF16))
        stage[step] = pack_rows(jnp.concatenate(kept, 1))

        @pl.when(step < 3 * per_share)
        def _():
            send_rows(step, stage_index).start()

        return carry

    lax.fori_loop(0, rows // sub, attend_rows, 0)
    keep = pltpu.make_async_copy(
        stage.at[pl.ds(3 * per_share, per_share)], got_ref.at[mp], here.at[3]
    )
    keep.start()
    last_weights(2)
    last_weights(3)
    for s in range(4):
        weights(s, 2).wait_recv()
        for kind in (4, 5, 6):
            weights(s, kind).wait_recv()
        for kind in range(7):
            weights(s, kind).wait_send()
    for copy in firsts + shared + lifts:
        copy.wait_send()

    @pl.when(inner)
    def _():
        for copy in inner_lifts:
            copy.wait_send()

    for copy in biases:
        copy.wait()
    for step in range(3 * per_share):
        send_rows(step, 3 - step // per_share).wait()
    own_bias.wait()
    keep.wait()


def front(frames, qkv_weight, up_weight, down_flip, out_flip, up_bias, qkv_bias, seg_ids, slots):
    rows, depth = frames.shape
    piece, hidden_cols = up_weight.shape
    width = slots * HD
    lanes = -(-(2 * hidden_cols + width) // 128) * 128
    sub = 256
    shape = lambda n: jax.ShapeDtypeStruct((slots, rows, n), BF16)
    vmem = pl.BlockSpec(memory_space=pltpu.VMEM)
    hbm = pl.BlockSpec(memory_space=pltpu.MemorySpace.HBM)
    dma = pltpu.SemaphoreType.DMA
    steps = rows // sub
    operands = (frames, qkv_weight, up_weight, down_flip, out_flip)
    return pl.pallas_call(
        functools.partial(front_kernel, slots, sub),
        in_specs=[hbm] * 5 + [vmem] * 3,
        out_specs=[vmem] * 9,
        out_shape=[
            jax.ShapeDtypeStruct((4, 8, piece, lanes), BF16),
            jax.ShapeDtypeStruct((8 * piece, 3 * width), BF16),
            jax.ShapeDtypeStruct((4, 1, HALF), F32),
            shape(AUG), shape(AUG), shape(VAUG),
            jax.ShapeDtypeStruct((rows, width), BF16),
            jax.ShapeDtypeStruct((rows, width), F32),
            jax.ShapeDtypeStruct((4, steps // 4, sub * 3 // 2, 2 * HD), BF16),
        ],
        scratch_shapes=[
            pltpu.VMEM(frames.shape, BF16), pltpu.VMEM(qkv_weight.shape, BF16),
            pltpu.VMEM(up_weight.shape, BF16), pltpu.VMEM(down_flip.shape, BF16),
            pltpu.VMEM(out_flip.shape, BF16),
            pltpu.VMEM((steps, sub * 3 // 2, 2 * HD), BF16),
            pltpu.VMEM((piece, 3 * width), BF16), pltpu.VMEM((piece, lanes), BF16),
            pltpu.VMEM((1, HALF), F32),
            dma((7,)), dma((7,)), dma((5,)), dma((4,)), dma((4, 7)), dma((4, 7)), dma((3,)), dma((3,)),
            dma((steps,)), dma((steps,)), dma((4,)), dma((len(operands),)),
        ],
        compiler_params=pltpu.CompilerParams(
            collective_id=1, has_side_effects=True, vmem_limit_bytes=20 << 20
        ),
        name="front",
    )(*operands, up_bias, qkv_bias, seg_ids.reshape(1, rows))


def project_kernel(slots, x_ref, w_ref, b_ref, seg_ref, qs_ref, ka_ref, va_ref, kk_ref):
    made = jnp.dot(x_ref[...], w_ref[...], preferred_element_type=F32) + b_ref[...]
    marks = seg_ref[...] == lax.broadcasted_iota(jnp.int32, (x_ref.shape[0], MAX_SEGS), 1)
    spread_rows(
        made.astype(BF16), jnp.where(marks, 1.0, 0.0), slots, qs_ref, ka_ref, va_ref, kk_ref, slice(None)
    )


def project(frames, weight, offsets, seg_ids, slots):
    rows, depth = frames.shape
    block = min(512, rows)
    spread = lambda n: pl.BlockSpec((slots, block, n), lambda i: (0, i, 0))
    shape = lambda n: jax.ShapeDtypeStruct((slots, rows, n), BF16)
    return pl.pallas_call(
        functools.partial(project_kernel, slots),
        grid=(rows // block,),
        in_specs=[
            pl.BlockSpec((block, depth), lambda i: (i, 0)),
            pl.BlockSpec(weight.shape, lambda i: (0, 0)),
            pl.BlockSpec((1, offsets.shape[1]), lambda i: (0, 0)),
            pl.BlockSpec((block, 1), lambda i: (i, 0)),
        ],
        out_specs=[
            spread(AUG), spread(AUG), spread(VAUG), pl.BlockSpec((block, slots * HD), lambda i: (i, 0)),
        ],
        out_shape=[
            shape(AUG), shape(AUG), shape(VAUG), jax.ShapeDtypeStruct((rows, slots * HD), BF16),
        ],
        compiler_params=pltpu.CompilerParams(vmem_limit_bytes=VMEM_LIMIT),
        name="project",
    )(frames, weight, offsets, seg_ids.reshape(rows, 1))


def attend_kernel(sub, qs_ref, ka_ref, va_ref, qn_ref, mixed_ref):
    for at in range(0, qs_ref.shape[1], sub):
        part = slice(at, at + sub)
        x = lax.dot_general(qs_ref[0, part, :], ka_ref[0], NT, preferred_element_type=F32)
        top = jnp.max(x, -1, keepdims=True)
        p = jnp.exp2(x - top).astype(BF16)
        made = jnp.dot(p, va_ref[0], preferred_element_type=F32)
        total = -made[:, HD : HD + 1]
        mixed_ref[0, part, :] = made[:, :HD] / total
        one, two, three = thirds(top + jnp.log2(total))
        base = 3 * HD + MAX_SEGS
        blank = jnp.zeros((sub, AUG - base - 3), BF16)
        qn_ref[0, part, :] = jnp.concatenate(
            [qs_ref[0, part, :base], one, two, three, blank], 1
        )


def attend(qs, ka, va):
    slots, rows, _ = qs.shape
    block = min(512, rows)
    sub = min(256, block)
    whole = lambda n: pl.BlockSpec((1, rows, n), lambda h, i: (h, 0, 0))
    some = lambda n: pl.BlockSpec((1, block, n), lambda h, i: (h, i, 0))
    return pl.pallas_call(
        functools.partial(attend_kernel, sub),
        grid=(slots, rows // block),
        in_specs=[some(AUG), whole(AUG), whole(VAUG)],
        out_specs=[some(AUG), some(HD)],
        out_shape=[
            jax.ShapeDtypeStruct((slots, rows, AUG), BF16),
            jax.ShapeDtypeStruct((slots, rows, HD), F32),
        ],
        compiler_params=pltpu.CompilerParams(vmem_limit_bytes=VMEM_LIMIT),
        name="attend",
    )(qs, ka, va)


def attend_back_kernel(
    sub, qs_ref, ka_ref, va_ref, kk_ref, mixed_ref, up_ref, dq_ref, dk_ref, dv_ref, dk_acc, dv_acc
):
    step = pl.program_id(1)

    @pl.when(step == 0)
    def _():
        dk_acc[...] = jnp.zeros_like(dk_acc)
        dv_acc[...] = jnp.zeros_like(dv_acc)

    for at in range(0, qs_ref.shape[1], sub):
        part = slice(at, at + sub)
        q = qs_ref[0, part, :HD]
        up = up_ref[0, part, :]
        d_one, d_two, d_three = thirds(
            jnp.sum(up.astype(F32) * mixed_ref[0, part, :], -1, keepdims=True)
        )
        blank = lambda n: jnp.zeros((sub, n), BF16)
        upper = jnp.concatenate([up, d_one, d_two, d_three, blank(VAUG - HD - 3)], 1)
        x = lax.dot_general(qs_ref[0, part, :], ka_ref[0], NT, preferred_element_type=F32)
        p = jnp.exp2(x)
        dp = lax.dot_general(upper, va_ref[0], NT, preferred_element_type=F32)
        ds = (p * dp).astype(BF16)
        dv_acc[...] += lax.dot_general(up, p.astype(BF16), TN, preferred_element_type=F32)
        dk_acc[...] += lax.dot_general(q, ds, TN, preferred_element_type=F32)
        dq_ref[0, part, :] = (
            jnp.dot(ds, kk_ref[0], preferred_element_type=F32) * SCALE
        ).astype(BF16)

    @pl.when(step == pl.num_programs(1) - 1)
    def _():
        dk_ref[0] = (dk_acc[...] * SCALE).T.astype(BF16)
        dv_ref[0] = dv_acc[...].T.astype(BF16)


def attend_back(qs, ka, va, kk, mixed, up):
    slots, rows, _ = qs.shape
    block = min(512, rows)
    sub = min(256, block)
    whole = lambda n: pl.BlockSpec((1, rows, n), lambda h, i: (h, 0, 0))
    some = lambda n: pl.BlockSpec((1, block, n), lambda h, i: (h, i, 0))
    shape = jax.ShapeDtypeStruct((slots, rows, HD), BF16)
    return pl.pallas_call(
        functools.partial(attend_back_kernel, sub),
        grid=(slots, rows // block),
        in_specs=[
            some(AUG), whole(AUG), whole(VAUG), whole(HD), some(HD), some(HD),
        ],
        out_specs=[some(HD), whole(HD), whole(HD)],
        out_shape=[shape, shape, shape],
        scratch_shapes=[pltpu.VMEM((HD, rows), F32), pltpu.VMEM((HD, rows), F32)],
        compiler_params=pltpu.CompilerParams(vmem_limit_bytes=VMEM_LIMIT),
        name="attend_back",
    )(qs, ka, va, kk, mixed, up)


def norm_forward(summed):
    centre = summed - jnp.mean(summed, -1, keepdims=True)
    spread = jnp.mean(centre * centre, -1, keepdims=True)
    factor = lax.rsqrt(spread + EPS)
    return (centre * factor, factor)


def norm_backward(upper, normed, factor, gain):
    scaled = upper * gain
    return factor * (
        scaled
        - jnp.mean(scaled, -1, keepdims=True)
        - normed * jnp.mean(scaled * normed, -1, keepdims=True)
    )


def middle_kernel(
    groups, hidden_cols, block, linked,
    x_ref, y_ref, got_ref, w_ref, ub_ref, v0, v1, v2, v3, v4, v5,
    out_ref, s1_ref, back_ref, grad_ref, small_ref, *scratch,
):
    x_own, y_own, ow, act, pre_low, slope, hid_flip, two_flip, one_flip, here = scratch[:10]
    share = out_ref.shape[0]
    width = ow.shape[2]
    gap = HALF - hidden_cols
    dp = lax.axis_index("dp")
    mp = lax.axis_index("mp")
    rows = pl.ds(pl.multiple_of(mp * share, share), share)
    loads = [
        pltpu.make_async_copy(x_ref.at[rows], x_own, here.at[0]),
        pltpu.make_async_copy(y_ref.at[rows], y_own, here.at[1]),
    ]
    for copy in loads:
        copy.start()
    if linked:
        back_own, got, grads, arrived, b_send, b_recv, g_send, g_recv = scratch[10:]
        core = lax.rem(dp, 2)
        sibling = (dp ^ 1, mp)
        plane_barrier([sibling] + [(dp, mp ^ s) for s in range(1, 4)])
    else:
        back_own, got, grads = back_ref, got_ref, grad_ref
    out_bias, gain_one, shift_one, down_bias, gain_two, shift_two = (
        v[...].reshape(1, v.shape[0]) for v in (v0, v1, v2, v3, v4, v5)
    )
    for g in range(groups):
        ow[g, :, :gap] = w_ref[g, :, hidden_cols:HALF]
        ow[g, :, gap:] = w_ref[g, :, HALF + hidden_cols : HALF + hidden_cols + width - gap]
    small_ref[...] = jnp.zeros_like(small_ref)
    real = lane_marks(1, HALF, hidden_cols)
    alive = [
        lane_marks(1, width, HD * (HEADS // groups + (g < HEADS % groups))) for g in range(groups)
    ]
    for copy in loads:
        copy.wait()

    def send_back(step, s):
        at = step * 3 + s - 1
        return remote(
            back_own.at[mp ^ s, step], back_ref.at[mp, step], b_send.at[at], b_recv.at[at], (dp, mp ^ s)
        )

    def some_rows(step, carry):
        part = pl.ds(pl.multiple_of(step * block, block), block)
        summed = x_own[part, :].astype(F32) + out_bias
        for g in range(groups):
            if linked:
                got[g, part, :] = unpack_rows(got_ref[g, step])
            summed += lax.dot_general(got[g, part, :], ow[g], NT, preferred_element_type=F32)
        normed_one, factor_one = norm_forward(summed)
        hidden = normed_one * gain_one + shift_one
        hidden_low = hidden.astype(BF16)
        hid_flip[:, part] = hidden_low.T
        feed = hidden + down_bias
        dots = [
            jnp.dot(hidden_low, w_ref[g, :, :HALF], preferred_element_type=F32)
            for g in range(groups)
        ]
        for g in range(groups):
            pre = dots[g] + ub_ref[g]
            half = 0.5 + 0.5 * lax.erf(pre * math.sqrt(0.5))
            bell = jnp.exp(pre * pre * -0.5) * (pre * (1.0 / math.sqrt(2.0 * math.pi)))
            slope[g] = jnp.where(real, half + bell, 0.0)
            made = jnp.where(real, pre * half, 0.0).astype(BF16)
            act[g, part, :] = made
        for g in range(groups):
            feed += lax.dot_general(
                act[g, part, :], w_ref[g, :, HALF : 2 * HALF], NT, preferred_element_type=F32
            )
        normed_two, factor_two = norm_forward(feed)
        out_ref[part, :] = (normed_two * gain_two + shift_two).astype(BF16)
        upstream = y_own[part, :].astype(F32)
        two_grad = norm_backward(upstream, normed_two, factor_two, gain_two)
        sum_two = two_grad.astype(BF16)
        two_flip[:, part] = sum_two.T
        hidden_grad = two_grad
        dots = [
            jnp.dot(sum_two, w_ref[g, :, HALF : 2 * HALF], preferred_element_type=F32)
            for g in range(groups)
        ]
        for g in range(groups):
            low = (slope[g] * dots[g]).astype(BF16)
            pre_low[g, part, :] = low
            small_ref[8 + g : 9 + g, :] += jnp.sum(low.astype(F32), 0, keepdims=True)
        for g in range(groups):
            hidden_grad += lax.dot_general(
                pre_low[g, part, :], w_ref[g, :, :HALF], NT, preferred_element_type=F32
            )
        one_grad = norm_backward(hidden_grad, normed_one, factor_one, gain_one)
        sum_one = one_grad.astype(BF16)
        s1_ref[part, :] = one_grad
        one_flip[:, part] = sum_one.T
        for g in range(groups):
            made = jnp.dot(sum_one, ow[g], preferred_element_type=F32)
            made = jnp.where(alive[g], made, 0.0).astype(BF16)
            if linked:
                back_own[g, step] = pack_rows(made)
            else:
                back_own[g, part, :] = made
        if linked:
            for s in range(1, 4):
                send_back(step, s).start()
        for at, term in enumerate((
            sum_one.astype(F32), hidden_grad * normed_one, hidden_grad,
            sum_two.astype(F32), upstream * normed_two, upstream,
        )):
            small_ref[at : at + 1, :] += jnp.sum(term, 0, keepdims=True)
        return carry

    lax.fori_loop(0, share // block, some_rows, 0)
    if linked:
        keep = pltpu.make_async_copy(back_own.at[mp], back_ref.at[mp], here.at[2])
        keep.start()
    depth = hid_flip.shape[0]
    rest = width - gap
    spare = w_ref.shape[2] - HALF - hidden_cols - rest
    span = depth // 2
    shared = []
    for g in range(groups):
        for part in range(2):
            cols = slice(part * span, (part + 1) * span)
            made = jnp.dot(hid_flip[cols], pre_low[g], preferred_element_type=F32).astype(BF16)
            grad_out = jnp.dot(one_flip[cols], got[g], preferred_element_type=F32).astype(BF16)
            left = jnp.concatenate([made[:, :hidden_cols], grad_out[:, :gap]], 1)
            made = jnp.dot(two_flip[cols], act[g], preferred_element_type=F32).astype(BF16)
            right = jnp.concatenate(
                [made[:, :hidden_cols], grad_out[:, gap:], jnp.zeros((span, spare), BF16)], 1
            )
            if not linked:
                grads[g, cols, :HALF] = left
                grads[g, cols, HALF:] = right
                continue
            piece = grad_ref.shape[2]
            for i in range(span // piece):
                d = part * (span // piece) + i
                at = slice(i * piece, (i + 1) * piece)

                @pl.when(core == d % 2)
                def _():
                    grad_ref[g, d // 2, :, :HALF] = left[at]
                    grad_ref[g, d // 2, :, HALF:] = right[at]

                @pl.when(core != d % 2)
                def _():
                    grads[g, d // 2, :, :HALF] = left[at]
                    grads[g, d // 2, :, HALF:] = right[at]

        if linked:
            copy = remote(grads.at[g], arrived.at[g], g_send.at[g], g_recv.at[g], sibling)
            copy.start()
            shared.append(copy)
    if linked:
        for g in range(groups):
            shared[g].wait_recv()
            for c in range(4):
                grad_ref[g, c] += arrived[g, c]
        for step in range(share // block):
            for s in range(1, 4):
                send_back(step, s).wait()
        for copy in shared:
            copy.wait_send()
        keep.wait()


def middle(frames, cotangent, got, weights, up_bias, vectors, hidden_cols, linked):
    groups = got.shape[0]
    share, depth = frames.shape[0] // groups, frames.shape[1]
    lanes = weights.shape[2]
    width = 3 * HD
    block = min(256, share)
    vmem = pl.BlockSpec(memory_space=pltpu.VMEM)
    rest = pl.BlockSpec(memory_space=pltpu.MemorySpace.HBM)
    dma = pltpu.SemaphoreType.DMA
    scratch = [
        pltpu.VMEM((share, depth), BF16),
        pltpu.VMEM((share, depth), BF16),
        pltpu.VMEM((groups, depth, width), BF16),
        pltpu.VMEM((groups, share, HALF), BF16),
        pltpu.VMEM((groups, share, HALF), BF16),
        pltpu.VMEM((groups, block, HALF), F32),
        pltpu.VMEM((depth, share), BF16),
        pltpu.VMEM((depth, share), BF16),
        pltpu.VMEM((depth, share), BF16),
        dma((3,)),
    ]
    grads = jax.ShapeDtypeStruct(weights.shape, BF16)
    if linked:
        piece = depth // 8
        grads = jax.ShapeDtypeStruct((groups, 4, piece, lanes), BF16)
        sends = 3 * (share // block)
        scratch += [
            pltpu.VMEM(got.shape, BF16),
            pltpu.VMEM((groups, share, width), BF16),
            pltpu.VMEM((groups, 4, piece, lanes), BF16),
            pltpu.VMEM((groups, 4, piece, lanes), BF16),
            dma((sends,)), dma((sends,)), dma((groups,)), dma((groups,)),
        ]
    extra = dict(collective_id=2, has_side_effects=True) if linked else {}
    return pl.pallas_call(
        functools.partial(middle_kernel, groups, hidden_cols, block, linked),
        in_specs=[rest, rest] + [vmem] * 9,
        out_specs=[vmem] * 5,
        out_shape=[
            jax.ShapeDtypeStruct((share, depth), BF16),
            jax.ShapeDtypeStruct((share, depth), F32),
            jax.ShapeDtypeStruct(got.shape, BF16),
            grads,
            jax.ShapeDtypeStruct((16, HALF), F32),
        ],
        scratch_shapes=scratch,
        compiler_params=pltpu.CompilerParams(
            vmem_limit_bytes=33 << 20 if linked else VMEM_LIMIT, **extra
        ),
        name="middle",
    )(frames, cotangent, got, weights, up_bias, *vectors)


STEPS = (
    (3, 3, 0), (3, 0, 0), (3, 1, 0), (3, 2, 0), (3, 0, 1), (3, 1, 1), (3, 2, 1),
    (2, 2, 0), (2, 0, 0), (2, 1, 0), (2, 0, 1), (2, 1, 1), (1, 1, 0), (1, 0, 0), (1, 0, 1), (0, 0, 0),
)
ENDS = {3: (3, 0), 6: (3, 1), 9: (2, 0), 11: (2, 1), 13: (1, 0), 14: (1, 1)}


def pick(table, step):
    made = jnp.int32(table[0])
    for at in range(1, len(table)):
        made = jnp.where(step >= at, jnp.int32(table[at]), made)
    return made


def back_kernel(
    slots,
    qs_ref, ka_ref, va_ref, kk_ref, mixed_ref, up_ref, sums_ref, x_hbm, wq_ref, one_ref, small_ref,
    fg_ref, gq_ref, gb_ref, gup_ref, gdown_ref, gout_ref, gub_ref, s0, s1, s2, s3, s4, s5,
    upper, up_flip, q_flip, dq_acc, dk_acc, dv_acc, low, part_out, chain, fresh, far_in, near_in, third,
    fresh_in, gq_own, gq_in, gb_own, gb_in, tiny, tiny_in,
    c_send, c_recv, f_send, f_recv, n_send, n_recv, t_send, t_recv, q_send, q_recv, b_send, b_recv,
    s_send, s_recv, small_sum, x_ref, loaded, gq_acc,
):
    dp = lax.axis_index("dp")
    mp = lax.axis_index("mp")
    chip = dp // 2
    rows, depth = x_hbm.shape
    share = rows // 4
    width = slots * HD
    others = [(dp ^ d, mp) for d in range(1, 8)]
    tall = [(dp, mp ^ s) for s in range(1, 4)]
    plane_barrier(others + tall)
    x_peer, y_peer = (dp ^ 2, mp), (dp ^ 4, mp)

    def rows_of(name):
        return pl.ds(pl.multiple_of((mp ^ name) * share, share), share)

    half_rows = share // 2

    def half_of(name, half):
        start = (mp ^ name) * share + half * half_rows
        return pl.ds(pl.multiple_of(start, half_rows), half_rows)

    def load_rows(name, half):
        return pltpu.make_async_copy(x_hbm.at[half_of(name, half)], x_ref, loaded.at[0])

    load_rows(3, 0).start()

    def far(s):
        return remote(
            sums_ref.at[mp ^ s, chip ^ 3], far_in.at[s], f_send.at[s], f_recv.at[s],
            y_peer if s % 2 == 0 else x_peer,
        )

    def near(s, kind):
        toward_x = (s % 2 == 0) == (kind == 1)
        source = third.at[s] if kind == 1 else sums_ref.at[mp ^ s, chip ^ (1 if toward_x else 2)]
        return remote(
            source, near_in.at[s, kind], n_send.at[s, kind], n_recv.at[s, kind],
            x_peer if toward_x else y_peer,
        )

    def begin_far(s):
        far(s).start()

    def begin_near(s):
        near(s, 0).start()

    def join_far(s):
        far(s).wait_recv()
        third[s] = sums_ref[mp ^ s, chip ^ (1 if s % 2 == 0 else 2)] + far_in[s]
        near(s, 1).start()

    def join_near(s):
        near(s, 0).wait_recv()
        near(s, 1).wait_recv()
        total = sums_ref[mp ^ s, chip].astype(F32) + near_in[s, 0].astype(F32)
        fresh[s] = (total + near_in[s, 1].astype(F32)).astype(BF16)

    partners = [(dp ^ 1, mp), (dp ^ 2, mp), (dp ^ 4, mp), (dp, mp ^ 1), (dp, mp ^ 2)]

    def swap(at):
        return remote(tiny.at[at], tiny_in.at[at], s_send.at[at], s_recv.at[at], partners[at])

    def small_step(at):
        if at == 0:
            tiny[0] = small_ref[...]
        else:
            swap(at - 1).wait_recv()
            made = tiny[at - 1] + tiny_in[at - 1]
            if at == len(partners):
                small_sum[...] = made
                for row, ref in enumerate((s0, s1, s2, s3, s4, s5)):
                    ref[...] = made[row : row + 1, :].reshape(ref.shape)
                cols = gub_ref.shape[-1]
                gub_ref[...] = small_sum[pl.ds(8 + mp, 1), :cols].reshape(gub_ref.shape)
                return
            tiny[at] = made
        swap(at).start()

    def chain_copy(name, half, slot, target):
        at = pl.ds(half * half_rows, half_rows)
        return remote(
            part_out.at[name, at], chain.at[slot, at], c_send.at[name, half], c_recv.at[slot, half],
            (dp, target),
        )

    def fresh_copy(name, slot, target):
        return remote(
            fresh.at[name], fresh_in.at[slot], t_send.at[name], t_recv.at[slot], (dp, target)
        )

    inner = (mp == 1) | (mp == 2)

    def down_the_chain(block, copy):
        for leftward in (True, False):

            @pl.when((block < mp) == leftward)
            def _():
                target = mp - 1 if leftward else mp + 1
                copy(jnp.where(block == target, 4, block) if leftward else block, target).start()

    def relay(name, half):
        block = mp ^ name
        at = pl.ds(half * half_rows, half_rows)

        @pl.when(inner)
        def _():
            chain_copy(name, half, block, mp ^ 1).wait_recv()
            part_out[name, at] = (
                part_out[name, at].astype(F32) + chain[block, at].astype(F32)
            ).astype(BF16)

        down_the_chain(block, functools.partial(chain_copy, name, half))

    def relay_fresh(name):
        block = mp ^ name

        @pl.when(inner)
        def _():
            fresh_copy(name, block, mp ^ 1).wait_recv()
            fresh[name] = (fresh[name].astype(F32) + fresh_in[block].astype(F32)).astype(BF16)

        down_the_chain(block, functools.partial(fresh_copy, name))

    def end_fresh(name):
        @pl.when(~inner)
        def _():
            relay_fresh(name)

    def inner_fresh(name):
        @pl.when(inner)
        def _():
            relay_fresh(name)

    def finish(name, half):
        at = half_of(name, half)
        for slot in range(slots):
            col = slot * HD
            low[:, col : col + HD] = (dq_acc[slot, at, :] * SCALE).astype(BF16)
            low[:, width + col : width + col + HD] = (dk_acc[slot, :, at] * SCALE).T.astype(BF16)
            low[:, 2 * width + col : 2 * width + col + HD] = dv_acc[slot, :, at].T.astype(BF16)
        part_out[name, half * half_rows : (half + 1) * half_rows] = lax.dot_general(
            low[...], wq_ref[...], NT, preferred_element_type=F32
        ).astype(BF16)

    def add_rows(name, half):
        ones = jnp.ones((16, half_rows), BF16)
        gb_own[...] += jnp.dot(ones, low[...], preferred_element_type=F32)[0:8, :]
        load_rows(name, half).wait()
        gq_acc[...] += lax.dot_general(x_ref[...], low[...], TN, preferred_element_type=F32)
        if (name, half) != (0, 1):
            load_rows(name - half, 1 - half).start()

    dq_acc[...] = jnp.zeros_like(dq_acc)
    dk_acc[...] = jnp.zeros_like(dk_acc)
    dv_acc[...] = jnp.zeros_like(dv_acc)
    gq_acc[...] = jnp.zeros_like(gq_acc)
    gb_own[...] = jnp.zeros_like(gb_own)
    far(3).start()
    far(2).start()
    small_step(0)

    def prepare(step, carry):
        at = pl.ds(pl.multiple_of(step * share, share), share)
        wide = jnp.concatenate([unpack_rows(up_ref[step, i]) for i in range(up_ref.shape[1])], 0)
        for slot in range(slots):
            up = wide[:, slot * HD : (slot + 1) * HD]
            one, two, three = thirds(
                jnp.sum(
                    up.astype(F32) * mixed_ref[at, slot * HD : (slot + 1) * HD], -1, keepdims=True
                )
            )
            blank = jnp.zeros((share, VAUG - HD - 3), BF16)
            upper[slot, at, :] = jnp.concatenate([up, one, two, three, blank], 1)
            up_flip[slot, :, at] = up.T
            q_flip[slot, :, at] = qs_ref[slot, at, :HD].T
        return carry

    lax.fori_loop(0, 4, prepare, 0)
    actions = {
        2: [(small_step, 1)],
        3: [(join_far, 3), (join_far, 2)],
        4: [(small_step, 2)],
        5: [(begin_near, 3), (begin_near, 2)],
        6: [(small_step, 3)],
        8: [(join_near, 3), (join_near, 2), (end_fresh, 3), (begin_far, 1), (begin_far, 0)],
        9: [(small_step, 4)],
        10: [(join_far, 1), (join_far, 0)],
        11: [(small_step, 5)],
        12: [(end_fresh, 2), (inner_fresh, 2), (begin_near, 1), (begin_near, 0)],
        15: [(join_near, 1), (join_near, 0), (end_fresh, 1), (inner_fresh, 1)],
    }

    def tiles(pairs):
        todo = [(slot, part, keys) for part, keys in pairs for slot in range(slots)]
        scores = [
            lax.dot_general(
                qs_ref[slot, part, :], ka_ref[slot, keys, :], NT, preferred_element_type=F32
            )
            for slot, part, keys in todo
        ]
        slopes = [
            lax.dot_general(
                upper[slot, part, :], va_ref[slot, keys, :], NT, preferred_element_type=F32
            )
            for slot, part, keys in todo
        ]
        probs = [jnp.exp2(x) for x in scores]
        lows = [(p * d).astype(BF16) for p, d in zip(probs, slopes)]
        for (slot, part, keys), p, ds in zip(todo, probs, lows):
            dv_acc[slot, :, keys] += jnp.dot(
                up_flip[slot, :, part], p.astype(BF16), preferred_element_type=F32
            )
            dk_acc[slot, :, keys] += jnp.dot(
                q_flip[slot, :, part], ds, preferred_element_type=F32
            )
            dq_acc[slot, part, :] += jnp.dot(
                ds, kk_ref[keys, slot * HD : (slot + 1) * HD], preferred_element_type=F32
            )

    def some_work(step, carry):
        name, other, half = (pick([s[i] for s in STEPS], step) for i in range(3))
        for when, todo in actions.items():

            @pl.when(step == when)
            def _():
                for act, s in todo:
                    act(s)

        @pl.when(name == other)
        def _():
            tiles([(rows_of(name), rows_of(name))])

        @pl.when(name != other)
        def _():
            tiles([(half_of(name, half), rows_of(other)), (rows_of(other), half_of(name, half))])

        for when, (n, h) in ENDS.items():

            @pl.when(step == when)
            def _():
                finish(n, h)
                if n == 3:

                    @pl.when(~inner)
                    def _():
                        relay(n, h)

                else:
                    relay(n, h)
                add_rows(n, h)

        @pl.when((step == 13) & inner)
        def _():
            relay(3, 0)

        return carry

    lax.fori_loop(0, len(STEPS), some_work, 0)
    for half in range(2):
        finish(0, half)
        add_rows(0, half)

    gb_in[dp] = gb_own[...]
    piece = depth // 8
    for d in range(8):
        gq_own[d] = gq_acc[d * piece : (d + 1) * piece, :].astype(BF16)
    q_copies = []
    for d in range(1, 8):
        to = dp ^ d
        q_copies.append(
            remote(gq_own.at[to], gq_in.at[d - 1], q_send.at[d - 1], q_recv.at[d - 1], others[d - 1])
        )
        q_copies.append(
            remote(gb_own, gb_in.at[dp], b_send.at[d - 1], b_recv.at[d - 1], others[d - 1])
        )
    for copy in q_copies:
        copy.start()
    @pl.when(inner)
    def _():
        relay(3, 1)
        relay_fresh(3)

    for half in range(2):

        @pl.when(mp > 0)
        def _():
            chain_copy(0, half, mp, mp ^ 1).wait_recv()

        @pl.when(mp < 3)
        def _():
            chain_copy(0, half, 4, mp ^ 1).wait_recv()

    @pl.when(mp > 0)
    def _():
        fresh_copy(0, mp, mp ^ 1).wait_recv()

    @pl.when(mp < 3)
    def _():
        fresh_copy(0, 4, mp ^ 1).wait_recv()

    total = fresh[0].astype(F32)
    total = total + jnp.where(mp > 0, fresh_in[mp].astype(F32), 0.0)
    total = total + jnp.where(mp < 3, fresh_in[4].astype(F32), 0.0)
    cols = gup_ref.shape[1]
    gap = HALF - cols
    gup_ref[...] = total[:, :cols]
    gdown_ref[...] = total[:, HALF : HALF + cols]
    gout_ref[:, :gap] = total[:, cols:HALF]
    gout_ref[:, gap:] = total[:, HALF + cols : HALF + cols + width - gap]
    for copy in q_copies:
        copy.wait_recv()
    total = gq_own[dp].astype(F32)
    for d in range(7):
        total = total + gq_in[d].astype(F32)
    for i in range(3):
        gq_ref[i] = total[:, i * width : (i + 1) * width]
    total = gb_in[0]
    for d in range(1, 8):
        total = total + gb_in[d]
    gb_ref[0:1, :] = total[0:1, :width]
    gb_ref[1:2, :] = total[0:1, 2 * width :]

    wide = one_ref[...] + part_out[0].astype(F32)
    left = jnp.where(mp > 0, chain[mp].astype(F32), 0.0)
    right = jnp.where(mp < 3, chain[4].astype(F32), 0.0)
    fg_ref[...] = (wide + left + right).astype(BF16)
    for name in (1, 2, 3):
        for half in range(2):
            chain_copy(name, half, 0, mp ^ 1).wait_send()
        fresh_copy(name, 0, mp ^ 1).wait_send()
    for s in range(4):
        far(s).wait_send()
        near(s, 0).wait_send()
        near(s, 1).wait_send()
    for at in range(len(partners)):
        swap(at).wait_send()
    for copy in q_copies:
        copy.wait_send()


def back_pass(qs, ka, va, kk, mixed, up, sums, frames, wq, one_grad, small, hidden_cols):
    slots, rows, _ = qs.shape
    depth = frames.shape[1]
    share = rows // 4
    piece, lanes = sums.shape[2:]
    cols = wq.shape[1]
    vmem = pl.BlockSpec(memory_space=pltpu.VMEM)
    hbm = pl.BlockSpec(memory_space=pltpu.MemorySpace.HBM)
    dma = pltpu.SemaphoreType.DMA
    V = pltpu.VMEM
    return pl.pallas_call(
        functools.partial(back_kernel, slots),
        in_specs=[vmem] * 7 + [hbm] + [vmem] * 3,
        out_specs=[vmem] * 13,
        out_shape=[
            jax.ShapeDtypeStruct((share, depth), BF16),
            jax.ShapeDtypeStruct((3, piece, cols // 3), F32),
            jax.ShapeDtypeStruct((2, cols // 3), F32),
            jax.ShapeDtypeStruct((piece, hidden_cols), F32),
            jax.ShapeDtypeStruct((piece, hidden_cols), F32),
            jax.ShapeDtypeStruct((piece, cols // 3), F32),
            jax.ShapeDtypeStruct((hidden_cols,), F32),
        ]
        + [jax.ShapeDtypeStruct((depth,), F32)] * 6,
        scratch_shapes=[
            V((slots, rows, VAUG), BF16), V((slots, HD, rows), BF16), V((slots, HD, rows), BF16),
            V((slots, rows, HD), F32), V((slots, HD, rows), F32), V((slots, HD, rows), F32),
            V((share // 2, cols), BF16), V((4, share, depth), BF16), V((5, share, depth), BF16),
            V((4, piece, lanes), BF16), V((4, piece, lanes), BF16), V((4, 2, piece, lanes), BF16),
            V((4, piece, lanes), BF16), V((5, piece, lanes), BF16),
            V((8, piece, cols), BF16), V((7, piece, cols), BF16),
            V((8, cols), F32), V((8, 8, cols), F32), V((5,) + small.shape, F32), V((5,) + small.shape, F32),
            dma((4, 2)), dma((5, 2)), dma((4,)), dma((4,)), dma((4, 2)), dma((4, 2)), dma((4,)), dma((5,)),
            dma((7,)), dma((7,)), dma((7,)), dma((7,)), dma((5,)), dma((5,)), V(small.shape, F32),
            V((share // 2, depth), BF16), dma((1,)), V((depth, cols), F32),
        ],
        compiler_params=pltpu.CompilerParams(
            collective_id=3, has_side_effects=True, vmem_limit_bytes=34 << 20
        ),
        name="back_pass",
    )(qs, ka, va, kk, mixed, up, sums, frames, wq, one_grad, small)


def deliver_kernel(count, *refs):
    sources, results, sem = refs[:count], refs[count : 2 * count], refs[2 * count]
    copies = [
        pltpu.make_async_copy(a, b, sem.at[i]) for i, (a, b) in enumerate(zip(sources, results))
    ]
    for copy in copies:
        copy.start()
    for copy in copies:
        copy.wait()


def deliver(arrays):
    count = len(arrays)
    return pl.pallas_call(
        functools.partial(deliver_kernel, count),
        in_specs=[pl.BlockSpec(memory_space=pltpu.VMEM)] * count,
        out_specs=[pl.BlockSpec(memory_space=pltpu.MemorySpace.HBM)] * count,
        out_shape=[jax.ShapeDtypeStruct(a.shape, a.dtype) for a in arrays],
        scratch_shapes=[pltpu.SemaphoreType.DMA((count,))],
        compiler_params=pltpu.CompilerParams(vmem_limit_bytes=4 << 20),
        name="deliver",
    )(*arrays)


def body(
    frames, seg_ids, qkv_weight, qkv_bias, out_weight, out_bias, gain_one, shift_one,
    up_weight, up_bias, down_weight, down_bias, gain_two, shift_two, cotangent,
):
    rows, depth = frames.shape
    mp_size = lax.axis_size("mp")
    dp_size = lax.axis_size("dp")
    mp_index = lax.axis_index("mp")
    share = rows // mp_size
    slots = qkv_weight.shape[2] // HD
    width = slots * HD
    hidden_cols = up_weight.shape[1]
    piece = qkv_weight.shape[1]
    gap = HALF - hidden_cols
    spare = -(HALF + hidden_cols + width - gap) % 128
    live_count = HEADS // mp_size + (mp_index < HEADS % mp_size).astype(jnp.int32)
    live = (jnp.arange(slots) < live_count).astype(F32)

    in_hbm = lambda a: pltpu.with_memory_space_constraint(a, pltpu.MemorySpace.HBM)
    out_flip = out_weight.T
    down_flip = down_weight.T
    vectors = (out_bias, gain_one, shift_one, down_bias, gain_two, shift_two)
    linked = (dp_size, mp_size, slots, rows) == (8, 4, 3, 2048)
    if linked:
        weights, qkv_full, ub_full, qs, ka, va, kk, mixed, got = front(
            *map(in_hbm, (frames, qkv_weight, up_weight, down_flip, out_flip)), up_bias, qkv_bias,
            seg_ids, slots,
        )
        weights = weights.reshape(mp_size, depth, -1)
    else:
        wq = jnp.transpose(qkv_weight, (1, 0, 2)).reshape(piece, 3 * width)
        packed = jnp.concatenate(
            [up_weight, out_flip[:, :gap], down_flip, out_flip[:, gap:], jnp.zeros((piece, spare), BF16)], 1
        )
        ub_pad = jnp.pad(up_bias, (0, gap))[None]
        offsets = jnp.concatenate([qkv_bias[0], jnp.zeros_like(qkv_bias[0]), qkv_bias[1]])[None]
        qkv_full = lax.all_gather(wq, "dp", axis=0, tiled=True)
        weights = lax.all_gather(packed, "mp", axis=0, tiled=False)
        weights = lax.all_gather(weights, "dp", axis=1, tiled=True)
        ub_full = lax.all_gather(ub_pad, "mp", axis=0, tiled=False)
        qs, ka, va, kk = project(frames, qkv_full, offsets, seg_ids, slots)
        qs, mixed = attend(qs, ka, va)
        mixed_low = (mixed * live[:, None, None]).astype(BF16)
        sent = mixed_low.reshape(slots, mp_size, share, HD).transpose(1, 2, 0, 3)
        got = lax.all_to_all(sent.reshape(mp_size, share, width), "mp", 0, 0, tiled=True)
    output_frames, sum_one_grad, back, partial, small = middle(
        in_hbm(frames), in_hbm(cotangent), got, weights, ub_full, vectors, hidden_cols, linked
    )
    if linked:
        made = back_pass(
            qs, ka, va, kk, mixed, back, partial, in_hbm(frames), qkv_full, sum_one_grad, small, hidden_cols
        )
        output_frames, *made = deliver([output_frames, *made])
        return (
            output_frames, made[0], made[1], made[2], made[5].T, made[7], made[8], made[9], made[3],
            made[6], made[4].T, made[10], made[11], made[12],
        )
    if not linked:
        back = lax.all_to_all(back, "mp", 0, 0, tiled=True)
        back = back.reshape(rows, slots, HD).transpose(1, 0, 2)
        partial = lax.psum_scatter(partial, "dp", scatter_dimension=1, tiled=True)
        partial = lax.psum_scatter(partial, "mp", scatter_dimension=0, tiled=True)[0].astype(F32)
        small = lax.psum(small, ("dp", "mp"))
        kk = kk.reshape(rows, slots, HD).transpose(1, 0, 2)
        dq, dk, dv = attend_back(qs, ka, va, kk, mixed, back)
        grads_low = jnp.stack([dq, dk, dv]).transpose(2, 0, 1, 3).reshape(rows, 3 * width)
        bias_sums = lax.psum(jnp.sum(grads_low.astype(F32), 0), "dp")
        grad_qkv = jnp.einsum("rd,rs->ds", frames, grads_low, preferred_element_type=F32)
        arrived = lax.all_to_all(
            grad_qkv.astype(BF16).reshape(dp_size, piece, 3 * width), "dp", 0, 0, tiled=True
        )
        grad_qkv = arrived.astype(F32).sum(0)
        input_part = jnp.einsum("rs,ds->rd", grads_low, qkv_full, preferred_element_type=F32)
        input_sum = lax.psum_scatter(input_part.astype(BF16), "mp", scatter_dimension=0, tiled=True)
        frames_grad = (input_sum.astype(F32) + sum_one_grad).astype(BF16)
    grad_qkv = grad_qkv.reshape(piece, 3, width).transpose(1, 0, 2)
    bias_sums = bias_sums.reshape(3, width)
    qkv_bias_grad = jnp.stack([bias_sums[0], bias_sums[2]])
    out_grad = jnp.concatenate(
        [partial[:, hidden_cols:HALF], partial[:, HALF + hidden_cols : HALF + hidden_cols + width - gap]], 1
    )
    return (
        output_frames,
        frames_grad,
        grad_qkv,
        qkv_bias_grad,
        out_grad.T,
        small[0],
        small[1],
        small[2],
        partial[:, :hidden_cols],
        lax.dynamic_index_in_dim(small, 8 + mp_index, 0, False)[:hidden_cols],
        partial[:, HALF : HALF + hidden_cols].T,
        small[3],
        small[4],
        small[5],
    )


def solution(mesh):
    in_specs = (
        P("dp", None), P("dp"), P(None, "dp", "mp"), P(None, "mp"), P("mp", "dp"), P(), P(), P(),
        P("dp", "mp"), P("mp"), P("mp", "dp"), P(), P(), P(), P("dp", None),
    )
    out_specs = (
        P(("dp", "mp"), None), P(("dp", "mp"), None), P(None, "dp", "mp"), P(None, "mp"),
        P("mp", "dp"), P(), P(), P(), P("dp", "mp"), P("mp"), P("mp", "dp"), P(), P(), P(),
    )
    return jax.shard_map(body, mesh=mesh, in_specs=in_specs, out_specs=out_specs, check_vma=False)
```

```python
import functools
import math

import jax
import jax.numpy as jnp
from jax import lax
from jax.experimental import pallas as pl
from jax.experimental.pallas import tpu as pltpu
from jax.sharding import PartitionSpec as P

HEADS = 10
HD = 64
EPS = 1e-05
SCALE = 0.125
MAX_SEGS = 16
MASKED = -1e30
UNIT = SCALE * math.log2(math.e)
AUG = 256
VAUG = 128
NT = (((1,), (1,)), ((), ()))
TN = (((0,), (0,)), ((), ()))
F32 = jnp.float32
BF16 = jnp.bfloat16
VMEM_LIMIT = 56 << 20
MESH = pl.DeviceIdType.MESH
CHIPS = 3
HALF = 640


def thirds(wide):
    first = wide.astype(BF16)
    rest = wide - first.astype(F32)
    second = rest.astype(BF16)
    third = (rest - second.astype(F32)).astype(BF16)
    return first, second, third


def lane_marks(rows, width, count):
    return lax.broadcasted_iota(jnp.int32, (rows, width), 1) < count


def spread_rows(made, picked, slots, qs_ref, ka_ref, va_ref, kk_ref, rows):
    count = made.shape[0]
    width = slots * HD
    chosen = picked.astype(BF16)
    barred = ((picked - 1.0) * -MASKED).astype(BF16)
    tail = AUG - 3 * HD - MAX_SEGS
    q_tail = jnp.zeros((count, tail), BF16)
    minus = jnp.where(lane_marks(count, tail, 3), -1.0, 0.0).astype(BF16)
    v_tail = jnp.where(lane_marks(count, VAUG - HD, 3), -1.0, 0.0).astype(BF16)
    for slot in range(slots):
        at = slot * HD
        q = made[:, at : at + HD]
        k = made[:, width + at : width + at + HD]
        v = made[:, 2 * width + at : 2 * width + at + HD]
        one, two, three = thirds(k.astype(F32) * UNIT)
        qs_ref[slot, rows, :] = jnp.concatenate([q, q, q, chosen, q_tail], 1)
        ka_ref[slot, rows, :] = jnp.concatenate([one, two, three, barred, minus], 1)
        va_ref[slot, rows, :] = jnp.concatenate([v, v_tail], 1)
    kk_ref[rows, :] = made[:, width : 2 * width]


def announce(peers):
    for peer in peers:
        pl.semaphore_signal(
            pltpu.get_barrier_semaphore(), inc=1, device_id=peer, device_id_type=MESH
        )


def await_peers(count):
    pl.semaphore_wait(pltpu.get_barrier_semaphore(), count)


def remote(src, dst, send, recv, peer):
    return pltpu.make_async_remote_copy(
        src_ref=src, dst_ref=dst, send_sem=send, recv_sem=recv, device_id=peer, device_id_type=MESH
    )


def pack_rows(wide):
    half = wide.shape[0] // 2
    third = wide[:, 2 * HD :]
    return jnp.concatenate(
        [wide[:, : 2 * HD], jnp.concatenate([third[:half], third[half:]], 1)], 0
    )


def unpack_rows(packed):
    rows = packed.shape[0] * 2 // 3
    rest = packed[rows:]
    return jnp.concatenate(
        [packed[:rows], jnp.concatenate([rest[:, :HD], rest[:, HD:]], 0)], 1
    )


def front_kernel(
    slots, sub,
    x_hbm, qkv_hbm, up_hbm, down_hbm, out_hbm, ub_ref, qb_ref, seg_ref,
    all_ref, wfull_ref, ball_ref, qs_ref, ka_ref, va_ref, kk_ref, mixed_ref, got_ref,
    x_ref, qkv_ref, up_ref, down_ref, out_ref, stage, wq_ref, pack_ref, bias_ref,
    q_send, q_recv, z_send, z_recv, w_send, w_recv, b_send, b_recv, a_send, a_recv, here, loaded,
):
    dp = lax.axis_index("dp")
    mp = lax.axis_index("mp")
    plane = [dp ^ 2, dp ^ 4, dp ^ 6]
    sibling = (dp ^ 1, mp)
    tall = [(dp, mp ^ s) for s in range(1, 4)]
    inner = (mp == 1) | (mp == 2)
    announce([sibling] + [(d, mp) for d in plane] + tall)
    width = slots * HD
    pairs = ((qkv_hbm, qkv_ref), (up_hbm, up_ref), (down_hbm, down_ref), (out_hbm, out_ref), (x_hbm, x_ref))
    loads = [pltpu.make_async_copy(a, b, loaded.at[i]) for i, (a, b) in enumerate(pairs)]
    for copy in loads:
        copy.start()
    bias_ref[...] = jnp.zeros_like(bias_ref)
    bias_ref[:, : up_hbm.shape[1]] = ub_ref[...].reshape(1, up_hbm.shape[1])
    for copy in loads[:4]:
        copy.wait()
    for i in range(3):
        wq_ref[:, i * width : (i + 1) * width] = qkv_ref[i]
    hidden_cols = up_ref.shape[1]
    gap = HALF - hidden_cols
    rest = width - gap
    pack_ref[:, :hidden_cols] = up_ref[...]
    pack_ref[:, hidden_cols:HALF] = out_ref[:, :gap]
    pack_ref[:, HALF : HALF + hidden_cols] = down_ref[...]
    pack_ref[:, HALF + hidden_cols : HALF + hidden_cols + rest] = out_ref[:, gap:]
    spare = pack_ref.shape[1] - HALF - hidden_cols - rest
    pack_ref[:, HALF + hidden_cols + rest :] = jnp.zeros((pack_ref.shape[0], spare), BF16)
    await_peers(7)
    rows = x_ref.shape[0]
    share = rows // 4

    piece = wq_ref.shape[0]

    def rows_of(d):
        return wfull_ref.at[pl.ds(pl.multiple_of(d * piece, piece), piece)]

    mine = pltpu.make_async_copy(wq_ref, rows_of(dp), here.at[0])
    mine.start()
    firsts = [
        remote(wq_ref, rows_of(dp), q_send.at[i], q_recv.at[i], (plane[i], mp))
        for i in range(CHIPS)
    ]
    for copy in firsts:
        copy.start()
    shared = [remote(wq_ref, rows_of(dp), q_send.at[3], q_recv.at[3], sibling)]
    shared[0].start()
    own = pltpu.make_async_copy(pack_ref, all_ref.at[mp, dp], here.at[1])
    own.start()
    def lift(at, s, landing, peer):
        ref = all_ref.at[mp ^ s, dp]
        return remote(pack_ref if s == 0 else ref, ref, z_send.at[at], z_recv.at[landing], peer)

    near, middle = tall[0], tall[2]
    lifts = [lift(0, 0, 1, near)]
    inner_lifts = [
        lift(1, 0, 3, middle), lift(2, 1, 2, middle), lift(3, 3, 2, near), lift(4, 2, 3, near),
    ]

    def arrive(s):
        lift(0, s, s, near).wait_recv()

    own_bias = pltpu.make_async_copy(bias_ref, ball_ref.at[mp], here.at[2])
    own_bias.start()
    lifts[0].start()

    @pl.when(inner)
    def _():
        inner_lifts[0].start()

    biases = [
        remote(bias_ref, ball_ref.at[mp], b_send.at[s], b_recv.at[s], tall[s]) for s in range(3)
    ]
    for copy in biases:
        copy.start()
    for i in range(CHIPS):
        firsts[i].wait_recv()
        passed = remote(
            rows_of(plane[i]), rows_of(plane[i]), q_send.at[4 + i], q_recv.at[4 + i], sibling
        )
        passed.start()
        shared.append(passed)
    own.wait()

    def weights(s, kind):
        group = mp ^ s
        block = {0: dp, 1: dp, 2: dp, 4: plane[0], 5: plane[1], 6: plane[2]}
        block[3] = plane[0] if s % 2 == 0 else plane[1]
        peer = {0: (plane[0], mp), 1: (plane[1], mp)}
        peer[3] = peer[1] if s % 2 == 0 else peer[0]
        ref = all_ref.at[group, block[kind]]
        return remote(ref, ref, w_send.at[s, kind], w_recv.at[s, kind], peer.get(kind, sibling))

    def start_weights(s):
        if s == 3:

            @pl.when(~inner)
            def _():
                arrive(3)

        for kind in (0, 1, 2):
            weights(s, kind).start()

    def pass_weights(s):
        weights(s, 0).wait_recv()
        weights(s, 1).wait_recv()
        for kind in (3, 4, 5):
            weights(s, kind).start()

    def last_weights(s):
        weights(s, 3).wait_recv()
        weights(s, 6).start()

    start_weights(0)
    mine.wait()
    for copy in shared:
        copy.wait_recv()
    arrive(1)

    @pl.when(inner)
    def _():
        inner_lifts[1].start()
        arrive(3)
        inner_lifts[2].start()

    start_weights(1)

    loads[4].wait()
    block = 512

    def project_rows(step, carry):
        part = pl.ds(pl.multiple_of(step * block, block), block)
        x = x_ref[part, :]
        offsets = jnp.concatenate(
            [qb_ref[0:1, :], jnp.zeros((1, width), F32), qb_ref[1:2, :]], 1
        )
        made = jnp.dot(x, wfull_ref[...], preferred_element_type=F32) + offsets
        marks = seg_ref[:, part] == lax.broadcasted_iota(jnp.int32, (MAX_SEGS, block), 0)
        picked = jnp.where(marks, 1.0, 0.0).T
        spread_rows(made.astype(BF16), picked, slots, qs_ref, ka_ref, va_ref, kk_ref, part)
        return carry

    lax.fori_loop(0, rows // block, project_rows, 0)
    arrive(2)

    @pl.when(inner)
    def _():
        inner_lifts[3].start()

    pass_weights(0)
    start_weights(2)

    live_count = HEADS // 4 + (mp < HEADS % 4).astype(jnp.int32)
    per_share = share // sub
    actions = {
        1: [(pass_weights, 1)],
        3: [(start_weights, 3)],
        4: [(last_weights, 0)],
        5: [(pass_weights, 2)],
        6: [(last_weights, 1)],
        7: [(pass_weights, 3)],
    }

    def send_rows(step, stage_index):
        return remote(
            stage.at[step], got_ref.at[mp, lax.rem(step, per_share)], a_send.at[step], a_recv.at[step],
            (dp, mp ^ stage_index),
        )

    def attend_rows(step, carry):
        stage_index = 3 - step // per_share
        group = mp ^ stage_index
        offset = lax.rem(step, per_share) * sub
        part = pl.ds(pl.multiple_of(group * share + offset, sub), sub)
        for when, todo in actions.items():

            @pl.when(step == when)
            def _():
                for act, s in todo:
                    act(s)

        kept = []
        scores = [
            lax.dot_general(qs_ref[slot, part, :], ka_ref[slot], NT, preferred_element_type=F32)
            for slot in range(slots)
        ]
        for slot in range(slots):
            x = scores[slot]
            top = jnp.max(x, -1, keepdims=True)
            p = jnp.exp2(x - top).astype(BF16)
            made = jnp.dot(p, va_ref[slot], preferred_element_type=F32)
            total = -made[:, HD : HD + 1]
            mixed = made[:, :HD] / total
            one, two, three = thirds(top + jnp.log2(total))
            base = 3 * HD + MAX_SEGS
            qs_ref[slot, part, base : base + 3] = jnp.concatenate([one, two, three], 1)
            mixed_ref[part, slot * HD : (slot + 1) * HD] = mixed
            alive = (slot < live_count).astype(F32)
            kept.append((mixed * alive).astype(BF16))
        stage[step] = pack_rows(jnp.concatenate(kept, 1))

        @pl.when(step < 3 * per_share)
        def _():
            send_rows(step, stage_index).start()

        return carry

    lax.fori_loop(0, rows // sub, attend_rows, 0)
    keep = pltpu.make_async_copy(
        stage.at[pl.ds(3 * per_share, per_share)], got_ref.at[mp], here.at[3]
    )
    keep.start()
    last_weights(2)
    last_weights(3)
    for s in range(4):
        weights(s, 2).wait_recv()
        for kind in (4, 5, 6):
            weights(s, kind).wait_recv()
        for kind in range(7):
            weights(s, kind).wait_send()
    for copy in firsts + shared + lifts:
        copy.wait_send()

    @pl.when(inner)
    def _():
        for copy in inner_lifts:
            copy.wait_send()

    for copy in biases:
        copy.wait()
    for step in range(3 * per_share):
        send_rows(step, 3 - step // per_share).wait()
    own_bias.wait()
    keep.wait()


def front(frames, qkv_weight, up_weight, down_flip, out_flip, up_bias, qkv_bias, seg_ids, slots):
    rows, depth = frames.shape
    piece, hidden_cols = up_weight.shape
    width = slots * HD
    lanes = -(-(2 * hidden_cols + width) // 128) * 128
    sub = 256
    shape = lambda n: jax.ShapeDtypeStruct((slots, rows, n), BF16)
    vmem = pl.BlockSpec(memory_space=pltpu.VMEM)
    hbm = pl.BlockSpec(memory_space=pltpu.MemorySpace.HBM)
    dma = pltpu.SemaphoreType.DMA
    steps = rows // sub
    operands = (frames, qkv_weight, up_weight, down_flip, out_flip)
    return pl.pallas_call(
        functools.partial(front_kernel, slots, sub),
        in_specs=[hbm] * 5 + [vmem] * 3,
        out_specs=[vmem] * 9,
        out_shape=[
            jax.ShapeDtypeStruct((4, 8, piece, lanes), BF16),
            jax.ShapeDtypeStruct((8 * piece, 3 * width), BF16),
            jax.ShapeDtypeStruct((4, 1, HALF), F32),
            shape(AUG), shape(AUG), shape(VAUG),
            jax.ShapeDtypeStruct((rows, width), BF16),
            jax.ShapeDtypeStruct((rows, width), F32),
            jax.ShapeDtypeStruct((4, steps // 4, sub * 3 // 2, 2 * HD), BF16),
        ],
        scratch_shapes=[
            pltpu.VMEM(frames.shape, BF16), pltpu.VMEM(qkv_weight.shape, BF16),
            pltpu.VMEM(up_weight.shape, BF16), pltpu.VMEM(down_flip.shape, BF16),
            pltpu.VMEM(out_flip.shape, BF16),
            pltpu.VMEM((steps, sub * 3 // 2, 2 * HD), BF16),
            pltpu.VMEM((piece, 3 * width), BF16), pltpu.VMEM((piece, lanes), BF16),
            pltpu.VMEM((1, HALF), F32),
            dma((7,)), dma((7,)), dma((5,)), dma((4,)), dma((4, 7)), dma((4, 7)), dma((3,)), dma((3,)),
            dma((steps,)), dma((steps,)), dma((4,)), dma((len(operands),)),
        ],
        compiler_params=pltpu.CompilerParams(
            collective_id=1, has_side_effects=True, vmem_limit_bytes=20 << 20
        ),
        name="front",
    )(*operands, up_bias, qkv_bias, seg_ids.reshape(1, rows))


def project_kernel(slots, x_ref, w_ref, b_ref, seg_ref, qs_ref, ka_ref, va_ref, kk_ref):
    made = jnp.dot(x_ref[...], w_ref[...], preferred_element_type=F32) + b_ref[...]
    marks = seg_ref[...] == lax.broadcasted_iota(jnp.int32, (x_ref.shape[0], MAX_SEGS), 1)
    spread_rows(
        made.astype(BF16), jnp.where(marks, 1.0, 0.0), slots, qs_ref, ka_ref, va_ref, kk_ref, slice(None)
    )


def project(frames, weight, offsets, seg_ids, slots):
    rows, depth = frames.shape
    block = min(512, rows)
    spread = lambda n: pl.BlockSpec((slots, block, n), lambda i: (0, i, 0))
    shape = lambda n: jax.ShapeDtypeStruct((slots, rows, n), BF16)
    return pl.pallas_call(
        functools.partial(project_kernel, slots),
        grid=(rows // block,),
        in_specs=[
            pl.BlockSpec((block, depth), lambda i: (i, 0)),
            pl.BlockSpec(weight.shape, lambda i: (0, 0)),
            pl.BlockSpec((1, offsets.shape[1]), lambda i: (0, 0)),
            pl.BlockSpec((block, 1), lambda i: (i, 0)),
        ],
        out_specs=[
            spread(AUG), spread(AUG), spread(VAUG), pl.BlockSpec((block, slots * HD), lambda i: (i, 0)),
        ],
        out_shape=[
            shape(AUG), shape(AUG), shape(VAUG), jax.ShapeDtypeStruct((rows, slots * HD), BF16),
        ],
        compiler_params=pltpu.CompilerParams(vmem_limit_bytes=VMEM_LIMIT),
        name="project",
    )(frames, weight, offsets, seg_ids.reshape(rows, 1))


def attend_kernel(sub, qs_ref, ka_ref, va_ref, qn_ref, mixed_ref):
    for at in range(0, qs_ref.shape[1], sub):
        part = slice(at, at + sub)
        x = lax.dot_general(qs_ref[0, part, :], ka_ref[0], NT, preferred_element_type=F32)
        top = jnp.max(x, -1, keepdims=True)
        p = jnp.exp2(x - top).astype(BF16)
        made = jnp.dot(p, va_ref[0], preferred_element_type=F32)
        total = -made[:, HD : HD + 1]
        mixed_ref[0, part, :] = made[:, :HD] / total
        one, two, three = thirds(top + jnp.log2(total))
        base = 3 * HD + MAX_SEGS
        blank = jnp.zeros((sub, AUG - base - 3), BF16)
        qn_ref[0, part, :] = jnp.concatenate(
            [qs_ref[0, part, :base], one, two, three, blank], 1
        )


def attend(qs, ka, va):
    slots, rows, _ = qs.shape
    block = min(512, rows)
    sub = min(256, block)
    whole = lambda n: pl.BlockSpec((1, rows, n), lambda h, i: (h, 0, 0))
    some = lambda n: pl.BlockSpec((1, block, n), lambda h, i: (h, i, 0))
    return pl.pallas_call(
        functools.partial(attend_kernel, sub),
        grid=(slots, rows // block),
        in_specs=[some(AUG), whole(AUG), whole(VAUG)],
        out_specs=[some(AUG), some(HD)],
        out_shape=[
            jax.ShapeDtypeStruct((slots, rows, AUG), BF16),
            jax.ShapeDtypeStruct((slots, rows, HD), F32),
        ],
        compiler_params=pltpu.CompilerParams(vmem_limit_bytes=VMEM_LIMIT),
        name="attend",
    )(qs, ka, va)


def attend_back_kernel(
    sub, qs_ref, ka_ref, va_ref, kk_ref, mixed_ref, up_ref, dq_ref, dk_ref, dv_ref, dk_acc, dv_acc
):
    step = pl.program_id(1)

    @pl.when(step == 0)
    def _():
        dk_acc[...] = jnp.zeros_like(dk_acc)
        dv_acc[...] = jnp.zeros_like(dv_acc)

    for at in range(0, qs_ref.shape[1], sub):
        part = slice(at, at + sub)
        q = qs_ref[0, part, :HD]
        up = up_ref[0, part, :]
        d_one, d_two, d_three = thirds(
            jnp.sum(up.astype(F32) * mixed_ref[0, part, :], -1, keepdims=True)
        )
        blank = lambda n: jnp.zeros((sub, n), BF16)
        upper = jnp.concatenate([up, d_one, d_two, d_three, blank(VAUG - HD - 3)], 1)
        x = lax.dot_general(qs_ref[0, part, :], ka_ref[0], NT, preferred_element_type=F32)
        p = jnp.exp2(x)
        dp = lax.dot_general(upper, va_ref[0], NT, preferred_element_type=F32)
        ds = (p * dp).astype(BF16)
        dv_acc[...] += lax.dot_general(up, p.astype(BF16), TN, preferred_element_type=F32)
        dk_acc[...] += lax.dot_general(q, ds, TN, preferred_element_type=F32)
        dq_ref[0, part, :] = (
            jnp.dot(ds, kk_ref[0], preferred_element_type=F32) * SCALE
        ).astype(BF16)

    @pl.when(step == pl.num_programs(1) - 1)
    def _():
        dk_ref[0] = (dk_acc[...] * SCALE).T.astype(BF16)
        dv_ref[0] = dv_acc[...].T.astype(BF16)


def attend_back(qs, ka, va, kk, mixed, up):
    slots, rows, _ = qs.shape
    block = min(512, rows)
    sub = min(256, block)
    whole = lambda n: pl.BlockSpec((1, rows, n), lambda h, i: (h, 0, 0))
    some = lambda n: pl.BlockSpec((1, block, n), lambda h, i: (h, i, 0))
    shape = jax.ShapeDtypeStruct((slots, rows, HD), BF16)
    return pl.pallas_call(
        functools.partial(attend_back_kernel, sub),
        grid=(slots, rows // block),
        in_specs=[
            some(AUG), whole(AUG), whole(VAUG), whole(HD), some(HD), some(HD),
        ],
        out_specs=[some(HD), whole(HD), whole(HD)],
        out_shape=[shape, shape, shape],
        scratch_shapes=[pltpu.VMEM((HD, rows), F32), pltpu.VMEM((HD, rows), F32)],
        compiler_params=pltpu.CompilerParams(vmem_limit_bytes=VMEM_LIMIT),
        name="attend_back",
    )(qs, ka, va, kk, mixed, up)


def norm_forward(summed):
    centre = summed - jnp.mean(summed, -1, keepdims=True)
    spread = jnp.mean(centre * centre, -1, keepdims=True)
    factor = lax.rsqrt(spread + EPS)
    return (centre * factor, factor)


def norm_backward(upper, normed, factor, gain):
    scaled = upper * gain
    return factor * (
        scaled
        - jnp.mean(scaled, -1, keepdims=True)
        - normed * jnp.mean(scaled * normed, -1, keepdims=True)
    )


def middle_kernel(
    groups, hidden_cols, block, linked,
    x_ref, y_ref, got_ref, w_ref, ub_ref, v0, v1, v2, v3, v4, v5,
    out_ref, s1_ref, back_ref, grad_ref, small_ref, *scratch,
):
    x_own, y_own, ow, act, pre_low, slope, hid_flip, two_flip, one_flip, here = scratch[:10]
    share = out_ref.shape[0]
    width = ow.shape[2]
    gap = HALF - hidden_cols
    dp = lax.axis_index("dp")
    mp = lax.axis_index("mp")
    rows = pl.ds(pl.multiple_of(mp * share, share), share)
    loads = [
        pltpu.make_async_copy(x_ref.at[rows], x_own, here.at[0]),
        pltpu.make_async_copy(y_ref.at[rows], y_own, here.at[1]),
    ]
    for copy in loads:
        copy.start()
    if linked:
        back_own, got, grads, arrived, b_send, b_recv, g_send, g_recv = scratch[10:]
        core = lax.rem(dp, 2)
        sibling = (dp ^ 1, mp)
        announce([sibling] + [(dp, mp ^ s) for s in range(1, 4)])
    else:
        back_own, got, grads = back_ref, got_ref, grad_ref
    out_bias, gain_one, shift_one, down_bias, gain_two, shift_two = (
        v[...].reshape(1, v.shape[0]) for v in (v0, v1, v2, v3, v4, v5)
    )
    for g in range(groups):
        ow[g, :, :gap] = w_ref[g, :, hidden_cols:HALF]
        ow[g, :, gap:] = w_ref[g, :, HALF + hidden_cols : HALF + hidden_cols + width - gap]
    small_ref[...] = jnp.zeros_like(small_ref)
    real = lane_marks(1, HALF, hidden_cols)
    alive = [
        lane_marks(1, width, HD * (HEADS // groups + (g < HEADS % groups))) for g in range(groups)
    ]
    for copy in loads:
        copy.wait()
    if linked:
        await_peers(4)

    def send_back(step, s):
        at = step * 3 + s - 1
        return remote(
            back_own.at[mp ^ s, step], back_ref.at[mp, step], b_send.at[at], b_recv.at[at], (dp, mp ^ s)
        )

    def some_rows(step, carry):
        part = pl.ds(pl.multiple_of(step * block, block), block)
        summed = x_own[part, :].astype(F32) + out_bias
        for g in range(groups):
            if linked:
                got[g, part, :] = unpack_rows(got_ref[g, step])
            summed += lax.dot_general(got[g, part, :], ow[g], NT, preferred_element_type=F32)
        normed_one, factor_one = norm_forward(summed)
        hidden = normed_one * gain_one + shift_one
        hidden_low = hidden.astype(BF16)
        hid_flip[:, part] = hidden_low.T
        feed = hidden + down_bias
        dots = [
            jnp.dot(hidden_low, w_ref[g, :, :HALF], preferred_element_type=F32)
            for g in range(groups)
        ]
        for g in range(groups):
            pre = dots[g] + ub_ref[g]
            half = 0.5 + 0.5 * lax.erf(pre * math.sqrt(0.5))
            bell = jnp.exp(pre * pre * -0.5) * (pre * (1.0 / math.sqrt(2.0 * math.pi)))
            slope[g] = jnp.where(real, half + bell, 0.0)
            made = jnp.where(real, pre * half, 0.0).astype(BF16)
            act[g, part, :] = made
        for g in range(groups):
            feed += lax.dot_general(
                act[g, part, :], w_ref[g, :, HALF : 2 * HALF], NT, preferred_element_type=F32
            )
        normed_two, factor_two = norm_forward(feed)
        out_ref[part, :] = (normed_two * gain_two + shift_two).astype(BF16)
        upstream = y_own[part, :].astype(F32)
        two_grad = norm_backward(upstream, normed_two, factor_two, gain_two)
        sum_two = two_grad.astype(BF16)
        two_flip[:, part] = sum_two.T
        hidden_grad = two_grad
        dots = [
            jnp.dot(sum_two, w_ref[g, :, HALF : 2 * HALF], preferred_element_type=F32)
            for g in range(groups)
        ]
        for g in range(groups):
            low = (slope[g] * dots[g]).astype(BF16)
            pre_low[g, part, :] = low
            small_ref[8 + g : 9 + g, :] += jnp.sum(low.astype(F32), 0, keepdims=True)
        for g in range(groups):
            hidden_grad += lax.dot_general(
                pre_low[g, part, :], w_ref[g, :, :HALF], NT, preferred_element_type=F32
            )
        one_grad = norm_backward(hidden_grad, normed_one, factor_one, gain_one)
        sum_one = one_grad.astype(BF16)
        s1_ref[part, :] = one_grad
        one_flip[:, part] = sum_one.T
        for g in range(groups):
            made = jnp.dot(sum_one, ow[g], preferred_element_type=F32)
            made = jnp.where(alive[g], made, 0.0).astype(BF16)
            if linked:
                back_own[g, step] = pack_rows(made)
            else:
                back_own[g, part, :] = made
        if linked:
            for s in range(1, 4):
                send_back(step, s).start()
        for at, term in enumerate((
            sum_one.astype(F32), hidden_grad * normed_one, hidden_grad,
            sum_two.astype(F32), upstream * normed_two, upstream,
        )):
            small_ref[at : at + 1, :] += jnp.sum(term, 0, keepdims=True)
        return carry

    lax.fori_loop(0, share // block, some_rows, 0)
    if linked:
        keep = pltpu.make_async_copy(back_own.at[mp], back_ref.at[mp], here.at[2])
        keep.start()
    depth = hid_flip.shape[0]
    rest = width - gap
    spare = w_ref.shape[2] - HALF - hidden_cols - rest
    span = depth // 2
    shared = []
    for g in range(groups):
        for part in range(2):
            cols = slice(part * span, (part + 1) * span)
            made = jnp.dot(hid_flip[cols], pre_low[g], preferred_element_type=F32).astype(BF16)
            grad_out = jnp.dot(one_flip[cols], got[g], preferred_element_type=F32).astype(BF16)
            left = jnp.concatenate([made[:, :hidden_cols], grad_out[:, :gap]], 1)
            made = jnp.dot(two_flip[cols], act[g], preferred_element_type=F32).astype(BF16)
            right = jnp.concatenate(
                [made[:, :hidden_cols], grad_out[:, gap:], jnp.zeros((span, spare), BF16)], 1
            )
            if not linked:
                grads[g, cols, :HALF] = left
                grads[g, cols, HALF:] = right
                continue
            piece = grad_ref.shape[2]
            for i in range(span // piece):
                d = part * (span // piece) + i
                at = slice(i * piece, (i + 1) * piece)

                @pl.when(core == d % 2)
                def _():
                    grad_ref[g, d // 2, :, :HALF] = left[at]
                    grad_ref[g, d // 2, :, HALF:] = right[at]

                @pl.when(core != d % 2)
                def _():
                    grads[g, d // 2, :, :HALF] = left[at]
                    grads[g, d // 2, :, HALF:] = right[at]

        if linked:
            copy = remote(grads.at[g], arrived.at[g], g_send.at[g], g_recv.at[g], sibling)
            copy.start()
            shared.append(copy)
    if linked:
        for g in range(groups):
            shared[g].wait_recv()
            for c in range(4):
                grad_ref[g, c] += arrived[g, c]
        for step in range(share // block):
            for s in range(1, 4):
                send_back(step, s).wait()
        for copy in shared:
            copy.wait_send()
        keep.wait()


def middle(frames, cotangent, got, weights, up_bias, vectors, hidden_cols, linked):
    groups = got.shape[0]
    share, depth = frames.shape[0] // groups, frames.shape[1]
    lanes = weights.shape[2]
    width = 3 * HD
    block = min(256, share)
    vmem = pl.BlockSpec(memory_space=pltpu.VMEM)
    rest = pl.BlockSpec(memory_space=pltpu.MemorySpace.HBM)
    dma = pltpu.SemaphoreType.DMA
    scratch = [
        pltpu.VMEM((share, depth), BF16),
        pltpu.VMEM((share, depth), BF16),
        pltpu.VMEM((groups, depth, width), BF16),
        pltpu.VMEM((groups, share, HALF), BF16),
        pltpu.VMEM((groups, share, HALF), BF16),
        pltpu.VMEM((groups, block, HALF), F32),
        pltpu.VMEM((depth, share), BF16),
        pltpu.VMEM((depth, share), BF16),
        pltpu.VMEM((depth, share), BF16),
        dma((3,)),
    ]
    grads = jax.ShapeDtypeStruct(weights.shape, BF16)
    if linked:
        piece = depth // 8
        grads = jax.ShapeDtypeStruct((groups, 4, piece, lanes), BF16)
        sends = 3 * (share // block)
        scratch += [
            pltpu.VMEM(got.shape, BF16),
            pltpu.VMEM((groups, share, width), BF16),
            pltpu.VMEM((groups, 4, piece, lanes), BF16),
            pltpu.VMEM((groups, 4, piece, lanes), BF16),
            dma((sends,)), dma((sends,)), dma((groups,)), dma((groups,)),
        ]
    extra = dict(collective_id=2, has_side_effects=True) if linked else {}
    return pl.pallas_call(
        functools.partial(middle_kernel, groups, hidden_cols, block, linked),
        in_specs=[rest, rest] + [vmem] * 9,
        out_specs=[vmem] * 5,
        out_shape=[
            jax.ShapeDtypeStruct((share, depth), BF16),
            jax.ShapeDtypeStruct((share, depth), F32),
            jax.ShapeDtypeStruct(got.shape, BF16),
            grads,
            jax.ShapeDtypeStruct((16, HALF), F32),
        ],
        scratch_shapes=scratch,
        compiler_params=pltpu.CompilerParams(
            vmem_limit_bytes=33 << 20 if linked else VMEM_LIMIT, **extra
        ),
        name="middle",
    )(frames, cotangent, got, weights, up_bias, *vectors)


STEPS = (
    (3, 3, 0), (3, 0, 0), (3, 1, 0), (3, 2, 0), (3, 0, 1), (3, 1, 1), (3, 2, 1),
    (2, 2, 0), (2, 0, 0), (2, 1, 0), (2, 0, 1), (2, 1, 1), (1, 1, 0), (1, 0, 0), (1, 0, 1), (0, 0, 0),
)
ENDS = {3: (3, 0), 6: (3, 1), 9: (2, 0), 11: (2, 1), 13: (1, 0), 14: (1, 1)}


def pick(table, step):
    made = jnp.int32(table[0])
    for at in range(1, len(table)):
        made = jnp.where(step >= at, jnp.int32(table[at]), made)
    return made


def back_kernel(
    slots,
    qs_ref, ka_ref, va_ref, kk_ref, mixed_ref, up_ref, sums_ref, x_hbm, wq_ref, one_ref, small_ref,
    fg_ref, gq_ref, gb_ref, gup_ref, gdown_ref, gout_ref, gub_ref, s0, s1, s2, s3, s4, s5,
    upper, up_flip, q_flip, dq_acc, dk_acc, dv_acc, low, part_out, chain, fresh, far_in, near_in, third,
    fresh_in, gq_own, gq_in, gb_own, gb_in, tiny, tiny_in,
    c_send, c_recv, f_send, f_recv, n_send, n_recv, t_send, t_recv, q_send, q_recv, b_send, b_recv,
    s_send, s_recv, small_sum, x_ref, loaded, gq_acc,
):
    dp = lax.axis_index("dp")
    mp = lax.axis_index("mp")
    chip = dp // 2
    rows, depth = x_hbm.shape
    share = rows // 4
    width = slots * HD
    others = [(dp ^ d, mp) for d in range(1, 8)]
    tall = [(dp, mp ^ s) for s in range(1, 4)]
    announce(others + tall)
    x_peer, y_peer = (dp ^ 2, mp), (dp ^ 4, mp)

    def rows_of(name):
        return pl.ds(pl.multiple_of((mp ^ name) * share, share), share)

    half_rows = share // 2

    def half_of(name, half):
        start = (mp ^ name) * share + half * half_rows
        return pl.ds(pl.multiple_of(start, half_rows), half_rows)

    def load_rows(name, half):
        return pltpu.make_async_copy(x_hbm.at[half_of(name, half)], x_ref, loaded.at[0])

    load_rows(3, 0).start()

    def far(s):
        return remote(
            sums_ref.at[mp ^ s, chip ^ 3], far_in.at[s], f_send.at[s], f_recv.at[s],
            y_peer if s % 2 == 0 else x_peer,
        )

    def near(s, kind):
        toward_x = (s % 2 == 0) == (kind == 1)
        source = third.at[s] if kind == 1 else sums_ref.at[mp ^ s, chip ^ (1 if toward_x else 2)]
        return remote(
            source, near_in.at[s, kind], n_send.at[s, kind], n_recv.at[s, kind],
            x_peer if toward_x else y_peer,
        )

    def begin_far(s):
        far(s).start()

    def begin_near(s):
        near(s, 0).start()

    def join_far(s):
        far(s).wait_recv()
        third[s] = sums_ref[mp ^ s, chip ^ (1 if s % 2 == 0 else 2)] + far_in[s]
        near(s, 1).start()

    def join_near(s):
        near(s, 0).wait_recv()
        near(s, 1).wait_recv()
        total = sums_ref[mp ^ s, chip].astype(F32) + near_in[s, 0].astype(F32)
        fresh[s] = (total + near_in[s, 1].astype(F32)).astype(BF16)

    partners = [(dp ^ 1, mp), (dp ^ 2, mp), (dp ^ 4, mp), (dp, mp ^ 1), (dp, mp ^ 2)]

    def swap(at):
        return remote(tiny.at[at], tiny_in.at[at], s_send.at[at], s_recv.at[at], partners[at])

    def small_step(at):
        if at == 0:
            tiny[0] = small_ref[...]
        else:
            swap(at - 1).wait_recv()
            made = tiny[at - 1] + tiny_in[at - 1]
            if at == len(partners):
                small_sum[...] = made
                for row, ref in enumerate((s0, s1, s2, s3, s4, s5)):
                    ref[...] = made[row : row + 1, :].reshape(ref.shape)
                cols = gub_ref.shape[-1]
                gub_ref[...] = small_sum[pl.ds(8 + mp, 1), :cols].reshape(gub_ref.shape)
                return
            tiny[at] = made
        swap(at).start()

    def chain_copy(name, half, slot, target):
        at = pl.ds(half * half_rows, half_rows)
        return remote(
            part_out.at[name, at], chain.at[slot, at], c_send.at[name, half], c_recv.at[slot, half],
            (dp, target),
        )

    def fresh_copy(name, slot, target):
        return remote(
            fresh.at[name], fresh_in.at[slot], t_send.at[name], t_recv.at[slot], (dp, target)
        )

    inner = (mp == 1) | (mp == 2)

    def down_the_chain(block, copy):
        for leftward in (True, False):

            @pl.when((block < mp) == leftward)
            def _():
                target = mp - 1 if leftward else mp + 1
                copy(jnp.where(block == target, 4, block) if leftward else block, target).start()

    def relay(name, half):
        block = mp ^ name
        at = pl.ds(half * half_rows, half_rows)

        @pl.when(inner)
        def _():
            chain_copy(name, half, block, mp ^ 1).wait_recv()
            part_out[name, at] = (
                part_out[name, at].astype(F32) + chain[block, at].astype(F32)
            ).astype(BF16)

        down_the_chain(block, functools.partial(chain_copy, name, half))

    def relay_fresh(name):
        block = mp ^ name

        @pl.when(inner)
        def _():
            fresh_copy(name, block, mp ^ 1).wait_recv()
            fresh[name] = (fresh[name].astype(F32) + fresh_in[block].astype(F32)).astype(BF16)

        down_the_chain(block, functools.partial(fresh_copy, name))

    def end_fresh(name):
        @pl.when(~inner)
        def _():
            relay_fresh(name)

    def inner_fresh(name):
        @pl.when(inner)
        def _():
            relay_fresh(name)

    def finish(name, half):
        at = half_of(name, half)
        for slot in range(slots):
            col = slot * HD
            low[:, col : col + HD] = (dq_acc[slot, at, :] * SCALE).astype(BF16)
            low[:, width + col : width + col + HD] = (dk_acc[slot, :, at] * SCALE).T.astype(BF16)
            low[:, 2 * width + col : 2 * width + col + HD] = dv_acc[slot, :, at].T.astype(BF16)
        part_out[name, half * half_rows : (half + 1) * half_rows] = lax.dot_general(
            low[...], wq_ref[...], NT, preferred_element_type=F32
        ).astype(BF16)

    def add_rows(name, half):
        ones = jnp.ones((16, half_rows), BF16)
        gb_own[...] += jnp.dot(ones, low[...], preferred_element_type=F32)[0:8, :]
        load_rows(name, half).wait()
        gq_acc[...] += lax.dot_general(x_ref[...], low[...], TN, preferred_element_type=F32)
        if (name, half) != (0, 1):
            load_rows(name - half, 1 - half).start()

    dq_acc[...] = jnp.zeros_like(dq_acc)
    dk_acc[...] = jnp.zeros_like(dk_acc)
    dv_acc[...] = jnp.zeros_like(dv_acc)
    gq_acc[...] = jnp.zeros_like(gq_acc)
    gb_own[...] = jnp.zeros_like(gb_own)

    def prepare(step, carry):
        at = pl.ds(pl.multiple_of(step * share, share), share)
        wide = jnp.concatenate([unpack_rows(up_ref[step, i]) for i in range(up_ref.shape[1])], 0)
        for slot in range(slots):
            up = wide[:, slot * HD : (slot + 1) * HD]
            one, two, three = thirds(
                jnp.sum(
                    up.astype(F32) * mixed_ref[at, slot * HD : (slot + 1) * HD], -1, keepdims=True
                )
            )
            blank = jnp.zeros((share, VAUG - HD - 3), BF16)
            upper[slot, at, :] = jnp.concatenate([up, one, two, three, blank], 1)
            up_flip[slot, :, at] = up.T
            q_flip[slot, :, at] = qs_ref[slot, at, :HD].T
        return carry

    lax.fori_loop(0, 4, prepare, 0)
    await_peers(10)
    far(3).start()
    far(2).start()
    small_step(0)
    actions = {
        2: [(small_step, 1)],
        3: [(join_far, 3), (join_far, 2)],
        4: [(small_step, 2)],
        5: [(begin_near, 3), (begin_near, 2)],
        6: [(small_step, 3)],
        8: [(join_near, 3), (join_near, 2), (end_fresh, 3), (begin_far, 1), (begin_far, 0)],
        9: [(small_step, 4)],
        10: [(join_far, 1), (join_far, 0)],
        11: [(small_step, 5)],
        12: [(end_fresh, 2), (inner_fresh, 2), (begin_near, 1), (begin_near, 0)],
        15: [(join_near, 1), (join_near, 0), (end_fresh, 1), (inner_fresh, 1)],
    }

    def tiles(pairs):
        todo = [(slot, part, keys) for part, keys in pairs for slot in range(slots)]
        scores = [
            lax.dot_general(
                qs_ref[slot, part, :], ka_ref[slot, keys, :], NT, preferred_element_type=F32
            )
            for slot, part, keys in todo
        ]
        slopes = [
            lax.dot_general(
                upper[slot, part, :], va_ref[slot, keys, :], NT, preferred_element_type=F32
            )
            for slot, part, keys in todo
        ]
        probs = [jnp.exp2(x) for x in scores]
        lows = [(p * d).astype(BF16) for p, d in zip(probs, slopes)]
        for (slot, part, keys), p, ds in zip(todo, probs, lows):
            dv_acc[slot, :, keys] += jnp.dot(
                up_flip[slot, :, part], p.astype(BF16), preferred_element_type=F32
            )
            dk_acc[slot, :, keys] += jnp.dot(
                q_flip[slot, :, part], ds, preferred_element_type=F32
            )
            dq_acc[slot, part, :] += jnp.dot(
                ds, kk_ref[keys, slot * HD : (slot + 1) * HD], preferred_element_type=F32
            )

    def some_work(step, carry):
        name, other, half = (pick([s[i] for s in STEPS], step) for i in range(3))
        for when, todo in actions.items():

            @pl.when(step == when)
            def _():
                for act, s in todo:
                    act(s)

        @pl.when(name == other)
        def _():
            tiles([(rows_of(name), rows_of(name))])

        @pl.when(name != other)
        def _():
            tiles([(half_of(name, half), rows_of(other)), (rows_of(other), half_of(name, half))])

        for when, (n, h) in ENDS.items():

            @pl.when(step == when)
            def _():
                finish(n, h)
                if n == 3:

                    @pl.when(~inner)
                    def _():
                        relay(n, h)

                else:
                    relay(n, h)
                add_rows(n, h)

        @pl.when((step == 13) & inner)
        def _():
            relay(3, 0)

        return carry

    lax.fori_loop(0, len(STEPS), some_work, 0)
    for half in range(2):
        finish(0, half)
        add_rows(0, half)

    gb_in[dp] = gb_own[...]
    piece = depth // 8
    for d in range(8):
        gq_own[d] = gq_acc[d * piece : (d + 1) * piece, :].astype(BF16)
    q_copies = []
    for d in range(1, 8):
        to = dp ^ d
        q_copies.append(
            remote(gq_own.at[to], gq_in.at[d - 1], q_send.at[d - 1], q_recv.at[d - 1], others[d - 1])
        )
        q_copies.append(
            remote(gb_own, gb_in.at[dp], b_send.at[d - 1], b_recv.at[d - 1], others[d - 1])
        )
    for copy in q_copies:
        copy.start()
    @pl.when(inner)
    def _():
        relay(3, 1)
        relay_fresh(3)

    for half in range(2):

        @pl.when(mp > 0)
        def _():
            chain_copy(0, half, mp, mp ^ 1).wait_recv()

        @pl.when(mp < 3)
        def _():
            chain_copy(0, half, 4, mp ^ 1).wait_recv()

    @pl.when(mp > 0)
    def _():
        fresh_copy(0, mp, mp ^ 1).wait_recv()

    @pl.when(mp < 3)
    def _():
        fresh_copy(0, 4, mp ^ 1).wait_recv()

    total = fresh[0].astype(F32)
    total = total + jnp.where(mp > 0, fresh_in[mp].astype(F32), 0.0)
    total = total + jnp.where(mp < 3, fresh_in[4].astype(F32), 0.0)
    cols = gup_ref.shape[1]
    gap = HALF - cols
    gup_ref[...] = total[:, :cols]
    gdown_ref[...] = total[:, HALF : HALF + cols]
    gout_ref[:, :gap] = total[:, cols:HALF]
    gout_ref[:, gap:] = total[:, HALF + cols : HALF + cols + width - gap]
    for copy in q_copies:
        copy.wait_recv()
    total = gq_own[dp].astype(F32)
    for d in range(7):
        total = total + gq_in[d].astype(F32)
    for i in range(3):
        gq_ref[i] = total[:, i * width : (i + 1) * width]
    total = gb_in[0]
    for d in range(1, 8):
        total = total + gb_in[d]
    gb_ref[0:1, :] = total[0:1, :width]
    gb_ref[1:2, :] = total[0:1, 2 * width :]

    wide = one_ref[...] + part_out[0].astype(F32)
    left = jnp.where(mp > 0, chain[mp].astype(F32), 0.0)
    right = jnp.where(mp < 3, chain[4].astype(F32), 0.0)
    fg_ref[...] = (wide + left + right).astype(BF16)
    for name in (1, 2, 3):
        for half in range(2):
            chain_copy(name, half, 0, mp ^ 1).wait_send()
        fresh_copy(name, 0, mp ^ 1).wait_send()
    for s in range(4):
        far(s).wait_send()
        near(s, 0).wait_send()
        near(s, 1).wait_send()
    for at in range(len(partners)):
        swap(at).wait_send()
    for copy in q_copies:
        copy.wait_send()


def back_pass(qs, ka, va, kk, mixed, up, sums, frames, wq, one_grad, small, hidden_cols):
    slots, rows, _ = qs.shape
    depth = frames.shape[1]
    share = rows // 4
    piece, lanes = sums.shape[2:]
    cols = wq.shape[1]
    vmem = pl.BlockSpec(memory_space=pltpu.VMEM)
    hbm = pl.BlockSpec(memory_space=pltpu.MemorySpace.HBM)
    dma = pltpu.SemaphoreType.DMA
    V = pltpu.VMEM
    return pl.pallas_call(
        functools.partial(back_kernel, slots),
        in_specs=[vmem] * 7 + [hbm] + [vmem] * 3,
        out_specs=[vmem] * 13,
        out_shape=[
            jax.ShapeDtypeStruct((share, depth), BF16),
            jax.ShapeDtypeStruct((3, piece, cols // 3), F32),
            jax.ShapeDtypeStruct((2, cols // 3), F32),
            jax.ShapeDtypeStruct((piece, hidden_cols), F32),
            jax.ShapeDtypeStruct((piece, hidden_cols), F32),
            jax.ShapeDtypeStruct((piece, cols // 3), F32),
            jax.ShapeDtypeStruct((hidden_cols,), F32),
        ]
        + [jax.ShapeDtypeStruct((depth,), F32)] * 6,
        scratch_shapes=[
            V((slots, rows, VAUG), BF16), V((slots, HD, rows), BF16), V((slots, HD, rows), BF16),
            V((slots, rows, HD), F32), V((slots, HD, rows), F32), V((slots, HD, rows), F32),
            V((share // 2, cols), BF16), V((4, share, depth), BF16), V((5, share, depth), BF16),
            V((4, piece, lanes), BF16), V((4, piece, lanes), BF16), V((4, 2, piece, lanes), BF16),
            V((4, piece, lanes), BF16), V((5, piece, lanes), BF16),
            V((8, piece, cols), BF16), V((7, piece, cols), BF16),
            V((8, cols), F32), V((8, 8, cols), F32), V((5,) + small.shape, F32), V((5,) + small.shape, F32),
            dma((4, 2)), dma((5, 2)), dma((4,)), dma((4,)), dma((4, 2)), dma((4, 2)), dma((4,)), dma((5,)),
            dma((7,)), dma((7,)), dma((7,)), dma((7,)), dma((5,)), dma((5,)), V(small.shape, F32),
            V((share // 2, depth), BF16), dma((1,)), V((depth, cols), F32),
        ],
        compiler_params=pltpu.CompilerParams(
            collective_id=3, has_side_effects=True, vmem_limit_bytes=34 << 20
        ),
        name="back_pass",
    )(qs, ka, va, kk, mixed, up, sums, frames, wq, one_grad, small)


def deliver_kernel(count, *refs):
    sources, results, sem = refs[:count], refs[count : 2 * count], refs[2 * count]
    copies = [
        pltpu.make_async_copy(a, b, sem.at[i]) for i, (a, b) in enumerate(zip(sources, results))
    ]
    for copy in copies:
        copy.start()
    for copy in copies:
        copy.wait()


def deliver(arrays):
    count = len(arrays)
    return pl.pallas_call(
        functools.partial(deliver_kernel, count),
        in_specs=[pl.BlockSpec(memory_space=pltpu.VMEM)] * count,
        out_specs=[pl.BlockSpec(memory_space=pltpu.MemorySpace.HBM)] * count,
        out_shape=[jax.ShapeDtypeStruct(a.shape, a.dtype) for a in arrays],
        scratch_shapes=[pltpu.SemaphoreType.DMA((count,))],
        compiler_params=pltpu.CompilerParams(vmem_limit_bytes=4 << 20),
        name="deliver",
    )(*arrays)


def body(
    frames, seg_ids, qkv_weight, qkv_bias, out_weight, out_bias, gain_one, shift_one,
    up_weight, up_bias, down_weight, down_bias, gain_two, shift_two, cotangent,
):
    rows, depth = frames.shape
    mp_size = lax.axis_size("mp")
    dp_size = lax.axis_size("dp")
    mp_index = lax.axis_index("mp")
    share = rows // mp_size
    slots = qkv_weight.shape[2] // HD
    width = slots * HD
    hidden_cols = up_weight.shape[1]
    piece = qkv_weight.shape[1]
    gap = HALF - hidden_cols
    spare = -(HALF + hidden_cols + width - gap) % 128
    live_count = HEADS // mp_size + (mp_index < HEADS % mp_size).astype(jnp.int32)
    live = (jnp.arange(slots) < live_count).astype(F32)

    in_hbm = lambda a: pltpu.with_memory_space_constraint(a, pltpu.MemorySpace.HBM)
    out_flip = out_weight.T
    down_flip = down_weight.T
    vectors = (out_bias, gain_one, shift_one, down_bias, gain_two, shift_two)
    linked = (dp_size, mp_size, slots, rows) == (8, 4, 3, 2048)
    if linked:
        weights, qkv_full, ub_full, qs, ka, va, kk, mixed, got = front(
            *map(in_hbm, (frames, qkv_weight, up_weight, down_flip, out_flip)), up_bias, qkv_bias,
            seg_ids, slots,
        )
        weights = weights.reshape(mp_size, depth, -1)
    else:
        wq = jnp.transpose(qkv_weight, (1, 0, 2)).reshape(piece, 3 * width)
        packed = jnp.concatenate(
            [up_weight, out_flip[:, :gap], down_flip, out_flip[:, gap:], jnp.zeros((piece, spare), BF16)], 1
        )
        ub_pad = jnp.pad(up_bias, (0, gap))[None]
        offsets = jnp.concatenate([qkv_bias[0], jnp.zeros_like(qkv_bias[0]), qkv_bias[1]])[None]
        qkv_full = lax.all_gather(wq, "dp", axis=0, tiled=True)
        weights = lax.all_gather(packed, "mp", axis=0, tiled=False)
        weights = lax.all_gather(weights, "dp", axis=1, tiled=True)
        ub_full = lax.all_gather(ub_pad, "mp", axis=0, tiled=False)
        qs, ka, va, kk = project(frames, qkv_full, offsets, seg_ids, slots)
        qs, mixed = attend(qs, ka, va)
        mixed_low = (mixed * live[:, None, None]).astype(BF16)
        sent = mixed_low.reshape(slots, mp_size, share, HD).transpose(1, 2, 0, 3)
        got = lax.all_to_all(sent.reshape(mp_size, share, width), "mp", 0, 0, tiled=True)
    output_frames, sum_one_grad, back, partial, small = middle(
        in_hbm(frames), in_hbm(cotangent), got, weights, ub_full, vectors, hidden_cols, linked
    )
    if linked:
        made = back_pass(
            qs, ka, va, kk, mixed, back, partial, in_hbm(frames), qkv_full, sum_one_grad, small, hidden_cols
        )
        output_frames, *made = deliver([output_frames, *made])
        return (
            output_frames, made[0], made[1], made[2], made[5].T, made[7], made[8], made[9], made[3],
            made[6], made[4].T, made[10], made[11], made[12],
        )
    if not linked:
        back = lax.all_to_all(back, "mp", 0, 0, tiled=True)
        back = back.reshape(rows, slots, HD).transpose(1, 0, 2)
        partial = lax.psum_scatter(partial, "dp", scatter_dimension=1, tiled=True)
        partial = lax.psum_scatter(partial, "mp", scatter_dimension=0, tiled=True)[0].astype(F32)
        small = lax.psum(small, ("dp", "mp"))
        kk = kk.reshape(rows, slots, HD).transpose(1, 0, 2)
        dq, dk, dv = attend_back(qs, ka, va, kk, mixed, back)
        grads_low = jnp.stack([dq, dk, dv]).transpose(2, 0, 1, 3).reshape(rows, 3 * width)
        bias_sums = lax.psum(jnp.sum(grads_low.astype(F32), 0), "dp")
        grad_qkv = jnp.einsum("rd,rs->ds", frames, grads_low, preferred_element_type=F32)
        arrived = lax.all_to_all(
            grad_qkv.astype(BF16).reshape(dp_size, piece, 3 * width), "dp", 0, 0, tiled=True
        )
        grad_qkv = arrived.astype(F32).sum(0)
        input_part = jnp.einsum("rs,ds->rd", grads_low, qkv_full, preferred_element_type=F32)
        input_sum = lax.psum_scatter(input_part.astype(BF16), "mp", scatter_dimension=0, tiled=True)
        frames_grad = (input_sum.astype(F32) + sum_one_grad).astype(BF16)
    grad_qkv = grad_qkv.reshape(piece, 3, width).transpose(1, 0, 2)
    bias_sums = bias_sums.reshape(3, width)
    qkv_bias_grad = jnp.stack([bias_sums[0], bias_sums[2]])
    out_grad = jnp.concatenate(
        [partial[:, hidden_cols:HALF], partial[:, HALF + hidden_cols : HALF + hidden_cols + width - gap]], 1
    )
    return (
        output_frames,
        frames_grad,
        grad_qkv,
        qkv_bias_grad,
        out_grad.T,
        small[0],
        small[1],
        small[2],
        partial[:, :hidden_cols],
        lax.dynamic_index_in_dim(small, 8 + mp_index, 0, False)[:hidden_cols],
        partial[:, HALF : HALF + hidden_cols].T,
        small[3],
        small[4],
        small[5],
    )


def solution(mesh):
    in_specs = (
        P("dp", None), P("dp"), P(None, "dp", "mp"), P(None, "mp"), P("mp", "dp"), P(), P(), P(),
        P("dp", "mp"), P("mp"), P("mp", "dp"), P(), P(), P(), P("dp", None),
    )
    out_specs = (
        P(("dp", "mp"), None), P(("dp", "mp"), None), P(None, "dp", "mp"), P(None, "mp"),
        P("mp", "dp"), P(), P(), P(), P("dp", "mp"), P("mp"), P("mp", "dp"), P(), P(), P(),
    )
    return jax.shard_map(body, mesh=mesh, in_specs=in_specs, out_specs=out_specs, check_vma=False)
```

```python
import functools
import math

import jax
import jax.numpy as jnp
from jax import lax
from jax.experimental import pallas as pl
from jax.experimental.pallas import tpu as pltpu
from jax.sharding import PartitionSpec as P

HEADS = 10
HD = 64
EPS = 1e-05
SCALE = 0.125
MAX_SEGS = 16
MASKED = -1e30
UNIT = SCALE * math.log2(math.e)
AUG = 256
VAUG = 128
NT = (((1,), (1,)), ((), ()))
TN = (((0,), (0,)), ((), ()))
F32 = jnp.float32
BF16 = jnp.bfloat16
VMEM_LIMIT = 56 << 20
MESH = pl.DeviceIdType.MESH
CHIPS = 3
HALF = 640


def thirds(wide):
    first = wide.astype(BF16)
    rest = wide - first.astype(F32)
    second = rest.astype(BF16)
    third = (rest - second.astype(F32)).astype(BF16)
    return first, second, third


def lane_marks(rows, width, count):
    return lax.broadcasted_iota(jnp.int32, (rows, width), 1) < count


def spread_rows(made, picked, slots, qs_ref, ka_ref, va_ref, kk_ref, rows):
    count = made.shape[0]
    width = slots * HD
    chosen = picked.astype(BF16)
    barred = ((picked - 1.0) * -MASKED).astype(BF16)
    tail = AUG - 3 * HD - MAX_SEGS
    q_tail = jnp.zeros((count, tail), BF16)
    minus = jnp.where(lane_marks(count, tail, 3), -1.0, 0.0).astype(BF16)
    v_tail = jnp.where(lane_marks(count, VAUG - HD, 3), -1.0, 0.0).astype(BF16)
    for slot in range(slots):
        at = slot * HD
        q = made[:, at : at + HD]
        k = made[:, width + at : width + at + HD]
        v = made[:, 2 * width + at : 2 * width + at + HD]
        one, two, three = thirds(k.astype(F32) * UNIT)
        qs_ref[slot, rows, :] = jnp.concatenate([q, q, q, chosen, q_tail], 1)
        ka_ref[slot, rows, :] = jnp.concatenate([one, two, three, barred, minus], 1)
        va_ref[slot, rows, :] = jnp.concatenate([v, v_tail], 1)
    kk_ref[rows, :] = made[:, width : 2 * width]


def announce(peers):
    for peer in peers:
        pl.semaphore_signal(
            pltpu.get_barrier_semaphore(), inc=1, device_id=peer, device_id_type=MESH
        )


def await_peers(count):
    pl.semaphore_wait(pltpu.get_barrier_semaphore(), count)


def remote(src, dst, send, recv, peer):
    return pltpu.make_async_remote_copy(
        src_ref=src, dst_ref=dst, send_sem=send, recv_sem=recv, device_id=peer, device_id_type=MESH
    )


def pack_rows(wide):
    half = wide.shape[0] // 2
    third = wide[:, 2 * HD :]
    return jnp.concatenate(
        [wide[:, : 2 * HD], jnp.concatenate([third[:half], third[half:]], 1)], 0
    )


def unpack_rows(packed):
    rows = packed.shape[0] * 2 // 3
    rest = packed[rows:]
    return jnp.concatenate(
        [packed[:rows], jnp.concatenate([rest[:, :HD], rest[:, HD:]], 0)], 1
    )


def front_kernel(
    slots, sub,
    x_hbm, qkv_hbm, up_hbm, down_hbm, out_hbm, ub_ref, qb_ref, seg_ref,
    all_ref, wfull_ref, ball_ref, qs_ref, ka_ref, va_ref, kk_ref, mixed_ref, got_ref,
    x_ref, qkv_ref, up_ref, down_ref, out_ref, stage, wq_ref, pack_ref, bias_ref,
    q_send, q_recv, z_send, z_recv, w_send, w_recv, b_send, b_recv, a_send, a_recv, here, loaded,
):
    dp = lax.axis_index("dp")
    mp = lax.axis_index("mp")
    plane = [dp ^ 2, dp ^ 4, dp ^ 6]
    sibling = (dp ^ 1, mp)
    tall = [(dp, mp ^ s) for s in range(1, 4)]
    inner = (mp == 1) | (mp == 2)
    announce([sibling] + [(d, mp) for d in plane] + tall)
    width = slots * HD
    pairs = ((qkv_hbm, qkv_ref), (up_hbm, up_ref), (down_hbm, down_ref), (out_hbm, out_ref), (x_hbm, x_ref))
    loads = [pltpu.make_async_copy(a, b, loaded.at[i]) for i, (a, b) in enumerate(pairs)]
    for copy in loads:
        copy.start()
    bias_ref[...] = jnp.zeros_like(bias_ref)
    bias_ref[:, : up_hbm.shape[1]] = ub_ref[...].reshape(1, up_hbm.shape[1])
    loads[0].wait()
    for i in range(3):
        wq_ref[:, i * width : (i + 1) * width] = qkv_ref[i]
    await_peers(7)
    rows = x_ref.shape[0]
    share = rows // 4

    piece = wq_ref.shape[0]

    def rows_of(d):
        return wfull_ref.at[pl.ds(pl.multiple_of(d * piece, piece), piece)]

    mine = pltpu.make_async_copy(wq_ref, rows_of(dp), here.at[0])
    mine.start()
    firsts = [
        remote(wq_ref, rows_of(dp), q_send.at[i], q_recv.at[i], (plane[i], mp))
        for i in range(CHIPS)
    ]
    for copy in firsts:
        copy.start()
    shared = [remote(wq_ref, rows_of(dp), q_send.at[3], q_recv.at[3], sibling)]
    shared[0].start()
    for copy in loads[1:4]:
        copy.wait()
    hidden_cols = up_ref.shape[1]
    gap = HALF - hidden_cols
    rest = width - gap
    pack_ref[:, :hidden_cols] = up_ref[...]
    pack_ref[:, hidden_cols:HALF] = out_ref[:, :gap]
    pack_ref[:, HALF : HALF + hidden_cols] = down_ref[...]
    pack_ref[:, HALF + hidden_cols : HALF + hidden_cols + rest] = out_ref[:, gap:]
    spare = pack_ref.shape[1] - HALF - hidden_cols - rest
    pack_ref[:, HALF + hidden_cols + rest :] = jnp.zeros((pack_ref.shape[0], spare), BF16)
    own = pltpu.make_async_copy(pack_ref, all_ref.at[mp, dp], here.at[1])
    own.start()
    def lift(at, s, landing, peer):
        ref = all_ref.at[mp ^ s, dp]
        return remote(pack_ref if s == 0 else ref, ref, z_send.at[at], z_recv.at[landing], peer)

    near, middle = tall[0], tall[2]
    lifts = [lift(0, 0, 1, near)]
    inner_lifts = [
        lift(1, 0, 3, middle), lift(2, 1, 2, middle), lift(3, 3, 2, near), lift(4, 2, 3, near),
    ]

    def arrive(s):
        lift(0, s, s, near).wait_recv()

    own_bias = pltpu.make_async_copy(bias_ref, ball_ref.at[mp], here.at[2])
    own_bias.start()
    lifts[0].start()

    @pl.when(inner)
    def _():
        inner_lifts[0].start()

    biases = [
        remote(bias_ref, ball_ref.at[mp], b_send.at[s], b_recv.at[s], tall[s]) for s in range(3)
    ]
    for copy in biases:
        copy.start()
    for i in range(CHIPS):
        firsts[i].wait_recv()
        passed = remote(
            rows_of(plane[i]), rows_of(plane[i]), q_send.at[4 + i], q_recv.at[4 + i], sibling
        )
        passed.start()
        shared.append(passed)
    own.wait()

    def weights(s, kind):
        group = mp ^ s
        block = {0: dp, 1: dp, 2: dp, 4: plane[0], 5: plane[1], 6: plane[2]}
        block[3] = plane[0] if s % 2 == 0 else plane[1]
        peer = {0: (plane[0], mp), 1: (plane[1], mp)}
        peer[3] = peer[1] if s % 2 == 0 else peer[0]
        ref = all_ref.at[group, block[kind]]
        return remote(ref, ref, w_send.at[s, kind], w_recv.at[s, kind], peer.get(kind, sibling))

    def start_weights(s):
        if s == 3:

            @pl.when(~inner)
            def _():
                arrive(3)

        for kind in (0, 1, 2):
            weights(s, kind).start()

    def pass_weights(s):
        weights(s, 0).wait_recv()
        weights(s, 1).wait_recv()
        for kind in (3, 4, 5):
            weights(s, kind).start()

    def last_weights(s):
        weights(s, 3).wait_recv()
        weights(s, 6).start()

    start_weights(0)
    mine.wait()
    for copy in shared:
        copy.wait_recv()
    arrive(1)

    @pl.when(inner)
    def _():
        inner_lifts[1].start()
        arrive(3)
        inner_lifts[2].start()

    start_weights(1)

    loads[4].wait()
    block = 512

    def project_rows(step, carry):
        part = pl.ds(pl.multiple_of(step * block, block), block)
        x = x_ref[part, :]
        offsets = jnp.concatenate(
            [qb_ref[0:1, :], jnp.zeros((1, width), F32), qb_ref[1:2, :]], 1
        )
        made = jnp.dot(x, wfull_ref[...], preferred_element_type=F32) + offsets
        marks = seg_ref[:, part] == lax.broadcasted_iota(jnp.int32, (MAX_SEGS, block), 0)
        picked = jnp.where(marks, 1.0, 0.0).T
        spread_rows(made.astype(BF16), picked, slots, qs_ref, ka_ref, va_ref, kk_ref, part)
        return carry

    lax.fori_loop(0, rows // block, project_rows, 0)
    arrive(2)

    @pl.when(inner)
    def _():
        inner_lifts[3].start()

    pass_weights(0)
    start_weights(2)

    live_count = HEADS // 4 + (mp < HEADS % 4).astype(jnp.int32)
    per_share = share // sub
    actions = {
        1: [(pass_weights, 1)],
        3: [(start_weights, 3)],
        4: [(last_weights, 0)],
        5: [(pass_weights, 2)],
        6: [(last_weights, 1)],
        7: [(pass_weights, 3)],
    }

    def send_rows(step, stage_index):
        return remote(
            stage.at[step], got_ref.at[mp, lax.rem(step, per_share)], a_send.at[step], a_recv.at[step],
            (dp, mp ^ stage_index),
        )

    def attend_rows(step, carry):
        stage_index = 3 - step // per_share
        group = mp ^ stage_index
        offset = lax.rem(step, per_share) * sub
        part = pl.ds(pl.multiple_of(group * share + offset, sub), sub)
        for when, todo in actions.items():

            @pl.when(step == when)
            def _():
                for act, s in todo:
                    act(s)

        kept = []
        scores = [
            lax.dot_general(qs_ref[slot, part, :], ka_ref[slot], NT, preferred_element_type=F32)
            for slot in range(slots)
        ]
        for slot in range(slots):
            x = scores[slot]
            top = jnp.max(x, -1, keepdims=True)
            p = jnp.exp2(x - top).astype(BF16)
            made = jnp.dot(p, va_ref[slot], preferred_element_type=F32)
            total = -made[:, HD : HD + 1]
            mixed = made[:, :HD] / total
            one, two, three = thirds(top + jnp.log2(total))
            base = 3 * HD + MAX_SEGS
            qs_ref[slot, part, base : base + 3] = jnp.concatenate([one, two, three], 1)
            mixed_ref[part, slot * HD : (slot + 1) * HD] = mixed
            alive = (slot < live_count).astype(F32)
            kept.append((mixed * alive).astype(BF16))
        stage[step] = pack_rows(jnp.concatenate(kept, 1))

        @pl.when(step < 3 * per_share)
        def _():
            send_rows(step, stage_index).start()

        return carry

    lax.fori_loop(0, rows // sub, attend_rows, 0)
    keep = pltpu.make_async_copy(
        stage.at[pl.ds(3 * per_share, per_share)], got_ref.at[mp], here.at[3]
    )
    keep.start()
    last_weights(2)
    last_weights(3)
    for s in range(4):
        weights(s, 2).wait_recv()
        for kind in (4, 5, 6):
            weights(s, kind).wait_recv()
        for kind in range(7):
            weights(s, kind).wait_send()
    for copy in firsts + shared + lifts:
        copy.wait_send()

    @pl.when(inner)
    def _():
        for copy in inner_lifts:
            copy.wait_send()

    for copy in biases:
        copy.wait()
    for step in range(3 * per_share):
        send_rows(step, 3 - step // per_share).wait()
    own_bias.wait()
    keep.wait()


def front(frames, qkv_weight, up_weight, down_flip, out_flip, up_bias, qkv_bias, seg_ids, slots):
    rows, depth = frames.shape
    piece, hidden_cols = up_weight.shape
    width = slots * HD
    lanes = -(-(2 * hidden_cols + width) // 128) * 128
    sub = 256
    shape = lambda n: jax.ShapeDtypeStruct((slots, rows, n), BF16)
    vmem = pl.BlockSpec(memory_space=pltpu.VMEM)
    hbm = pl.BlockSpec(memory_space=pltpu.MemorySpace.HBM)
    dma = pltpu.SemaphoreType.DMA
    steps = rows // sub
    operands = (frames, qkv_weight, up_weight, down_flip, out_flip)
    return pl.pallas_call(
        functools.partial(front_kernel, slots, sub),
        in_specs=[hbm] * 5 + [vmem] * 3,
        out_specs=[vmem] * 9,
        out_shape=[
            jax.ShapeDtypeStruct((4, 8, piece, lanes), BF16),
            jax.ShapeDtypeStruct((8 * piece, 3 * width), BF16),
            jax.ShapeDtypeStruct((4, 1, HALF), F32),
            shape(AUG), shape(AUG), shape(VAUG),
            jax.ShapeDtypeStruct((rows, width), BF16),
            jax.ShapeDtypeStruct((rows, width), F32),
            jax.ShapeDtypeStruct((4, steps // 4, sub * 3 // 2, 2 * HD), BF16),
        ],
        scratch_shapes=[
            pltpu.VMEM(frames.shape, BF16), pltpu.VMEM(qkv_weight.shape, BF16),
            pltpu.VMEM(up_weight.shape, BF16), pltpu.VMEM(down_flip.shape, BF16),
            pltpu.VMEM(out_flip.shape, BF16),
            pltpu.VMEM((steps, sub * 3 // 2, 2 * HD), BF16),
            pltpu.VMEM((piece, 3 * width), BF16), pltpu.VMEM((piece, lanes), BF16),
            pltpu.VMEM((1, HALF), F32),
            dma((7,)), dma((7,)), dma((5,)), dma((4,)), dma((4, 7)), dma((4, 7)), dma((3,)), dma((3,)),
            dma((steps,)), dma((steps,)), dma((4,)), dma((len(operands),)),
        ],
        compiler_params=pltpu.CompilerParams(
            collective_id=1, has_side_effects=True, vmem_limit_bytes=20 << 20
        ),
        name="front",
    )(*operands, up_bias, qkv_bias, seg_ids.reshape(1, rows))


def project_kernel(slots, x_ref, w_ref, b_ref, seg_ref, qs_ref, ka_ref, va_ref, kk_ref):
    made = jnp.dot(x_ref[...], w_ref[...], preferred_element_type=F32) + b_ref[...]
    marks = seg_ref[...] == lax.broadcasted_iota(jnp.int32, (x_ref.shape[0], MAX_SEGS), 1)
    spread_rows(
        made.astype(BF16), jnp.where(marks, 1.0, 0.0), slots, qs_ref, ka_ref, va_ref, kk_ref, slice(None)
    )


def project(frames, weight, offsets, seg_ids, slots):
    rows, depth = frames.shape
    block = min(512, rows)
    spread = lambda n: pl.BlockSpec((slots, block, n), lambda i: (0, i, 0))
    shape = lambda n: jax.ShapeDtypeStruct((slots, rows, n), BF16)
    return pl.pallas_call(
        functools.partial(project_kernel, slots),
        grid=(rows // block,),
        in_specs=[
            pl.BlockSpec((block, depth), lambda i: (i, 0)),
            pl.BlockSpec(weight.shape, lambda i: (0, 0)),
            pl.BlockSpec((1, offsets.shape[1]), lambda i: (0, 0)),
            pl.BlockSpec((block, 1), lambda i: (i, 0)),
        ],
        out_specs=[
            spread(AUG), spread(AUG), spread(VAUG), pl.BlockSpec((block, slots * HD), lambda i: (i, 0)),
        ],
        out_shape=[
            shape(AUG), shape(AUG), shape(VAUG), jax.ShapeDtypeStruct((rows, slots * HD), BF16),
        ],
        compiler_params=pltpu.CompilerParams(vmem_limit_bytes=VMEM_LIMIT),
        name="project",
    )(frames, weight, offsets, seg_ids.reshape(rows, 1))


def attend_kernel(sub, qs_ref, ka_ref, va_ref, qn_ref, mixed_ref):
    for at in range(0, qs_ref.shape[1], sub):
        part = slice(at, at + sub)
        x = lax.dot_general(qs_ref[0, part, :], ka_ref[0], NT, preferred_element_type=F32)
        top = jnp.max(x, -1, keepdims=True)
        p = jnp.exp2(x - top).astype(BF16)
        made = jnp.dot(p, va_ref[0], preferred_element_type=F32)
        total = -made[:, HD : HD + 1]
        mixed_ref[0, part, :] = made[:, :HD] / total
        one, two, three = thirds(top + jnp.log2(total))
        base = 3 * HD + MAX_SEGS
        blank = jnp.zeros((sub, AUG - base - 3), BF16)
        qn_ref[0, part, :] = jnp.concatenate(
            [qs_ref[0, part, :base], one, two, three, blank], 1
        )


def attend(qs, ka, va):
    slots, rows, _ = qs.shape
    block = min(512, rows)
    sub = min(256, block)
    whole = lambda n: pl.BlockSpec((1, rows, n), lambda h, i: (h, 0, 0))
    some = lambda n: pl.BlockSpec((1, block, n), lambda h, i: (h, i, 0))
    return pl.pallas_call(
        functools.partial(attend_kernel, sub),
        grid=(slots, rows // block),
        in_specs=[some(AUG), whole(AUG), whole(VAUG)],
        out_specs=[some(AUG), some(HD)],
        out_shape=[
            jax.ShapeDtypeStruct((slots, rows, AUG), BF16),
            jax.ShapeDtypeStruct((slots, rows, HD), F32),
        ],
        compiler_params=pltpu.CompilerParams(vmem_limit_bytes=VMEM_LIMIT),
        name="attend",
    )(qs, ka, va)


def attend_back_kernel(
    sub, qs_ref, ka_ref, va_ref, kk_ref, mixed_ref, up_ref, dq_ref, dk_ref, dv_ref, dk_acc, dv_acc
):
    step = pl.program_id(1)

    @pl.when(step == 0)
    def _():
        dk_acc[...] = jnp.zeros_like(dk_acc)
        dv_acc[...] = jnp.zeros_like(dv_acc)

    for at in range(0, qs_ref.shape[1], sub):
        part = slice(at, at + sub)
        q = qs_ref[0, part, :HD]
        up = up_ref[0, part, :]
        d_one, d_two, d_three = thirds(
            jnp.sum(up.astype(F32) * mixed_ref[0, part, :], -1, keepdims=True)
        )
        blank = lambda n: jnp.zeros((sub, n), BF16)
        upper = jnp.concatenate([up, d_one, d_two, d_three, blank(VAUG - HD - 3)], 1)
        x = lax.dot_general(qs_ref[0, part, :], ka_ref[0], NT, preferred_element_type=F32)
        p = jnp.exp2(x)
        dp = lax.dot_general(upper, va_ref[0], NT, preferred_element_type=F32)
        ds = (p * dp).astype(BF16)
        dv_acc[...] += lax.dot_general(up, p.astype(BF16), TN, preferred_element_type=F32)
        dk_acc[...] += lax.dot_general(q, ds, TN, preferred_element_type=F32)
        dq_ref[0, part, :] = (
            jnp.dot(ds, kk_ref[0], preferred_element_type=F32) * SCALE
        ).astype(BF16)

    @pl.when(step == pl.num_programs(1) - 1)
    def _():
        dk_ref[0] = (dk_acc[...] * SCALE).T.astype(BF16)
        dv_ref[0] = dv_acc[...].T.astype(BF16)


def attend_back(qs, ka, va, kk, mixed, up):
    slots, rows, _ = qs.shape
    block = min(512, rows)
    sub = min(256, block)
    whole = lambda n: pl.BlockSpec((1, rows, n), lambda h, i: (h, 0, 0))
    some = lambda n: pl.BlockSpec((1, block, n), lambda h, i: (h, i, 0))
    shape = jax.ShapeDtypeStruct((slots, rows, HD), BF16)
    return pl.pallas_call(
        functools.partial(attend_back_kernel, sub),
        grid=(slots, rows // block),
        in_specs=[
            some(AUG), whole(AUG), whole(VAUG), whole(HD), some(HD), some(HD),
        ],
        out_specs=[some(HD), whole(HD), whole(HD)],
        out_shape=[shape, shape, shape],
        scratch_shapes=[pltpu.VMEM((HD, rows), F32), pltpu.VMEM((HD, rows), F32)],
        compiler_params=pltpu.CompilerParams(vmem_limit_bytes=VMEM_LIMIT),
        name="attend_back",
    )(qs, ka, va, kk, mixed, up)


def norm_forward(summed):
    centre = summed - jnp.mean(summed, -1, keepdims=True)
    spread = jnp.mean(centre * centre, -1, keepdims=True)
    factor = lax.rsqrt(spread + EPS)
    return (centre * factor, factor)


def norm_backward(upper, normed, factor, gain):
    scaled = upper * gain
    return factor * (
        scaled
        - jnp.mean(scaled, -1, keepdims=True)
        - normed * jnp.mean(scaled * normed, -1, keepdims=True)
    )


def middle_kernel(
    groups, hidden_cols, block, linked,
    x_ref, y_ref, got_ref, w_ref, ub_ref, v0, v1, v2, v3, v4, v5,
    out_ref, s1_ref, back_ref, grad_ref, small_ref, *scratch,
):
    x_own, y_own, ow, act, pre_low, slope, hid_flip, two_flip, one_flip, here = scratch[:10]
    share = out_ref.shape[0]
    width = ow.shape[2]
    gap = HALF - hidden_cols
    dp = lax.axis_index("dp")
    mp = lax.axis_index("mp")
    rows = pl.ds(pl.multiple_of(mp * share, share), share)
    loads = [
        pltpu.make_async_copy(x_ref.at[rows], x_own, here.at[0]),
        pltpu.make_async_copy(y_ref.at[rows], y_own, here.at[1]),
    ]
    for copy in loads:
        copy.start()
    if linked:
        back_own, got, grads, arrived, b_send, b_recv, g_send, g_recv = scratch[10:]
        core = lax.rem(dp, 2)
        sibling = (dp ^ 1, mp)
        announce([sibling] + [(dp, mp ^ s) for s in range(1, 4)])
    else:
        back_own, got, grads = back_ref, got_ref, grad_ref
    out_bias, gain_one, shift_one, down_bias, gain_two, shift_two = (
        v[...].reshape(1, v.shape[0]) for v in (v0, v1, v2, v3, v4, v5)
    )
    for g in range(groups):
        ow[g, :, :gap] = w_ref[g, :, hidden_cols:HALF]
        ow[g, :, gap:] = w_ref[g, :, HALF + hidden_cols : HALF + hidden_cols + width - gap]
    small_ref[...] = jnp.zeros_like(small_ref)
    real = lane_marks(1, HALF, hidden_cols)
    alive = [
        lane_marks(1, width, HD * (HEADS // groups + (g < HEADS % groups))) for g in range(groups)
    ]
    for copy in loads:
        copy.wait()
    if linked:
        await_peers(4)

    def send_back(step, s):
        at = step * 3 + s - 1
        return remote(
            back_own.at[mp ^ s, step], back_ref.at[mp, step], b_send.at[at], b_recv.at[at], (dp, mp ^ s)
        )

    def some_rows(step, carry):
        part = pl.ds(pl.multiple_of(step * block, block), block)
        summed = x_own[part, :].astype(F32) + out_bias
        for g in range(groups):
            if linked:
                got[g, part, :] = unpack_rows(got_ref[g, step])
            summed += lax.dot_general(got[g, part, :], ow[g], NT, preferred_element_type=F32)
        normed_one, factor_one = norm_forward(summed)
        hidden = normed_one * gain_one + shift_one
        hidden_low = hidden.astype(BF16)
        hid_flip[:, part] = hidden_low.T
        feed = hidden + down_bias
        dots = [
            jnp.dot(hidden_low, w_ref[g, :, :HALF], preferred_element_type=F32)
            for g in range(groups)
        ]
        for g in range(groups):
            pre = dots[g] + ub_ref[g]
            half = 0.5 + 0.5 * lax.erf(pre * math.sqrt(0.5))
            bell = jnp.exp(pre * pre * -0.5) * (pre * (1.0 / math.sqrt(2.0 * math.pi)))
            slope[g] = jnp.where(real, half + bell, 0.0)
            made = jnp.where(real, pre * half, 0.0).astype(BF16)
            act[g, part, :] = made
        for g in range(groups):
            feed += lax.dot_general(
                act[g, part, :], w_ref[g, :, HALF : 2 * HALF], NT, preferred_element_type=F32
            )
        normed_two, factor_two = norm_forward(feed)
        out_ref[part, :] = (normed_two * gain_two + shift_two).astype(BF16)
        upstream = y_own[part, :].astype(F32)
        two_grad = norm_backward(upstream, normed_two, factor_two, gain_two)
        sum_two = two_grad.astype(BF16)
        two_flip[:, part] = sum_two.T
        hidden_grad = two_grad
        dots = [
            jnp.dot(sum_two, w_ref[g, :, HALF : 2 * HALF], preferred_element_type=F32)
            for g in range(groups)
        ]
        for g in range(groups):
            low = (slope[g] * dots[g]).astype(BF16)
            pre_low[g, part, :] = low
            small_ref[8 + g : 9 + g, :] += jnp.sum(low.astype(F32), 0, keepdims=True)
        for g in range(groups):
            hidden_grad += lax.dot_general(
                pre_low[g, part, :], w_ref[g, :, :HALF], NT, preferred_element_type=F32
            )
        one_grad = norm_backward(hidden_grad, normed_one, factor_one, gain_one)
        sum_one = one_grad.astype(BF16)
        s1_ref[part, :] = one_grad
        one_flip[:, part] = sum_one.T
        for g in range(groups):
            made = jnp.dot(sum_one, ow[g], preferred_element_type=F32)
            made = jnp.where(alive[g], made, 0.0).astype(BF16)
            if linked:
                back_own[g, step] = pack_rows(made)
            else:
                back_own[g, part, :] = made
        if linked:
            for s in range(1, 4):
                send_back(step, s).start()
        for at, term in enumerate((
            sum_one.astype(F32), hidden_grad * normed_one, hidden_grad,
            sum_two.astype(F32), upstream * normed_two, upstream,
        )):
            small_ref[at : at + 1, :] += jnp.sum(term, 0, keepdims=True)
        return carry

    lax.fori_loop(0, share // block, some_rows, 0)
    if linked:
        keep = pltpu.make_async_copy(back_own.at[mp], back_ref.at[mp], here.at[2])
        keep.start()
    depth = hid_flip.shape[0]
    rest = width - gap
    spare = w_ref.shape[2] - HALF - hidden_cols - rest
    span = depth // 2
    shared = []
    for g in range(groups):
        for part in range(2):
            cols = slice(part * span, (part + 1) * span)
            made = jnp.dot(hid_flip[cols], pre_low[g], preferred_element_type=F32).astype(BF16)
            grad_out = jnp.dot(one_flip[cols], got[g], preferred_element_type=F32).astype(BF16)
            left = jnp.concatenate([made[:, :hidden_cols], grad_out[:, :gap]], 1)
            made = jnp.dot(two_flip[cols], act[g], preferred_element_type=F32).astype(BF16)
            right = jnp.concatenate(
                [made[:, :hidden_cols], grad_out[:, gap:], jnp.zeros((span, spare), BF16)], 1
            )
            if not linked:
                grads[g, cols, :HALF] = left
                grads[g, cols, HALF:] = right
                continue
            piece = grad_ref.shape[2]
            for i in range(span // piece):
                d = part * (span // piece) + i
                at = slice(i * piece, (i + 1) * piece)

                @pl.when(core == d % 2)
                def _():
                    grad_ref[g, d // 2, :, :HALF] = left[at]
                    grad_ref[g, d // 2, :, HALF:] = right[at]

                @pl.when(core != d % 2)
                def _():
                    grads[g, d // 2, :, :HALF] = left[at]
                    grads[g, d // 2, :, HALF:] = right[at]

        if linked:
            copy = remote(grads.at[g], arrived.at[g], g_send.at[g], g_recv.at[g], sibling)
            copy.start()
            shared.append(copy)
    if linked:
        for g in range(groups):
            shared[g].wait_recv()
            for c in range(4):
                grad_ref[g, c] += arrived[g, c]
        for step in range(share // block):
            for s in range(1, 4):
                send_back(step, s).wait()
        for copy in shared:
            copy.wait_send()
        keep.wait()


def middle(frames, cotangent, got, weights, up_bias, vectors, hidden_cols, linked):
    groups = got.shape[0]
    share, depth = frames.shape[0] // groups, frames.shape[1]
    lanes = weights.shape[2]
    width = 3 * HD
    block = min(256, share)
    vmem = pl.BlockSpec(memory_space=pltpu.VMEM)
    rest = pl.BlockSpec(memory_space=pltpu.MemorySpace.HBM)
    dma = pltpu.SemaphoreType.DMA
    scratch = [
        pltpu.VMEM((share, depth), BF16),
        pltpu.VMEM((share, depth), BF16),
        pltpu.VMEM((groups, depth, width), BF16),
        pltpu.VMEM((groups, share, HALF), BF16),
        pltpu.VMEM((groups, share, HALF), BF16),
        pltpu.VMEM((groups, block, HALF), F32),
        pltpu.VMEM((depth, share), BF16),
        pltpu.VMEM((depth, share), BF16),
        pltpu.VMEM((depth, share), BF16),
        dma((3,)),
    ]
    grads = jax.ShapeDtypeStruct(weights.shape, BF16)
    if linked:
        piece = depth // 8
        grads = jax.ShapeDtypeStruct((groups, 4, piece, lanes), BF16)
        sends = 3 * (share // block)
        scratch += [
            pltpu.VMEM(got.shape, BF16),
            pltpu.VMEM((groups, share, width), BF16),
            pltpu.VMEM((groups, 4, piece, lanes), BF16),
            pltpu.VMEM((groups, 4, piece, lanes), BF16),
            dma((sends,)), dma((sends,)), dma((groups,)), dma((groups,)),
        ]
    extra = dict(collective_id=2, has_side_effects=True) if linked else {}
    return pl.pallas_call(
        functools.partial(middle_kernel, groups, hidden_cols, block, linked),
        in_specs=[rest, rest] + [vmem] * 9,
        out_specs=[vmem] * 5,
        out_shape=[
            jax.ShapeDtypeStruct((share, depth), BF16),
            jax.ShapeDtypeStruct((share, depth), F32),
            jax.ShapeDtypeStruct(got.shape, BF16),
            grads,
            jax.ShapeDtypeStruct((16, HALF), F32),
        ],
        scratch_shapes=scratch,
        compiler_params=pltpu.CompilerParams(
            vmem_limit_bytes=33 << 20 if linked else VMEM_LIMIT, **extra
        ),
        name="middle",
    )(frames, cotangent, got, weights, up_bias, *vectors)


STEPS = (
    (3, 3, 0), (3, 0, 0), (3, 1, 0), (3, 2, 0), (3, 0, 1), (3, 1, 1), (3, 2, 1),
    (2, 2, 0), (2, 0, 0), (2, 1, 0), (2, 0, 1), (2, 1, 1), (1, 1, 0), (1, 0, 0), (1, 0, 1), (0, 0, 0),
)
ENDS = {3: (3, 0), 6: (3, 1), 9: (2, 0), 11: (2, 1), 13: (1, 0), 14: (1, 1)}


def pick(table, step):
    made = jnp.int32(table[0])
    for at in range(1, len(table)):
        made = jnp.where(step >= at, jnp.int32(table[at]), made)
    return made


def back_kernel(
    slots,
    qs_ref, ka_ref, va_ref, kk_ref, mixed_ref, up_ref, sums_ref, x_hbm, wq_ref, one_ref, small_ref,
    fg_ref, gq_ref, gb_ref, gup_ref, gdown_ref, gout_ref, gub_ref, s0, s1, s2, s3, s4, s5,
    upper, up_flip, q_flip, dq_acc, dk_acc, dv_acc, low, part_out, chain, fresh, far_in, near_in, third,
    fresh_in, gq_own, gq_in, gb_own, gb_in, tiny, tiny_in,
    c_send, c_recv, f_send, f_recv, n_send, n_recv, t_send, t_recv, q_send, q_recv, b_send, b_recv,
    s_send, s_recv, small_sum, x_ref, loaded, gq_acc,
):
    dp = lax.axis_index("dp")
    mp = lax.axis_index("mp")
    chip = dp // 2
    rows, depth = x_hbm.shape
    share = rows // 4
    width = slots * HD
    others = [(dp ^ d, mp) for d in range(1, 8)]
    tall = [(dp, mp ^ s) for s in range(1, 4)]
    announce(others + tall)
    x_peer, y_peer = (dp ^ 2, mp), (dp ^ 4, mp)

    def rows_of(name):
        return pl.ds(pl.multiple_of((mp ^ name) * share, share), share)

    half_rows = share // 2

    def half_of(name, half):
        start = (mp ^ name) * share + half * half_rows
        return pl.ds(pl.multiple_of(start, half_rows), half_rows)

    def load_rows(name, half):
        return pltpu.make_async_copy(x_hbm.at[half_of(name, half)], x_ref, loaded.at[0])

    load_rows(3, 0).start()

    def far(s):
        return remote(
            sums_ref.at[mp ^ s, chip ^ 3], far_in.at[s], f_send.at[s], f_recv.at[s],
            y_peer if s % 2 == 0 else x_peer,
        )

    def near(s, kind):
        toward_x = (s % 2 == 0) == (kind == 1)
        source = third.at[s] if kind == 1 else sums_ref.at[mp ^ s, chip ^ (1 if toward_x else 2)]
        return remote(
            source, near_in.at[s, kind], n_send.at[s, kind], n_recv.at[s, kind],
            x_peer if toward_x else y_peer,
        )

    def begin_far(s):
        far(s).start()

    def begin_near(s):
        near(s, 0).start()

    def join_far(s):
        far(s).wait_recv()
        third[s] = sums_ref[mp ^ s, chip ^ (1 if s % 2 == 0 else 2)] + far_in[s]
        near(s, 1).start()

    def join_near(s):
        near(s, 0).wait_recv()
        near(s, 1).wait_recv()
        total = sums_ref[mp ^ s, chip].astype(F32) + near_in[s, 0].astype(F32)
        fresh[s] = (total + near_in[s, 1].astype(F32)).astype(BF16)

    partners = [(dp ^ 1, mp), (dp ^ 2, mp), (dp ^ 4, mp), (dp, mp ^ 1), (dp, mp ^ 2)]

    def swap(at):
        return remote(tiny.at[at], tiny_in.at[at], s_send.at[at], s_recv.at[at], partners[at])

    def small_step(at):
        if at == 0:
            tiny[0] = small_ref[...]
        else:
            swap(at - 1).wait_recv()
            made = tiny[at - 1] + tiny_in[at - 1]
            if at == len(partners):
                small_sum[...] = made
                for row, ref in enumerate((s0, s1, s2, s3, s4, s5)):
                    ref[...] = made[row : row + 1, :].reshape(ref.shape)
                cols = gub_ref.shape[-1]
                gub_ref[...] = small_sum[pl.ds(8 + mp, 1), :cols].reshape(gub_ref.shape)
                return
            tiny[at] = made
        swap(at).start()

    def chain_copy(name, half, slot, target):
        at = pl.ds(half * half_rows, half_rows)
        return remote(
            part_out.at[name, at], chain.at[slot, at], c_send.at[name, half], c_recv.at[slot, half],
            (dp, target),
        )

    def fresh_copy(name, slot, target):
        return remote(
            fresh.at[name], fresh_in.at[slot], t_send.at[name], t_recv.at[slot], (dp, target)
        )

    inner = (mp == 1) | (mp == 2)

    def down_the_chain(block, copy):
        for leftward in (True, False):

            @pl.when((block < mp) == leftward)
            def _():
                target = mp - 1 if leftward else mp + 1
                copy(jnp.where(block == target, 4, block) if leftward else block, target).start()

    def relay(name, half):
        block = mp ^ name
        at = pl.ds(half * half_rows, half_rows)

        @pl.when(inner)
        def _():
            chain_copy(name, half, block, mp ^ 1).wait_recv()
            part_out[name, at] = (
                part_out[name, at].astype(F32) + chain[block, at].astype(F32)
            ).astype(BF16)

        down_the_chain(block, functools.partial(chain_copy, name, half))

    def relay_fresh(name):
        block = mp ^ name

        @pl.when(inner)
        def _():
            fresh_copy(name, block, mp ^ 1).wait_recv()
            fresh[name] = (fresh[name].astype(F32) + fresh_in[block].astype(F32)).astype(BF16)

        down_the_chain(block, functools.partial(fresh_copy, name))

    def end_fresh(name):
        @pl.when(~inner)
        def _():
            relay_fresh(name)

    def inner_fresh(name):
        @pl.when(inner)
        def _():
            relay_fresh(name)

    def finish(name, half):
        at = half_of(name, half)
        for slot in range(slots):
            col = slot * HD
            low[:, col : col + HD] = (dq_acc[slot, at, :] * SCALE).astype(BF16)
            low[:, width + col : width + col + HD] = (dk_acc[slot, :, at] * SCALE).T.astype(BF16)
            low[:, 2 * width + col : 2 * width + col + HD] = dv_acc[slot, :, at].T.astype(BF16)
        part_out[name, half * half_rows : (half + 1) * half_rows] = lax.dot_general(
            low[...], wq_ref[...], NT, preferred_element_type=F32
        ).astype(BF16)

    def add_rows(name, half):
        ones = jnp.ones((16, half_rows), BF16)
        gb_own[...] += jnp.dot(ones, low[...], preferred_element_type=F32)[0:8, :]
        load_rows(name, half).wait()
        gq_acc[...] += lax.dot_general(x_ref[...], low[...], TN, preferred_element_type=F32)
        if (name, half) != (0, 1):
            load_rows(name - half, 1 - half).start()

    dq_acc[...] = jnp.zeros_like(dq_acc)
    dk_acc[...] = jnp.zeros_like(dk_acc)
    dv_acc[...] = jnp.zeros_like(dv_acc)
    gq_acc[...] = jnp.zeros_like(gq_acc)
    gb_own[...] = jnp.zeros_like(gb_own)

    def prepare(step, carry):
        at = pl.ds(pl.multiple_of(step * share, share), share)
        wide = jnp.concatenate([unpack_rows(up_ref[step, i]) for i in range(up_ref.shape[1])], 0)
        for slot in range(slots):
            up = wide[:, slot * HD : (slot + 1) * HD]
            one, two, three = thirds(
                jnp.sum(
                    up.astype(F32) * mixed_ref[at, slot * HD : (slot + 1) * HD], -1, keepdims=True
                )
            )
            blank = jnp.zeros((share, VAUG - HD - 3), BF16)
            upper[slot, at, :] = jnp.concatenate([up, one, two, three, blank], 1)
            up_flip[slot, :, at] = up.T
            q_flip[slot, :, at] = qs_ref[slot, at, :HD].T
        return carry

    lax.fori_loop(0, 4, prepare, 0)
    await_peers(10)
    far(3).start()
    far(2).start()
    small_step(0)
    actions = {
        2: [(small_step, 1)],
        3: [(join_far, 3), (join_far, 2)],
        4: [(small_step, 2)],
        5: [(begin_near, 3), (begin_near, 2)],
        6: [(small_step, 3)],
        8: [(join_near, 3), (join_near, 2), (end_fresh, 3), (begin_far, 1), (begin_far, 0)],
        9: [(small_step, 4)],
        10: [(join_far, 1), (join_far, 0)],
        11: [(small_step, 5)],
        12: [(end_fresh, 2), (inner_fresh, 2), (begin_near, 1), (begin_near, 0)],
        15: [(join_near, 1), (join_near, 0), (end_fresh, 1), (inner_fresh, 1)],
    }

    def tiles(pairs):
        todo = [(slot, part, keys) for part, keys in pairs for slot in range(slots)]
        scores = [
            lax.dot_general(
                qs_ref[slot, part, :], ka_ref[slot, keys, :], NT, preferred_element_type=F32
            )
            for slot, part, keys in todo
        ]
        slopes = [
            lax.dot_general(
                upper[slot, part, :], va_ref[slot, keys, :], NT, preferred_element_type=F32
            )
            for slot, part, keys in todo
        ]
        probs = [jnp.exp2(x) for x in scores]
        lows = [(p * d).astype(BF16) for p, d in zip(probs, slopes)]
        for (slot, part, keys), p, ds in zip(todo, probs, lows):
            dv_acc[slot, :, keys] += jnp.dot(
                up_flip[slot, :, part], p.astype(BF16), preferred_element_type=F32
            )
            dk_acc[slot, :, keys] += jnp.dot(
                q_flip[slot, :, part], ds, preferred_element_type=F32
            )
            dq_acc[slot, part, :] += jnp.dot(
                ds, kk_ref[keys, slot * HD : (slot + 1) * HD], preferred_element_type=F32
            )

    def some_work(step, carry):
        name, other, half = (pick([s[i] for s in STEPS], step) for i in range(3))
        for when, todo in actions.items():

            @pl.when(step == when)
            def _():
                for act, s in todo:
                    act(s)

        @pl.when(name == other)
        def _():
            tiles([(rows_of(name), rows_of(name))])

        @pl.when(name != other)
        def _():
            tiles([(half_of(name, half), rows_of(other)), (rows_of(other), half_of(name, half))])

        for when, (n, h) in ENDS.items():

            @pl.when(step == when)
            def _():
                finish(n, h)
                if n == 3:

                    @pl.when(~inner)
                    def _():
                        relay(n, h)

                else:
                    relay(n, h)
                add_rows(n, h)

        @pl.when((step == 13) & inner)
        def _():
            relay(3, 0)

        return carry

    lax.fori_loop(0, len(STEPS), some_work, 0)
    for half in range(2):
        finish(0, half)
        add_rows(0, half)

    gb_in[dp] = gb_own[...]
    piece = depth // 8
    for d in range(8):
        gq_own[d] = gq_acc[d * piece : (d + 1) * piece, :].astype(BF16)
    q_copies = []
    for d in range(1, 8):
        to = dp ^ d
        q_copies.append(
            remote(gq_own.at[to], gq_in.at[d - 1], q_send.at[d - 1], q_recv.at[d - 1], others[d - 1])
        )
        q_copies.append(
            remote(gb_own, gb_in.at[dp], b_send.at[d - 1], b_recv.at[d - 1], others[d - 1])
        )
    for copy in q_copies:
        copy.start()
    @pl.when(inner)
    def _():
        relay(3, 1)
        relay_fresh(3)

    for half in range(2):

        @pl.when(mp > 0)
        def _():
            chain_copy(0, half, mp, mp ^ 1).wait_recv()

        @pl.when(mp < 3)
        def _():
            chain_copy(0, half, 4, mp ^ 1).wait_recv()

    @pl.when(mp > 0)
    def _():
        fresh_copy(0, mp, mp ^ 1).wait_recv()

    @pl.when(mp < 3)
    def _():
        fresh_copy(0, 4, mp ^ 1).wait_recv()

    total = fresh[0].astype(F32)
    total = total + jnp.where(mp > 0, fresh_in[mp].astype(F32), 0.0)
    total = total + jnp.where(mp < 3, fresh_in[4].astype(F32), 0.0)
    cols = gup_ref.shape[1]
    gap = HALF - cols
    gup_ref[...] = total[:, :cols]
    gdown_ref[...] = total[:, HALF : HALF + cols]
    gout_ref[:, :gap] = total[:, cols:HALF]
    gout_ref[:, gap:] = total[:, HALF + cols : HALF + cols + width - gap]
    for copy in q_copies:
        copy.wait_recv()
    total = gq_own[dp].astype(F32)
    for d in range(7):
        total = total + gq_in[d].astype(F32)
    for i in range(3):
        gq_ref[i] = total[:, i * width : (i + 1) * width]
    total = gb_in[0]
    for d in range(1, 8):
        total = total + gb_in[d]
    gb_ref[0:1, :] = total[0:1, :width]
    gb_ref[1:2, :] = total[0:1, 2 * width :]

    wide = one_ref[...] + part_out[0].astype(F32)
    left = jnp.where(mp > 0, chain[mp].astype(F32), 0.0)
    right = jnp.where(mp < 3, chain[4].astype(F32), 0.0)
    fg_ref[...] = (wide + left + right).astype(BF16)
    for name in (1, 2, 3):
        for half in range(2):
            chain_copy(name, half, 0, mp ^ 1).wait_send()
        fresh_copy(name, 0, mp ^ 1).wait_send()
    for s in range(4):
        far(s).wait_send()
        near(s, 0).wait_send()
        near(s, 1).wait_send()
    for at in range(len(partners)):
        swap(at).wait_send()
    for copy in q_copies:
        copy.wait_send()


def back_pass(qs, ka, va, kk, mixed, up, sums, frames, wq, one_grad, small, hidden_cols):
    slots, rows, _ = qs.shape
    depth = frames.shape[1]
    share = rows // 4
    piece, lanes = sums.shape[2:]
    cols = wq.shape[1]
    vmem = pl.BlockSpec(memory_space=pltpu.VMEM)
    hbm = pl.BlockSpec(memory_space=pltpu.MemorySpace.HBM)
    dma = pltpu.SemaphoreType.DMA
    V = pltpu.VMEM
    return pl.pallas_call(
        functools.partial(back_kernel, slots),
        in_specs=[vmem] * 7 + [hbm] + [vmem] * 3,
        out_specs=[vmem] * 13,
        out_shape=[
            jax.ShapeDtypeStruct((share, depth), BF16),
            jax.ShapeDtypeStruct((3, piece, cols // 3), F32),
            jax.ShapeDtypeStruct((2, cols // 3), F32),
            jax.ShapeDtypeStruct((piece, hidden_cols), F32),
            jax.ShapeDtypeStruct((piece, hidden_cols), F32),
            jax.ShapeDtypeStruct((piece, cols // 3), F32),
            jax.ShapeDtypeStruct((hidden_cols,), F32),
        ]
        + [jax.ShapeDtypeStruct((depth,), F32)] * 6,
        scratch_shapes=[
            V((slots, rows, VAUG), BF16), V((slots, HD, rows), BF16), V((slots, HD, rows), BF16),
            V((slots, rows, HD), F32), V((slots, HD, rows), F32), V((slots, HD, rows), F32),
            V((share // 2, cols), BF16), V((4, share, depth), BF16), V((5, share, depth), BF16),
            V((4, piece, lanes), BF16), V((4, piece, lanes), BF16), V((4, 2, piece, lanes), BF16),
            V((4, piece, lanes), BF16), V((5, piece, lanes), BF16),
            V((8, piece, cols), BF16), V((7, piece, cols), BF16),
            V((8, cols), F32), V((8, 8, cols), F32), V((5,) + small.shape, F32), V((5,) + small.shape, F32),
            dma((4, 2)), dma((5, 2)), dma((4,)), dma((4,)), dma((4, 2)), dma((4, 2)), dma((4,)), dma((5,)),
            dma((7,)), dma((7,)), dma((7,)), dma((7,)), dma((5,)), dma((5,)), V(small.shape, F32),
            V((share // 2, depth), BF16), dma((1,)), V((depth, cols), F32),
        ],
        compiler_params=pltpu.CompilerParams(
            collective_id=3, has_side_effects=True, vmem_limit_bytes=34 << 20
        ),
        name="back_pass",
    )(qs, ka, va, kk, mixed, up, sums, frames, wq, one_grad, small)


def deliver_kernel(count, *refs):
    sources, results, sem = refs[:count], refs[count : 2 * count], refs[2 * count]
    copies = [
        pltpu.make_async_copy(a, b, sem.at[i]) for i, (a, b) in enumerate(zip(sources, results))
    ]
    for copy in copies:
        copy.start()
    for copy in copies:
        copy.wait()


def deliver(arrays):
    count = len(arrays)
    return pl.pallas_call(
        functools.partial(deliver_kernel, count),
        in_specs=[pl.BlockSpec(memory_space=pltpu.VMEM)] * count,
        out_specs=[pl.BlockSpec(memory_space=pltpu.MemorySpace.HBM)] * count,
        out_shape=[jax.ShapeDtypeStruct(a.shape, a.dtype) for a in arrays],
        scratch_shapes=[pltpu.SemaphoreType.DMA((count,))],
        compiler_params=pltpu.CompilerParams(vmem_limit_bytes=4 << 20),
        name="deliver",
    )(*arrays)


def body(
    frames, seg_ids, qkv_weight, qkv_bias, out_weight, out_bias, gain_one, shift_one,
    up_weight, up_bias, down_weight, down_bias, gain_two, shift_two, cotangent,
):
    rows, depth = frames.shape
    mp_size = lax.axis_size("mp")
    dp_size = lax.axis_size("dp")
    mp_index = lax.axis_index("mp")
    share = rows // mp_size
    slots = qkv_weight.shape[2] // HD
    width = slots * HD
    hidden_cols = up_weight.shape[1]
    piece = qkv_weight.shape[1]
    gap = HALF - hidden_cols
    spare = -(HALF + hidden_cols + width - gap) % 128
    live_count = HEADS // mp_size + (mp_index < HEADS % mp_size).astype(jnp.int32)
    live = (jnp.arange(slots) < live_count).astype(F32)

    in_hbm = lambda a: pltpu.with_memory_space_constraint(a, pltpu.MemorySpace.HBM)
    out_flip = out_weight.T
    down_flip = down_weight.T
    vectors = (out_bias, gain_one, shift_one, down_bias, gain_two, shift_two)
    linked = (dp_size, mp_size, slots, rows) == (8, 4, 3, 2048)
    if linked:
        weights, qkv_full, ub_full, qs, ka, va, kk, mixed, got = front(
            *map(in_hbm, (frames, qkv_weight, up_weight, down_flip, out_flip)), up_bias, qkv_bias,
            seg_ids, slots,
        )
        weights = weights.reshape(mp_size, depth, -1)
    else:
        wq = jnp.transpose(qkv_weight, (1, 0, 2)).reshape(piece, 3 * width)
        packed = jnp.concatenate(
            [up_weight, out_flip[:, :gap], down_flip, out_flip[:, gap:], jnp.zeros((piece, spare), BF16)], 1
        )
        ub_pad = jnp.pad(up_bias, (0, gap))[None]
        offsets = jnp.concatenate([qkv_bias[0], jnp.zeros_like(qkv_bias[0]), qkv_bias[1]])[None]
        qkv_full = lax.all_gather(wq, "dp", axis=0, tiled=True)
        weights = lax.all_gather(packed, "mp", axis=0, tiled=False)
        weights = lax.all_gather(weights, "dp", axis=1, tiled=True)
        ub_full = lax.all_gather(ub_pad, "mp", axis=0, tiled=False)
        qs, ka, va, kk = project(frames, qkv_full, offsets, seg_ids, slots)
        qs, mixed = attend(qs, ka, va)
        mixed_low = (mixed * live[:, None, None]).astype(BF16)
        sent = mixed_low.reshape(slots, mp_size, share, HD).transpose(1, 2, 0, 3)
        got = lax.all_to_all(sent.reshape(mp_size, share, width), "mp", 0, 0, tiled=True)
    output_frames, sum_one_grad, back, partial, small = middle(
        in_hbm(frames), in_hbm(cotangent), got, weights, ub_full, vectors, hidden_cols, linked
    )
    if linked:
        made = back_pass(
            qs, ka, va, kk, mixed, back, partial, in_hbm(frames), qkv_full, sum_one_grad, small, hidden_cols
        )
        output_frames, *made = deliver([output_frames, *made])
        return (
            output_frames, made[0], made[1], made[2], made[5].T, made[7], made[8], made[9], made[3],
            made[6], made[4].T, made[10], made[11], made[12],
        )
    if not linked:
        back = lax.all_to_all(back, "mp", 0, 0, tiled=True)
        back = back.reshape(rows, slots, HD).transpose(1, 0, 2)
        partial = lax.psum_scatter(partial, "dp", scatter_dimension=1, tiled=True)
        partial = lax.psum_scatter(partial, "mp", scatter_dimension=0, tiled=True)[0].astype(F32)
        small = lax.psum(small, ("dp", "mp"))
        kk = kk.reshape(rows, slots, HD).transpose(1, 0, 2)
        dq, dk, dv = attend_back(qs, ka, va, kk, mixed, back)
        grads_low = jnp.stack([dq, dk, dv]).transpose(2, 0, 1, 3).reshape(rows, 3 * width)
        bias_sums = lax.psum(jnp.sum(grads_low.astype(F32), 0), "dp")
        grad_qkv = jnp.einsum("rd,rs->ds", frames, grads_low, preferred_element_type=F32)
        arrived = lax.all_to_all(
            grad_qkv.astype(BF16).reshape(dp_size, piece, 3 * width), "dp", 0, 0, tiled=True
        )
        grad_qkv = arrived.astype(F32).sum(0)
        input_part = jnp.einsum("rs,ds->rd", grads_low, qkv_full, preferred_element_type=F32)
        input_sum = lax.psum_scatter(input_part.astype(BF16), "mp", scatter_dimension=0, tiled=True)
        frames_grad = (input_sum.astype(F32) + sum_one_grad).astype(BF16)
    grad_qkv = grad_qkv.reshape(piece, 3, width).transpose(1, 0, 2)
    bias_sums = bias_sums.reshape(3, width)
    qkv_bias_grad = jnp.stack([bias_sums[0], bias_sums[2]])
    out_grad = jnp.concatenate(
        [partial[:, hidden_cols:HALF], partial[:, HALF + hidden_cols : HALF + hidden_cols + width - gap]], 1
    )
    return (
        output_frames,
        frames_grad,
        grad_qkv,
        qkv_bias_grad,
        out_grad.T,
        small[0],
        small[1],
        small[2],
        partial[:, :hidden_cols],
        lax.dynamic_index_in_dim(small, 8 + mp_index, 0, False)[:hidden_cols],
        partial[:, HALF : HALF + hidden_cols].T,
        small[3],
        small[4],
        small[5],
    )


def solution(mesh):
    in_specs = (
        P("dp", None), P("dp"), P(None, "dp", "mp"), P(None, "mp"), P("mp", "dp"), P(), P(), P(),
        P("dp", "mp"), P("mp"), P("mp", "dp"), P(), P(), P(), P("dp", None),
    )
    out_specs = (
        P(("dp", "mp"), None), P(("dp", "mp"), None), P(None, "dp", "mp"), P(None, "mp"),
        P("mp", "dp"), P(), P(), P(), P("dp", "mp"), P("mp"), P("mp", "dp"), P(), P(), P(),
    )
    return jax.shard_map(body, mesh=mesh, in_specs=in_specs, out_specs=out_specs, check_vma=False)
```
